32 devices in a mesh: tower: 2 (over core), dp: 16 (over z, y, x).
Axes of the slice: x: 2, y: 2, z: 4, core: 2. Of those that a mesh axis runs over, the one named last changes fastest.
Arguments:
- tokens: bfloat16 [2, 8192, 768], P('tower', 'dp'), may hold values from -6 to 6
- doc_ids: int32 [2, 8192], P('tower', 'dp'), may hold values from 0 to 11, as said below
- pad_mask: int32 [2, 8192], P('tower', 'dp'), may hold values 0 or 1
- targets: int32 [12], replicated, may hold values from 0 to 11, each once
- w_qkv: bfloat16 [768, 2304], replicated, may hold values from -0.21875 to 0.21875
- w_out: bfloat16 [768, 768], replicated, may hold values from -0.875 to 0.875
- ln1_gain: float32 [768], replicated, may hold values from 0.5 to 1.5
- ln1_bias: float32 [768], replicated, may hold values from -0.6 to 0.6
- w_gate: bfloat16 [768, 3072], replicated, may hold values from -0.21875 to 0.21875
- w_up: bfloat16 [768, 3072], replicated, may hold values from -0.21875 to 0.21875
- w_down: bfloat16 [3072, 768], replicated, may hold values from -0.109375 to 0.109375
- ln2_gain: float32 [768], replicated, may hold values from 0.5 to 1.5
- ln2_bias: float32 [768], replicated, may hold values from -0.6 to 0.6
Outputs:
- scores: float32 [12, 12], replicated
- loss: float32 [], replicated
- token_grad: float32 [2, 8192, 768], P('tower', 'dp')
- w_qkv_grad: float32 [768, 2304], P('dp')
- w_out_grad: float32 [768, 768], P('dp')
- ln1_gain_grad: float32 [768], P('dp')
- ln1_bias_grad: float32 [768], P('dp')
- w_gate_grad: float32 [768, 3072], P('dp')
- w_up_grad: float32 [768, 3072], P('dp')
- w_down_grad: float32 [3072, 768], P('dp')
- ln2_gain_grad: float32 [768], P('dp')
- ln2_bias_grad: float32 [768], P('dp')
The draws below stay inside these ranges and needn't reach their ends.
Inputs may be any that keep to these rules, and one draw needn't show every extreme that they name: `doc_ids`: within each tower the ids never fall; the k-th aligned group of 2048 slots holds exactly the documents k * 3 to k * 3 + 2, one of them exactly 1024 slots long. `targets`: each document of the second tower is the target of exactly one query.
All inputs are finite; a program needn't handle non-finite values. No bound on the sum of `pad_mask` on one device may be relied on, other than what follows from the above.
Results may differ from the reference program's by a relative error of at most 0.015.
Values may be sent and summed in bfloat16 or wider, within the bound.
A program may use at most 192 MiB of HBM per device.

```python
from functools import partial
import jax
import jax.numpy as jnp
from jax import lax

D = 768
HEADS = 12
HEAD_DIM = 64
FF = 3072
DOCS_GRP = 3
GROUP_TOK = 2048
MOST = 1024
GROUPS = 4
DOCS = 12
TOKENS = 8192


def draw_doc_ids(key, part):
    count = 2 * GROUPS
    cut_key, place_key = jax.random.split(key)
    shorter = jax.random.randint(cut_key, (count,), 1, MOST)
    placed = jax.random.randint(place_key, (count,), 0, 3)
    remain = MOST - shorter
    length_first = jnp.where(placed == 0, MOST, shorter)
    length_second = jnp.where(placed == 1, MOST, jnp.where(placed == 0, shorter, remain))
    slots = jnp.arange(GROUP_TOK, dtype=jnp.int32)[None, :]
    local = (slots >= length_first[:, None]).astype(jnp.int32) + (slots >= (length_first + length_second)[:, None]).astype(jnp.int32)
    groups = (jnp.arange(count, dtype=jnp.int32) % GROUPS)[:, None]
    return (local + DOCS_GRP * groups).reshape(2, TOKENS)


def plant(values, own_key, least, largest):
    longest = values.shape.index(max(values.shape))
    spots = []
    for shift in (0, 1):
        where = [jax.random.randint(jax.random.fold_in(own_key, axis), (), 0, length) for axis, length in enumerate(values.shape)]
        where[longest] = (where[longest] + shift) % values.shape[longest]
        spots.append(tuple(where))
    return values.at[spots[0]].set(least).at[spots[1]].set(largest)


def raised(values, own_key, source, target, blocks, factor):
    def block_of(axis_at):
        return (jnp.arange(values.shape[axis_at]) // (values.shape[axis_at] // blocks)).reshape((-1,) + (1,) * (values.ndim - 1 - axis_at))

    first = jax.random.permutation(own_key, blocks)[block_of(target)]
    other_side = (block_of(target) + blocks // 2) % blocks
    return jnp.where((block_of(source) == first) | (block_of(source) == other_side), factor * values, values)


def level_of(key, shape, shards, low, top_value):
    loudness = 1.0
    for position, blocks in shards:
        heights = jax.random.uniform(jax.random.fold_in(jax.random.fold_in(key, 6), position), (blocks,), jnp.float32, low / len(shards), top_value / len(shards))
        loudness = loudness * jnp.repeat(jnp.exp(heights), shape[position] // blocks).reshape((-1,) + (1,) * (len(shape) - 1 - position))
    return loudness


def bell_draw(key, extent, deviation, bound, shards=(), kind=jnp.bfloat16):
    level = level_of(key, extent, shards, -0.22, 0.18) if shards else 1.0
    result = jax.random.normal(key, extent, jnp.float32) * deviation * level
    return jnp.minimum(jnp.maximum(result, -bound), bound).astype(kind)


def heavy_noise(key, dims, scale, limit, shards, heavy, held_as=jnp.bfloat16):
    drawn = scale * jax.random.normal(key, dims, jnp.float32)
    if shards:
        drawn = drawn * level_of(key, dims, shards, -0.22, 0.18)
    return jnp.clip(raised(drawn, jax.random.fold_in(key, 3), *heavy), -limit, limit).astype(held_as)


def setup_inputs(seed: int = 0) -> dict:
    arg_keys = jax.random.split(jax.random.key(seed), 14)
    return {
        "tokens": heavy_noise(arg_keys[0], (2, TOKENS, D), 1.0, 6.0, ((0, 2), (1, 16)), (1, 2, 16, 2.0)),
        "doc_ids": draw_doc_ids(jax.random.fold_in(arg_keys[13], 71), 0),
        "pad_mask": plant((jax.random.randint(arg_keys[2], (2, TOKENS), 0, 8) < 7).astype(jnp.int32), jax.random.fold_in(arg_keys[2], 1), 0, 1),
        "targets": jax.random.permutation(arg_keys[3], DOCS).astype(jnp.int32),
        "w_qkv": bell_draw(arg_keys[4], (D, 3 * D), D ** -0.5, 0.21875),
        "w_out": bell_draw(arg_keys[5], (D, D), (D // 16) ** -0.5, 0.875),
        "ln1_gain": jnp.clip(1.0 + 0.1 * jax.random.normal(arg_keys[6], (D,), jnp.float32), 0.5, 1.5),
        "ln1_bias": bell_draw(arg_keys[7], (D,), 0.1, 0.6, (), jnp.float32),
        "w_gate": bell_draw(arg_keys[8], (D, FF), D ** -0.5, 0.21875),
        "w_up": bell_draw(arg_keys[9], (D, FF), D ** -0.5, 0.21875),
        "w_down": bell_draw(arg_keys[10], (FF, D), FF ** -0.5, 0.109375),
        "ln2_gain": jnp.clip(1.0 + 0.1 * jax.random.normal(arg_keys[11], (D,), jnp.float32), 0.5, 1.5),
        "ln2_bias": bell_draw(arg_keys[12], (D,), 0.1, 0.6, (), jnp.float32),
    }


precise = lax.Precision.HIGHEST
norm_eps = 1e-05

@jax.custom_vjp
def low(v):
    return lax.optimization_barrier(v.astype(jnp.bfloat16)).astype(jnp.float32)

@jax.custom_vjp
def low_back(v):
    return v

def low_keep(v):
    return (low(v), None)

def low_pass(kept, grad):
    return (grad,)

def back_keep(v):
    return (v, None)

def back_low(kept, grad):
    return (low(grad),)
low.defvjp(low_keep, low_pass)
low_back.defvjp(back_keep, back_low)

def angles_for(positions, half):
    freqs = 1000.0 ** (-jnp.arange(half, dtype=jnp.float32) / half)
    theta = positions.astype(jnp.float32)[:, None] * freqs[None, :]
    return (jnp.cos(theta)[:, None, :], jnp.sin(theta)[:, None, :])

def rotate(values, cosine, sine):
    half = values.shape[-1] // 2
    upper = values[..., :half]
    lower = values[..., half:]
    return jnp.concatenate([upper * cosine - lower * sine, lower * cosine + upper * sine], -1)

def norm_rows(values, gain, bias):
    centred = values - lax.optimization_barrier(jnp.mean(values, -1, keepdims=True))
    spread = lax.optimization_barrier(jnp.mean(centred * centred, -1, keepdims=True))
    return centred * lax.rsqrt(spread + norm_eps) * gain + bias

def group_pass(weights, block):
    w_qkv, w_out, gain_one, bias_one, w_gate, w_up, w_down, gain_two, bias_two = weights
    rows, ids, pads = block
    length = rows.shape[0]
    width = w_out.shape[0]
    tags = ids % DOCS_GRP
    cosine, sine = angles_for(jnp.arange(length), HEAD_DIM // 2)
    mixed = low_back(jnp.dot(rows, w_qkv, precision=precise))
    query = low(rotate(mixed[:, :width].reshape(length, HEADS, HEAD_DIM), cosine, sine))
    keys = low(rotate(mixed[:, width:2 * width].reshape(length, HEADS, HEAD_DIM), cosine, sine))
    values = low(mixed[:, 2 * width:].reshape(length, HEADS, HEAD_DIM))
    live = (tags[:, None] == tags[None, :]) & (pads[None, :] == 1)

    def attend(parts):
        head_query, head_keys, head_values = parts
        scores = low_back(jnp.dot(head_query, head_keys.T, precision=precise) * 0.125)
        masked = jnp.where(live, scores, -1e+30)
        top = lax.optimization_barrier(jnp.max(masked, -1, keepdims=True))
        expo = jnp.exp(masked - top)
        probs = low(expo / lax.optimization_barrier(jnp.sum(expo, -1, keepdims=True)))
        return jnp.dot(probs, head_values, precision=precise)
    outputs = lax.map(jax.checkpoint(attend), (query.transpose(1, 0, 2), keys.transpose(1, 0, 2), values.transpose(1, 0, 2)))
    attended = low(low_back(outputs.transpose(1, 0, 2).reshape(length, width)))
    branch = low_back(jnp.dot(attended, w_out, precision=precise))
    first = norm_rows(rows + branch, gain_one, bias_one)
    inner = low(first)
    gate = low_back(jnp.dot(inner, w_gate, precision=precise))
    upper = low_back(jnp.dot(inner, w_up, precision=precise))
    hidden = low(jax.nn.silu(gate) * upper)
    second = norm_rows(first + low_back(jnp.dot(hidden, w_down, precision=precise)), gain_two, bias_two)
    member = ((tags[:, None] == jnp.arange(DOCS_GRP)[None, :]) & (pads[:, None] == 1)).astype(jnp.float32)
    return jnp.dot(member.T, second, precision=precise)

def forward(tokens, w_qkv, w_out, ln1_gain, ln1_bias, w_gate, w_up, w_down, ln2_gain, ln2_bias, doc_ids, pad_mask, targets):
    weights = (w_qkv, w_out, ln1_gain, ln1_bias, w_gate, w_up, w_down, ln2_gain, ln2_bias)
    blocks = (tokens.reshape(2 * GROUPS, GROUP_TOK, D), doc_ids.reshape(2 * GROUPS, GROUP_TOK), pad_mask.reshape(2 * GROUPS, GROUP_TOK))
    sums = lax.map(jax.checkpoint(partial(group_pass, weights)), blocks)
    pooled = sums.reshape(2, DOCS, D)
    embed = pooled * lax.rsqrt(lax.optimization_barrier(jnp.sum(pooled * pooled, -1, keepdims=True)) + 1e-06)
    scores = jnp.dot(embed[0], embed[1].T, precision=precise) * 50.0
    top = lax.optimization_barrier(jnp.max(scores, -1, keepdims=True))
    totals = top[:, 0] + jnp.log(lax.optimization_barrier(jnp.sum(jnp.exp(scores - top), -1)))
    chosen = lax.optimization_barrier(jnp.sum(jnp.where(jnp.arange(DOCS)[None, :] == targets[:, None], scores, 0.0), -1))
    loss = jnp.mean(totals - chosen)
    return (loss, scores)

def reference(tokens, doc_ids, pad_mask, targets, w_qkv, w_out, ln1_gain, ln1_bias, w_gate, w_up, w_down, ln2_gain, ln2_bias):
    floats = tuple((item.astype(jnp.float32) for item in (tokens, w_qkv, w_out, ln1_gain, ln1_bias, w_gate, w_up, w_down, ln2_gain, ln2_bias)))

    def objective(*params):
        return forward(*params, doc_ids, pad_mask, targets)
    loss, pullback, scores = jax.vjp(objective, *floats, has_aux=True)
    grads = pullback(jnp.ones_like(loss))
    return (scores, loss, grads[0], grads[1], grads[2], grads[3], grads[4], grads[5], grads[6], grads[7], grads[8], grads[9])
```

```python
import functools

import jax
import jax.numpy as jnp
import numpy as np
from jax import lax
from jax.experimental import pallas as pl
from jax.experimental.pallas import tpu as pltpu
from jax.sharding import PartitionSpec as P

HEADS = 12
HEAD_DIM = 64
SPAN = 4
DOCS_GRP = 3
NH = HEADS // SPAN
HW = NH * HEAD_DIM
CHUNK = 512
VLIM = 62 * 2**20
MESH = pl.DeviceIdType.MESH
f32 = jnp.float32
bf = jnp.bfloat16
precise = lax.Precision.HIGHEST
norm_eps = 1e-05
ANY = pl.BlockSpec(memory_space=pl.ANY)
VM = pl.BlockSpec(memory_space=pltpu.VMEM)


def nn(a, b):
    return lax.dot_general(a, b, (((1,), (0,)), ((), ())), preferred_element_type=f32)


def nt(a, b):
    return lax.dot_general(a, b, (((1,), (1,)), ((), ())), preferred_element_type=f32)


def tn(a, b):
    return lax.dot_general(a, b, (((0,), (0,)), ((), ())), preferred_element_type=f32)


def split3(v):
    one = v.astype(bf).astype(f32)
    rest = v - one
    two = rest.astype(bf).astype(f32)
    return [one, two, rest - two]


def here():
    t = lax.axis_index("tower")
    p = lax.axis_index("dp")
    x = lax.rem(p, 2)
    y = lax.rem(lax.div(p, 2), 2)
    return t, p, x, y, lax.div(p, SPAN)


def plane_peers():
    t, p, x, y, g = here()
    px = p + 1 - 2 * x
    py = p + 2 - 4 * y
    pd = px + 2 - 4 * y
    return (t, px), (t, py), (t, pd)


def greet(peers):
    barrier = pltpu.get_barrier_semaphore()
    for peer in peers:
        pl.semaphore_signal(barrier, inc=1, device_id=peer, device_id_type=MESH)
    pl.semaphore_wait(barrier, len(peers))


def remote(src, dst, send, recv, peer):
    return pltpu.make_async_remote_copy(
        src_ref=src, dst_ref=dst, send_sem=send, recv_sem=recv, device_id=peer, device_id_type=MESH
    )


def dma_sems(n):
    return pltpu.SemaphoreType.DMA((n,))


def comm_params(cid):
    return pltpu.CompilerParams(collective_id=cid, has_side_effects=True, vmem_limit_bytes=VLIM)


def gather_kernel(tok_ref, code_ref, out_ref, codes_ref, send, recv, csend, crecv, lsem):
    t, p, x, y, g = here()
    count = tok_ref.shape[0]
    half = count // 2
    me = lax.rem(p, SPAN)
    ex, ey, ed = plane_peers()
    mx = lax.rem(ex[1], SPAN)
    my = lax.rem(ey[1], SPAN)

    def rows(m, h):
        return pl.ds(pl.multiple_of(m * count + h * half, half), half)

    def lanes(m):
        return pl.ds(pl.multiple_of(m * count, count), count)

    greet((ex, ey, ed))
    first = []
    for i, (peer, h) in enumerate(((ex, 0), (ey, 1), (ex, 1), (ey, 0))):
        c = remote(
            tok_ref.at[pl.ds(h * half, half)], out_ref.at[rows(me, h)], send.at[i], recv.at[i], peer
        )
        c.start()
        first.append(c)
    small = []
    for i, peer in enumerate((ex, ey, ed)):
        c = remote(code_ref, codes_ref.at[:, lanes(me)], csend.at[i], crecv.at[i], peer)
        c.start()
        small.append(c)
    own = pltpu.make_async_copy(tok_ref, out_ref.at[lanes(me)], lsem.at[0])
    own.start()
    own_code = pltpu.make_async_copy(code_ref, codes_ref.at[:, lanes(me)], lsem.at[1])
    own_code.start()
    first[0].wait_recv()
    f0 = remote(out_ref.at[rows(mx, 0)], out_ref.at[rows(mx, 0)], send.at[4], recv.at[4], ey)
    f0.start()
    first[1].wait_recv()
    f1 = remote(out_ref.at[rows(my, 1)], out_ref.at[rows(my, 1)], send.at[5], recv.at[5], ex)
    f1.start()
    first[2].wait_recv()
    first[3].wait_recv()
    f0.wait_recv()
    f1.wait_recv()
    for c in first + [f0, f1]:
        c.wait_send()
    for c in small:
        c.wait()
    own.wait()
    own_code.wait()


def gather(tok, code):
    count, width = tok.shape
    return pl.pallas_call(
        gather_kernel,
        out_shape=(
            jax.ShapeDtypeStruct((SPAN * count, width), bf),
            jax.ShapeDtypeStruct((1, SPAN * count), f32),
        ),
        in_specs=[VM, VM],
        out_specs=(ANY, ANY),
        scratch_shapes=[dma_sems(6), dma_sems(6), dma_sems(3), dma_sems(3), dma_sems(2)],
        compiler_params=comm_params(0),
        name="gather",
    )(tok, code)


def heads_to_tokens_kernel(parts, in_ref, out_ref, send, recv, lsem):
    t, p, x, y, g = here()
    count = out_ref.shape[1]
    me = lax.rem(p, SPAN)
    peers = plane_peers()
    width = parts and out_ref.shape[0] // parts
    greet(peers)
    copies = []
    for i, peer in enumerate((peers[2], peers[0], peers[1])):
        m = lax.rem(peer[1], SPAN)
        for k in range(parts):
            c = remote(
                in_ref.at[pl.ds(k * HW, HW), pl.ds(pl.multiple_of(m * count, count), count)],
                out_ref.at[pl.ds(pl.multiple_of(k * width + me * HW, HW), HW)],
                send.at[i * parts + k],
                recv.at[i * parts + k],
                peer,
            )
            c.start()
            copies.append(c)
    for k in range(parts):
        c = pltpu.make_async_copy(
            in_ref.at[pl.ds(k * HW, HW), pl.ds(pl.multiple_of(me * count, count), count)],
            out_ref.at[pl.ds(pl.multiple_of(k * width + me * HW, HW), HW)],
            lsem.at[k],
        )
        c.start()
        copies.append(c)
    for c in copies:
        c.wait()


def heads_to_tokens(a, cid, name):
    parts = a.shape[0] // HW
    count = a.shape[1] // SPAN
    return pl.pallas_call(
        functools.partial(heads_to_tokens_kernel, parts),
        out_shape=jax.ShapeDtypeStruct((parts * HEADS * HEAD_DIM, count), a.dtype),
        in_specs=[VM],
        out_specs=ANY,
        scratch_shapes=[dma_sems(3 * parts), dma_sems(3 * parts), dma_sems(parts)],
        compiler_params=comm_params(cid),
        name=name,
    )(a)


def tokens_to_heads_kernel(in_ref, out_ref, send, recv, lsem):
    t, p, x, y, g = here()
    count = in_ref.shape[1]
    me = lax.rem(p, SPAN)
    peers = plane_peers()
    greet(peers)
    mine = pl.ds(pl.multiple_of(me * count, count), count)
    copies = []
    for i, peer in enumerate((peers[2], peers[0], peers[1])):
        m = lax.rem(peer[1], SPAN)
        c = remote(
            in_ref.at[pl.ds(pl.multiple_of(m * HW, HW), HW)],
            out_ref.at[:, mine],
            send.at[i],
            recv.at[i],
            peer,
        )
        c.start()
        copies.append(c)
    c = pltpu.make_async_copy(
        in_ref.at[pl.ds(pl.multiple_of(me * HW, HW), HW)], out_ref.at[:, mine], lsem.at[0]
    )
    c.start()
    for c in copies + [c]:
        c.wait()


def tokens_to_heads(a, cid, name):
    return pl.pallas_call(
        tokens_to_heads_kernel,
        out_shape=jax.ShapeDtypeStruct((HW, SPAN * a.shape[1]), a.dtype),
        in_specs=[VM],
        out_specs=ANY,
        scratch_shapes=[dma_sems(3), dma_sems(3), dma_sems(1)],
        compiler_params=comm_params(cid),
        name=name,
    )(a)


def loss_kernel(groups, sums_ref, goal_ref, gp_ref, scores_ref, loss_ref, plane, allp, ge, send, recv):
    t, p, x, y, g = here()
    docs = groups * DOCS_GRP
    me = lax.rem(p, SPAN)
    peers = plane_peers()
    sibling = (1 - t, p)
    line = [(t, lax.rem(p + SPAN * k, SPAN * groups)) for k in range(1, groups)]
    greet(tuple(peers) + tuple(line) + (sibling,))
    copies = []
    for i, peer in enumerate(peers):
        c = remote(sums_ref, plane.at[i], send.at[i], recv.at[i], peer)
        c.start()
        copies.append(c)
    for c in copies:
        c.wait()
    own = sums_ref[...] + plane[0]
    own = own + (plane[1] + plane[2])
    allp[t, g] = own
    rows = allp.at[t, g]
    copies = []
    for i, peer in enumerate(line):
        c = remote(rows, rows, send.at[3 + i], recv.at[3 + i], peer)
        c.start()
        copies.append(c)
    for c in copies:
        c.wait()
    c = remote(allp.at[t], allp.at[t], send.at[2 + groups], recv.at[2 + groups], sibling)
    c.start()
    c.wait()
    width = sums_ref.shape[1]
    size = groups * 8
    pools = [allp[k].reshape(size, width) for k in range(2)]
    invs = [lax.rsqrt(jnp.sum(v * v, -1, keepdims=True) + 1e-06) for v in pools]
    embeds = [v * r for v, r in zip(pools, invs)]
    dot = functools.partial(lax.dot_general, precision=precise, preferred_element_type=f32)
    scores = dot(embeds[0], embeds[1], (((1,), (1,)), ((), ()))) * 50.0
    col = lax.broadcasted_iota(jnp.int32, (size, size), 1)
    row = lax.broadcasted_iota(jnp.int32, (size, size), 0)
    live = lax.rem(col, 8) < DOCS_GRP
    alive = lax.rem(row, 8) < DOCS_GRP
    masked = jnp.where(live, scores, -1e30)
    top = jnp.max(masked, -1, keepdims=True)
    total = jnp.sum(jnp.exp(masked - top), -1, keepdims=True)
    log_sums = top + jnp.log(total)
    hot = jnp.where(col.astype(f32) == goal_ref[:, 0:1], 1.0, 0.0)
    chosen = jnp.sum(hot * scores, -1, keepdims=True)
    each = jnp.where(alive[:, 0:1], log_sums - chosen, 0.0)
    loss_ref[...] = jnp.broadcast_to(jnp.sum(each, 0, keepdims=True) / docs, loss_ref.shape)
    scores_ref[...] = scores
    gs = jnp.where(alive & live, (jnp.exp(masked - log_sums) - hot) / docs, 0.0)
    gq = dot(gs, embeds[1], (((1,), (0,)), ((), ())))
    gd = dot(gs, embeds[0], (((0,), (0,)), ((), ())))
    ge[...] = jnp.where(t == 0, gq, gd) * 50.0
    mine = ge[pl.ds(pl.multiple_of(g * 8, 8), 8), :]
    pooled = allp[t, g]
    inv = lax.rsqrt(jnp.sum(pooled * pooled, -1, keepdims=True) + 1e-06)
    gp_ref[...] = inv * mine - inv * inv * inv * pooled * jnp.sum(pooled * mine, -1, keepdims=True)


def contrast(sums, goal, groups):
    size = groups * 8
    width = sums.shape[1]
    return pl.pallas_call(
        functools.partial(loss_kernel, groups),
        out_shape=(
            jax.ShapeDtypeStruct((8, width), f32),
            jax.ShapeDtypeStruct((size, size), f32),
            jax.ShapeDtypeStruct((8, 128), f32),
        ),
        in_specs=[VM, VM],
        out_specs=(VM, VM, VM),
        scratch_shapes=[
            pltpu.VMEM((3, 8, width), f32),
            pltpu.VMEM((2, groups, 8, width), f32),
            pltpu.VMEM((size, width), f32),
            dma_sems(3 + groups),
            dma_sems(3 + groups),
        ],
        compiler_params=comm_params(1),
        name="contrast",
    )(sums, goal)


def doc_limits(code):
    pad = code >= 4.0
    mem = jnp.where(pad, code - 4.0, code)
    n0 = jnp.sum(jnp.where(mem < 0.5, 1.0, 0.0)).astype(jnp.int32)
    n1 = jnp.sum(jnp.where(mem < 1.5, 1.0, 0.0)).astype(jnp.int32)
    l = [jnp.sum(jnp.where(code == float(d), 1.0, 0.0)).astype(jnp.int32) for d in range(3)]
    return n0, n1, l

def block_range(lims, a, size, total):
    n0, n1, l = lims
    b = a + size - 1
    first = (a >= n0).astype(jnp.int32) + (a >= n1).astype(jnp.int32)
    last = (b >= n0).astype(jnp.int32) + (b >= n1).astype(jnp.int32)
    lo = jnp.where(first == 0, 0, jnp.where(first == 1, n0, n1))
    hi = jnp.where(last == 0, n0, jnp.where(last == 1, n1, total))
    dead = jnp.zeros((), jnp.bool_)
    for d in range(3):
        dead = dead | ((first <= d) & (d <= last) & (l[d] == 0))
    return jnp.where(dead, 0, lo), jnp.where(dead, total, hi)

def fwd_kernel(KB, QB, tok_ref, wt_ref, cos_ref, sin_ref, code_ref, out_ref, lse_ref, o32_ref, qa_ref, ka_ref, va_ref,
               kt_ref, acc_ref):
    T = tok_ref.shape[0]
    CH = 512
    hw = HW
    code = code_ref[...]
    lims = doc_limits(code)
    def proj(c, _):
        sl = pl.ds(pl.multiple_of(c*CH, CH), CH)
        mx = nt(wt_ref[...], tok_ref[sl, :])
        cos = cos_ref[:, sl]; sin = sin_ref[:, sl]
        cd = code_ref[:, sl]
        mem = jnp.where(cd >= 4.0, cd-4.0, cd)
        hot = jnp.concatenate([jnp.where(mem == float(d), 1.0, 0.0) for d in range(3)] + [jnp.zeros((13, CH), f32)], 0)
        neg = jnp.concatenate([jnp.where(cd == float(d), 0.0, -1e30) for d in range(3)] + [jnp.zeros((13, CH), f32)], 0)
        zer = jnp.zeros((48, CH), f32)
        one = jnp.concatenate([jnp.ones((1, CH), f32), jnp.zeros((63, CH), f32)], 0)
        def rope(u):
            a = u[:32]; b = u[32:]
            return jnp.concatenate([a*cos - b*sin, b*cos + a*sin], 0)
        for h in range(NH):
            q = rope(mx[h*HEAD_DIM:(h+1)*HEAD_DIM]).astype(bf).astype(f32)*0.125
            k = rope(mx[hw+h*HEAD_DIM:hw+(h+1)*HEAD_DIM])
            v = mx[2*hw+h*HEAD_DIM:2*hw+(h+1)*HEAD_DIM]
            qa_ref[h, :, sl] = jnp.concatenate([q, hot, zer], 0).astype(bf)
            ka_ref[h, sl, :] = jnp.concatenate([k, neg, zer], 0).T.astype(bf)
            va_ref[h, :, sl] = jnp.concatenate([v, one], 0).astype(bf)
            kt_ref[h, :, sl] = k.astype(bf)
        return 0
    lax.fori_loop(0, T//CH, proj, 0)
    def qblock(i, _):
        a = i*QB
        qs = pl.ds(pl.multiple_of(a, QB), QB)
        lo, hi = block_range(lims, a, QB, T)
        jlo = lo//KB; jhi = (hi+KB-1)//KB
        for h in range(NH):
            acc_ref[h] = jnp.zeros_like(acc_ref[h])
        def kv(j, ms):
            ks = pl.ds(pl.multiple_of(j*KB, KB), KB)
            new = []
            ss = [nn(ka_ref[h, ks, :], qa_ref[h, :, qs]) for h in range(NH)]
            for h in range(NH):
                s = ss[h]
                mn = jnp.maximum(ms[h], jnp.max(s, 0, keepdims=True))
                p = jnp.exp(s - mn).astype(bf)
                al = jnp.exp(ms[h]-mn)
                acc_ref[h] = acc_ref[h]*al + nn(va_ref[h, :80, ks], p)
                new.append(mn)
            return tuple(new)
        ms = lax.fori_loop(jlo, jhi, kv, tuple(jnp.full((1, QB), -3e38, f32) for _ in range(NH)))
        for h in range(NH):
            tot = acc_ref[h, 64:65, :]
            o = acc_ref[h, :64, :]/tot
            o32_ref[h*HEAD_DIM:(h+1)*HEAD_DIM, qs] = o
            lse_ref[h:h+1, qs] = jnp.where(ms[h] < -1e29, 0.0, ms[h] + jnp.log(tot))
            out_ref[h*HEAD_DIM:(h+1)*HEAD_DIM, qs] = o.astype(bf)
        return 0
    lax.fori_loop(0, T//QB, qblock, 0)

def attn_fwd(tok, wt, cos, sin, code, KB=512, QB=256):
    T = tok.shape[0]
    return pl.pallas_call(functools.partial(fwd_kernel, KB, QB),
        out_shape=(jax.ShapeDtypeStruct((NH*HEAD_DIM, T), bf), jax.ShapeDtypeStruct((NH, T), f32), jax.ShapeDtypeStruct((NH*HEAD_DIM, T), f32),
                   jax.ShapeDtypeStruct((NH,128,T), bf), jax.ShapeDtypeStruct((NH,T,128), bf), jax.ShapeDtypeStruct((NH,128,T), bf), jax.ShapeDtypeStruct((NH,HEAD_DIM,T), bf)),
        in_specs=[pl.BlockSpec(memory_space=pltpu.VMEM)]*5, out_specs=tuple([pl.BlockSpec(memory_space=pltpu.VMEM)]*7),
        scratch_shapes=[pltpu.VMEM((NH,80,QB), f32)],
        compiler_params=pltpu.CompilerParams(vmem_limit_bytes=VLIM), name="attn_fwd",
        cost_estimate=pl.CostEstimate(flops=int(2*T*768*576+4*T*T*128*3), bytes_accessed=12<<20, transcendentals=T*T*3))(tok, wt, cos, sin, code)

def bwd_kernel(KB, QB, do_ref, o32_ref, lse_ref, qa_ref, ka_ref, va_ref, kt_ref, cos_ref, sin_ref, code_ref, g_ref,
               vn_ref, dn_ref, da_ref, qb_ref, acc_ref, dq_ref):
    T = do_ref.shape[1]
    hw = HW
    CH = 512
    lims = doc_limits(code_ref[...])
    def prep(c, _):
        sl = pl.ds(pl.multiple_of(c*CH, CH), CH)
        for h in range(NH):
            do = do_ref[h*HEAD_DIM:(h+1)*HEAD_DIM, sl].astype(f32)
            delta = jnp.sum(do*o32_ref[h*HEAD_DIM:(h+1)*HEAD_DIM, sl], 0, keepdims=True)
            def split(x):
                x1 = x.astype(bf).astype(f32); r = x-x1
                x2 = r.astype(bf).astype(f32); x3 = r-x2
                return [x1, x2, x3]
            z13 = jnp.zeros((13, CH), f32); z48 = jnp.zeros((48, CH), f32)
            da_ref[h, :, sl] = jnp.concatenate([do]+split(-delta)+[z13, z48], 0).astype(bf)
            one = jnp.concatenate([jnp.ones((3, CH), f32), jnp.zeros((61, CH), f32)], 0)
            v = va_ref[h, :64, sl].astype(f32)
            vn_ref[h, sl, :] = jnp.concatenate([v, one], 0).T.astype(bf)
            z64 = jnp.zeros((64, CH), f32)
            q = qa_ref[h, :64, sl].astype(f32)
            dn_ref[h, sl, :] = jnp.concatenate([do, z64], 0).T.astype(bf)
            qb_ref[h, sl, :] = jnp.concatenate([z64, q], 0).T.astype(bf)
            acc_ref[h, sl, :] = jnp.zeros((CH, 128), f32)
        return 0
    lax.fori_loop(0, T//CH, prep, 0)
    def qblock(i, _):
        a = i*QB
        qs = pl.ds(pl.multiple_of(a, QB), QB)
        lo, hi = block_range(lims, a, QB, T)
        jlo = lo//KB; jhi = (hi+KB-1)//KB
        dq_ref[...] = jnp.zeros_like(dq_ref)
        def kv(j, _):
            ks = pl.ds(pl.multiple_of(j*KB, KB), KB)
            for h in range(NH):
                s = nn(ka_ref[h, ks, :], qa_ref[h, :, qs])
                dp = nn(vn_ref[h, ks, :], da_ref[h, :, qs])
                p = jnp.exp(s - lse_ref[h:h+1, qs])
                ds = (p*dp).astype(bf)
                acc_ref[h, ks, :] += nn(p.astype(bf), dn_ref[h, qs, :]) + nn(ds, qb_ref[h, qs, :])
                dq_ref[h] += nn(kt_ref[h, :, ks], ds)
            return 0
        lax.fori_loop(jlo, jhi, kv, 0)
        cos = cos_ref[:, qs]; sin = sin_ref[:, qs]
        for h in range(NH):
            u = dq_ref[h]*0.125
            x1 = u[:32]; x2 = u[32:]
            g_ref[h*HEAD_DIM:(h+1)*HEAD_DIM, qs] = jnp.concatenate([x1*cos+x2*sin, x2*cos-x1*sin], 0).astype(bf)
        return 0
    lax.fori_loop(0, T//QB, qblock, 0)
    def fin(c, _):
        sl = pl.ds(pl.multiple_of(c*CH, CH), CH)
        cos = cos_ref[:, sl]; sin = sin_ref[:, sl]
        for h in range(NH):
            t = acc_ref[h, sl, :].T
            x1 = t[64:96]; x2 = t[96:128]
            g_ref[hw+h*HEAD_DIM:hw+(h+1)*HEAD_DIM, sl] = jnp.concatenate([x1*cos+x2*sin, x2*cos-x1*sin], 0).astype(bf)
            g_ref[2*hw+h*HEAD_DIM:2*hw+(h+1)*HEAD_DIM, sl] = t[:64].astype(bf)
        return 0
    lax.fori_loop(0, T//CH, fin, 0)

def attn_bwd(do, o32, lse, qa, ka, va, kt, cos, sin, code, KB=512, QB=256):
    T = do.shape[1]
    return pl.pallas_call(functools.partial(bwd_kernel, KB, QB),
        out_shape=jax.ShapeDtypeStruct((3*NH*HEAD_DIM, T), bf),
        in_specs=[pl.BlockSpec(memory_space=pltpu.VMEM)]*10, out_specs=pl.BlockSpec(memory_space=pltpu.VMEM),
        scratch_shapes=[pltpu.VMEM((NH,T,128), bf), pltpu.VMEM((NH,T,128), bf), pltpu.VMEM((NH,128,T), bf), pltpu.VMEM((NH,T,128), bf),
                        pltpu.VMEM((NH,T,128), f32), pltpu.VMEM((NH,HEAD_DIM,QB), f32)],
        compiler_params=pltpu.CompilerParams(vmem_limit_bytes=VLIM), name="attn_bwd",
        cost_estimate=pl.CostEstimate(flops=int(10*T*T*128*3), bytes_accessed=12<<20, transcendentals=T*T*3))(do, o32, lse, qa, ka, va, kt, cos, sin, code)


def weights_kernel(
    shards, ia, ib, ga, gb, ha, hb, ma, mb, aa, ab, ba, bb, out_ref, it_ref
):
    width = ia.shape[1]
    half = width // 2
    one = width // shards
    steps = ga.shape[1] // half
    down = ha.shape[1] // shards
    count = ia.shape[0]
    it_ref[:, :count] = ia[...].T
    it_ref[:, count:] = ib[...].T

    def upward(j, _):
        cols = pl.ds(pl.multiple_of(j * half, half), half)
        r = nn(it_ref[:, :count], ga[:, cols]) + nn(it_ref[:, count:], gb[:, cols])
        out_ref[:, pl.ds(pl.multiple_of(j * one, one), one), :] = r.astype(bf).reshape(
            shards, one, half
        )
        return 0

    lax.fori_loop(0, steps, upward, 0)
    top = steps * one
    per = half // down

    def downward(j, _):
        cols = pl.ds(pl.multiple_of(j * half, half), half)
        r = tn(ha[:, cols], ma[...]) + tn(hb[:, cols], mb[...])
        out_ref[pl.ds(j * per, per), top : top + down, :] = r.astype(bf).reshape(per, down, half)
        return 0

    lax.fori_loop(0, ha.shape[1] // half, downward, 0)
    r = nn(aa[...], ba[...]) + nn(ab[...], bb[...])
    out_ref[:, top + down :, :] = r.astype(bf).reshape(shards, one, half)


def weight_grads(shards, *arrays):
    width = arrays[0].shape[1]
    count = arrays[0].shape[0]
    half = width // 2
    one = width // shards
    rows = one * (arrays[2].shape[1] // half) + arrays[4].shape[1] // shards + one
    return pl.pallas_call(
        functools.partial(weights_kernel, shards),
        out_shape=jax.ShapeDtypeStruct((shards, rows, half), bf),
        in_specs=[VM] * 12,
        out_specs=VM,
        scratch_shapes=[pltpu.VMEM((width, 2 * count), bf)],
        compiler_params=pltpu.CompilerParams(vmem_limit_bytes=VLIM),
        name="weight_grads",
    )(*arrays)


def add_rows(dst, a, b, rows):
    def step(i, _):
        sl = pl.ds(pl.multiple_of(i * 16, 16), 16)
        dst[sl, :] = (a[sl, :].astype(f32) + b[sl, :].astype(f32)).astype(bf)
        return 0

    lax.fori_loop(0, rows // 16, step, 0)


class Line:
    def __init__(self, z, zt, groups, part, up, down, sems, t, p):
        self.z, self.zt, self.groups = z, zt, groups
        self.part, self.up, self.down = part, up, down
        us, ur, ds, dr = sems
        above = (t, lax.rem(p + SPAN, SPAN * groups))
        below = (t, lax.rem(p + SPAN * (groups - 1), SPAN * groups))
        self.up_first = remote(part, up, us, ur, above)
        self.up_next = remote(up, up, us, ur, above)
        self.down_first = remote(part, down, ds, dr, below)
        self.down_next = remote(down, down, ds, dr, below)

    def start(self):
        if self.zt > 0:
            pl.when(self.z == 0)(lambda: self.up_first.start())
        if self.zt < self.groups - 1:
            pl.when(self.z == self.groups - 1)(lambda: self.down_first.start())

    def relay(self, hop, rows):
        def up():
            self.up_next.wait_recv()
            add_rows(self.up, self.up, self.part, rows)
            self.up_next.start()

        def down():
            self.down_next.wait_recv()
            add_rows(self.down, self.down, self.part, rows)
            self.down_next.start()

        if 0 < hop < self.zt:
            pl.when(self.z == hop)(up)
        if self.zt < self.groups - 1 - hop:
            pl.when(self.z == self.groups - 1 - hop)(down)

    def finish(self, dst, rows):
        def done():
            if self.zt > 0:
                self.up_next.wait_recv()
            if self.zt < self.groups - 1:
                self.down_next.wait_recv()
            if 0 < self.zt < self.groups - 1:
                add_rows(self.up, self.up, self.down, rows)
            add_rows(dst, self.up if self.zt > 0 else self.down, self.part, rows)

        pl.when(self.z == self.zt)(done)

    def drain(self):
        if self.zt > 0:
            pl.when(self.z < self.zt)(lambda: self.up_first.wait_send())
        if self.zt < self.groups - 1:
            pl.when(self.z > self.zt)(lambda: self.down_first.wait_send())


def outward(groups):
    order = []
    lo, hi = 0, groups - 1
    while lo <= hi:
        order.append(hi)
        if lo < hi:
            order.append(lo)
        lo, hi = lo + 1, hi - 1
    return order


def scatter_kernel(groups, w_ref, gain_ref, out_ref, sum_ref, r1a, r1b, r2a, r2b, ua, ub, da, db,
                   s1, q1, s2, q2, us, ur, ds, dr, plane, line, gs, gr, fs, fr):
    t, p, x, y, z = here()
    ex, ey, ed = plane_peers()
    sibling = (1 - t, p)
    others = [(t, lax.rem(p + SPAN * k, SPAN * groups)) for k in range(1, groups)]
    greet((ex, ey, ed, sibling) + tuple(others))
    rows = w_ref.shape[1]
    ra = r1a.shape[1]
    rb = rows - ra
    order = outward(groups)
    colours = (
        (ex, ey, r1a, r2a, ua, da, pl.ds(0, ra), ra,
         lambda zt, k: zt * 4 + k * 2 + (1 - x), lambda zt, k: zt * 4 + k * 2 + x, y),
        (ey, ex, r1b, r2b, ub, db, pl.ds(ra, rb), rb,
         lambda zt, k: zt * 4 + (1 - y) * 2 + k, lambda zt, k: zt * 4 + y * 2 + k, x),
    )

    def first(c, zt, k):
        one, two, r1, r2, u, d, sl, n, away, own, mine = colours[c]
        i = (c * groups + zt) * 2 + k
        return remote(w_ref.at[away(zt, k), sl], r1.at[zt * 2 + k], s1.at[i], q1.at[i], one)

    def second(c, zt):
        one, two, r1, r2, u, d, sl, n, away, own, mine = colours[c]
        i = c * groups + zt
        return remote(r1.at[zt * 2 + 1 - mine], r2.at[zt], s2.at[i], q2.at[i], two)

    def chain(c, zt):
        one, two, r1, r2, u, d, sl, n, away, own, mine = colours[c]
        i = c * groups + zt
        return Line(z, zt, groups, r2.at[zt], u.at[zt], d.at[zt],
                    (us.at[i], ur.at[i], ds.at[i], dr.at[i]), t, p)

    def issue(zt):
        for k in range(2):
            for c in range(2):
                first(c, zt, k).start()

    def half_way(zt):
        for k in range(2):
            for c in range(2):
                one, two, r1, r2, u, d, sl, n, away, own, mine = colours[c]
                first(c, zt, k).wait_recv()
                dst = r1.at[zt * 2 + k]
                add_rows(dst, dst, w_ref.at[own(zt, k), sl], n)
        for c in range(2):
            second(c, zt).start()

    def in_plane(zt):
        for c in range(2):
            one, two, r1, r2, u, d, sl, n, away, own, mine = colours[c]
            second(c, zt).wait_recv()
            dst = r2.at[zt]
            add_rows(dst, dst, r1.at[zt * 2 + mine], n)
            chain(c, zt).start()

    def relay(zt, hop):
        for c in range(2):
            chain(c, zt).relay(hop, colours[c][7])

    issue(order[0])
    if groups > 1:
        issue(order[1])
    gain_copies = []
    for i, peer in enumerate((ex, ey, ed)):
        c = remote(gain_ref, plane.at[i], gs.at[i], gr.at[i], peer)
        c.start()
        gain_copies.append(c)
    todo = []
    for i, zt in enumerate(order):
        half_way(zt)
        if i + 2 < groups:
            issue(order[i + 2])
        if i >= 1:
            in_plane(order[i - 1])
            todo.append((order[i - 1], 0))
        if i == 0:
            for c in gain_copies:
                c.wait()
            sum_ref[...] = gain_ref[...] + plane[0]
            sum_ref[...] = sum_ref[...] + (plane[1] + plane[2])
            line[0] = sum_ref[...]
            gain_copies = []
            for k, peer in enumerate(others):
                c = remote(line.at[0], line.at[1 + k], gs.at[3 + k], gr.at[3 + k], peer)
                c.start()
                gain_copies.append(c)
        if i == 1:
            for c in gain_copies:
                c.wait()
            total = line[0]
            for k in range(1, groups):
                total = total + line[k]
            line[groups] = total
            c = remote(line.at[groups], line.at[groups + 1], gs.at[2 + groups], gr.at[2 + groups], sibling)
            c.start()
            gain_copies = [c]
        if i >= 2:
            for hop in range(1, groups - 1):
                if hop == 1:
                    relay(order[i - 2], hop)
    in_plane(order[groups - 1])
    for hop in range(1, groups - 1):
        for i, zt in enumerate(order):
            if hop > 1 or i >= groups - 2:
                relay(zt, hop)
    for zt in order:
        for c in range(2):
            sl, n = colours[c][6], colours[c][7]
            chain(c, zt).finish(out_ref.at[t, sl], n)
    last = remote(out_ref.at[t], out_ref.at[t], fs.at[0], fr.at[0], sibling)
    last.start()
    for c in gain_copies:
        c.wait()
    sum_ref[...] = line[groups] + line[groups + 1]
    for zt in order:
        for c in range(2):
            for k in range(2):
                first(c, zt, k).wait_send()
            second(c, zt).wait_send()
            chain(c, zt).drain()
    last.wait()


def scatter(w, gains, groups):
    rows, half = w.shape[1:]
    ra = (rows // 32 + 1) * 16 if rows % 32 else rows // 2
    rb = rows - ra
    buf = lambda n, r: pltpu.VMEM((n, r, half), bf)
    return pl.pallas_call(
        functools.partial(scatter_kernel, groups),
        out_shape=(
            jax.ShapeDtypeStruct((2, rows, half), bf),
            jax.ShapeDtypeStruct(gains.shape, f32),
        ),
        in_specs=[VM, VM],
        out_specs=(VM, VM),
        scratch_shapes=[
            buf(2 * groups, ra), buf(2 * groups, rb), buf(groups, ra), buf(groups, rb),
            buf(groups, ra), buf(groups, rb), buf(groups, ra), buf(groups, rb),
            dma_sems(4 * groups), dma_sems(4 * groups), dma_sems(2 * groups), dma_sems(2 * groups),
            dma_sems(2 * groups), dma_sems(2 * groups), dma_sems(2 * groups), dma_sems(2 * groups),
            pltpu.VMEM((3,) + gains.shape, f32), pltpu.VMEM((groups + 2,) + gains.shape, f32),
            dma_sems(3 + groups), dma_sems(3 + groups), dma_sems(1), dma_sems(1),
        ],
        compiler_params=comm_params(2),
        name="scatter",
    )(w, gains)


def tail_kernel(groups, g_ref, tok_ref, gm_ref, out_ref, w2, sib, ub, db, fin, send, recv, ts, tr,
                us, ur, ds, dr, ps, pr, lsem):
    t, p, x, y, z = here()
    count = gm_ref.shape[1]
    me = lax.rem(p, SPAN)
    peers = plane_peers()
    sibling = (1 - t, p)
    others = [(t, lax.rem(p + SPAN * k, SPAN * groups)) for k in range(1, groups)]
    across = [(1 - t, q[1]) for q in peers]
    greet(tuple(peers) + tuple(across) + (sibling,) + tuple(others))
    width = gm_ref.shape[0] // 3
    copies = []
    for i, peer in enumerate((peers[2], peers[0], peers[1])):
        m = lax.rem(peer[1], SPAN)
        for k in range(3):
            c = remote(
                g_ref.at[pl.ds(k * HW, HW), pl.ds(pl.multiple_of(m * count, count), count)],
                gm_ref.at[pl.ds(pl.multiple_of(k * width + me * HW, HW), HW)],
                send.at[i * 3 + k], recv.at[i * 3 + k], peer,
            )
            c.start()
            copies.append(c)
    for k in range(3):
        c = pltpu.make_async_copy(
            g_ref.at[pl.ds(k * HW, HW), pl.ds(pl.multiple_of(me * count, count), count)],
            gm_ref.at[pl.ds(pl.multiple_of(k * width + me * HW, HW), HW)],
            lsem.at[k],
        )
        c.start()
        copies.append(c)
    shards = SPAN * groups
    one = width // shards
    half = width // 2
    for h in range(2):
        r = nn(g_ref[...], tok_ref[:, h * half : (h + 1) * half]).T
        w2[h * (shards // 2) : (h + 1) * (shards // 2)] = r.astype(bf).reshape(shards // 2, one, 3 * HW)
    swaps = []
    for zt in outward(groups):
        c = remote(w2.at[pl.ds(zt * 4 + (1 - t) * 2, 2)], sib.at[zt], ts.at[zt], tr.at[zt], sibling)
        c.start()
        swaps.append(c)

    def chain(zt, k):
        i = zt * 2 + k
        return Line(z, zt, groups, sib.at[zt, k], ub.at[zt, k], db.at[zt, k],
                    (us.at[i], ur.at[i], ds.at[i], dr.at[i]), t, p)

    for c, zt in zip(swaps, outward(groups)):
        c.wait_recv()
        for k in range(2):
            dst = sib.at[zt, k]
            add_rows(dst, dst, w2.at[zt * 4 + t * 2 + k], one)
            chain(zt, k).start()
    for hop in range(1, groups - 1):
        for zt in outward(groups):
            for k in range(2):
                chain(zt, k).relay(hop, one)
    for zt in outward(groups):
        for k in range(2):
            chain(zt, k).finish(fin.at[k], one)
    here_id = t * SPAN + me

    def hand(k, tt):
        m = t * 2 + k
        peer = (tt, z * SPAN + m)
        i = k * 2 + tt
        away = remote(fin.at[k], out_ref.at[me], ps.at[i], pr.at[me], peer)
        stay = pltpu.make_async_copy(fin.at[k], out_ref.at[me], lsem.at[3])
        return away, stay, (tt * SPAN + m) == here_id

    for k in range(2):
        for tt in range(2):
            away, stay, same = hand(k, tt)
            pl.when(jnp.logical_not(same))(lambda away=away: away.start())
            pl.when(same)(lambda stay=stay: stay.start())
    for s in range(SPAN):
        mine = jnp.logical_and(s == me, y == t)
        got = remote(fin.at[0], out_ref.at[s], ps.at[0], pr.at[s], sibling)
        pl.when(jnp.logical_not(mine))(lambda got=got: got.wait_recv())
    for k in range(2):
        for tt in range(2):
            away, stay, same = hand(k, tt)
            pl.when(jnp.logical_not(same))(lambda away=away: away.wait_send())
            pl.when(same)(lambda stay=stay: stay.wait())
    for c in swaps:
        c.wait_send()
    for zt in range(groups):
        for k in range(2):
            chain(zt, k).drain()
    for c in copies:
        c.wait()


def tail(g, tok, groups):
    width = tok.shape[1]
    count = tok.shape[0] // SPAN
    one = width // (SPAN * groups)
    buf = lambda *n: pltpu.VMEM(n + (one, 3 * HW), bf)
    return pl.pallas_call(
        functools.partial(tail_kernel, groups),
        out_shape=(
            jax.ShapeDtypeStruct((3 * width, count), bf),
            jax.ShapeDtypeStruct((SPAN, one, 3 * HW), bf),
        ),
        in_specs=[VM, VM],
        out_specs=(ANY, VM),
        scratch_shapes=[
            buf(SPAN * groups), buf(groups, 2), buf(groups, 2), buf(groups, 2), buf(2),
            dma_sems(9), dma_sems(9), dma_sems(groups), dma_sems(groups),
            dma_sems(2 * groups), dma_sems(2 * groups), dma_sems(2 * groups), dma_sems(2 * groups),
            dma_sems(4), dma_sems(SPAN), dma_sems(4),
        ],
        compiler_params=comm_params(3),
        name="tail",
    )(g, tok)


def swapped(value):
    return lax.ppermute(value, "tower", [(0, 1), (1, 0)])


def norm_rows(values, gain, bias):
    centred = values - jnp.mean(values, -1, keepdims=True)
    spread = jnp.mean(centred * centred, -1, keepdims=True)
    scale = lax.rsqrt(spread + norm_eps)
    normed = centred * scale
    return normed * gain + bias, normed, scale


def norm_back(grad, normed, scale, gain):
    shaped = grad * gain
    inner = (
        shaped
        - jnp.mean(shaped, -1, keepdims=True)
        - normed * jnp.mean(shaped * normed, -1, keepdims=True)
    )
    return inner * scale, jnp.sum(grad * normed, 0), jnp.sum(grad, 0)


def angle_tables(total):
    half = HEAD_DIM // 2
    freqs = np.float32(1000.0) ** (-np.arange(half, dtype=np.float32) / np.float32(half))
    theta = freqs[:, None].astype(np.float32) * np.arange(total, dtype=np.float32)[None, :]
    return np.cos(theta).astype(np.float32), np.sin(theta).astype(np.float32)


def spread_sum(value):
    part = lax.psum_scatter(value, "dp", scatter_dimension=0, tiled=True)
    return lax.psum(part.astype(bf), "tower").astype(f32)


def local(
    tokens, doc_ids, pad_mask, targets, w_qkv, w_out, ln1_gain, ln1_bias,
    w_gate, w_up, w_down, ln2_gain, ln2_bias,
):
    width = w_out.shape[0]
    rows = tokens[0]
    count = rows.shape[0]
    places = lax.axis_size("dp")
    groups = places // SPAN
    tower = lax.axis_index("tower")
    place = lax.axis_index("dp")
    me = place % SPAN
    member_of = doc_ids[0] % DOCS_GRP
    live = pad_mask[0] == 1
    code = jnp.where(live, member_of, member_of + 4).astype(f32)[None, :]
    docs = groups * DOCS_GRP
    slot = jnp.arange(groups * 8)
    goal = jnp.where(
        slot % 8 < DOCS_GRP, targets[jnp.minimum(slot // 8 * DOCS_GRP + slot % 8, docs - 1)], 0
    )
    goal = jnp.where(slot % 8 < DOCS_GRP, goal // DOCS_GRP * 8 + goal % DOCS_GRP, -1)
    goal = jnp.broadcast_to(goal.astype(f32)[:, None], (groups * 8, 128))
    w_mine = lax.dynamic_index_in_dim(w_qkv.reshape(width, 3, SPAN, HW), me, 2, keepdims=False)
    w_mine = w_mine.reshape(width, 3 * HW).T
    cos, sin = angle_tables(SPAN * count)
    tok_all, codes = gather(rows, code)
    heads_out, lse, exact, qa, ka, va, kt = attn_fwd(tok_all, w_mine, cos, sin, codes)
    attended = heads_to_tokens(heads_out, 4, "to_tokens")
    branch = tn(attended, w_out)
    first, normed_one, scale_one = norm_rows(rows.astype(f32) + branch, ln1_gain, ln1_bias)
    inner = first.astype(bf)
    gate = nn(inner, w_gate)
    upper = nn(inner, w_up)
    sigmoid = jax.nn.sigmoid(gate)
    activated = gate * sigmoid
    hidden = (activated * upper).astype(bf)
    second, normed_two, scale_two = norm_rows(first + nn(hidden, w_down), ln2_gain, ln2_bias)
    member = ((member_of[:, None] == jnp.arange(8)[None, :]) & live[:, None]).astype(f32)
    sums = jnp.dot(member.T, second, precision=precise)
    grad_pool, scores_all, loss = contrast(sums, goal, groups)
    scores = scores_all.reshape(groups, 8, groups, 8)[:, :DOCS_GRP, :, :DOCS_GRP].reshape(docs, docs)
    grad_second = jnp.dot(member, grad_pool, precision=precise)
    grad_h2, gain_two, bias_two = norm_back(grad_second, normed_two, scale_two, ln2_gain)
    grad_mlp = grad_h2.astype(bf)
    grad_hidden = nt(grad_mlp, w_down)
    grad_gate = (grad_hidden * upper * sigmoid * (1.0 + gate * (1.0 - sigmoid))).astype(bf)
    grad_up = (grad_hidden * activated).astype(bf)
    grad_first = grad_h2 + nt(grad_gate, w_gate) + nt(grad_up, w_up)
    grad_h1, gain_one, bias_one = norm_back(grad_first, normed_one, scale_one, ln1_gain)
    grad_branch = grad_h1.astype(bf)
    grad_attended = nt(w_out, grad_branch).astype(bf)
    gains = jnp.stack([gain_one, bias_one, gain_two, bias_two], 0)
    here_first = tower == 0
    by_hand = width % (16 * places) == 0
    if by_hand:
        half = width // 2
        own = lambda v: lax.dynamic_slice_in_dim(v, tower * half, half, 1)
        its = lambda v: lax.dynamic_slice_in_dim(v, (1 - tower) * half, half, 1)
        kept = jnp.where(here_first, grad_gate, grad_up)
        sent = jnp.where(here_first, grad_up, grad_gate)
        w_parts = weight_grads(
            places,
            inner, swapped(inner), kept, swapped(sent), hidden, swapped(hidden),
            own(grad_mlp), swapped(its(grad_mlp)), attended, swapped(attended),
            own(grad_branch), swapped(its(grad_branch)),
        )
    d_heads = tokens_to_heads(grad_attended, 5, "to_heads")
    mixed = attn_bwd(d_heads, exact, lse, qa, ka, va, kt, cos, sin, codes)
    if by_hand:
        one = width // places
        down = w_down.shape[0] // places
        pair, gain_sums = scatter(w_parts, jnp.concatenate([gains, jnp.zeros_like(gains)], 0), groups)
        top = pair.shape[1] - down - one
        unfold = lambda v: v.reshape(top // one, one, half).transpose(1, 0, 2).reshape(one, -1)
        sides = lambda v: jnp.concatenate([v[0], v[1]], 1).astype(f32)
        gate_out = unfold(pair[0, :top]).astype(f32)
        up_out = unfold(pair[1, :top]).astype(f32)
        down_out = sides(pair[:, top : top + down])
        out_out = sides(pair[:, top + down :])
        gains_out = lax.dynamic_slice_in_dim(gain_sums[:4], place * one, one, 1)
        grad_mixed, qkv_parts = tail(mixed, tok_all, groups)
        qkv_out = (
            qkv_parts.reshape(SPAN, one, 3, HW).transpose(1, 2, 0, 3).reshape(one, 3 * width).astype(f32)
        )
    else:
        grad_mixed = heads_to_tokens(mixed, 6, "to_tokens_back")
        qkv_out = spread_sum(tn(rows, grad_mixed.T))
        out_out = spread_sum(nn(attended, grad_branch))
        gate_out = spread_sum(tn(inner, grad_gate))
        up_out = spread_sum(tn(inner, grad_up))
        down_out = spread_sum(tn(hidden, grad_mlp))
        gains_out = spread_sum(gains.T).T
    token_grad = grad_h1 + lax.dot_general(
        grad_mixed, w_qkv, (((0,), (1,)), ((), ())), preferred_element_type=f32
    )
    return (
        scores, loss[0, 0], token_grad[None], qkv_out, out_out, gains_out[0], gains_out[1],
        gate_out, up_out, down_out, gains_out[2], gains_out[3],
    )


def solution(mesh):
    shard = P("dp", None)
    lone = P("dp")
    return jax.shard_map(
        local,
        mesh=mesh,
        in_specs=(P("tower", "dp", None), P("tower", "dp"), P("tower", "dp")) + (P(),) * 10,
        out_specs=(
            P(), P(), P("tower", "dp", None), shard, shard, lone, lone, shard, shard, shard, lone, lone,
        ),
        check_vma=False,
    )
```

```python
import functools

import jax
import jax.numpy as jnp
import numpy as np
from jax import lax
from jax.experimental import pallas as pl
from jax.experimental.pallas import tpu as pltpu
from jax.sharding import PartitionSpec as P

HEADS = 12
HEAD_DIM = 64
SPAN = 4
DOCS_GRP = 3
NH = HEADS // SPAN
HW = NH * HEAD_DIM
CHUNK = 512
VLIM = 62 * 2**20
MESH = pl.DeviceIdType.MESH
f32 = jnp.float32
bf = jnp.bfloat16
precise = lax.Precision.HIGHEST
norm_eps = 1e-05
ANY = pl.BlockSpec(memory_space=pl.ANY)
VM = pl.BlockSpec(memory_space=pltpu.VMEM)


def nn(a, b):
    return lax.dot_general(a, b, (((1,), (0,)), ((), ())), preferred_element_type=f32)


def nt(a, b):
    return lax.dot_general(a, b, (((1,), (1,)), ((), ())), preferred_element_type=f32)


def tn(a, b):
    return lax.dot_general(a, b, (((0,), (0,)), ((), ())), preferred_element_type=f32)


def split3(v):
    one = v.astype(bf).astype(f32)
    rest = v - one
    two = rest.astype(bf).astype(f32)
    return [one, two, rest - two]


def here():
    t = lax.axis_index("tower")
    p = lax.axis_index("dp")
    x = lax.rem(p, 2)
    y = lax.rem(lax.div(p, 2), 2)
    return t, p, x, y, lax.div(p, SPAN)


def plane_peers():
    t, p, x, y, g = here()
    px = p + 1 - 2 * x
    py = p + 2 - 4 * y
    pd = px + 2 - 4 * y
    return (t, px), (t, py), (t, pd)


def greet(peers):
    barrier = pltpu.get_barrier_semaphore()
    for peer in peers:
        pl.semaphore_signal(barrier, inc=1, device_id=peer, device_id_type=MESH)
    pl.semaphore_wait(barrier, len(peers))


def remote(src, dst, send, recv, peer):
    return pltpu.make_async_remote_copy(
        src_ref=src, dst_ref=dst, send_sem=send, recv_sem=recv, device_id=peer, device_id_type=MESH
    )


def dma_sems(n):
    return pltpu.SemaphoreType.DMA((n,))


def comm_params(cid):
    return pltpu.CompilerParams(collective_id=cid, has_side_effects=True, vmem_limit_bytes=VLIM)


def gather_kernel(tok_ref, code_ref, out_ref, codes_ref, send, recv, csend, crecv, lsem):
    t, p, x, y, g = here()
    count = tok_ref.shape[0]
    half = count // 2
    me = lax.rem(p, SPAN)
    ex, ey, ed = plane_peers()
    mx = lax.rem(ex[1], SPAN)
    my = lax.rem(ey[1], SPAN)

    def rows(m, h):
        return pl.ds(pl.multiple_of(m * count + h * half, half), half)

    def lanes(m):
        return pl.ds(pl.multiple_of(m * count, count), count)

    greet((ex, ey, ed))
    first = []
    for i, (peer, h) in enumerate(((ex, 0), (ey, 1), (ex, 1), (ey, 0))):
        c = remote(
            tok_ref.at[pl.ds(h * half, half)], out_ref.at[rows(me, h)], send.at[i], recv.at[i], peer
        )
        c.start()
        first.append(c)
    small = []
    for i, peer in enumerate((ex, ey, ed)):
        c = remote(code_ref, codes_ref.at[:, lanes(me)], csend.at[i], crecv.at[i], peer)
        c.start()
        small.append(c)
    own = pltpu.make_async_copy(tok_ref, out_ref.at[lanes(me)], lsem.at[0])
    own.start()
    own_code = pltpu.make_async_copy(code_ref, codes_ref.at[:, lanes(me)], lsem.at[1])
    own_code.start()
    first[0].wait_recv()
    f0 = remote(out_ref.at[rows(mx, 0)], out_ref.at[rows(mx, 0)], send.at[4], recv.at[4], ey)
    f0.start()
    first[1].wait_recv()
    f1 = remote(out_ref.at[rows(my, 1)], out_ref.at[rows(my, 1)], send.at[5], recv.at[5], ex)
    f1.start()
    first[2].wait_recv()
    first[3].wait_recv()
    f0.wait_recv()
    f1.wait_recv()
    for c in first + [f0, f1]:
        c.wait_send()
    for c in small:
        c.wait()
    own.wait()
    own_code.wait()


def gather(tok, code):
    count, width = tok.shape
    return pl.pallas_call(
        gather_kernel,
        out_shape=(
            jax.ShapeDtypeStruct((SPAN * count, width), bf),
            jax.ShapeDtypeStruct((1, SPAN * count), f32),
        ),
        in_specs=[VM, VM],
        out_specs=(ANY, ANY),
        scratch_shapes=[dma_sems(6), dma_sems(6), dma_sems(3), dma_sems(3), dma_sems(2)],
        compiler_params=comm_params(0),
        name="gather",
    )(tok, code)


def heads_to_tokens_kernel(parts, in_ref, out_ref, send, recv, lsem):
    t, p, x, y, g = here()
    count = out_ref.shape[1]
    me = lax.rem(p, SPAN)
    peers = plane_peers()
    width = parts and out_ref.shape[0] // parts
    greet(peers)
    copies = []
    for i, peer in enumerate((peers[2], peers[0], peers[1])):
        m = lax.rem(peer[1], SPAN)
        for k in range(parts):
            c = remote(
                in_ref.at[pl.ds(k * HW, HW), pl.ds(pl.multiple_of(m * count, count), count)],
                out_ref.at[pl.ds(pl.multiple_of(k * width + me * HW, HW), HW)],
                send.at[i * parts + k],
                recv.at[i * parts + k],
                peer,
            )
            c.start()
            copies.append(c)
    for k in range(parts):
        c = pltpu.make_async_copy(
            in_ref.at[pl.ds(k * HW, HW), pl.ds(pl.multiple_of(me * count, count), count)],
            out_ref.at[pl.ds(pl.multiple_of(k * width + me * HW, HW), HW)],
            lsem.at[k],
        )
        c.start()
        copies.append(c)
    for c in copies:
        c.wait()


def heads_to_tokens(a, cid, name):
    parts = a.shape[0] // HW
    count = a.shape[1] // SPAN
    return pl.pallas_call(
        functools.partial(heads_to_tokens_kernel, parts),
        out_shape=jax.ShapeDtypeStruct((parts * HEADS * HEAD_DIM, count), a.dtype),
        in_specs=[VM],
        out_specs=ANY,
        scratch_shapes=[dma_sems(3 * parts), dma_sems(3 * parts), dma_sems(parts)],
        compiler_params=comm_params(cid),
        name=name,
    )(a)


def tokens_to_heads_kernel(in_ref, out_ref, send, recv, lsem):
    t, p, x, y, g = here()
    count = in_ref.shape[1]
    me = lax.rem(p, SPAN)
    peers = plane_peers()
    greet(peers)
    mine = pl.ds(pl.multiple_of(me * count, count), count)
    copies = []
    for i, peer in enumerate((peers[2], peers[0], peers[1])):
        m = lax.rem(peer[1], SPAN)
        c = remote(
            in_ref.at[pl.ds(pl.multiple_of(m * HW, HW), HW)],
            out_ref.at[:, mine],
            send.at[i],
            recv.at[i],
            peer,
        )
        c.start()
        copies.append(c)
    c = pltpu.make_async_copy(
        in_ref.at[pl.ds(pl.multiple_of(me * HW, HW), HW)], out_ref.at[:, mine], lsem.at[0]
    )
    c.start()
    for c in copies + [c]:
        c.wait()


def tokens_to_heads(a, cid, name):
    return pl.pallas_call(
        tokens_to_heads_kernel,
        out_shape=jax.ShapeDtypeStruct((HW, SPAN * a.shape[1]), a.dtype),
        in_specs=[VM],
        out_specs=ANY,
        scratch_shapes=[dma_sems(3), dma_sems(3), dma_sems(1)],
        compiler_params=comm_params(cid),
        name=name,
    )(a)


def loss_kernel(groups, sums_ref, goal_ref, gp_ref, scores_ref, loss_ref, plane, allp, ge, send, recv):
    t, p, x, y, g = here()
    docs = groups * DOCS_GRP
    me = lax.rem(p, SPAN)
    peers = plane_peers()
    sibling = (1 - t, p)
    line = [(t, lax.rem(p + SPAN * k, SPAN * groups)) for k in range(1, groups)]
    greet(tuple(peers) + tuple(line) + (sibling,))
    copies = []
    for i, peer in enumerate(peers):
        c = remote(sums_ref, plane.at[i], send.at[i], recv.at[i], peer)
        c.start()
        copies.append(c)
    for c in copies:
        c.wait()
    own = sums_ref[...] + plane[0]
    own = own + (plane[1] + plane[2])
    allp[t, g] = own
    rows = allp.at[t, g]
    copies = []
    for i, peer in enumerate(line):
        c = remote(rows, rows, send.at[3 + i], recv.at[3 + i], peer)
        c.start()
        copies.append(c)
    for c in copies:
        c.wait()
    c = remote(allp.at[t], allp.at[t], send.at[2 + groups], recv.at[2 + groups], sibling)
    c.start()
    c.wait()
    width = sums_ref.shape[1]
    size = groups * 8
    pools = [allp[k].reshape(size, width) for k in range(2)]
    invs = [lax.rsqrt(jnp.sum(v * v, -1, keepdims=True) + 1e-06) for v in pools]
    embeds = [v * r for v, r in zip(pools, invs)]
    dot = functools.partial(lax.dot_general, precision=precise, preferred_element_type=f32)
    scores = dot(embeds[0], embeds[1], (((1,), (1,)), ((), ()))) * 50.0
    col = lax.broadcasted_iota(jnp.int32, (size, size), 1)
    row = lax.broadcasted_iota(jnp.int32, (size, size), 0)
    live = lax.rem(col, 8) < DOCS_GRP
    alive = lax.rem(row, 8) < DOCS_GRP
    masked = jnp.where(live, scores, -1e30)
    top = jnp.max(masked, -1, keepdims=True)
    total = jnp.sum(jnp.exp(masked - top), -1, keepdims=True)
    log_sums = top + jnp.log(total)
    hot = jnp.where(col.astype(f32) == goal_ref[:, 0:1], 1.0, 0.0)
    chosen = jnp.sum(hot * scores, -1, keepdims=True)
    each = jnp.where(alive[:, 0:1], log_sums - chosen, 0.0)
    loss_ref[...] = jnp.broadcast_to(jnp.sum(each, 0, keepdims=True) / docs, loss_ref.shape)
    scores_ref[...] = scores
    gs = jnp.where(alive & live, (jnp.exp(masked - log_sums) - hot) / docs, 0.0)
    gq = dot(gs, embeds[1], (((1,), (0,)), ((), ())))
    gd = dot(gs, embeds[0], (((0,), (0,)), ((), ())))
    ge[...] = jnp.where(t == 0, gq, gd) * 50.0
    mine = ge[pl.ds(pl.multiple_of(g * 8, 8), 8), :]
    pooled = allp[t, g]
    inv = lax.rsqrt(jnp.sum(pooled * pooled, -1, keepdims=True) + 1e-06)
    gp_ref[...] = inv * mine - inv * inv * inv * pooled * jnp.sum(pooled * mine, -1, keepdims=True)


def contrast(sums, goal, groups):
    size = groups * 8
    width = sums.shape[1]
    return pl.pallas_call(
        functools.partial(loss_kernel, groups),
        out_shape=(
            jax.ShapeDtypeStruct((8, width), f32),
            jax.ShapeDtypeStruct((size, size), f32),
            jax.ShapeDtypeStruct((8, 128), f32),
        ),
        in_specs=[VM, VM],
        out_specs=(VM, VM, VM),
        scratch_shapes=[
            pltpu.VMEM((3, 8, width), f32),
            pltpu.VMEM((2, groups, 8, width), f32),
            pltpu.VMEM((size, width), f32),
            dma_sems(3 + groups),
            dma_sems(3 + groups),
        ],
        compiler_params=comm_params(1),
        name="contrast",
    )(sums, goal)


def doc_limits(code):
    pad = code >= 4.0
    mem = jnp.where(pad, code - 4.0, code)
    n0 = jnp.sum(jnp.where(mem < 0.5, 1.0, 0.0)).astype(jnp.int32)
    n1 = jnp.sum(jnp.where(mem < 1.5, 1.0, 0.0)).astype(jnp.int32)
    l = [jnp.sum(jnp.where(code == float(d), 1.0, 0.0)).astype(jnp.int32) for d in range(3)]
    return n0, n1, l

def block_range(lims, a, size, total):
    n0, n1, l = lims
    b = a + size - 1
    first = (a >= n0).astype(jnp.int32) + (a >= n1).astype(jnp.int32)
    last = (b >= n0).astype(jnp.int32) + (b >= n1).astype(jnp.int32)
    lo = jnp.where(first == 0, 0, jnp.where(first == 1, n0, n1))
    hi = jnp.where(last == 0, n0, jnp.where(last == 1, n1, total))
    dead = jnp.zeros((), jnp.bool_)
    for d in range(3):
        dead = dead | ((first <= d) & (d <= last) & (l[d] == 0))
    return jnp.where(dead, 0, lo), jnp.where(dead, total, hi)

def fwd_kernel(KB, QB, tok_ref, wt_ref, cos_ref, sin_ref, code_ref, out_ref, lse_ref, o32_ref, qa_ref, ka_ref, va_ref,
               kt_ref, acc_ref):
    T = tok_ref.shape[0]
    CH = 512
    hw = HW
    code = code_ref[...]
    lims = doc_limits(code)
    def proj(c, _):
        sl = pl.ds(pl.multiple_of(c*CH, CH), CH)
        mx = nt(wt_ref[...], tok_ref[sl, :])
        cos = cos_ref[:, sl]; sin = sin_ref[:, sl]
        cd = code_ref[:, sl]
        mem = jnp.where(cd >= 4.0, cd-4.0, cd)
        hot = jnp.concatenate([jnp.where(mem == float(d), 1.0, 0.0) for d in range(3)] + [jnp.zeros((13, CH), f32)], 0)
        neg = jnp.concatenate([jnp.where(cd == float(d), 0.0, -1e30) for d in range(3)] + [jnp.zeros((13, CH), f32)], 0)
        zer = jnp.zeros((48, CH), f32)
        one = jnp.concatenate([jnp.ones((1, CH), f32), jnp.zeros((63, CH), f32)], 0)
        def rope(u):
            a = u[:32]; b = u[32:]
            return jnp.concatenate([a*cos - b*sin, b*cos + a*sin], 0)
        for h in range(NH):
            q = rope(mx[h*HEAD_DIM:(h+1)*HEAD_DIM]).astype(bf).astype(f32)*0.125
            k = rope(mx[hw+h*HEAD_DIM:hw+(h+1)*HEAD_DIM])
            v = mx[2*hw+h*HEAD_DIM:2*hw+(h+1)*HEAD_DIM]
            qa_ref[h, :, sl] = jnp.concatenate([q, hot, zer], 0).astype(bf)
            ka_ref[h, sl, :] = jnp.concatenate([k, neg, zer], 0).T.astype(bf)
            va_ref[h, :, sl] = jnp.concatenate([v, one], 0).astype(bf)
            kt_ref[h, :, sl] = k.astype(bf)
        return 0
    lax.fori_loop(0, T//CH, proj, 0)
    def qblock(i, _):
        a = i*QB
        qs = pl.ds(pl.multiple_of(a, QB), QB)
        lo, hi = block_range(lims, a, QB, T)
        jlo = lo//KB; jhi = (hi+KB-1)//KB
        for h in range(NH):
            acc_ref[h] = jnp.zeros_like(acc_ref[h])
        def kv(j, ms):
            ks = pl.ds(pl.multiple_of(j*KB, KB), KB)
            new = []
            ss = [nn(ka_ref[h, ks, :], qa_ref[h, :, qs]) for h in range(NH)]
            for h in range(NH):
                s = ss[h]
                mn = jnp.maximum(ms[h], jnp.max(s, 0, keepdims=True))
                p = jnp.exp(s - mn).astype(bf)
                al = jnp.exp(ms[h]-mn)
                acc_ref[h] = acc_ref[h]*al + nn(va_ref[h, :80, ks], p)
                new.append(mn)
            return tuple(new)
        ms = lax.fori_loop(jlo, jhi, kv, tuple(jnp.full((1, QB), -3e38, f32) for _ in range(NH)))
        for h in range(NH):
            tot = acc_ref[h, 64:65, :]
            o = acc_ref[h, :64, :]/tot
            o32_ref[h*HEAD_DIM:(h+1)*HEAD_DIM, qs] = o
            lse_ref[h:h+1, qs] = jnp.where(ms[h] < -1e29, 0.0, ms[h] + jnp.log(tot))
            out_ref[h*HEAD_DIM:(h+1)*HEAD_DIM, qs] = o.astype(bf)
        return 0
    lax.fori_loop(0, T//QB, qblock, 0)

def attn_fwd(tok, wt, cos, sin, code, KB=512, QB=256):
    T = tok.shape[0]
    return pl.pallas_call(functools.partial(fwd_kernel, KB, QB),
        out_shape=(jax.ShapeDtypeStruct((NH*HEAD_DIM, T), bf), jax.ShapeDtypeStruct((NH, T), f32), jax.ShapeDtypeStruct((NH*HEAD_DIM, T), f32),
                   jax.ShapeDtypeStruct((NH,128,T), bf), jax.ShapeDtypeStruct((NH,T,128), bf), jax.ShapeDtypeStruct((NH,128,T), bf), jax.ShapeDtypeStruct((NH,HEAD_DIM,T), bf)),
        in_specs=[pl.BlockSpec(memory_space=pltpu.VMEM)]*5, out_specs=tuple([pl.BlockSpec(memory_space=pltpu.VMEM)]*7),
        scratch_shapes=[pltpu.VMEM((NH,80,QB), f32)],
        compiler_params=pltpu.CompilerParams(vmem_limit_bytes=VLIM), name="attn_fwd",
        cost_estimate=pl.CostEstimate(flops=int(2*T*768*576+4*T*T*128*3), bytes_accessed=12<<20, transcendentals=T*T*3))(tok, wt, cos, sin, code)

def bwd_kernel(KB, QB, do_ref, o32_ref, lse_ref, qa_ref, ka_ref, va_ref, kt_ref, cos_ref, sin_ref, code_ref, g_ref,
               vn_ref, dn_ref, da_ref, qb_ref, acc_ref, dq_ref):
    T = do_ref.shape[1]
    hw = HW
    CH = 512
    lims = doc_limits(code_ref[...])
    def prep(c, _):
        sl = pl.ds(pl.multiple_of(c*CH, CH), CH)
        for h in range(NH):
            do = do_ref[h*HEAD_DIM:(h+1)*HEAD_DIM, sl].astype(f32)
            delta = jnp.sum(do*o32_ref[h*HEAD_DIM:(h+1)*HEAD_DIM, sl], 0, keepdims=True)
            def split(x):
                x1 = x.astype(bf).astype(f32); r = x-x1
                x2 = r.astype(bf).astype(f32); x3 = r-x2
                return [x1, x2, x3]
            z13 = jnp.zeros((13, CH), f32); z48 = jnp.zeros((48, CH), f32)
            da_ref[h, :, sl] = jnp.concatenate([do]+split(-delta)+[z13, z48], 0).astype(bf)
            one = jnp.concatenate([jnp.ones((3, CH), f32), jnp.zeros((61, CH), f32)], 0)
            v = va_ref[h, :64, sl].astype(f32)
            vn_ref[h, sl, :] = jnp.concatenate([v, one], 0).T.astype(bf)
            z64 = jnp.zeros((64, CH), f32)
            q = qa_ref[h, :64, sl].astype(f32)
            dn_ref[h, sl, :] = jnp.concatenate([do, z64], 0).T.astype(bf)
            qb_ref[h, sl, :] = jnp.concatenate([z64, q], 0).T.astype(bf)
            acc_ref[h, sl, :] = jnp.zeros((CH, 128), f32)
        return 0
    lax.fori_loop(0, T//CH, prep, 0)
    def qblock(i, _):
        a = i*QB
        qs = pl.ds(pl.multiple_of(a, QB), QB)
        lo, hi = block_range(lims, a, QB, T)
        jlo = lo//KB; jhi = (hi+KB-1)//KB
        dq_ref[...] = jnp.zeros_like(dq_ref)
        def kv(j, _):
            ks = pl.ds(pl.multiple_of(j*KB, KB), KB)
            for h in range(NH):
                s = nn(ka_ref[h, ks, :], qa_ref[h, :, qs])
                dp = nn(vn_ref[h, ks, :], da_ref[h, :, qs])
                p = jnp.exp(s - lse_ref[h:h+1, qs])
                ds = (p*dp).astype(bf)
                acc_ref[h, ks, :] += nn(p.astype(bf), dn_ref[h, qs, :]) + nn(ds, qb_ref[h, qs, :])
                dq_ref[h] += nn(kt_ref[h, :, ks], ds)
            return 0
        lax.fori_loop(jlo, jhi, kv, 0)
        cos = cos_ref[:, qs]; sin = sin_ref[:, qs]
        for h in range(NH):
            u = dq_ref[h]*0.125
            x1 = u[:32]; x2 = u[32:]
            g_ref[h*HEAD_DIM:(h+1)*HEAD_DIM, qs] = jnp.concatenate([x1*cos+x2*sin, x2*cos-x1*sin], 0).astype(bf)
        return 0
    lax.fori_loop(0, T//QB, qblock, 0)
    def fin(c, _):
        sl = pl.ds(pl.multiple_of(c*CH, CH), CH)
        cos = cos_ref[:, sl]; sin = sin_ref[:, sl]
        for h in range(NH):
            t = acc_ref[h, sl, :].T
            x1 = t[64:96]; x2 = t[96:128]
            g_ref[hw+h*HEAD_DIM:hw+(h+1)*HEAD_DIM, sl] = jnp.concatenate([x1*cos+x2*sin, x2*cos-x1*sin], 0).astype(bf)
            g_ref[2*hw+h*HEAD_DIM:2*hw+(h+1)*HEAD_DIM, sl] = t[:64].astype(bf)
        return 0
    lax.fori_loop(0, T//CH, fin, 0)

def attn_bwd(do, o32, lse, qa, ka, va, kt, cos, sin, code, KB=512, QB=256):
    T = do.shape[1]
    return pl.pallas_call(functools.partial(bwd_kernel, KB, QB),
        out_shape=jax.ShapeDtypeStruct((3*NH*HEAD_DIM, T), bf),
        in_specs=[pl.BlockSpec(memory_space=pltpu.VMEM)]*10, out_specs=pl.BlockSpec(memory_space=pltpu.VMEM),
        scratch_shapes=[pltpu.VMEM((NH,T,128), bf), pltpu.VMEM((NH,T,128), bf), pltpu.VMEM((NH,128,T), bf), pltpu.VMEM((NH,T,128), bf),
                        pltpu.VMEM((NH,T,128), f32), pltpu.VMEM((NH,HEAD_DIM,QB), f32)],
        compiler_params=pltpu.CompilerParams(vmem_limit_bytes=VLIM), name="attn_bwd",
        cost_estimate=pl.CostEstimate(flops=int(10*T*T*128*3), bytes_accessed=12<<20, transcendentals=T*T*3))(do, o32, lse, qa, ka, va, kt, cos, sin, code)


def weights_kernel(
    groups, ia, ib, ga, gb, ha, hb, ma, mb, aa, ab, ba, bb, in_ref,
    sa_ref, ka_ref, sb_ref, kb_ref, heads_ref,
    iv, it, gv, hv, mv, av, bv, gs, ds, os, isem, osem, send, recv, lsem,
):
    t, p, x, y, g = here()
    peers = plane_peers()
    greet(peers)
    tokens = in_ref.shape[1]
    me = lax.rem(p, SPAN)
    mine = pl.ds(pl.multiple_of(me * tokens, tokens), tokens)
    moves = []
    for i, peer in enumerate((peers[2], peers[0], peers[1])):
        m = lax.rem(peer[1], SPAN)
        moves.append(remote(
            in_ref.at[pl.ds(pl.multiple_of(m * HW, HW), HW)], heads_ref.at[:, mine],
            send.at[i], recv.at[i], peer,
        ))
    moves.append(pltpu.make_async_copy(
        in_ref.at[pl.ds(pl.multiple_of(me * HW, HW), HW)], heads_ref.at[:, mine], lsem.at[0]
    ))
    for c in moves:
        c.start()
    count, width = ia.shape
    half = width // 2
    tiles = gv.shape[1]
    shards = SPAN * groups
    one = width // shards
    down = ha.shape[1] // shards

    def load(i, src, dst):
        return pltpu.make_async_copy(src, dst, isem.at[i])

    def tile(pair, j, buf, base):
        cols = pl.ds(pl.multiple_of(j * half, half), half)
        return [load(base + i * tiles + j, a.at[:, cols], buf.at[i, j]) for i, a in enumerate(pair)]

    few = [(ma, mv.at[0]), (mb, mv.at[1]), (aa, av.at[0]), (ab, av.at[1]),
           (ba, bv.at[0]), (bb, bv.at[1]), (ia, iv.at[0]), (ib, iv.at[1])]
    few = [load(i, a, b) for i, (a, b) in enumerate(few)]
    for c in few[:2]:
        c.start()
    for j in range(tiles):
        for c in tile((ha, hb), j, hv, 8):
            c.start()
    for c in few[2:]:
        c.start()
    for j in range(tiles):
        for c in tile((ga, gb), j, gv, 8 + 2 * tiles):
            c.start()
    for c in few[:2]:
        c.wait()

    def downward(j, _):
        for c in tile((ha, hb), j, hv, 8):
            c.wait()
        r = tn(hv[0, j], mv[0]) + tn(hv[1, j], mv[1])
        ds[pl.ds(j * (half // down), half // down)] = r.astype(bf).reshape(half // down, down, half)
        return 0

    lax.fori_loop(0, tiles, downward, 0)
    for c in few[2:]:
        c.wait()
    r = nn(av[0], bv[0]) + nn(av[1], bv[1])
    os[...] = r.astype(bf).reshape(shards, one, half)
    for i in range(2):
        it[:, i * count : (i + 1) * count] = iv[i].T
    fours = lambda ref, n: ref.reshape(groups, 2, 2, n, half)

    def put(i, src, dst):
        return pltpu.make_async_copy(src, dst, osem.at[i])

    last = (tiles - 1) * one
    outs = []
    for i, (ref, k) in enumerate(((sb_ref, 1 - y), (kb_ref, y))):
        outs.append(put(4 * i, fours(ds, down).at[:, k], ref.at[:, :, pl.ds(one, down)]))
        outs.append(put(4 * i + 1, fours(os, one).at[:, k], ref.at[:, :, pl.ds(one + down, one)]))
    for c in outs:
        c.start()

    def upward(j, _):
        for c in tile((ga, gb), j, gv, 8 + 2 * tiles):
            c.wait()
        r = nn(it[:, :count], gv[0, j]) + nn(it[:, count:], gv[1, j])
        gs[j] = r.astype(bf).reshape(shards, one, half)
        return 0

    def upper(j, _):
        upward(j, 0)
        rows = pl.ds(pl.multiple_of(j * one, one), one)
        piece = fours(gs.at[j], one)
        put(8 + j, piece.at[:, :, 1 - x], sa_ref.at[:, :, rows]).start()
        put(8 + tiles + j, piece.at[:, :, x], ka_ref.at[:, :, rows]).start()
        return 0

    lax.fori_loop(0, tiles - 1, upper, 0)
    upward(tiles - 1, 0)
    piece = fours(gs.at[tiles - 1], one)
    for i, (ref, k) in enumerate(((sb_ref, 1 - y), (kb_ref, y))):
        c = put(4 * i + 2, piece.at[:, k], ref.at[:, :, pl.ds(0, one)])
        c.start()
        outs.append(c)

    def landed(j, _):
        rows = pl.ds(pl.multiple_of(j * one, one), one)
        put(8 + j, fours(gs.at[j], one).at[:, :, 0], sa_ref.at[:, :, rows]).wait()
        put(8 + tiles + j, fours(gs.at[j], one).at[:, :, 0], ka_ref.at[:, :, rows]).wait()
        return 0

    lax.fori_loop(0, tiles - 1, landed, 0)
    for c in outs + moves:
        c.wait()


def weight_grads(groups, grad_heads, *arrays):
    count, width = arrays[0].shape
    half = width // 2
    shards = SPAN * groups
    one = width // shards
    tiles = arrays[2].shape[1] // half
    down = arrays[4].shape[1] // shards
    ra = (tiles - 1) * one
    rb = down + 2 * one
    part = lambda r: jax.ShapeDtypeStruct((groups, 2, r, half), bf)
    vm = lambda *n: pltpu.VMEM(n, bf)
    return pl.pallas_call(
        functools.partial(weights_kernel, groups),
        out_shape=(
            part(ra), part(ra), part(rb), part(rb),
            jax.ShapeDtypeStruct((HW, SPAN * grad_heads.shape[1]), bf),
        ),
        in_specs=[ANY] * 12 + [VM],
        out_specs=(ANY,) * 5,
        scratch_shapes=[
            vm(2, count, width), vm(width, 2 * count), vm(2, tiles, count, half), vm(2, tiles, count, half),
            vm(2, count, half), vm(2, width, count), vm(2, count, half),
            vm(tiles, shards, one, half), vm(shards, down, half), vm(shards, one, half),
            dma_sems(8 + 4 * tiles), dma_sems(8 + 2 * tiles), dma_sems(3), dma_sems(3), dma_sems(1),
        ],
        compiler_params=comm_params(2),
        name="weight_grads",
        cost_estimate=pl.CostEstimate(flops=int(2 * 2 * count * half * width * 8.5), bytes_accessed=30 << 20, transcendentals=0),
    )(*arrays, grad_heads)


def add_rows(dst, a, b, rows):
    def step(i, _):
        sl = pl.ds(pl.multiple_of(i * 16, 16), 16)
        dst[sl, :] = (a[sl, :].astype(f32) + b[sl, :].astype(f32)).astype(bf)
        return 0

    lax.fori_loop(0, rows // 16, step, 0)


class Line:
    def __init__(self, z, zt, groups, part, up, down, sems, t, p):
        self.z, self.zt, self.groups = z, zt, groups
        self.part, self.up, self.down = part, up, down
        us, ur, ds, dr = sems
        above = (t, lax.rem(p + SPAN, SPAN * groups))
        below = (t, lax.rem(p + SPAN * (groups - 1), SPAN * groups))
        self.up_first = lambda: remote(part, up, us, ur, above)
        self.up_next = lambda: remote(up, up, us, ur, above)
        self.down_first = lambda: remote(part, down, ds, dr, below)
        self.down_next = lambda: remote(down, down, ds, dr, below)

    def start(self):
        if self.zt > 0:
            pl.when(self.z == 0)(lambda: self.up_first().start())
        if self.zt < self.groups - 1:
            pl.when(self.z == self.groups - 1)(lambda: self.down_first().start())

    def relay(self, hop, rows):
        def up():
            self.up_next().wait_recv()
            add_rows(self.up, self.up, self.part, rows)
            self.up_next().start()

        def down():
            self.down_next().wait_recv()
            add_rows(self.down, self.down, self.part, rows)
            self.down_next().start()

        if 0 < hop < self.zt:
            pl.when(self.z == hop)(up)
        if self.zt < self.groups - 1 - hop:
            pl.when(self.z == self.groups - 1 - hop)(down)

    def finish(self, dst, rows):
        def done():
            if self.zt > 0:
                self.up_next().wait_recv()
            if self.zt < self.groups - 1:
                self.down_next().wait_recv()
            if 0 < self.zt < self.groups - 1:
                add_rows(self.up, self.up, self.down, rows)
            add_rows(dst, self.up if self.zt > 0 else self.down, self.part, rows)

        pl.when(self.z == self.zt)(done)

    def drain(self):
        if self.zt > 0:
            pl.when(self.z < self.zt)(lambda: self.up_first().wait_send())
        if self.zt < self.groups - 1:
            pl.when(self.z > self.zt)(lambda: self.down_first().wait_send())


def outward(groups):
    order = []
    lo, hi = 0, groups - 1
    while lo <= hi:
        order.append(hi)
        if lo < hi:
            order.append(lo)
        lo, hi = lo + 1, hi - 1
    return order


def finish_kernel(
    groups, ka_ref, kb_ref, ra_ref, rb_ref, g_ref, tok_ref, gain_ref,
    pair_ref, sum_ref, gm_ref, out_ref,
    kva, kvb, rva, rvb, r2a, r2b, ua, ub, da, db, isem, s2, q2, us, ur, ds, dr,
    plane, line, gs, gr, fs, fr,
    w2, sib, ub2, db2, fin, send, recv, ts, tr, us2, ur2, ds2, dr2, ps, pr, lsem,
):
    t, p, x, y, z = here()
    ex, ey, ed = plane_peers()
    peers = (ex, ey, ed)
    sibling = (1 - t, p)
    others = [(t, lax.rem(p + SPAN * k, SPAN * groups)) for k in range(1, groups)]
    across = tuple((1 - t, q[1]) for q in peers)
    order = outward(groups)
    colours = (
        (ey, ka_ref, ra_ref, kva, rva, r2a, ua, da, y),
        (ex, kb_ref, rb_ref, kvb, rvb, r2b, ub, db, x),
    )

    def loads(c, zt):
        peer, kr, rr, kv, rv = colours[c][:5]
        i = 2 * (c * groups + zt)
        return (
            pltpu.make_async_copy(kr.at[zt], kv.at[zt], isem.at[i]),
            pltpu.make_async_copy(rr.at[zt], rv.at[zt], isem.at[i + 1]),
        )

    for zt in order:
        for c in range(2):
            for d in loads(c, zt):
                d.start()
    greet(peers + across + (sibling,) + tuple(others))
    for i, peer in enumerate(peers):
        remote(gain_ref, plane.at[i], gs.at[i], gr.at[i], peer).start()

    def second(c, zt):
        peer, kr, rr, kv, rv, r2, u, d, mine = colours[c]
        i = c * groups + zt
        return remote(rv.at[zt, 1 - mine], r2.at[zt], s2.at[i], q2.at[i], peer)

    def chain(c, zt):
        peer, kr, rr, kv, rv, r2, u, d, mine = colours[c]
        i = c * groups + zt
        return Line(z, zt, groups, r2.at[zt], u.at[zt], d.at[zt],
                    (us.at[i], ur.at[i], ds.at[i], dr.at[i]), t, p)

    def size(c):
        return colours[c][3].shape[2]

    for zt in order:
        for c in range(2):
            for d in loads(c, zt):
                d.wait()
            peer, kr, rr, kv, rv, r2, u, d, mine = colours[c]
            away = rv.at[zt, 1 - mine]
            add_rows(away, away, kv.at[zt, 1 - mine], size(c))
            second(c, zt).start()
    count = gm_ref.shape[1]
    me = lax.rem(p, SPAN)
    width = gm_ref.shape[0] // 3
    copies = []
    for i, peer in enumerate((peers[2], peers[0], peers[1])):
        m = lax.rem(peer[1], SPAN)
        for k in range(3):
            copies.append(remote(
                g_ref.at[pl.ds(k * HW, HW), pl.ds(pl.multiple_of(m * count, count), count)],
                gm_ref.at[pl.ds(pl.multiple_of(k * width + me * HW, HW), HW)],
                send.at[i * 3 + k], recv.at[i * 3 + k], peer,
            ))
    for k in range(3):
        copies.append(pltpu.make_async_copy(
            g_ref.at[pl.ds(k * HW, HW), pl.ds(pl.multiple_of(me * count, count), count)],
            gm_ref.at[pl.ds(pl.multiple_of(k * width + me * HW, HW), HW)],
            lsem.at[k],
        ))
    for c in copies:
        c.start()
    for zt in order:
        for c in range(2):
            peer, kr, rr, kv, rv, r2, u, d, mine = colours[c]
            keep = rv.at[zt, mine]
            add_rows(keep, keep, kv.at[zt, mine], size(c))
    for i, peer in enumerate(peers):
        remote(gain_ref, plane.at[i], gs.at[i], gr.at[i], peer).wait()
    line[0] = (gain_ref[...] + plane[0]) + (plane[1] + plane[2])
    ring = [remote(line.at[0], line.at[1 + k], gs.at[3 + k], gr.at[3 + k], peer) for k, peer in enumerate(others)]
    for c in ring:
        c.start()

    def in_plane(zt):
        for c in range(2):
            peer, kr, rr, kv, rv, r2, u, d, mine = colours[c]
            second(c, zt).wait_recv()
            dst = r2.at[zt]
            add_rows(dst, dst, rv.at[zt, mine], size(c))
            chain(c, zt).start()

    def relay(zt, hop):
        for c in range(2):
            chain(c, zt).relay(hop, size(c))

    in_plane(order[0])
    shards = SPAN * groups
    one = width // shards
    half = width // 2
    for h in range(2):
        r = nn(g_ref[...], tok_ref[:, h * half : (h + 1) * half]).T
        w2[h * (shards // 2) : (h + 1) * (shards // 2)] = r.astype(bf).reshape(shards // 2, one, 3 * HW)

    def swap(zt):
        return remote(w2.at[pl.ds(zt * 4 + (1 - t) * 2, 2)], sib.at[zt], ts.at[zt], tr.at[zt], sibling)

    for zt in order:
        swap(zt).start()

    def chain2(zt, k):
        i = zt * 2 + k
        return Line(z, zt, groups, sib.at[zt, k], ub2.at[zt, k], db2.at[zt, k],
                    (us2.at[i], ur2.at[i], ds2.at[i], dr2.at[i]), t, p)

    for i, zt in enumerate(order):
        if i >= 1:
            in_plane(zt)
        swap(zt).wait_recv()
        for k in range(2):
            dst = sib.at[zt, k]
            add_rows(dst, dst, w2.at[zt * 4 + t * 2 + k], one)
            chain2(zt, k).start()
        if i >= 1:
            relay(order[i - 1], 1)
            for k in range(2):
                chain2(order[i - 1], k).relay(1, one)
    for c in ring:
        c.wait()
    total = line[0]
    for k in range(1, groups):
        total = total + line[k]
    line[groups] = total
    both = remote(line.at[groups], line.at[groups + 1], gs.at[2 + groups], gr.at[2 + groups], sibling)
    both.start()
    for hop in range(1, groups - 1):
        for i, zt in enumerate(order):
            if hop > 1 or i == groups - 1:
                relay(zt, hop)
                for k in range(2):
                    chain2(zt, k).relay(hop, one)
    for zt in order:
        for k in range(2):
            chain2(zt, k).finish(fin.at[k], one)
    here_id = t * SPAN + me

    def hand(k, tt):
        m = t * 2 + k
        peer = (tt, z * SPAN + m)
        i = k * 2 + tt
        away = lambda: remote(fin.at[k], out_ref.at[me], ps.at[i], pr.at[me], peer)
        stay = lambda: pltpu.make_async_copy(fin.at[k], out_ref.at[me], lsem.at[3])
        return away, stay, (tt * SPAN + m) == here_id

    for k in range(2):
        for tt in range(2):
            away, stay, same = hand(k, tt)
            pl.when(jnp.logical_not(same))(lambda away=away: away().start())
            pl.when(same)(lambda stay=stay: stay().start())
    for zt in order:
        for c, sl in ((0, pl.ds(0, size(0))), (1, pl.ds(size(0), size(1)))):
            chain(c, zt).finish(pair_ref.at[t, sl], size(c))
    last = remote(pair_ref.at[t], pair_ref.at[t], fs.at[0], fr.at[0], sibling)
    last.start()
    both.wait()
    sum_ref[...] = line[groups] + line[groups + 1]
    for s in range(SPAN):
        from_here = jnp.logical_and(s == me, y == t)
        pl.when(jnp.logical_not(from_here))(
            lambda s=s: remote(fin.at[0], out_ref.at[s], ps.at[0], pr.at[s], sibling).wait_recv()
        )
    for k in range(2):
        for tt in range(2):
            away, stay, same = hand(k, tt)
            pl.when(jnp.logical_not(same))(lambda away=away: away().wait_send())
            pl.when(same)(lambda stay=stay: stay().wait())
    for zt in range(groups):
        swap(zt).wait_send()
        for k in range(2):
            chain2(zt, k).drain()
        for c in range(2):
            second(c, zt).wait_send()
            chain(c, zt).drain()
    for c in copies:
        c.wait()
    last.wait()


def finish(ka, kb, ra, rb, g, tok, gains, groups):
    width = tok.shape[1]
    count = tok.shape[0] // SPAN
    one = width // (SPAN * groups)
    na, nb = ka.shape[2], kb.shape[2]
    half = ka.shape[3]
    buf = lambda *n: pltpu.VMEM(n, bf)
    mix = lambda *n: pltpu.VMEM(n + (one, 3 * HW), bf)
    return pl.pallas_call(
        functools.partial(finish_kernel, groups),
        out_shape=(
            jax.ShapeDtypeStruct((2, na + nb, half), bf),
            jax.ShapeDtypeStruct(gains.shape, f32),
            jax.ShapeDtypeStruct((3 * width, count), bf),
            jax.ShapeDtypeStruct((SPAN, one, 3 * HW), bf),
        ),
        in_specs=[ANY] * 4 + [VM] * 3,
        out_specs=(VM, VM, ANY, VM),
        scratch_shapes=[
            buf(groups, 2, na, half), buf(groups, 2, nb, half), buf(groups, 2, na, half), buf(groups, 2, nb, half),
            buf(groups, na, half), buf(groups, nb, half), buf(groups, na, half), buf(groups, nb, half),
            buf(groups, na, half), buf(groups, nb, half),
            dma_sems(4 * groups), dma_sems(2 * groups), dma_sems(2 * groups),
            dma_sems(2 * groups), dma_sems(2 * groups), dma_sems(2 * groups), dma_sems(2 * groups),
            pltpu.VMEM((3,) + gains.shape, f32), pltpu.VMEM((groups + 2,) + gains.shape, f32),
            dma_sems(3 + groups), dma_sems(3 + groups), dma_sems(1), dma_sems(1),
            mix(SPAN * groups), mix(groups, 2), mix(groups, 2), mix(groups, 2), mix(2),
            dma_sems(9), dma_sems(9), dma_sems(groups), dma_sems(groups),
            dma_sems(2 * groups), dma_sems(2 * groups), dma_sems(2 * groups), dma_sems(2 * groups),
            dma_sems(4), dma_sems(SPAN), dma_sems(4),
        ],
        compiler_params=comm_params(3),
        name="finish",
    )(ka, kb, ra, rb, g, tok, gains)


def swapped(value):
    return lax.ppermute(value, "tower", [(0, 1), (1, 0)])


def norm_rows(values, gain, bias):
    centred = values - jnp.mean(values, -1, keepdims=True)
    spread = jnp.mean(centred * centred, -1, keepdims=True)
    scale = lax.rsqrt(spread + norm_eps)
    normed = centred * scale
    return normed * gain + bias, normed, scale


def norm_back(grad, normed, scale, gain):
    shaped = grad * gain
    inner = (
        shaped
        - jnp.mean(shaped, -1, keepdims=True)
        - normed * jnp.mean(shaped * normed, -1, keepdims=True)
    )
    return inner * scale, jnp.sum(grad * normed, 0), jnp.sum(grad, 0)


def angle_tables(total):
    half = HEAD_DIM // 2
    freqs = np.float32(1000.0) ** (-np.arange(half, dtype=np.float32) / np.float32(half))
    theta = freqs[:, None].astype(np.float32) * np.arange(total, dtype=np.float32)[None, :]
    return np.cos(theta).astype(np.float32), np.sin(theta).astype(np.float32)


def spread_sum(value):
    part = lax.psum_scatter(value, "dp", scatter_dimension=0, tiled=True)
    return lax.psum(part.astype(bf), "tower").astype(f32)


def local(
    tokens, doc_ids, pad_mask, targets, w_qkv, w_out, ln1_gain, ln1_bias,
    w_gate, w_up, w_down, ln2_gain, ln2_bias,
):
    width = w_out.shape[0]
    rows = tokens[0]
    count = rows.shape[0]
    places = lax.axis_size("dp")
    groups = places // SPAN
    tower = lax.axis_index("tower")
    place = lax.axis_index("dp")
    me = place % SPAN
    member_of = doc_ids[0] % DOCS_GRP
    live = pad_mask[0] == 1
    code = jnp.where(live, member_of, member_of + 4).astype(f32)[None, :]
    docs = groups * DOCS_GRP
    slot = jnp.arange(groups * 8)
    goal = jnp.where(
        slot % 8 < DOCS_GRP, targets[jnp.minimum(slot // 8 * DOCS_GRP + slot % 8, docs - 1)], 0
    )
    goal = jnp.where(slot % 8 < DOCS_GRP, goal // DOCS_GRP * 8 + goal % DOCS_GRP, -1)
    goal = jnp.broadcast_to(goal.astype(f32)[:, None], (groups * 8, 128))
    cols = [lax.dynamic_slice_in_dim(w_qkv, k * width + me * HW, HW, 1) for k in range(3)]
    w_mine = jnp.concatenate(cols, 1).T
    cos, sin = angle_tables(SPAN * count)
    tok_all, codes = gather(rows, code)
    heads_out, lse, exact, qa, ka, va, kt = attn_fwd(tok_all, w_mine, cos, sin, codes)
    attended = heads_to_tokens(heads_out, 4, "to_tokens")
    branch = tn(attended, w_out)
    first, normed_one, scale_one = norm_rows(rows.astype(f32) + branch, ln1_gain, ln1_bias)
    inner = first.astype(bf)
    gate = nn(inner, w_gate)
    upper = nn(inner, w_up)
    sigmoid = jax.nn.sigmoid(gate)
    activated = gate * sigmoid
    hidden = (activated * upper).astype(bf)
    second, normed_two, scale_two = norm_rows(first + nn(hidden, w_down), ln2_gain, ln2_bias)
    member = ((member_of[:, None] == jnp.arange(8)[None, :]) & live[:, None]).astype(f32)
    sums = jnp.dot(member.T, second, precision=precise)
    grad_pool, scores_all, loss = contrast(sums, goal, groups)
    scores = scores_all.reshape(groups, 8, groups, 8)[:, :DOCS_GRP, :, :DOCS_GRP].reshape(docs, docs)
    grad_second = jnp.dot(member, grad_pool, precision=precise)
    grad_h2, gain_two, bias_two = norm_back(grad_second, normed_two, scale_two, ln2_gain)
    grad_mlp = grad_h2.astype(bf)
    grad_hidden = nt(grad_mlp, w_down)
    grad_gate = (grad_hidden * upper * sigmoid * (1.0 + gate * (1.0 - sigmoid))).astype(bf)
    grad_up = (grad_hidden * activated).astype(bf)
    grad_first = grad_h2 + nt(grad_gate, w_gate) + nt(grad_up, w_up)
    grad_h1, gain_one, bias_one = norm_back(grad_first, normed_one, scale_one, ln1_gain)
    grad_branch = grad_h1.astype(bf)
    grad_attended = nt(w_out, grad_branch).astype(bf)
    gains = jnp.stack([gain_one, bias_one, gain_two, bias_two], 0)
    here_first = tower == 0
    by_hand = width % (16 * places) == 0
    if by_hand:
        half = width // 2
        own = lambda v: lax.dynamic_slice_in_dim(v, tower * half, half, 1)
        its = lambda v: lax.dynamic_slice_in_dim(v, (1 - tower) * half, half, 1)
        kept = jnp.where(here_first, grad_gate, grad_up)
        sent = jnp.where(here_first, grad_up, grad_gate)
        send_a, keep_a, send_b, keep_b, d_heads = weight_grads(
            groups, grad_attended, inner, swapped(inner), kept, swapped(sent), hidden, swapped(hidden),
            own(grad_mlp), swapped(its(grad_mlp)), attended, swapped(attended),
            own(grad_branch), swapped(its(grad_branch)),
        )
        exchange = lambda v, bit: lax.ppermute(v, "dp", [(i, i ^ bit) for i in range(places)])
        came_a, came_b = exchange(send_a, 1), exchange(send_b, 2)
    else:
        d_heads = tokens_to_heads(grad_attended, 5, "to_heads")
    mixed = attn_bwd(d_heads, exact, lse, qa, ka, va, kt, cos, sin, codes)
    if by_hand:
        one = width // places
        down = w_down.shape[0] // places
        padded = jnp.concatenate([gains, jnp.zeros_like(gains)], 0)
        pair, gain_sums, grad_mixed, qkv_parts = finish(
            keep_a, keep_b, came_a, came_b, mixed, tok_all, padded, groups
        )
        top = pair.shape[1] - down - one
        unfold = lambda v: v.reshape(top // one, one, half).transpose(1, 0, 2).reshape(one, -1)
        sides = lambda v: jnp.concatenate([v[0], v[1]], 1).astype(f32)
        gate_out = unfold(pair[0, :top]).astype(f32)
        up_out = unfold(pair[1, :top]).astype(f32)
        down_out = sides(pair[:, top : top + down])
        out_out = sides(pair[:, top + down :])
        gains_out = lax.dynamic_slice_in_dim(gain_sums[:4], place * one, one, 1)
        qkv_out = (
            qkv_parts.reshape(SPAN, one, 3, HW).transpose(1, 2, 0, 3).reshape(one, 3 * width).astype(f32)
        )
    else:
        grad_mixed = heads_to_tokens(mixed, 6, "to_tokens_back")
        qkv_out = spread_sum(tn(rows, grad_mixed.T))
        out_out = spread_sum(nn(attended, grad_branch))
        gate_out = spread_sum(tn(inner, grad_gate))
        up_out = spread_sum(tn(inner, grad_up))
        down_out = spread_sum(tn(hidden, grad_mlp))
        gains_out = spread_sum(gains.T).T
    token_grad = grad_h1 + lax.dot_general(
        grad_mixed, w_qkv, (((0,), (1,)), ((), ())), preferred_element_type=f32
    )
    return (
        scores, loss[0, 0], token_grad[None], qkv_out, out_out, gains_out[0], gains_out[1],
        gate_out, up_out, down_out, gains_out[2], gains_out[3],
    )


def solution(mesh):
    shard = P("dp", None)
    lone = P("dp")
    return jax.shard_map(
        local,
        mesh=mesh,
        in_specs=(P("tower", "dp", None), P("tower", "dp"), P("tower", "dp")) + (P(),) * 10,
        out_specs=(
            P(), P(), P("tower", "dp", None), shard, shard, lone, lone, shard, shard, shard, lone, lone,
        ),
        check_vma=False,
    )
```

```python
import functools

import jax
import jax.numpy as jnp
import numpy as np
from jax import lax
from jax.experimental import pallas as pl
from jax.experimental.pallas import tpu as pltpu
from jax.sharding import PartitionSpec as P

HEADS = 12
HEAD_DIM = 64
SPAN = 4
DOCS_GRP = 3
NH = HEADS // SPAN
HW = NH * HEAD_DIM
CHUNK = 512
VLIM = 62 * 2**20
MESH = pl.DeviceIdType.MESH
f32 = jnp.float32
bf = jnp.bfloat16
precise = lax.Precision.HIGHEST
norm_eps = 1e-05
ANY = pl.BlockSpec(memory_space=pl.ANY)
VM = pl.BlockSpec(memory_space=pltpu.VMEM)


def nn(a, b):
    return lax.dot_general(a, b, (((1,), (0,)), ((), ())), preferred_element_type=f32)


def nt(a, b):
    return lax.dot_general(a, b, (((1,), (1,)), ((), ())), preferred_element_type=f32)


def tn(a, b):
    return lax.dot_general(a, b, (((0,), (0,)), ((), ())), preferred_element_type=f32)


def split3(v):
    one = v.astype(bf).astype(f32)
    rest = v - one
    two = rest.astype(bf).astype(f32)
    return [one, two, rest - two]


def here():
    t = lax.axis_index("tower")
    p = lax.axis_index("dp")
    x = lax.rem(p, 2)
    y = lax.rem(lax.div(p, 2), 2)
    return t, p, x, y, lax.div(p, SPAN)


def plane_peers():
    t, p, x, y, g = here()
    px = p + 1 - 2 * x
    py = p + 2 - 4 * y
    pd = px + 2 - 4 * y
    return (t, px), (t, py), (t, pd)


def greet(peers):
    barrier = pltpu.get_barrier_semaphore()
    for peer in peers:
        pl.semaphore_signal(barrier, inc=1, device_id=peer, device_id_type=MESH)
    pl.semaphore_wait(barrier, len(peers))


def remote(src, dst, send, recv, peer):
    return pltpu.make_async_remote_copy(
        src_ref=src, dst_ref=dst, send_sem=send, recv_sem=recv, device_id=peer, device_id_type=MESH
    )


def dma_sems(n):
    return pltpu.SemaphoreType.DMA((n,))


def comm_params(cid):
    return pltpu.CompilerParams(collective_id=cid, has_side_effects=True, vmem_limit_bytes=VLIM)


def gather_kernel(tok_ref, code_ref, out_ref, codes_ref, send, recv, csend, crecv, lsem):
    t, p, x, y, g = here()
    count = tok_ref.shape[0]
    half = count // 2
    me = lax.rem(p, SPAN)
    ex, ey, ed = plane_peers()
    mx = lax.rem(ex[1], SPAN)
    my = lax.rem(ey[1], SPAN)

    def rows(m, h):
        return pl.ds(pl.multiple_of(m * count + h * half, half), half)

    def lanes(m):
        return pl.ds(pl.multiple_of(m * count, count), count)

    greet((ex, ey, ed))
    first = []
    for i, (peer, h) in enumerate(((ex, 0), (ey, 1), (ex, 1), (ey, 0))):
        c = remote(
            tok_ref.at[pl.ds(h * half, half)], out_ref.at[rows(me, h)], send.at[i], recv.at[i], peer
        )
        c.start()
        first.append(c)
    small = []
    for i, peer in enumerate((ex, ey, ed)):
        c = remote(code_ref, codes_ref.at[:, lanes(me)], csend.at[i], crecv.at[i], peer)
        c.start()
        small.append(c)
    own = pltpu.make_async_copy(tok_ref, out_ref.at[lanes(me)], lsem.at[0])
    own.start()
    own_code = pltpu.make_async_copy(code_ref, codes_ref.at[:, lanes(me)], lsem.at[1])
    own_code.start()
    first[0].wait_recv()
    f0 = remote(out_ref.at[rows(mx, 0)], out_ref.at[rows(mx, 0)], send.at[4], recv.at[4], ey)
    f0.start()
    first[1].wait_recv()
    f1 = remote(out_ref.at[rows(my, 1)], out_ref.at[rows(my, 1)], send.at[5], recv.at[5], ex)
    f1.start()
    first[2].wait_recv()
    first[3].wait_recv()
    f0.wait_recv()
    f1.wait_recv()
    for c in first + [f0, f1]:
        c.wait_send()
    for c in small:
        c.wait()
    own.wait()
    own_code.wait()


def gather(tok, code):
    count, width = tok.shape
    return pl.pallas_call(
        gather_kernel,
        out_shape=(
            jax.ShapeDtypeStruct((SPAN * count, width), bf),
            jax.ShapeDtypeStruct((1, SPAN * count), f32),
        ),
        in_specs=[VM, VM],
        out_specs=(ANY, ANY),
        scratch_shapes=[dma_sems(6), dma_sems(6), dma_sems(3), dma_sems(3), dma_sems(2)],
        compiler_params=comm_params(0),
        name="gather",
    )(tok, code)


def heads_to_tokens_kernel(parts, in_ref, out_ref, send, recv, lsem):
    t, p, x, y, g = here()
    count = out_ref.shape[1]
    me = lax.rem(p, SPAN)
    peers = plane_peers()
    width = parts and out_ref.shape[0] // parts
    greet(peers)
    copies = []
    for i, peer in enumerate((peers[2], peers[0], peers[1])):
        m = lax.rem(peer[1], SPAN)
        for k in range(parts):
            c = remote(
                in_ref.at[pl.ds(k * HW, HW), pl.ds(pl.multiple_of(m * count, count), count)],
                out_ref.at[pl.ds(pl.multiple_of(k * width + me * HW, HW), HW)],
                send.at[i * parts + k],
                recv.at[i * parts + k],
                peer,
            )
            c.start()
            copies.append(c)
    for k in range(parts):
        c = pltpu.make_async_copy(
            in_ref.at[pl.ds(k * HW, HW), pl.ds(pl.multiple_of(me * count, count), count)],
            out_ref.at[pl.ds(pl.multiple_of(k * width + me * HW, HW), HW)],
            lsem.at[k],
        )
        c.start()
        copies.append(c)
    for c in copies:
        c.wait()


def heads_to_tokens(a, cid, name):
    parts = a.shape[0] // HW
    count = a.shape[1] // SPAN
    return pl.pallas_call(
        functools.partial(heads_to_tokens_kernel, parts),
        out_shape=jax.ShapeDtypeStruct((parts * HEADS * HEAD_DIM, count), a.dtype),
        in_specs=[VM],
        out_specs=ANY,
        scratch_shapes=[dma_sems(3 * parts), dma_sems(3 * parts), dma_sems(parts)],
        compiler_params=comm_params(cid),
        name=name,
    )(a)


def tokens_to_heads_kernel(in_ref, out_ref, send, recv, lsem):
    t, p, x, y, g = here()
    count = in_ref.shape[1]
    me = lax.rem(p, SPAN)
    peers = plane_peers()
    greet(peers)
    mine = pl.ds(pl.multiple_of(me * count, count), count)
    copies = []
    for i, peer in enumerate((peers[2], peers[0], peers[1])):
        m = lax.rem(peer[1], SPAN)
        c = remote(
            in_ref.at[pl.ds(pl.multiple_of(m * HW, HW), HW)],
            out_ref.at[:, mine],
            send.at[i],
            recv.at[i],
            peer,
        )
        c.start()
        copies.append(c)
    c = pltpu.make_async_copy(
        in_ref.at[pl.ds(pl.multiple_of(me * HW, HW), HW)], out_ref.at[:, mine], lsem.at[0]
    )
    c.start()
    for c in copies + [c]:
        c.wait()


def tokens_to_heads(a, cid, name):
    return pl.pallas_call(
        tokens_to_heads_kernel,
        out_shape=jax.ShapeDtypeStruct((HW, SPAN * a.shape[1]), a.dtype),
        in_specs=[VM],
        out_specs=ANY,
        scratch_shapes=[dma_sems(3), dma_sems(3), dma_sems(1)],
        compiler_params=comm_params(cid),
        name=name,
    )(a)


def doc_limits(code):
    pad = code >= 4.0
    mem = jnp.where(pad, code - 4.0, code)
    n0 = jnp.sum(jnp.where(mem < 0.5, 1.0, 0.0)).astype(jnp.int32)
    n1 = jnp.sum(jnp.where(mem < 1.5, 1.0, 0.0)).astype(jnp.int32)
    l = [jnp.sum(jnp.where(code == float(d), 1.0, 0.0)).astype(jnp.int32) for d in range(3)]
    return n0, n1, l

def block_range(lims, a, size, total):
    n0, n1, l = lims
    b = a + size - 1
    first = (a >= n0).astype(jnp.int32) + (a >= n1).astype(jnp.int32)
    last = (b >= n0).astype(jnp.int32) + (b >= n1).astype(jnp.int32)
    lo = jnp.where(first == 0, 0, jnp.where(first == 1, n0, n1))
    hi = jnp.where(last == 0, n0, jnp.where(last == 1, n1, total))
    dead = jnp.zeros((), jnp.bool_)
    for d in range(3):
        dead = dead | ((first <= d) & (d <= last) & (l[d] == 0))
    return jnp.where(dead, 0, lo), jnp.where(dead, total, hi)

def fwd_kernel(KB, QB, tok_ref, wt_ref, cos_ref, sin_ref, code_ref, out_ref, lse_ref, o32_ref, qa_ref, ka_ref, va_ref,
               kt_ref, acc_ref):
    T = tok_ref.shape[0]
    CH = 512
    hw = HW
    code = code_ref[...]
    lims = doc_limits(code)
    def proj(c, _):
        sl = pl.ds(pl.multiple_of(c*CH, CH), CH)
        mx = nt(wt_ref[...], tok_ref[sl, :])
        cos = cos_ref[:, sl]; sin = sin_ref[:, sl]
        cd = code_ref[:, sl]
        mem = jnp.where(cd >= 4.0, cd-4.0, cd)
        hot = jnp.concatenate([jnp.where(mem == float(d), 1.0, 0.0) for d in range(3)] + [jnp.zeros((13, CH), f32)], 0)
        neg = jnp.concatenate([jnp.where(cd == float(d), 0.0, -1e30) for d in range(3)] + [jnp.zeros((13, CH), f32)], 0)
        zer = jnp.zeros((48, CH), f32)
        one = jnp.concatenate([jnp.ones((1, CH), f32), jnp.zeros((63, CH), f32)], 0)
        def rope(u):
            a = u[:32]; b = u[32:]
            return jnp.concatenate([a*cos - b*sin, b*cos + a*sin], 0)
        for h in range(NH):
            q = rope(mx[h*HEAD_DIM:(h+1)*HEAD_DIM]).astype(bf).astype(f32)*0.125
            k = rope(mx[hw+h*HEAD_DIM:hw+(h+1)*HEAD_DIM])
            v = mx[2*hw+h*HEAD_DIM:2*hw+(h+1)*HEAD_DIM]
            qa_ref[h, :, sl] = jnp.concatenate([q, hot, zer], 0).astype(bf)
            ka_ref[h, sl, :] = jnp.concatenate([k, neg, zer], 0).T.astype(bf)
            va_ref[h, :, sl] = jnp.concatenate([v, one], 0).astype(bf)
            kt_ref[h, :, sl] = k.astype(bf)
        return 0
    lax.fori_loop(0, T//CH, proj, 0)
    def qblock(i, _):
        a = i*QB
        qs = pl.ds(pl.multiple_of(a, QB), QB)
        lo, hi = block_range(lims, a, QB, T)
        jlo = lo//KB; jhi = (hi+KB-1)//KB
        for h in range(NH):
            acc_ref[h] = jnp.zeros_like(acc_ref[h])
        def kv(j, ms):
            ks = pl.ds(pl.multiple_of(j*KB, KB), KB)
            new = []
            ss = [nn(ka_ref[h, ks, :], qa_ref[h, :, qs]) for h in range(NH)]
            for h in range(NH):
                s = ss[h]
                mn = jnp.maximum(ms[h], jnp.max(s, 0, keepdims=True))
                p = jnp.exp(s - mn).astype(bf)
                al = jnp.exp(ms[h]-mn)
                acc_ref[h] = acc_ref[h]*al + nn(va_ref[h, :80, ks], p)
                new.append(mn)
            return tuple(new)
        ms = lax.fori_loop(jlo, jhi, kv, tuple(jnp.full((1, QB), -3e38, f32) for _ in range(NH)))
        for h in range(NH):
            tot = acc_ref[h, 64:65, :]
            o = acc_ref[h, :64, :]/tot
            o32_ref[h*HEAD_DIM:(h+1)*HEAD_DIM, qs] = o
            lse_ref[h:h+1, qs] = jnp.where(ms[h] < -1e29, 0.0, ms[h] + jnp.log(tot))
            out_ref[h*HEAD_DIM:(h+1)*HEAD_DIM, qs] = o.astype(bf)
        return 0
    lax.fori_loop(0, T//QB, qblock, 0)

def attn_fwd(tok, wt, cos, sin, code, KB=512, QB=256):
    T = tok.shape[0]
    return pl.pallas_call(functools.partial(fwd_kernel, KB, QB),
        out_shape=(jax.ShapeDtypeStruct((NH*HEAD_DIM, T), bf), jax.ShapeDtypeStruct((NH, T), f32), jax.ShapeDtypeStruct((NH*HEAD_DIM, T), f32),
                   jax.ShapeDtypeStruct((NH,128,T), bf), jax.ShapeDtypeStruct((NH,T,128), bf), jax.ShapeDtypeStruct((NH,128,T), bf), jax.ShapeDtypeStruct((NH,HEAD_DIM,T), bf)),
        in_specs=[pl.BlockSpec(memory_space=pltpu.VMEM)]*5, out_specs=tuple([pl.BlockSpec(memory_space=pltpu.VMEM)]*7),
        scratch_shapes=[pltpu.VMEM((NH,80,QB), f32)],
        compiler_params=pltpu.CompilerParams(vmem_limit_bytes=VLIM), name="attn_fwd",
        cost_estimate=pl.CostEstimate(flops=int(2*T*768*576+4*T*T*128*3), bytes_accessed=12<<20, transcendentals=T*T*3))(tok, wt, cos, sin, code)

def bwd_kernel(KB, QB, do_ref, o32_ref, lse_ref, qa_ref, ka_ref, va_ref, kt_ref, cos_ref, sin_ref, code_ref, g_ref,
               vn_ref, dn_ref, da_ref, qb_ref, acc_ref, dq_ref):
    T = do_ref.shape[1]
    hw = HW
    CH = 512
    lims = doc_limits(code_ref[...])
    def prep(c, _):
        sl = pl.ds(pl.multiple_of(c*CH, CH), CH)
        for h in range(NH):
            do = do_ref[h*HEAD_DIM:(h+1)*HEAD_DIM, sl].astype(f32)
            delta = jnp.sum(do*o32_ref[h*HEAD_DIM:(h+1)*HEAD_DIM, sl], 0, keepdims=True)
            def split(x):
                x1 = x.astype(bf).astype(f32); r = x-x1
                x2 = r.astype(bf).astype(f32); x3 = r-x2
                return [x1, x2, x3]
            z13 = jnp.zeros((13, CH), f32); z48 = jnp.zeros((48, CH), f32)
            da_ref[h, :, sl] = jnp.concatenate([do]+split(-delta)+[z13, z48], 0).astype(bf)
            one = jnp.concatenate([jnp.ones((3, CH), f32), jnp.zeros((61, CH), f32)], 0)
            v = va_ref[h, :64, sl].astype(f32)
            vn_ref[h, sl, :] = jnp.concatenate([v, one], 0).T.astype(bf)
            z64 = jnp.zeros((64, CH), f32)
            q = qa_ref[h, :64, sl].astype(f32)
            dn_ref[h, sl, :] = jnp.concatenate([do, z64], 0).T.astype(bf)
            qb_ref[h, sl, :] = jnp.concatenate([z64, q], 0).T.astype(bf)
            acc_ref[h, sl, :] = jnp.zeros((CH, 128), f32)
        return 0
    lax.fori_loop(0, T//CH, prep, 0)
    def qblock(i, _):
        a = i*QB
        qs = pl.ds(pl.multiple_of(a, QB), QB)
        lo, hi = block_range(lims, a, QB, T)
        jlo = lo//KB; jhi = (hi+KB-1)//KB
        dq_ref[...] = jnp.zeros_like(dq_ref)
        def kv(j, _):
            ks = pl.ds(pl.multiple_of(j*KB, KB), KB)
            for h in range(NH):
                s = nn(ka_ref[h, ks, :], qa_ref[h, :, qs])
                dp = nn(vn_ref[h, ks, :], da_ref[h, :, qs])
                p = jnp.exp(s - lse_ref[h:h+1, qs])
                ds = (p*dp).astype(bf)
                acc_ref[h, ks, :] += nn(p.astype(bf), dn_ref[h, qs, :]) + nn(ds, qb_ref[h, qs, :])
                dq_ref[h] += nn(kt_ref[h, :, ks], ds)
            return 0
        lax.fori_loop(jlo, jhi, kv, 0)
        cos = cos_ref[:, qs]; sin = sin_ref[:, qs]
        for h in range(NH):
            u = dq_ref[h]*0.125
            x1 = u[:32]; x2 = u[32:]
            g_ref[h*HEAD_DIM:(h+1)*HEAD_DIM, qs] = jnp.concatenate([x1*cos+x2*sin, x2*cos-x1*sin], 0).astype(bf)
        return 0
    lax.fori_loop(0, T//QB, qblock, 0)
    def fin(c, _):
        sl = pl.ds(pl.multiple_of(c*CH, CH), CH)
        cos = cos_ref[:, sl]; sin = sin_ref[:, sl]
        for h in range(NH):
            t = acc_ref[h, sl, :].T
            x1 = t[64:96]; x2 = t[96:128]
            g_ref[hw+h*HEAD_DIM:hw+(h+1)*HEAD_DIM, sl] = jnp.concatenate([x1*cos+x2*sin, x2*cos-x1*sin], 0).astype(bf)
            g_ref[2*hw+h*HEAD_DIM:2*hw+(h+1)*HEAD_DIM, sl] = t[:64].astype(bf)
        return 0
    lax.fori_loop(0, T//CH, fin, 0)

def attn_bwd(do, o32, lse, qa, ka, va, kt, cos, sin, code, KB=512, QB=256):
    T = do.shape[1]
    return pl.pallas_call(functools.partial(bwd_kernel, KB, QB),
        out_shape=jax.ShapeDtypeStruct((3*NH*HEAD_DIM, T), bf),
        in_specs=[pl.BlockSpec(memory_space=pltpu.VMEM)]*10, out_specs=pl.BlockSpec(memory_space=pltpu.VMEM),
        scratch_shapes=[pltpu.VMEM((NH,T,128), bf), pltpu.VMEM((NH,T,128), bf), pltpu.VMEM((NH,128,T), bf), pltpu.VMEM((NH,T,128), bf),
                        pltpu.VMEM((NH,T,128), f32), pltpu.VMEM((NH,HEAD_DIM,QB), f32)],
        compiler_params=pltpu.CompilerParams(vmem_limit_bytes=VLIM), name="attn_bwd",
        cost_estimate=pl.CostEstimate(flops=int(10*T*T*128*3), bytes_accessed=12<<20, transcendentals=T*T*3))(do, o32, lse, qa, ka, va, kt, cos, sin, code)


def contrast_part(groups, sums, goals_ref, plane, allp, ge, send, recv, scores_ref, loss_ref):
    t, p, x, y, g = here()
    docs = groups * DOCS_GRP
    size = groups * 8
    peers = plane_peers()
    line = [(t, lax.rem(p + SPAN * k, SPAN * groups)) for k in range(1, groups)]
    plane[3] = sums
    copies = [remote(plane.at[3], plane.at[i], send.at[i], recv.at[i], q) for i, q in enumerate(peers)]
    for c in copies:
        c.start()
    col = lax.broadcasted_iota(jnp.int32, (size, size), 1)
    row = lax.broadcasted_iota(jnp.int32, (size, size), 0)

    def mark(i, hot):
        goal = goals_ref[i]
        at = (row == i // DOCS_GRP * 8 + i % DOCS_GRP) & (col == goal // DOCS_GRP * 8 + goal % DOCS_GRP)
        return hot + jnp.where(at, 1.0, 0.0)

    hot = lax.fori_loop(0, docs, mark, jnp.zeros((size, size), f32))
    for c in copies:
        c.wait()
    own = (plane[3] + plane[0]) + (plane[1] + plane[2])
    allp[t, g] = own
    rows = allp.at[t, g]
    copies = [remote(rows, rows, send.at[3 + i], recv.at[3 + i], q) for i, q in enumerate(line)]
    for c in copies:
        c.start()
    for c in copies:
        c.wait()
    c = remote(allp.at[t], allp.at[t], send.at[2 + groups], recv.at[2 + groups], (1 - t, p))
    c.start()
    c.wait()
    width = allp.shape[3]
    pools = [allp[k].reshape(size, width) for k in range(2)]
    embeds = [v * lax.rsqrt(jnp.sum(v * v, -1, keepdims=True) + 1e-06) for v in pools]
    dot = functools.partial(lax.dot_general, precision=precise, preferred_element_type=f32)
    scores = dot(embeds[0], embeds[1], (((1,), (1,)), ((), ()))) * 50.0
    live = lax.rem(col, 8) < DOCS_GRP
    alive = lax.rem(row, 8) < DOCS_GRP
    masked = jnp.where(live, scores, -1e30)
    top = jnp.max(masked, -1, keepdims=True)
    total = jnp.sum(jnp.exp(masked - top), -1, keepdims=True)
    log_sums = top + jnp.log(total)
    chosen = jnp.sum(hot * scores, -1, keepdims=True)
    each = jnp.where(alive[:, 0:1], log_sums - chosen, 0.0)
    loss_ref[...] = jnp.broadcast_to(jnp.sum(each, 0, keepdims=True) / docs, loss_ref.shape)
    scores_ref[...] = scores
    gs = jnp.where(alive & live, (jnp.exp(masked - log_sums) - hot) / docs, 0.0)
    gq = dot(gs, embeds[1], (((1,), (0,)), ((), ())))
    gd = dot(gs, embeds[0], (((0,), (0,)), ((), ())))
    ge[...] = jnp.where(t == 0, gq, gd) * 50.0
    mine = ge[pl.ds(pl.multiple_of(g * 8, 8), 8), :]
    pooled = allp[t, g]
    inv = lax.rsqrt(jnp.sum(pooled * pooled, -1, keepdims=True) + 1e-06)
    return inv * mine - inv * inv * inv * pooled * jnp.sum(pooled * mine, -1, keepdims=True)


def block_kernel(
    groups, heads_ref, rows_ref, code_ref, goals_ref, norms_ref, wo_h, wg_h, wu_h, wd_h,
    att_o, inner_o, hid_o, gm_o, gg_o, gb_o, ga_o, gh1_o, gains_o, scores_o, loss_o,
    att, wo, wg, wu, wd, inner, x1, s1, acc, hid, ab, x2, s2, sec, gm, gm2, gb, gb2, plane, allp, ge,
    wsem, send, recv, lsem, tsend, trecv, osem, csend, crecv,
):
    t, p, x, y, g = here()
    peers = plane_peers()
    sibling = (1 - t, p)
    line = tuple((t, lax.rem(p + SPAN * k, SPAN * groups)) for k in range(1, groups))
    count, width = rows_ref.shape
    half = width // 2
    tiles = wg.shape[0]
    me = lax.rem(p, SPAN)

    def weight(j, k):
        cols = pl.ds(j * width, width)
        src, dst = ((wg_h.at[:, cols], wg.at[j]), (wu_h.at[:, cols], wu.at[j]), (wd_h.at[cols], wd.at[j]))[k]
        return pltpu.make_async_copy(src, dst, wsem.at[1 + 3 * j + k])

    first_load = pltpu.make_async_copy(wo_h, wo, wsem.at[0])
    first_load.start()
    for j in range(tiles):
        for k in range(3):
            weight(j, k).start()
    greet(peers + (sibling,) + line)
    moves = []
    for i, peer in enumerate((peers[2], peers[0], peers[1])):
        m = lax.rem(peer[1], SPAN)
        moves.append(remote(
            heads_ref.at[:, pl.ds(pl.multiple_of(m * count, count), count)],
            att.at[pl.ds(pl.multiple_of(me * HW, HW), HW)], send.at[i], recv.at[i], peer,
        ))
    moves.append(pltpu.make_async_copy(
        heads_ref.at[:, pl.ds(pl.multiple_of(me * count, count), count)],
        att.at[pl.ds(pl.multiple_of(me * HW, HW), HW)], lsem.at[0],
    ))
    for c in moves:
        c.start()
    code = code_ref[...]
    zero = jnp.zeros((8 - DOCS_GRP, count), f32)
    mem = jnp.concatenate([jnp.where(code == float(d), 1.0, 0.0) for d in range(DOCS_GRP)] + [zero], 0)
    mem = jnp.concatenate([mem, mem, mem, jnp.zeros((8, count), f32)], 0).astype(bf)
    first_load.wait()
    for c in moves:
        c.wait()

    def pair(i, mine, its, out):
        return (
            pltpu.make_async_copy(mine, out.at[0], osem.at[i]),
            remote(its, out.at[1], tsend.at[i], trecv.at[i], sibling),
        )

    def both(i, mine, its, out):
        for c in pair(i, mine, its, out):
            c.start()

    both(0, att, att, att_o)
    acc[...] = tn(att[...], wo[...])
    step = 64
    gain1, bias1 = norms_ref[0:1, :], norms_ref[1:2, :]
    gain2, bias2 = norms_ref[2:3, :], norms_ref[3:4, :]

    def chunk(i):
        return pl.ds(pl.multiple_of(i * step, step), step)

    def norm(h, sl, xs, ss):
        c = h - jnp.mean(h, -1, keepdims=True)
        s = lax.rsqrt(jnp.mean(c * c, -1, keepdims=True) + norm_eps)
        xh = c * s
        xs[sl, :] = xh
        ss[sl, :] = s
        return xh

    def norm_one(i, _):
        sl = chunk(i)
        xh = norm(rows_ref[sl, :].astype(f32) + acc[sl, :], sl, x1, s1)
        v = xh * gain1 + bias1
        inner[sl, :] = v.astype(bf)
        acc[sl, :] = v
        return 0

    lax.fori_loop(0, count // step, norm_one, 0)
    both(1, inner, inner, inner_o)

    def tile_of(j, i, mine, its, out):
        return (
            pltpu.make_async_copy(mine, out.at[0, j], osem.at[i + j]),
            remote(its, out.at[1, j], tsend.at[i + j], trecv.at[i + j], sibling),
        )

    for j in range(tiles):
        for k in range(3):
            weight(j, k).wait()
        gate = nn(inner[...], wg[j])
        upper = nn(inner[...], wu[j])
        sig = jax.nn.sigmoid(gate)
        silu = gate * sig
        hid[j] = (silu * upper).astype(bf)
        ab[0, j] = (upper * (sig * (1.0 + gate * (1.0 - sig)))).astype(bf)
        ab[1, j] = silu.astype(bf)
        for c in tile_of(j, 2, hid.at[j], hid.at[j], hid_o):
            c.start()
        acc[...] += nn(hid[j], wd[j])

    def norm_two(i, _):
        sl = chunk(i)
        v = norm(acc[sl, :], sl, x2, s2) * gain2 + bias2
        for k, part in enumerate(split3(v)):
            sec[k, sl, :] = part.astype(bf)
        return 0

    lax.fori_loop(0, count // step, norm_two, 0)
    sums = (nn(mem[:16], sec[0]) + nn(mem[:16], sec[1]) + nn(mem[:16], sec[2]))[:8]
    top = lax.broadcasted_iota(jnp.int32, sums.shape, 0) < DOCS_GRP
    sums = jnp.where(top, sums, 0.0)
    gp = contrast_part(groups, sums, goals_ref, plane, allp, ge, csend, crecv, scores_o, loss_o)
    gp3 = jnp.concatenate(split3(gp) + [jnp.zeros_like(gp)], 0).astype(bf)
    acc[...] = tn(mem, gp3)

    def fold(v):
        return jnp.sum(v.reshape(step // 8, 8, width), 0)

    def norm_back(gr, xh, s, gain):
        e = gr * gain
        v = e - jnp.mean(e, -1, keepdims=True) - xh * jnp.mean(e * xh, -1, keepdims=True)
        return v * s

    zeros = jnp.zeros((8, width), f32)

    def back_two(i, sums):
        sl = chunk(i)
        gr, xh = acc[sl, :], x2[sl, :]
        v = norm_back(gr, xh, s2[sl, :], gain2)
        acc[sl, :] = v
        low = v.astype(bf)
        gm[sl, :] = low
        gm2[0, sl, :] = low[:, :half]
        gm2[1, sl, :] = low[:, half:]
        return sums[0] + fold(gr * xh), sums[1] + fold(gr)

    g2, b2 = lax.fori_loop(0, count // step, back_two, (zeros, zeros))
    both(2 + 2 * tiles, gm2.at[t], gm2.at[1 - t], gm_o)
    for j in range(tiles):
        gh = nt(gm[...], wd[j])
        gg = (gh * ab[0, j].astype(f32)).astype(bf)
        gu = (gh * ab[1, j].astype(f32)).astype(bf)
        ab[0, j] = gg
        ab[1, j] = gu
        for c in tile_of(j, 2 + tiles, ab.at[t, j], ab.at[1 - t, j], gg_o):
            c.start()
        acc[...] += nt(gg, wg[j]) + nt(gu, wu[j])

    def back_one(i, sums):
        sl = chunk(i)
        gr, xh = acc[sl, :], x1[sl, :]
        v = norm_back(gr, xh, s1[sl, :], gain1)
        gh1_o[sl, :] = v
        low = v.astype(bf)
        gb[sl, :] = low
        gb2[0, sl, :] = low[:, :half]
        gb2[1, sl, :] = low[:, half:]
        return sums[0] + fold(gr * xh), sums[1] + fold(gr)

    g1, b1 = lax.fori_loop(0, count // step, back_one, (zeros, zeros))
    both(3 + 2 * tiles, gb2.at[t], gb2.at[1 - t], gb_o)
    flat = [jnp.sum(v, 0, keepdims=True) for v in (g1, b1, g2, b2)]
    gains_o[...] = jnp.concatenate(flat + [jnp.zeros((4, width), f32)], 0)
    ga_o[...] = nt(wo[...], gb[...]).astype(bf)
    done = [pair(0, att, att, att_o), pair(1, inner, inner, inner_o)]
    for j in range(tiles):
        done.append(tile_of(j, 2, hid.at[j], hid.at[j], hid_o))
        done.append(tile_of(j, 2 + tiles, ab.at[t, j], ab.at[1 - t, j], gg_o))
    done.append(pair(2 + 2 * tiles, gm2.at[t], gm2.at[1 - t], gm_o))
    done.append(pair(3 + 2 * tiles, gb2.at[t], gb2.at[1 - t], gb_o))
    for c in done:
        for d in c:
            d.wait()


def block(heads, rows, code, goals, norms, w_out, w_gate, w_up, w_down, groups):
    count, width = rows.shape
    tiles = w_gate.shape[1] // width
    half = width // 2
    size = groups * 8
    sds = jax.ShapeDtypeStruct
    vm = lambda *n: pltpu.VMEM(n, bf)
    vf = lambda *n: pltpu.VMEM(n, f32)
    return pl.pallas_call(
        functools.partial(block_kernel, groups),
        out_shape=(
            sds((2, width, count), bf), sds((2, count, width), bf), sds((2, tiles, count, width), bf),
            sds((2, count, half), bf), sds((2, tiles, count, width), bf), sds((2, count, half), bf),
            sds((width, count), bf), sds((count, width), f32), sds((8, width), f32),
            sds((size, size), f32), sds((8, 128), f32),
        ),
        in_specs=[VM, VM, VM, pl.BlockSpec(memory_space=pltpu.SMEM), VM] + [ANY] * 4,
        out_specs=(ANY,) * 6 + (VM,) * 5,
        scratch_shapes=[
            vm(width, count), vm(width, width), vm(tiles, width, width), vm(tiles, width, width),
            vm(tiles, width, width), vm(count, width), vf(count, width), vf(count, 1), vf(count, width),
            vm(tiles, count, width), vm(2, tiles, count, width), vf(count, width), vf(count, 1),
            vm(3, count, width), vm(count, width), vm(2, count, half), vm(count, width), vm(2, count, half),
            vf(4, 8, width), vf(2, groups, 8, width), vf(size, width),
            dma_sems(1 + 3 * tiles), dma_sems(3), dma_sems(3), dma_sems(1),
            dma_sems(4 + 2 * tiles), dma_sems(4 + 2 * tiles), dma_sems(4 + 2 * tiles),
            dma_sems(3 + groups), dma_sems(3 + groups),
        ],
        compiler_params=comm_params(1),
        name="block",
    )(heads, rows, code, goals, norms, w_out, w_gate, w_up, w_down)


def weights_kernel(
    groups, i_ref, g_ref, h_ref, m_ref, a_ref, b_ref, in_ref,
    sa_ref, ka_ref, sb_ref, kb_ref, heads_ref,
    iv, it, gv, hv, mv, av, bv, gs, ds, os, isem, osem, send, recv, lsem,
):
    t, p, x, y, g = here()
    peers = plane_peers()
    greet(peers)
    tokens = in_ref.shape[1]
    me = lax.rem(p, SPAN)
    mine = pl.ds(pl.multiple_of(me * tokens, tokens), tokens)
    moves = []
    for i, peer in enumerate((peers[2], peers[0], peers[1])):
        m = lax.rem(peer[1], SPAN)
        moves.append(remote(
            in_ref.at[pl.ds(pl.multiple_of(m * HW, HW), HW)], heads_ref.at[:, mine],
            send.at[i], recv.at[i], peer,
        ))
    moves.append(pltpu.make_async_copy(
        in_ref.at[pl.ds(pl.multiple_of(me * HW, HW), HW)], heads_ref.at[:, mine], lsem.at[0]
    ))
    for c in moves:
        c.start()
    count, width = i_ref.shape[1:]
    half = width // 2
    tiles = gv.shape[1]
    shards = SPAN * groups
    one = width // shards
    down = ds.shape[1]

    def load(i, src, dst):
        return pltpu.make_async_copy(src, dst, isem.at[i])

    def tile(ref, j, buf, base):
        return load(base + j, ref.at[:, j], buf.at[:, j])

    few = [load(i, a, b) for i, (a, b) in enumerate(((m_ref, mv), (a_ref, av), (b_ref, bv), (i_ref, iv)))]
    few[0].start()
    for j in range(tiles):
        tile(h_ref, j, hv, 4).start()
    for c in few[1:]:
        c.start()
    for j in range(tiles):
        tile(g_ref, j, gv, 4 + tiles).start()
    few[0].wait()

    def downward(j, _):
        tile(h_ref, j, hv, 4).wait()
        r = tn(hv[0, j], mv[0]) + tn(hv[1, j], mv[1])
        ds[pl.ds(j * (width // down), width // down)] = r.astype(bf).reshape(width // down, down, half)
        return 0

    lax.fori_loop(0, tiles, downward, 0)
    for c in few[1:]:
        c.wait()
    r = nn(av[0], bv[0]) + nn(av[1], bv[1])
    os[...] = r.astype(bf).reshape(shards, one, half)
    for i in range(2):
        it[:, i * count : (i + 1) * count] = iv[i].T
    fours = lambda ref, n: ref.reshape(groups, 2, 2, n, half)

    def put(i, src, dst):
        return pltpu.make_async_copy(src, dst, osem.at[i])

    outs = []
    for i, (ref, k) in enumerate(((sb_ref, 1 - y), (kb_ref, y))):
        outs.append(put(4 * i, fours(ds, down).at[:, k], ref.at[:, :, pl.ds(one, down)]))
        outs.append(put(4 * i + 1, fours(os, one).at[:, k], ref.at[:, :, pl.ds(one + down, one)]))
    for c in outs:
        c.start()

    def top(j):
        rows = pl.ds(pl.multiple_of(j * one, one), one)
        piece = fours(gs.at[j], one)
        return (
            put(8 + j, piece.at[:, :, 1 - x], sa_ref.at[:, :, rows]),
            put(8 + 2 * tiles + j, piece.at[:, :, x], ka_ref.at[:, :, rows]),
        )

    for j in range(tiles):
        tile(g_ref, j, gv, 4 + tiles).wait()
        r = (nn(it[:, :count], gv[0, j]) + nn(it[:, count:], gv[1, j])).astype(bf)
        for h in range(2):
            k = 2 * j + h
            gs[k] = r[:, h * half : (h + 1) * half].reshape(shards, one, half)
            if k < 2 * tiles - 1:
                outs.extend(top(k))
                for c in outs[-2:]:
                    c.start()
    piece = fours(gs.at[2 * tiles - 1], one)
    for i, (ref, k) in enumerate(((sb_ref, 1 - y), (kb_ref, y))):
        c = put(4 * i + 2, piece.at[:, k], ref.at[:, :, pl.ds(0, one)])
        c.start()
        outs.append(c)
    for c in outs + moves:
        c.wait()


def weight_grads(groups, grad_heads, inner, grads, hidden, grad_mlp, attended, grad_branch):
    count, width = inner.shape[1:]
    half = width // 2
    shards = SPAN * groups
    one = width // shards
    tiles = grads.shape[1]
    down = tiles * one
    ra = (2 * tiles - 1) * one
    rb = down + 2 * one
    part = lambda r: jax.ShapeDtypeStruct((groups, 2, r, half), bf)
    vm = lambda *n: pltpu.VMEM(n, bf)
    return pl.pallas_call(
        functools.partial(weights_kernel, groups),
        out_shape=(
            part(ra), part(ra), part(rb), part(rb),
            jax.ShapeDtypeStruct((HW, SPAN * grad_heads.shape[1]), bf),
        ),
        in_specs=[ANY] * 6 + [VM],
        out_specs=(ANY,) * 5,
        scratch_shapes=[
            vm(2, count, width), vm(width, 2 * count), vm(2, tiles, count, width), vm(2, tiles, count, width),
            vm(2, count, half), vm(2, width, count), vm(2, count, half),
            vm(2 * tiles, shards, one, half), vm(shards, down, half), vm(shards, one, half),
            dma_sems(4 + 2 * tiles), dma_sems(8 + 4 * tiles), dma_sems(3), dma_sems(3), dma_sems(1),
        ],
        compiler_params=comm_params(2),
        name="weight_grads",
        cost_estimate=pl.CostEstimate(
            flops=int(2 * 2 * count * half * width * 8.5), bytes_accessed=30 << 20, transcendentals=0
        ),
    )(inner, grads, hidden, grad_mlp, attended, grad_branch, grad_heads)


def add_rows(dst, a, b, rows):
    def step(i, _):
        sl = pl.ds(pl.multiple_of(i * 16, 16), 16)
        dst[sl, :] = (a[sl, :].astype(f32) + b[sl, :].astype(f32)).astype(bf)
        return 0

    lax.fori_loop(0, rows // 16, step, 0)


class Line:
    def __init__(self, z, zt, groups, part, up, down, sems, t, p):
        self.z, self.zt, self.groups = z, zt, groups
        self.part, self.up, self.down = part, up, down
        us, ur, ds, dr = sems
        above = (t, lax.rem(p + SPAN, SPAN * groups))
        below = (t, lax.rem(p + SPAN * (groups - 1), SPAN * groups))
        self.up_first = lambda: remote(part, up, us, ur, above)
        self.up_next = lambda: remote(up, up, us, ur, above)
        self.down_first = lambda: remote(part, down, ds, dr, below)
        self.down_next = lambda: remote(down, down, ds, dr, below)

    def start(self):
        if self.zt > 0:
            pl.when(self.z == 0)(lambda: self.up_first().start())
        if self.zt < self.groups - 1:
            pl.when(self.z == self.groups - 1)(lambda: self.down_first().start())

    def relay(self, hop, rows):
        def up():
            self.up_next().wait_recv()
            add_rows(self.up, self.up, self.part, rows)
            self.up_next().start()

        def down():
            self.down_next().wait_recv()
            add_rows(self.down, self.down, self.part, rows)
            self.down_next().start()

        if 0 < hop < self.zt:
            pl.when(self.z == hop)(up)
        if self.zt < self.groups - 1 - hop:
            pl.when(self.z == self.groups - 1 - hop)(down)

    def finish(self, dst, rows):
        def done():
            if self.zt > 0:
                self.up_next().wait_recv()
            if self.zt < self.groups - 1:
                self.down_next().wait_recv()
            if 0 < self.zt < self.groups - 1:
                add_rows(self.up, self.up, self.down, rows)
            add_rows(dst, self.up if self.zt > 0 else self.down, self.part, rows)

        pl.when(self.z == self.zt)(done)

    def drain(self):
        if self.zt > 0:
            pl.when(self.z < self.zt)(lambda: self.up_first().wait_send())
        if self.zt < self.groups - 1:
            pl.when(self.z > self.zt)(lambda: self.down_first().wait_send())


def outward(groups):
    order = []
    lo, hi = 0, groups - 1
    while lo <= hi:
        order.append(hi)
        if lo < hi:
            order.append(lo)
        lo, hi = lo + 1, hi - 1
    return order


def finish_kernel(
    groups, ka_ref, kb_ref, ra_ref, rb_ref, g_ref, tok_ref, gain_ref,
    pair_ref, sum_ref, gm_ref, out_ref,
    kva, kvb, rva, rvb, r2a, r2b, ua, ub, da, db, isem, s2, q2, us, ur, ds, dr,
    plane, line, gs, gr, fs, fr,
    w2, sib, ub2, db2, fin, send, recv, ts, tr, us2, ur2, ds2, dr2, ps, pr, lsem,
):
    t, p, x, y, z = here()
    ex, ey, ed = plane_peers()
    peers = (ex, ey, ed)
    sibling = (1 - t, p)
    others = [(t, lax.rem(p + SPAN * k, SPAN * groups)) for k in range(1, groups)]
    across = tuple((1 - t, q[1]) for q in peers)
    order = outward(groups)
    colours = (
        (ey, ka_ref, ra_ref, kva, rva, r2a, ua, da, y),
        (ex, kb_ref, rb_ref, kvb, rvb, r2b, ub, db, x),
    )

    def loads(c, zt):
        peer, kr, rr, kv, rv = colours[c][:5]
        i = 2 * (c * groups + zt)
        return (
            pltpu.make_async_copy(kr.at[zt], kv.at[zt], isem.at[i]),
            pltpu.make_async_copy(rr.at[zt], rv.at[zt], isem.at[i + 1]),
        )

    for zt in order:
        for c in range(2):
            for d in loads(c, zt):
                d.start()
    greet(peers + across + (sibling,) + tuple(others))
    for i, peer in enumerate(peers):
        remote(gain_ref, plane.at[i], gs.at[i], gr.at[i], peer).start()

    def second(c, zt):
        peer, kr, rr, kv, rv, r2, u, d, mine = colours[c]
        i = c * groups + zt
        return remote(rv.at[zt, 1 - mine], r2.at[zt], s2.at[i], q2.at[i], peer)

    def chain(c, zt):
        peer, kr, rr, kv, rv, r2, u, d, mine = colours[c]
        i = c * groups + zt
        return Line(z, zt, groups, r2.at[zt], u.at[zt], d.at[zt],
                    (us.at[i], ur.at[i], ds.at[i], dr.at[i]), t, p)

    def size(c):
        return colours[c][3].shape[2]

    for zt in order:
        for c in range(2):
            for d in loads(c, zt):
                d.wait()
            peer, kr, rr, kv, rv, r2, u, d, mine = colours[c]
            away = rv.at[zt, 1 - mine]
            add_rows(away, away, kv.at[zt, 1 - mine], size(c))
            second(c, zt).start()
    count = gm_ref.shape[1]
    me = lax.rem(p, SPAN)
    width = gm_ref.shape[0] // 3
    copies = []
    for i, peer in enumerate((peers[2], peers[0], peers[1])):
        m = lax.rem(peer[1], SPAN)
        for k in range(3):
            copies.append(remote(
                g_ref.at[pl.ds(k * HW, HW), pl.ds(pl.multiple_of(m * count, count), count)],
                gm_ref.at[pl.ds(pl.multiple_of(k * width + me * HW, HW), HW)],
                send.at[i * 3 + k], recv.at[i * 3 + k], peer,
            ))
    for k in range(3):
        copies.append(pltpu.make_async_copy(
            g_ref.at[pl.ds(k * HW, HW), pl.ds(pl.multiple_of(me * count, count), count)],
            gm_ref.at[pl.ds(pl.multiple_of(k * width + me * HW, HW), HW)],
            lsem.at[k],
        ))
    for c in copies:
        c.start()
    for zt in order:
        for c in range(2):
            peer, kr, rr, kv, rv, r2, u, d, mine = colours[c]
            keep = rv.at[zt, mine]
            add_rows(keep, keep, kv.at[zt, mine], size(c))
    for i, peer in enumerate(peers):
        remote(gain_ref, plane.at[i], gs.at[i], gr.at[i], peer).wait()
    line[0] = (gain_ref[...] + plane[0]) + (plane[1] + plane[2])
    ring = [remote(line.at[0], line.at[1 + k], gs.at[3 + k], gr.at[3 + k], peer) for k, peer in enumerate(others)]
    for c in ring:
        c.start()

    def in_plane(zt):
        for c in range(2):
            peer, kr, rr, kv, rv, r2, u, d, mine = colours[c]
            second(c, zt).wait_recv()
            dst = r2.at[zt]
            add_rows(dst, dst, rv.at[zt, mine], size(c))
            chain(c, zt).start()

    def relay(zt, hop):
        for c in range(2):
            chain(c, zt).relay(hop, size(c))

    in_plane(order[0])
    shards = SPAN * groups
    one = width // shards
    half = width // 2
    for h in range(2):
        r = nn(g_ref[...], tok_ref[:, h * half : (h + 1) * half]).T
        w2[h * (shards // 2) : (h + 1) * (shards // 2)] = r.astype(bf).reshape(shards // 2, one, 3 * HW)

    def swap(zt):
        return remote(w2.at[pl.ds(zt * 4 + (1 - t) * 2, 2)], sib.at[zt], ts.at[zt], tr.at[zt], sibling)

    for zt in order:
        swap(zt).start()

    def chain2(zt, k):
        i = zt * 2 + k
        return Line(z, zt, groups, sib.at[zt, k], ub2.at[zt, k], db2.at[zt, k],
                    (us2.at[i], ur2.at[i], ds2.at[i], dr2.at[i]), t, p)

    for i, zt in enumerate(order):
        if i >= 1:
            in_plane(zt)
        swap(zt).wait_recv()
        for k in range(2):
            dst = sib.at[zt, k]
            add_rows(dst, dst, w2.at[zt * 4 + t * 2 + k], one)
            chain2(zt, k).start()
        if i >= 1:
            relay(order[i - 1], 1)
            for k in range(2):
                chain2(order[i - 1], k).relay(1, one)
    for c in ring:
        c.wait()
    total = line[0]
    for k in range(1, groups):
        total = total + line[k]
    line[groups] = total
    both = remote(line.at[groups], line.at[groups + 1], gs.at[2 + groups], gr.at[2 + groups], sibling)
    both.start()
    for hop in range(1, groups - 1):
        for i, zt in enumerate(order):
            if hop > 1 or i == groups - 1:
                relay(zt, hop)
                for k in range(2):
                    chain2(zt, k).relay(hop, one)
    for zt in order:
        for k in range(2):
            chain2(zt, k).finish(fin.at[k], one)
    here_id = t * SPAN + me

    def hand(k, tt):
        m = t * 2 + k
        peer = (tt, z * SPAN + m)
        i = k * 2 + tt
        away = lambda: remote(fin.at[k], out_ref.at[me], ps.at[i], pr.at[me], peer)
        stay = lambda: pltpu.make_async_copy(fin.at[k], out_ref.at[me], lsem.at[3])
        return away, stay, (tt * SPAN + m) == here_id

    for k in range(2):
        for tt in range(2):
            away, stay, same = hand(k, tt)
            pl.when(jnp.logical_not(same))(lambda away=away: away().start())
            pl.when(same)(lambda stay=stay: stay().start())
    for zt in order:
        for c, sl in ((0, pl.ds(0, size(0))), (1, pl.ds(size(0), size(1)))):
            chain(c, zt).finish(pair_ref.at[t, sl], size(c))
    last = remote(pair_ref.at[t], pair_ref.at[t], fs.at[0], fr.at[0], sibling)
    last.start()
    both.wait()
    sum_ref[...] = line[groups] + line[groups + 1]
    for s in range(SPAN):
        from_here = jnp.logical_and(s == me, y == t)
        pl.when(jnp.logical_not(from_here))(
            lambda s=s: remote(fin.at[0], out_ref.at[s], ps.at[0], pr.at[s], sibling).wait_recv()
        )
    for k in range(2):
        for tt in range(2):
            away, stay, same = hand(k, tt)
            pl.when(jnp.logical_not(same))(lambda away=away: away().wait_send())
            pl.when(same)(lambda stay=stay: stay().wait())
    for zt in range(groups):
        swap(zt).wait_send()
        for k in range(2):
            chain2(zt, k).drain()
        for c in range(2):
            second(c, zt).wait_send()
            chain(c, zt).drain()
    for c in copies:
        c.wait()
    last.wait()


def finish(ka, kb, ra, rb, g, tok, gains, groups):
    width = tok.shape[1]
    count = tok.shape[0] // SPAN
    one = width // (SPAN * groups)
    na, nb = ka.shape[2], kb.shape[2]
    half = ka.shape[3]
    buf = lambda *n: pltpu.VMEM(n, bf)
    mix = lambda *n: pltpu.VMEM(n + (one, 3 * HW), bf)
    return pl.pallas_call(
        functools.partial(finish_kernel, groups),
        out_shape=(
            jax.ShapeDtypeStruct((2, na + nb, half), bf),
            jax.ShapeDtypeStruct(gains.shape, f32),
            jax.ShapeDtypeStruct((3 * width, count), bf),
            jax.ShapeDtypeStruct((SPAN, one, 3 * HW), bf),
        ),
        in_specs=[ANY] * 4 + [VM] * 3,
        out_specs=(VM, VM, ANY, VM),
        scratch_shapes=[
            buf(groups, 2, na, half), buf(groups, 2, nb, half), buf(groups, 2, na, half), buf(groups, 2, nb, half),
            buf(groups, na, half), buf(groups, nb, half), buf(groups, na, half), buf(groups, nb, half),
            buf(groups, na, half), buf(groups, nb, half),
            dma_sems(4 * groups), dma_sems(2 * groups), dma_sems(2 * groups),
            dma_sems(2 * groups), dma_sems(2 * groups), dma_sems(2 * groups), dma_sems(2 * groups),
            pltpu.VMEM((3,) + gains.shape, f32), pltpu.VMEM((groups + 2,) + gains.shape, f32),
            dma_sems(3 + groups), dma_sems(3 + groups), dma_sems(1), dma_sems(1),
            mix(SPAN * groups), mix(groups, 2), mix(groups, 2), mix(groups, 2), mix(2),
            dma_sems(9), dma_sems(9), dma_sems(groups), dma_sems(groups),
            dma_sems(2 * groups), dma_sems(2 * groups), dma_sems(2 * groups), dma_sems(2 * groups),
            dma_sems(4), dma_sems(SPAN), dma_sems(4),
        ],
        compiler_params=comm_params(3),
        name="finish",
    )(ka, kb, ra, rb, g, tok, gains)


def angle_tables(total):
    half = HEAD_DIM // 2
    freqs = np.float32(1000.0) ** (-np.arange(half, dtype=np.float32) / np.float32(half))
    theta = freqs[:, None].astype(np.float32) * np.arange(total, dtype=np.float32)[None, :]
    return np.cos(theta).astype(np.float32), np.sin(theta).astype(np.float32)


def spread_sum(value):
    part = lax.psum_scatter(value, "dp", scatter_dimension=0, tiled=True)
    return lax.psum(part.astype(bf), "tower").astype(f32)


def local(
    tokens, doc_ids, pad_mask, targets, w_qkv, w_out, ln1_gain, ln1_bias,
    w_gate, w_up, w_down, ln2_gain, ln2_bias,
):
    width = w_out.shape[0]
    rows = tokens[0]
    count = rows.shape[0]
    places = lax.axis_size("dp")
    groups = places // SPAN
    tower = lax.axis_index("tower")
    place = lax.axis_index("dp")
    me = place % SPAN
    member_of = doc_ids[0] % DOCS_GRP
    live = pad_mask[0] == 1
    code = jnp.where(live, member_of, member_of + 4).astype(f32)[None, :]
    docs = groups * DOCS_GRP
    cols = [lax.dynamic_slice_in_dim(w_qkv, k * width + me * HW, HW, 1) for k in range(3)]
    w_mine = jnp.concatenate(cols, 1).T
    cos, sin = angle_tables(SPAN * count)
    tok_all, codes = gather(rows, code)
    heads_out, lse, exact, qa, ka, va, kt = attn_fwd(tok_all, w_mine, cos, sin, codes)
    norms = jnp.stack([ln1_gain, ln1_bias, ln2_gain, ln2_bias] + [jnp.zeros_like(ln1_gain)] * 4, 0)
    (
        attended, inner, hidden, grad_mlp, grads, grad_branch, grad_attended, grad_h1, gains, scores_all, loss
    ) = block(heads_out, rows, code, targets, norms, w_out, w_gate, w_up, w_down, groups)
    scores = scores_all.reshape(groups, 8, groups, 8)[:, :DOCS_GRP, :, :DOCS_GRP].reshape(docs, docs)
    by_hand = width % (16 * places) == 0
    if by_hand:
        send_a, keep_a, send_b, keep_b, d_heads = weight_grads(
            groups, grad_attended, inner, grads, hidden, grad_mlp, attended, grad_branch
        )
        exchange = lambda v, bit: lax.ppermute(v, "dp", [(i, i ^ bit) for i in range(places)])
        came_a, came_b = exchange(send_a, 1), exchange(send_b, 2)
    else:
        d_heads = tokens_to_heads(grad_attended, 5, "to_heads")
    mixed = attn_bwd(d_heads, exact, lse, qa, ka, va, kt, cos, sin, codes)
    if by_hand:
        half = width // 2
        one = width // places
        down = w_down.shape[0] // places
        pair, gain_sums, grad_mixed, qkv_parts = finish(
            keep_a, keep_b, came_a, came_b, mixed, tok_all, gains, groups
        )
        top = pair.shape[1] - down - one
        unfold = lambda v: v.reshape(top // one, one, half).transpose(1, 0, 2).reshape(one, -1)
        sides = lambda v: jnp.concatenate([v[0], v[1]], 1).astype(f32)
        gate_out = unfold(pair[0, :top]).astype(f32)
        up_out = unfold(pair[1, :top]).astype(f32)
        down_out = sides(pair[:, top : top + down])
        out_out = sides(pair[:, top + down :])
        gains_out = lax.dynamic_slice_in_dim(gain_sums[:4], place * one, one, 1)
        qkv_out = (
            qkv_parts.reshape(SPAN, one, 3, HW).transpose(1, 2, 0, 3).reshape(one, 3 * width).astype(f32)
        )
    else:
        grad_mixed = heads_to_tokens(mixed, 6, "to_tokens_back")
        qkv_out = spread_sum(tn(rows, grad_mixed.T))
        side = lambda v: lax.psum_scatter(v, "dp", scatter_dimension=0, tiled=True)
        halves = lambda v: lax.all_gather(side(v).astype(bf), "tower", axis=1, tiled=True).astype(f32)
        both = lambda a, b: tn(a[0], b[0]) + tn(a[1], b[1])
        flat = lambda v: v.transpose(0, 2, 1, 3).reshape(2, count, -1)
        out_out = halves(nn(attended[0], grad_branch[0]) + nn(attended[1], grad_branch[1]))
        two = lax.all_gather(side(both(inner, flat(grads))).astype(bf), "tower").astype(f32)
        gate_out, up_out = two[0], two[1]
        down_out = halves(both(flat(hidden), grad_mlp))
        gains_out = spread_sum(gains[:4].T).T
    token_grad = grad_h1 + lax.dot_general(
        grad_mixed, w_qkv, (((0,), (1,)), ((), ())), preferred_element_type=f32
    )
    return (
        scores, loss[0, 0], token_grad[None], qkv_out, out_out, gains_out[0], gains_out[1],
        gate_out, up_out, down_out, gains_out[2], gains_out[3],
    )


def solution(mesh):
    shard = P("dp", None)
    lone = P("dp")
    return jax.shard_map(
        local,
        mesh=mesh,
        in_specs=(P("tower", "dp", None), P("tower", "dp"), P("tower", "dp")) + (P(),) * 10,
        out_specs=(
            P(), P(), P("tower", "dp", None), shard, shard, lone, lone, shard, shard, shard, lone, lone,
        ),
        check_vma=False,
    )
```

```python
import functools

import jax
import jax.numpy as jnp
import numpy as np
from jax import lax
from jax.experimental import pallas as pl
from jax.experimental.pallas import tpu as pltpu
from jax.sharding import PartitionSpec as P

HEADS = 12
HEAD_DIM = 64
SPAN = 4
DOCS_GRP = 3
NH = HEADS // SPAN
HW = NH * HEAD_DIM
CHUNK = 512
VLIM = 62 * 2**20
MESH = pl.DeviceIdType.MESH
f32 = jnp.float32
bf = jnp.bfloat16
precise = lax.Precision.HIGHEST
norm_eps = 1e-05
ANY = pl.BlockSpec(memory_space=pl.ANY)
VM = pl.BlockSpec(memory_space=pltpu.VMEM)


def nn(a, b):
    return lax.dot_general(a, b, (((1,), (0,)), ((), ())), preferred_element_type=f32)


def nt(a, b):
    return lax.dot_general(a, b, (((1,), (1,)), ((), ())), preferred_element_type=f32)


def tn(a, b):
    return lax.dot_general(a, b, (((0,), (0,)), ((), ())), preferred_element_type=f32)


def split3(v):
    one = v.astype(bf).astype(f32)
    rest = v - one
    two = rest.astype(bf).astype(f32)
    return [one, two, rest - two]


def here():
    t = lax.axis_index("tower")
    p = lax.axis_index("dp")
    x = lax.rem(p, 2)
    y = lax.rem(lax.div(p, 2), 2)
    return t, p, x, y, lax.div(p, SPAN)


def plane_peers():
    t, p, x, y, g = here()
    px = p + 1 - 2 * x
    py = p + 2 - 4 * y
    pd = px + 2 - 4 * y
    return (t, px), (t, py), (t, pd)


def greet(peers):
    barrier = pltpu.get_barrier_semaphore()
    for peer in peers:
        pl.semaphore_signal(barrier, inc=1, device_id=peer, device_id_type=MESH)
    pl.semaphore_wait(barrier, len(peers))


def remote(src, dst, send, recv, peer):
    return pltpu.make_async_remote_copy(
        src_ref=src, dst_ref=dst, send_sem=send, recv_sem=recv, device_id=peer, device_id_type=MESH
    )


def dma_sems(n):
    return pltpu.SemaphoreType.DMA((n,))


def comm_params(cid):
    return pltpu.CompilerParams(collective_id=cid, has_side_effects=True, vmem_limit_bytes=VLIM)


def gather_kernel(
    tok_ref, code_ref, cos_ref, sin_ref, w_ref, out_ref, codes_ref, qa_ref, ka_ref, va_ref, kt_ref,
    toks, codes, wraw, wturn, wt, qa, ka, va, kt, send, recv, csend, crecv, wsem, osem,
):
    t, p, x, y, g = here()
    count, width = tok_ref.shape
    half = count // 2
    me = lax.rem(p, SPAN)
    odd = lax.rem(me, 2)
    wide = wraw.shape[2]
    loads = []
    for k in range(3):
        at = pl.multiple_of(k * width + me * HW - odd * HEAD_DIM, 128)
        loads.append(pltpu.make_async_copy(w_ref.at[:, pl.ds(at, wide)], wraw.at[k], wsem.at[k]))
        loads[-1].start()
    ex, ey, ed = plane_peers()
    mx, my, md = (lax.rem(q[1], SPAN) for q in (ex, ey, ed))

    def rows(m, h):
        return pl.ds(pl.multiple_of(m * count + h * half, half), half)

    def whole(m):
        return pl.ds(pl.multiple_of(m * count, count), count)

    greet((ex, ey, ed))
    first = []
    for i, (peer, h) in enumerate(((ex, 0), (ey, 1), (ex, 1), (ey, 0))):
        c = remote(tok_ref.at[pl.ds(h * half, half)], toks.at[rows(me, h)], send.at[i], recv.at[i], peer)
        c.start()
        first.append(c)
    small = []
    for i, peer in enumerate((ex, ey, ed)):
        c = remote(code_ref, codes.at[:, whole(me)], csend.at[i], crecv.at[i], peer)
        c.start()
        small.append(c)
    codes[:, whole(me)] = code_ref[...]
    for k in range(3):
        loads[k].wait()
        wturn[...] = wraw[k].T
        wt[k * HW : (k + 1) * HW, :] = wturn[pl.ds(pl.multiple_of(odd * HEAD_DIM, HEAD_DIM), HW), :]

    def project(rows_ref, m, n):
        sl = whole(m)
        mx = nt(wt[...], rows_ref[...])
        cos, sin = cos_ref[:, sl], sin_ref[:, sl]
        cd = codes[:, sl]
        mem = jnp.where(cd >= 4.0, cd - 4.0, cd)
        pad = [jnp.zeros((13, count), f32)]
        hot = jnp.concatenate([jnp.where(mem == float(d), 1.0, 0.0) for d in range(DOCS_GRP)] + pad, 0)
        neg = jnp.concatenate([jnp.where(cd == float(d), 0.0, -1e30) for d in range(DOCS_GRP)] + pad, 0)
        rest = jnp.zeros((48, count), f32)
        one = jnp.concatenate([jnp.ones((1, count), f32), jnp.zeros((63, count), f32)], 0)

        def rope(u):
            a, b = u[:32], u[32:]
            return jnp.concatenate([a * cos - b * sin, b * cos + a * sin], 0)

        for h in range(NH):
            q = rope(mx[h * HEAD_DIM : (h + 1) * HEAD_DIM]).astype(bf).astype(f32) * 0.125
            k = rope(mx[HW + h * HEAD_DIM : HW + (h + 1) * HEAD_DIM])
            v = mx[2 * HW + h * HEAD_DIM : 2 * HW + (h + 1) * HEAD_DIM]
            qa[h, :, sl] = jnp.concatenate([q, hot, rest], 0).astype(bf)
            ka[h, sl, :] = jnp.concatenate([k, neg, rest], 0).T.astype(bf)
            va[h, :, sl] = jnp.concatenate([v, one], 0).astype(bf)
            kt[h, :, sl] = k.astype(bf)
        puts = (
            (rows_ref, out_ref.at[sl]),
            (qa.at[:, :, sl], qa_ref.at[:, :, sl]),
            (ka.at[:, sl, :], ka_ref.at[:, sl, :]),
            (va.at[:, :, sl], va_ref.at[:, :, sl]),
            (kt.at[:, :, sl], kt_ref.at[:, :, sl]),
        )
        puts = [pltpu.make_async_copy(a, b, osem.at[5 * n + i]) for i, (a, b) in enumerate(puts)]
        for c in puts:
            c.start()
        return puts

    done = project(tok_ref, me, 0)
    first[0].wait_recv()
    f0 = remote(toks.at[rows(mx, 0)], toks.at[rows(mx, 0)], send.at[4], recv.at[4], ey)
    f0.start()
    first[1].wait_recv()
    f1 = remote(toks.at[rows(my, 1)], toks.at[rows(my, 1)], send.at[5], recv.at[5], ex)
    f1.start()
    for c in small:
        c.wait()
    first[2].wait_recv()
    done += project(toks.at[whole(mx)], mx, 1)
    first[3].wait_recv()
    done += project(toks.at[whole(my)], my, 2)
    f0.wait_recv()
    f1.wait_recv()
    done += project(toks.at[whole(md)], md, 3)
    codes_ref[...] = codes[...]
    for c in first + [f0, f1]:
        c.wait_send()
    for c in done:
        c.wait()


def gather(tok, code, cos, sin, w_qkv):
    count, width = tok.shape
    total = SPAN * count
    shapes = ((NH, 128, total), (NH, total, 128), (NH, 128, total), (NH, HEAD_DIM, total))
    return pl.pallas_call(
        gather_kernel,
        out_shape=(jax.ShapeDtypeStruct((total, width), bf), jax.ShapeDtypeStruct((1, total), f32))
        + tuple(jax.ShapeDtypeStruct(s, bf) for s in shapes),
        in_specs=[VM] * 4 + [ANY],
        out_specs=(ANY, VM) + (ANY,) * 4,
        scratch_shapes=[
            pltpu.VMEM((total, width), bf), pltpu.VMEM((1, total), f32), pltpu.VMEM((3, width, 256), bf),
            pltpu.VMEM((256, width), bf), pltpu.VMEM((3 * HW, width), bf),
        ]
        + [pltpu.VMEM(s, bf) for s in shapes]
        + [dma_sems(6), dma_sems(6), dma_sems(3), dma_sems(3), dma_sems(3), dma_sems(20)],
        compiler_params=comm_params(0),
        name="gather",
    )(tok, code, cos, sin, w_qkv)


def heads_to_tokens_kernel(parts, in_ref, out_ref, send, recv, lsem):
    t, p, x, y, g = here()
    count = out_ref.shape[1]
    me = lax.rem(p, SPAN)
    peers = plane_peers()
    width = parts and out_ref.shape[0] // parts
    greet(peers)
    copies = []
    for i, peer in enumerate((peers[2], peers[0], peers[1])):
        m = lax.rem(peer[1], SPAN)
        for k in range(parts):
            c = remote(
                in_ref.at[pl.ds(k * HW, HW), pl.ds(pl.multiple_of(m * count, count), count)],
                out_ref.at[pl.ds(pl.multiple_of(k * width + me * HW, HW), HW)],
                send.at[i * parts + k],
                recv.at[i * parts + k],
                peer,
            )
            c.start()
            copies.append(c)
    for k in range(parts):
        c = pltpu.make_async_copy(
            in_ref.at[pl.ds(k * HW, HW), pl.ds(pl.multiple_of(me * count, count), count)],
            out_ref.at[pl.ds(pl.multiple_of(k * width + me * HW, HW), HW)],
            lsem.at[k],
        )
        c.start()
        copies.append(c)
    for c in copies:
        c.wait()


def heads_to_tokens(a, cid, name):
    parts = a.shape[0] // HW
    count = a.shape[1] // SPAN
    return pl.pallas_call(
        functools.partial(heads_to_tokens_kernel, parts),
        out_shape=jax.ShapeDtypeStruct((parts * HEADS * HEAD_DIM, count), a.dtype),
        in_specs=[VM],
        out_specs=ANY,
        scratch_shapes=[dma_sems(3 * parts), dma_sems(3 * parts), dma_sems(parts)],
        compiler_params=comm_params(cid),
        name=name,
    )(a)


def tokens_to_heads_kernel(in_ref, out_ref, send, recv, lsem):
    t, p, x, y, g = here()
    count = in_ref.shape[1]
    me = lax.rem(p, SPAN)
    peers = plane_peers()
    greet(peers)
    mine = pl.ds(pl.multiple_of(me * count, count), count)
    copies = []
    for i, peer in enumerate((peers[2], peers[0], peers[1])):
        m = lax.rem(peer[1], SPAN)
        c = remote(
            in_ref.at[pl.ds(pl.multiple_of(m * HW, HW), HW)],
            out_ref.at[:, mine],
            send.at[i],
            recv.at[i],
            peer,
        )
        c.start()
        copies.append(c)
    c = pltpu.make_async_copy(
        in_ref.at[pl.ds(pl.multiple_of(me * HW, HW), HW)], out_ref.at[:, mine], lsem.at[0]
    )
    c.start()
    for c in copies + [c]:
        c.wait()


def tokens_to_heads(a, cid, name):
    return pl.pallas_call(
        tokens_to_heads_kernel,
        out_shape=jax.ShapeDtypeStruct((HW, SPAN * a.shape[1]), a.dtype),
        in_specs=[VM],
        out_specs=ANY,
        scratch_shapes=[dma_sems(3), dma_sems(3), dma_sems(1)],
        compiler_params=comm_params(cid),
        name=name,
    )(a)


def doc_limits(code):
    pad = code >= 4.0
    mem = jnp.where(pad, code - 4.0, code)
    n0 = jnp.sum(jnp.where(mem < 0.5, 1.0, 0.0)).astype(jnp.int32)
    n1 = jnp.sum(jnp.where(mem < 1.5, 1.0, 0.0)).astype(jnp.int32)
    l = [jnp.sum(jnp.where(code == float(d), 1.0, 0.0)).astype(jnp.int32) for d in range(3)]
    return n0, n1, l

def block_range(lims, a, size, total):
    n0, n1, l = lims
    b = a + size - 1
    first = (a >= n0).astype(jnp.int32) + (a >= n1).astype(jnp.int32)
    last = (b >= n0).astype(jnp.int32) + (b >= n1).astype(jnp.int32)
    lo = jnp.where(first == 0, 0, jnp.where(first == 1, n0, n1))
    hi = jnp.where(last == 0, n0, jnp.where(last == 1, n1, total))
    dead = jnp.zeros((), jnp.bool_)
    for d in range(3):
        dead = dead | ((first <= d) & (d <= last) & (l[d] == 0))
    return jnp.where(dead, 0, lo), jnp.where(dead, total, hi)

def fwd_kernel(KB, QB, code_ref, qa_ref, ka_ref, va_ref, out_ref, lse_ref, o32_ref, acc_ref):
    T = code_ref.shape[1]
    lims = doc_limits(code_ref[...])

    def qblock(i, _):
        a = i*QB
        qs = pl.ds(pl.multiple_of(a, QB), QB)
        lo, hi = block_range(lims, a, QB, T)
        jlo = lo//KB; jhi = (hi+KB-1)//KB
        for h in range(NH):
            acc_ref[h] = jnp.zeros_like(acc_ref[h])
        def kv(j, ms):
            ks = pl.ds(pl.multiple_of(j*KB, KB), KB)
            new = []
            ss = [nn(ka_ref[h, ks, :], qa_ref[h, :, qs]) for h in range(NH)]
            for h in range(NH):
                s = ss[h]
                mn = jnp.maximum(ms[h], jnp.max(s, 0, keepdims=True))
                p = jnp.exp(s - mn).astype(bf)
                al = jnp.exp(ms[h]-mn)
                acc_ref[h] = acc_ref[h]*al + nn(va_ref[h, :80, ks], p)
                new.append(mn)
            return tuple(new)
        ms = lax.fori_loop(jlo, jhi, kv, tuple(jnp.full((1, QB), -3e38, f32) for _ in range(NH)))
        for h in range(NH):
            tot = acc_ref[h, 64:65, :]
            o = acc_ref[h, :64, :]/tot
            o32_ref[h*HEAD_DIM:(h+1)*HEAD_DIM, qs] = o
            lse_ref[h:h+1, qs] = jnp.where(ms[h] < -1e29, 0.0, ms[h] + jnp.log(tot))
            out_ref[h*HEAD_DIM:(h+1)*HEAD_DIM, qs] = o.astype(bf)
        return 0
    lax.fori_loop(0, T//QB, qblock, 0)

def attn_fwd(code, qa, ka, va, KB=512, QB=256):
    T = code.shape[1]
    sds = jax.ShapeDtypeStruct
    return pl.pallas_call(
        functools.partial(fwd_kernel, KB, QB),
        out_shape=(sds((HW, T), bf), sds((NH, T), f32), sds((HW, T), f32)),
        in_specs=[VM] * 4,
        out_specs=(VM,) * 3,
        scratch_shapes=[pltpu.VMEM((NH, 80, QB), f32)],
        compiler_params=pltpu.CompilerParams(vmem_limit_bytes=VLIM),
        name="attn_fwd",
    )(code, qa, ka, va)


def bwd_kernel(KB, QB, do_ref, o32_ref, lse_ref, qa_ref, ka_ref, va_ref, kt_ref, cos_ref, sin_ref, code_ref, g_ref,
               vn_ref, dn_ref, da_ref, qb_ref, acc_ref, dq_ref):
    T = do_ref.shape[1]
    hw = HW
    CH = 512
    lims = doc_limits(code_ref[...])
    def prep(c, _):
        sl = pl.ds(pl.multiple_of(c*CH, CH), CH)
        for h in range(NH):
            do = do_ref[h*HEAD_DIM:(h+1)*HEAD_DIM, sl].astype(f32)
            delta = jnp.sum(do*o32_ref[h*HEAD_DIM:(h+1)*HEAD_DIM, sl], 0, keepdims=True)
            def split(x):
                x1 = x.astype(bf).astype(f32); r = x-x1
                x2 = r.astype(bf).astype(f32); x3 = r-x2
                return [x1, x2, x3]
            z13 = jnp.zeros((13, CH), f32); z48 = jnp.zeros((48, CH), f32)
            da_ref[h, :, sl] = jnp.concatenate([do]+split(-delta)+[z13, z48], 0).astype(bf)
            one = jnp.concatenate([jnp.ones((3, CH), f32), jnp.zeros((61, CH), f32)], 0)
            v = va_ref[h, :64, sl].astype(f32)
            vn_ref[h, sl, :] = jnp.concatenate([v, one], 0).T.astype(bf)
            z64 = jnp.zeros((64, CH), f32)
            q = qa_ref[h, :64, sl].astype(f32)
            dn_ref[h, sl, :] = jnp.concatenate([do, z64], 0).T.astype(bf)
            qb_ref[h, sl, :] = jnp.concatenate([z64, q], 0).T.astype(bf)
            acc_ref[h, sl, :] = jnp.zeros((CH, 128), f32)
        return 0
    lax.fori_loop(0, T//CH, prep, 0)
    def qblock(i, _):
        a = i*QB
        qs = pl.ds(pl.multiple_of(a, QB), QB)
        lo, hi = block_range(lims, a, QB, T)
        jlo = lo//KB; jhi = (hi+KB-1)//KB
        dq_ref[...] = jnp.zeros_like(dq_ref)
        def kv(j, _):
            ks = pl.ds(pl.multiple_of(j*KB, KB), KB)
            for h in range(NH):
                s = nn(ka_ref[h, ks, :], qa_ref[h, :, qs])
                dp = nn(vn_ref[h, ks, :], da_ref[h, :, qs])
                p = jnp.exp(s - lse_ref[h:h+1, qs])
                ds = (p*dp).astype(bf)
                acc_ref[h, ks, :] += nn(p.astype(bf), dn_ref[h, qs, :]) + nn(ds, qb_ref[h, qs, :])
                dq_ref[h] += nn(kt_ref[h, :, ks], ds)
            return 0
        lax.fori_loop(jlo, jhi, kv, 0)
        cos = cos_ref[:, qs]; sin = sin_ref[:, qs]
        for h in range(NH):
            u = dq_ref[h]*0.125
            x1 = u[:32]; x2 = u[32:]
            g_ref[h*HEAD_DIM:(h+1)*HEAD_DIM, qs] = jnp.concatenate([x1*cos+x2*sin, x2*cos-x1*sin], 0).astype(bf)
        return 0
    lax.fori_loop(0, T//QB, qblock, 0)
    def fin(c, _):
        sl = pl.ds(pl.multiple_of(c*CH, CH), CH)
        cos = cos_ref[:, sl]; sin = sin_ref[:, sl]
        for h in range(NH):
            t = acc_ref[h, sl, :].T
            x1 = t[64:96]; x2 = t[96:128]
            g_ref[hw+h*HEAD_DIM:hw+(h+1)*HEAD_DIM, sl] = jnp.concatenate([x1*cos+x2*sin, x2*cos-x1*sin], 0).astype(bf)
            g_ref[2*hw+h*HEAD_DIM:2*hw+(h+1)*HEAD_DIM, sl] = t[:64].astype(bf)
        return 0
    lax.fori_loop(0, T//CH, fin, 0)

def attn_bwd(do, o32, lse, qa, ka, va, kt, cos, sin, code, KB=512, QB=256):
    T = do.shape[1]
    return pl.pallas_call(functools.partial(bwd_kernel, KB, QB),
        out_shape=jax.ShapeDtypeStruct((3*NH*HEAD_DIM, T), bf),
        in_specs=[pl.BlockSpec(memory_space=pltpu.VMEM)]*10, out_specs=pl.BlockSpec(memory_space=pltpu.VMEM),
        scratch_shapes=[pltpu.VMEM((NH,T,128), bf), pltpu.VMEM((NH,T,128), bf), pltpu.VMEM((NH,128,T), bf), pltpu.VMEM((NH,T,128), bf),
                        pltpu.VMEM((NH,T,128), f32), pltpu.VMEM((NH,HEAD_DIM,QB), f32)],
        compiler_params=pltpu.CompilerParams(vmem_limit_bytes=VLIM), name="attn_bwd",
        cost_estimate=pl.CostEstimate(flops=int(10*T*T*128*3), bytes_accessed=12<<20, transcendentals=T*T*3))(do, o32, lse, qa, ka, va, kt, cos, sin, code)


def contrast_part(groups, sums, goals_ref, plane, allp, ge, send, recv, scores_ref, loss_ref):
    t, p, x, y, g = here()
    docs = groups * DOCS_GRP
    size = groups * 8
    peers = plane_peers()
    line = [(t, lax.rem(p + SPAN * k, SPAN * groups)) for k in range(1, groups)]
    plane[3] = sums
    copies = [remote(plane.at[3], plane.at[i], send.at[i], recv.at[i], q) for i, q in enumerate(peers)]
    for c in copies:
        c.start()
    col = lax.broadcasted_iota(jnp.int32, (size, size), 1)
    row = lax.broadcasted_iota(jnp.int32, (size, size), 0)

    def mark(i, hot):
        goal = goals_ref[i]
        at = (row == i // DOCS_GRP * 8 + i % DOCS_GRP) & (col == goal // DOCS_GRP * 8 + goal % DOCS_GRP)
        return hot + jnp.where(at, 1.0, 0.0)

    hot = lax.fori_loop(0, docs, mark, jnp.zeros((size, size), f32))
    for c in copies:
        c.wait()
    own = (plane[3] + plane[0]) + (plane[1] + plane[2])
    allp[t, g] = own
    rows = allp.at[t, g]
    copies = [remote(rows, rows, send.at[3 + i], recv.at[3 + i], q) for i, q in enumerate(line)]
    for c in copies:
        c.start()
    for c in copies:
        c.wait()
    c = remote(allp.at[t], allp.at[t], send.at[2 + groups], recv.at[2 + groups], (1 - t, p))
    c.start()
    c.wait()
    width = allp.shape[3]
    pools = [allp[k].reshape(size, width) for k in range(2)]
    embeds = [v * lax.rsqrt(jnp.sum(v * v, -1, keepdims=True) + 1e-06) for v in pools]
    dot = functools.partial(lax.dot_general, precision=precise, preferred_element_type=f32)
    scores = dot(embeds[0], embeds[1], (((1,), (1,)), ((), ()))) * 50.0
    live = lax.rem(col, 8) < DOCS_GRP
    alive = lax.rem(row, 8) < DOCS_GRP
    masked = jnp.where(live, scores, -1e30)
    top = jnp.max(masked, -1, keepdims=True)
    total = jnp.sum(jnp.exp(masked - top), -1, keepdims=True)
    log_sums = top + jnp.log(total)
    chosen = jnp.sum(hot * scores, -1, keepdims=True)
    each = jnp.where(alive[:, 0:1], log_sums - chosen, 0.0)
    loss_ref[...] = jnp.broadcast_to(jnp.sum(each, 0, keepdims=True) / docs, loss_ref.shape)
    scores_ref[...] = scores
    gs = jnp.where(alive & live, (jnp.exp(masked - log_sums) - hot) / docs, 0.0)
    gq = dot(gs, embeds[1], (((1,), (0,)), ((), ())))
    gd = dot(gs, embeds[0], (((0,), (0,)), ((), ())))
    ge[...] = jnp.where(t == 0, gq, gd) * 50.0
    mine = ge[pl.ds(pl.multiple_of(g * 8, 8), 8), :]
    pooled = allp[t, g]
    inv = lax.rsqrt(jnp.sum(pooled * pooled, -1, keepdims=True) + 1e-06)
    return inv * mine - inv * inv * inv * pooled * jnp.sum(pooled * mine, -1, keepdims=True)


def block_kernel(
    groups, heads_ref, rows_ref, code_ref, goals_ref, norms_ref, wo_h, wg_h, wu_h, wd_h,
    att_o, inner_o, hid_o, gm_o, gg_o, gb_o, ga_o, gh1_o, gains_o, scores_o, loss_o,
    att, wo, wg, wu, wd, inner, x1, s1, acc, hid, ab, x2, s2, sec, gm, gm2, gb, gb2, plane, allp, ge,
    wsem, send, recv, lsem, tsend, trecv, osem, csend, crecv,
):
    t, p, x, y, g = here()
    peers = plane_peers()
    sibling = (1 - t, p)
    line = tuple((t, lax.rem(p + SPAN * k, SPAN * groups)) for k in range(1, groups))
    count, width = rows_ref.shape
    half = width // 2
    tiles = wg.shape[0]
    me = lax.rem(p, SPAN)

    def weight(j, k):
        cols = pl.ds(j * width, width)
        src, dst = ((wg_h.at[:, cols], wg.at[j]), (wu_h.at[:, cols], wu.at[j]), (wd_h.at[cols], wd.at[j]))[k]
        return pltpu.make_async_copy(src, dst, wsem.at[1 + 3 * j + k])

    first_load = pltpu.make_async_copy(wo_h, wo, wsem.at[0])
    first_load.start()
    for j in range(tiles):
        for k in range(3):
            weight(j, k).start()
    greet(peers + (sibling,) + line)
    moves = []
    for i, peer in enumerate((peers[2], peers[0], peers[1])):
        m = lax.rem(peer[1], SPAN)
        moves.append(remote(
            heads_ref.at[:, pl.ds(pl.multiple_of(m * count, count), count)],
            att.at[pl.ds(pl.multiple_of(me * HW, HW), HW)], send.at[i], recv.at[i], peer,
        ))
    moves.append(pltpu.make_async_copy(
        heads_ref.at[:, pl.ds(pl.multiple_of(me * count, count), count)],
        att.at[pl.ds(pl.multiple_of(me * HW, HW), HW)], lsem.at[0],
    ))
    for c in moves:
        c.start()
    code = code_ref[...]
    zero = jnp.zeros((8 - DOCS_GRP, count), f32)
    mem = jnp.concatenate([jnp.where(code == float(d), 1.0, 0.0) for d in range(DOCS_GRP)] + [zero], 0)
    mem = jnp.concatenate([mem, mem, mem, jnp.zeros((8, count), f32)], 0).astype(bf)
    first_load.wait()
    for c in moves:
        c.wait()

    def pair(i, mine, its, out):
        return (
            pltpu.make_async_copy(mine, out.at[0], osem.at[i]),
            remote(its, out.at[1], tsend.at[i], trecv.at[i], sibling),
        )

    def both(i, mine, its, out):
        for c in pair(i, mine, its, out):
            c.start()

    both(0, att, att, att_o)
    acc[...] = tn(att[...], wo[...])
    step = 64
    gain1, bias1 = norms_ref[0:1, :], norms_ref[1:2, :]
    gain2, bias2 = norms_ref[2:3, :], norms_ref[3:4, :]

    def chunk(i):
        return pl.ds(pl.multiple_of(i * step, step), step)

    def norm(h, sl, xs, ss):
        c = h - jnp.mean(h, -1, keepdims=True)
        s = lax.rsqrt(jnp.mean(c * c, -1, keepdims=True) + norm_eps)
        xh = c * s
        xs[sl, :] = xh
        ss[sl, :] = s
        return xh

    def norm_one(i, _):
        sl = chunk(i)
        xh = norm(rows_ref[sl, :].astype(f32) + acc[sl, :], sl, x1, s1)
        v = xh * gain1 + bias1
        inner[sl, :] = v.astype(bf)
        acc[sl, :] = v
        return 0

    lax.fori_loop(0, count // step, norm_one, 0)
    both(1, inner, inner, inner_o)

    def tile_of(j, i, mine, its, out):
        return (
            pltpu.make_async_copy(mine, out.at[0, j], osem.at[i + j]),
            remote(its, out.at[1, j], tsend.at[i + j], trecv.at[i + j], sibling),
        )

    for j in range(tiles):
        for k in range(3):
            weight(j, k).wait()
        gate = nn(inner[...], wg[j])
        upper = nn(inner[...], wu[j])
        sig = jax.nn.sigmoid(gate)
        silu = gate * sig
        hid[j] = (silu * upper).astype(bf)
        ab[0, j] = (upper * (sig * (1.0 + gate * (1.0 - sig)))).astype(bf)
        ab[1, j] = silu.astype(bf)
        for c in tile_of(j, 2, hid.at[j], hid.at[j], hid_o):
            c.start()
        acc[...] += nn(hid[j], wd[j])

    def norm_two(i, _):
        sl = chunk(i)
        v = norm(acc[sl, :], sl, x2, s2) * gain2 + bias2
        for k, part in enumerate(split3(v)):
            sec[k, sl, :] = part.astype(bf)
        return 0

    lax.fori_loop(0, count // step, norm_two, 0)
    sums = (nn(mem[:16], sec[0]) + nn(mem[:16], sec[1]) + nn(mem[:16], sec[2]))[:8]
    top = lax.broadcasted_iota(jnp.int32, sums.shape, 0) < DOCS_GRP
    sums = jnp.where(top, sums, 0.0)
    gp = contrast_part(groups, sums, goals_ref, plane, allp, ge, csend, crecv, scores_o, loss_o)
    gp3 = jnp.concatenate(split3(gp) + [jnp.zeros_like(gp)], 0).astype(bf)
    acc[...] = tn(mem, gp3)

    def fold(v):
        return jnp.sum(v.reshape(step // 8, 8, width), 0)

    def norm_back(gr, xh, s, gain):
        e = gr * gain
        v = e - jnp.mean(e, -1, keepdims=True) - xh * jnp.mean(e * xh, -1, keepdims=True)
        return v * s

    zeros = jnp.zeros((8, width), f32)

    def back_two(i, sums):
        sl = chunk(i)
        gr, xh = acc[sl, :], x2[sl, :]
        v = norm_back(gr, xh, s2[sl, :], gain2)
        acc[sl, :] = v
        low = v.astype(bf)
        gm[sl, :] = low
        gm2[0, sl, :] = low[:, :half]
        gm2[1, sl, :] = low[:, half:]
        return sums[0] + fold(gr * xh), sums[1] + fold(gr)

    g2, b2 = lax.fori_loop(0, count // step, back_two, (zeros, zeros))
    both(2 + 2 * tiles, gm2.at[t], gm2.at[1 - t], gm_o)
    for j in range(tiles):
        gh = nt(gm[...], wd[j])
        gg = (gh * ab[0, j].astype(f32)).astype(bf)
        gu = (gh * ab[1, j].astype(f32)).astype(bf)
        ab[0, j] = gg
        ab[1, j] = gu
        for c in tile_of(j, 2 + tiles, ab.at[t, j], ab.at[1 - t, j], gg_o):
            c.start()
        acc[...] += nt(gg, wg[j]) + nt(gu, wu[j])

    def back_one(i, sums):
        sl = chunk(i)
        gr, xh = acc[sl, :], x1[sl, :]
        v = norm_back(gr, xh, s1[sl, :], gain1)
        gh1_o[sl, :] = v
        low = v.astype(bf)
        gb[sl, :] = low
        gb2[0, sl, :] = low[:, :half]
        gb2[1, sl, :] = low[:, half:]
        return sums[0] + fold(gr * xh), sums[1] + fold(gr)

    g1, b1 = lax.fori_loop(0, count // step, back_one, (zeros, zeros))
    both(3 + 2 * tiles, gb2.at[t], gb2.at[1 - t], gb_o)
    flat = [jnp.sum(v, 0, keepdims=True) for v in (g1, b1, g2, b2)]
    gains_o[...] = jnp.concatenate(flat + [jnp.zeros((4, width), f32)], 0)
    ga_o[...] = nt(wo[...], gb[...]).astype(bf)
    done = [pair(0, att, att, att_o), pair(1, inner, inner, inner_o)]
    for j in range(tiles):
        done.append(tile_of(j, 2, hid.at[j], hid.at[j], hid_o))
        done.append(tile_of(j, 2 + tiles, ab.at[t, j], ab.at[1 - t, j], gg_o))
    done.append(pair(2 + 2 * tiles, gm2.at[t], gm2.at[1 - t], gm_o))
    done.append(pair(3 + 2 * tiles, gb2.at[t], gb2.at[1 - t], gb_o))
    for c in done:
        for d in c:
            d.wait()


def block(heads, rows, code, goals, norms, w_out, w_gate, w_up, w_down, groups):
    count, width = rows.shape
    tiles = w_gate.shape[1] // width
    half = width // 2
    size = groups * 8
    sds = jax.ShapeDtypeStruct
    vm = lambda *n: pltpu.VMEM(n, bf)
    vf = lambda *n: pltpu.VMEM(n, f32)
    return pl.pallas_call(
        functools.partial(block_kernel, groups),
        out_shape=(
            sds((2, width, count), bf), sds((2, count, width), bf), sds((2, tiles, count, width), bf),
            sds((2, count, half), bf), sds((2, tiles, count, width), bf), sds((2, count, half), bf),
            sds((width, count), bf), sds((count, width), f32), sds((8, width), f32),
            sds((size, size), f32), sds((8, 128), f32),
        ),
        in_specs=[VM, VM, VM, pl.BlockSpec(memory_space=pltpu.SMEM), VM] + [ANY] * 4,
        out_specs=(ANY,) * 6 + (VM,) * 5,
        scratch_shapes=[
            vm(width, count), vm(width, width), vm(tiles, width, width), vm(tiles, width, width),
            vm(tiles, width, width), vm(count, width), vf(count, width), vf(count, 1), vf(count, width),
            vm(tiles, count, width), vm(2, tiles, count, width), vf(count, width), vf(count, 1),
            vm(3, count, width), vm(count, width), vm(2, count, half), vm(count, width), vm(2, count, half),
            vf(4, 8, width), vf(2, groups, 8, width), vf(size, width),
            dma_sems(1 + 3 * tiles), dma_sems(3), dma_sems(3), dma_sems(1),
            dma_sems(4 + 2 * tiles), dma_sems(4 + 2 * tiles), dma_sems(4 + 2 * tiles),
            dma_sems(3 + groups), dma_sems(3 + groups),
        ],
        compiler_params=comm_params(1),
        name="block",
    )(heads, rows, code, goals, norms, w_out, w_gate, w_up, w_down)


def weights_kernel(
    groups, i_ref, g_ref, h_ref, m_ref, a_ref, b_ref, in_ref, gain_ref,
    sa_ref, ka_ref, sb_ref, kb_ref, heads_ref, sum_ref,
    iv, it, gv, hv, mv, av, bv, gs, ds, os, plane, line, isem, osem, send, recv, lsem, nsend, nrecv,
):
    t, p, x, y, g = here()
    peers = plane_peers()
    sibling = (1 - t, p)
    others = tuple((t, lax.rem(p + SPAN * k, SPAN * groups)) for k in range(1, groups))
    greet(peers + (sibling,) + others)
    around = [remote(gain_ref, plane.at[i], nsend.at[i], nrecv.at[i], q) for i, q in enumerate(peers)]
    for c in around:
        c.start()
    tokens = in_ref.shape[1]
    me = lax.rem(p, SPAN)
    mine = pl.ds(pl.multiple_of(me * tokens, tokens), tokens)
    moves = []
    for i, peer in enumerate((peers[2], peers[0], peers[1])):
        m = lax.rem(peer[1], SPAN)
        moves.append(remote(
            in_ref.at[pl.ds(pl.multiple_of(m * HW, HW), HW)], heads_ref.at[:, mine],
            send.at[i], recv.at[i], peer,
        ))
    moves.append(pltpu.make_async_copy(
        in_ref.at[pl.ds(pl.multiple_of(me * HW, HW), HW)], heads_ref.at[:, mine], lsem.at[0]
    ))
    for c in moves:
        c.start()
    count, width = i_ref.shape[1:]
    half = width // 2
    tiles = gv.shape[1]
    shards = SPAN * groups
    one = width // shards
    down = ds.shape[1]

    def load(i, src, dst):
        return pltpu.make_async_copy(src, dst, isem.at[i])

    def tile(ref, j, buf, base):
        return load(base + j, ref.at[:, j], buf.at[:, j])

    few = [load(i, a, b) for i, (a, b) in enumerate(((m_ref, mv), (a_ref, av), (b_ref, bv), (i_ref, iv)))]
    few[0].start()
    for j in range(tiles):
        tile(h_ref, j, hv, 4).start()
    for c in few[1:]:
        c.start()
    for j in range(tiles):
        tile(g_ref, j, gv, 4 + tiles).start()
    few[0].wait()

    def downward(j, _):
        tile(h_ref, j, hv, 4).wait()
        r = tn(hv[0, j], mv[0]) + tn(hv[1, j], mv[1])
        ds[pl.ds(j * (width // down), width // down)] = r.astype(bf).reshape(width // down, down, half)
        return 0

    lax.fori_loop(0, tiles, downward, 0)
    for c in few[1:] + around:
        c.wait()
    line[0] = (gain_ref[...] + plane[0]) + (plane[1] + plane[2])
    ring = [
        remote(line.at[0], line.at[1 + k], nsend.at[3 + k], nrecv.at[3 + k], q) for k, q in enumerate(others)
    ]
    for c in ring:
        c.start()
    r = nn(av[0], bv[0]) + nn(av[1], bv[1])
    os[...] = r.astype(bf).reshape(shards, one, half)
    for i in range(2):
        it[:, i * count : (i + 1) * count] = iv[i].T
    fours = lambda ref, n: ref.reshape(groups, 2, 2, n, half)

    def put(i, src, dst):
        return pltpu.make_async_copy(src, dst, osem.at[i])

    outs = []
    for i, (ref, k) in enumerate(((sb_ref, 1 - y), (kb_ref, y))):
        outs.append(put(4 * i, fours(ds, down).at[:, k], ref.at[:, :, pl.ds(one, down)]))
        outs.append(put(4 * i + 1, fours(os, one).at[:, k], ref.at[:, :, pl.ds(one + down, one)]))
    for c in outs:
        c.start()

    def top(j):
        rows = pl.ds(pl.multiple_of(j * one, one), one)
        piece = fours(gs.at[j], one)
        return (
            put(8 + j, piece.at[:, :, 1 - x], sa_ref.at[:, :, rows]),
            put(8 + 2 * tiles + j, piece.at[:, :, x], ka_ref.at[:, :, rows]),
        )

    for j in range(tiles):
        tile(g_ref, j, gv, 4 + tiles).wait()
        r = (nn(it[:, :count], gv[0, j]) + nn(it[:, count:], gv[1, j])).astype(bf)
        for h in range(2):
            k = 2 * j + h
            gs[k] = r[:, h * half : (h + 1) * half].reshape(shards, one, half)
            if k < 2 * tiles - 1:
                outs.extend(top(k))
                for c in outs[-2:]:
                    c.start()
    for c in ring:
        c.wait()
    total = line[0]
    for k in range(1, groups):
        total = total + line[k]
    line[groups] = total
    last = remote(line.at[groups], line.at[groups + 1], nsend.at[2 + groups], nrecv.at[2 + groups], sibling)
    last.start()
    piece = fours(gs.at[2 * tiles - 1], one)
    for i, (ref, k) in enumerate(((sb_ref, 1 - y), (kb_ref, y))):
        c = put(4 * i + 2, piece.at[:, k], ref.at[:, :, pl.ds(0, one)])
        c.start()
        outs.append(c)
    last.wait()
    sum_ref[...] = line[groups] + line[groups + 1]
    for c in outs + moves:
        c.wait()


def weight_grads(groups, grad_heads, gains, inner, grads, hidden, grad_mlp, attended, grad_branch):
    count, width = inner.shape[1:]
    half = width // 2
    shards = SPAN * groups
    one = width // shards
    tiles = grads.shape[1]
    down = tiles * one
    ra = (2 * tiles - 1) * one
    rb = down + 2 * one
    part = lambda r: jax.ShapeDtypeStruct((groups, 2, r, half), bf)
    vm = lambda *n: pltpu.VMEM(n, bf)
    return pl.pallas_call(
        functools.partial(weights_kernel, groups),
        out_shape=(
            part(ra), part(ra), part(rb), part(rb),
            jax.ShapeDtypeStruct((HW, SPAN * grad_heads.shape[1]), bf), jax.ShapeDtypeStruct(gains.shape, f32),
        ),
        in_specs=[ANY] * 6 + [VM] * 2,
        out_specs=(ANY,) * 5 + (VM,),
        scratch_shapes=[
            vm(2, count, width), vm(width, 2 * count), vm(2, tiles, count, width), vm(2, tiles, count, width),
            vm(2, count, half), vm(2, width, count), vm(2, count, half),
            vm(2 * tiles, shards, one, half), vm(shards, down, half), vm(shards, one, half),
            pltpu.VMEM((3,) + gains.shape, f32), pltpu.VMEM((groups + 2,) + gains.shape, f32),
            dma_sems(4 + 2 * tiles), dma_sems(8 + 4 * tiles), dma_sems(3), dma_sems(3), dma_sems(1),
            dma_sems(3 + groups), dma_sems(3 + groups),
        ],
        compiler_params=comm_params(2),
        name="weight_grads",
        cost_estimate=pl.CostEstimate(
            flops=int(2 * 2 * count * half * width * 8.5), bytes_accessed=30 << 20, transcendentals=0
        ),
    )(inner, grads, hidden, grad_mlp, attended, grad_branch, grad_heads, gains)


def add_rows(dst, a, b, rows):
    step = rows // 3 if rows % 48 == 0 and rows > 48 else rows

    def part(i, _):
        sl = pl.ds(pl.multiple_of(i * step, step), step)
        dst[sl, :] = a[sl, :] + b[sl, :]
        return 0

    lax.fori_loop(0, rows // step, part, 0)


class Line:
    def __init__(self, z, zt, groups, part, up, down, sems, t, p):
        self.z, self.zt, self.groups = z, zt, groups
        self.part, self.up, self.down = part, up, down
        us, ur, ds, dr = sems
        above = (t, lax.rem(p + SPAN, SPAN * groups))
        below = (t, lax.rem(p + SPAN * (groups - 1), SPAN * groups))
        self.up_first = lambda: remote(part, up, us, ur, above)
        self.up_next = lambda: remote(up, up, us, ur, above)
        self.down_first = lambda: remote(part, down, ds, dr, below)
        self.down_next = lambda: remote(down, down, ds, dr, below)

    def start(self):
        if self.zt > 0:
            pl.when(self.z == 0)(lambda: self.up_first().start())
        if self.zt < self.groups - 1:
            pl.when(self.z == self.groups - 1)(lambda: self.down_first().start())

    def relay(self, hop, rows):
        def up():
            self.up_next().wait_recv()
            add_rows(self.up, self.up, self.part, rows)
            self.up_next().start()

        def down():
            self.down_next().wait_recv()
            add_rows(self.down, self.down, self.part, rows)
            self.down_next().start()

        if 0 < hop < self.zt:
            pl.when(self.z == hop)(up)
        if self.zt < self.groups - 1 - hop:
            pl.when(self.z == self.groups - 1 - hop)(down)

    def finish(self, dst, rows):
        def done():
            if self.zt > 0:
                self.up_next().wait_recv()
            if self.zt < self.groups - 1:
                self.down_next().wait_recv()
            if 0 < self.zt < self.groups - 1:
                add_rows(self.up, self.up, self.down, rows)
            add_rows(dst, self.up if self.zt > 0 else self.down, self.part, rows)

        pl.when(self.z == self.zt)(done)

    def drain(self):
        if self.zt > 0:
            pl.when(self.z < self.zt)(lambda: self.up_first().wait_send())
        if self.zt < self.groups - 1:
            pl.when(self.z > self.zt)(lambda: self.down_first().wait_send())


def outward(groups):
    order = []
    lo, hi = 0, groups - 1
    while lo <= hi:
        order.append(hi)
        if lo < hi:
            order.append(lo)
        lo, hi = lo + 1, hi - 1
    return order


def finish_kernel(
    groups, ka_ref, kb_ref, ra_ref, rb_ref, wq_ref, gh_ref, g_ref, tok_ref,
    pair_ref, tg_ref, out_ref,
    kva, kvb, rva, rvb, r2a, r2b, ua, ub, da, db, isem, s2, q2, us, ur, ds, dr,
    gm_ref, wq, gh, wsem, fs, fr,
    w2, sib, ub2, db2, fin, send, recv, ts, tr, us2, ur2, ds2, dr2, ps, pr, lsem,
):
    t, p, x, y, z = here()
    ex, ey, ed = plane_peers()
    peers = (ex, ey, ed)
    sibling = (1 - t, p)
    others = [(t, lax.rem(p + SPAN * k, SPAN * groups)) for k in range(1, groups)]
    across = tuple((1 - t, q[1]) for q in peers)
    order = outward(groups)
    colours = (
        (ey, ka_ref, ra_ref, kva, rva, r2a, ua, da, y),
        (ex, kb_ref, rb_ref, kvb, rvb, r2b, ub, db, x),
    )

    def loads(c, zt):
        peer, kr, rr, kv, rv = colours[c][:5]
        i = 2 * (c * groups + zt)
        return (
            pltpu.make_async_copy(kr.at[zt], kv.at[zt], isem.at[i]),
            pltpu.make_async_copy(rr.at[zt], rv.at[zt], isem.at[i + 1]),
        )

    for zt in order:
        for c in range(2):
            for d in loads(c, zt):
                d.start()
    more = (pltpu.make_async_copy(wq_ref, wq, wsem.at[0]), pltpu.make_async_copy(gh_ref, gh, wsem.at[1]))
    for c in more:
        c.start()
    greet(peers + across + (sibling,) + tuple(others))

    def second(c, zt):
        peer, kr, rr, kv, rv, r2, u, d, mine = colours[c]
        i = c * groups + zt
        return remote(rv.at[zt, 1 - mine], r2.at[zt], s2.at[i], q2.at[i], peer)

    def chain(c, zt):
        peer, kr, rr, kv, rv, r2, u, d, mine = colours[c]
        i = c * groups + zt
        return Line(z, zt, groups, r2.at[zt], u.at[zt], d.at[zt],
                    (us.at[i], ur.at[i], ds.at[i], dr.at[i]), t, p)

    def size(c):
        return colours[c][3].shape[2]

    for zt in order:
        for c in range(2):
            for d in loads(c, zt):
                d.wait()
            peer, kr, rr, kv, rv, r2, u, d, mine = colours[c]
            away = rv.at[zt, 1 - mine]
            add_rows(away, away, kv.at[zt, 1 - mine], size(c))
            second(c, zt).start()
    count = gm_ref.shape[1]
    me = lax.rem(p, SPAN)
    width = gm_ref.shape[0] // 3
    copies = []
    for i, peer in enumerate((peers[2], peers[0], peers[1])):
        m = lax.rem(peer[1], SPAN)
        for k in range(3):
            copies.append(remote(
                g_ref.at[pl.ds(k * HW, HW), pl.ds(pl.multiple_of(m * count, count), count)],
                gm_ref.at[pl.ds(pl.multiple_of(k * width + me * HW, HW), HW)],
                send.at[i * 3 + k], recv.at[i * 3 + k], peer,
            ))
    for k in range(3):
        copies.append(pltpu.make_async_copy(
            g_ref.at[pl.ds(k * HW, HW), pl.ds(pl.multiple_of(me * count, count), count)],
            gm_ref.at[pl.ds(pl.multiple_of(k * width + me * HW, HW), HW)],
            lsem.at[k],
        ))
    for c in copies:
        c.start()
    for zt in order:
        for c in range(2):
            peer, kr, rr, kv, rv, r2, u, d, mine = colours[c]
            keep = rv.at[zt, mine]
            add_rows(keep, keep, kv.at[zt, mine], size(c))

    def in_plane(zt):
        for c in range(2):
            peer, kr, rr, kv, rv, r2, u, d, mine = colours[c]
            second(c, zt).wait_recv()
            dst = r2.at[zt]
            add_rows(dst, dst, rv.at[zt, mine], size(c))
            chain(c, zt).start()

    def relay(zt, hop):
        for c in range(2):
            chain(c, zt).relay(hop, size(c))

    in_plane(order[0])
    shards = SPAN * groups
    one = width // shards
    half = width // 2
    for h in range(2):
        r = nn(g_ref[...], tok_ref[:, h * half : (h + 1) * half]).T
        w2[h * (shards // 2) : (h + 1) * (shards // 2)] = r.astype(bf).reshape(shards // 2, one, 3 * HW)

    def swap(zt):
        return remote(w2.at[pl.ds(zt * 4 + (1 - t) * 2, 2)], sib.at[zt], ts.at[zt], tr.at[zt], sibling)

    for zt in order:
        swap(zt).start()

    def chain2(zt, k):
        i = zt * 2 + k
        return Line(z, zt, groups, sib.at[zt, k], ub2.at[zt, k], db2.at[zt, k],
                    (us2.at[i], ur2.at[i], ds2.at[i], dr2.at[i]), t, p)

    for i, zt in enumerate(order):
        if i >= 1:
            in_plane(zt)
        swap(zt).wait_recv()
        for k in range(2):
            dst = sib.at[zt, k]
            add_rows(dst, dst, w2.at[zt * 4 + t * 2 + k], one)
            chain2(zt, k).start()
        if i >= 1:
            relay(order[i - 1], 1)
            for k in range(2):
                chain2(order[i - 1], k).relay(1, one)
    for hop in range(1, groups - 1):
        for i, zt in enumerate(order):
            if hop > 1 or i == groups - 1:
                relay(zt, hop)
                for k in range(2):
                    chain2(zt, k).relay(hop, one)
    for zt in order:
        for k in range(2):
            chain2(zt, k).finish(fin.at[k], one)
    here_id = t * SPAN + me

    def hand(k, tt):
        m = t * 2 + k
        peer = (tt, z * SPAN + m)
        i = k * 2 + tt
        away = lambda: remote(fin.at[k], out_ref.at[me], ps.at[i], pr.at[me], peer)
        stay = lambda: pltpu.make_async_copy(fin.at[k], out_ref.at[me], lsem.at[3])
        return away, stay, (tt * SPAN + m) == here_id

    for k in range(2):
        for tt in range(2):
            away, stay, same = hand(k, tt)
            pl.when(jnp.logical_not(same))(lambda away=away: away().start())
            pl.when(same)(lambda stay=stay: stay().start())
    for zt in order:
        for c, sl in ((0, pl.ds(0, size(0))), (1, pl.ds(size(0), size(1)))):
            chain(c, zt).finish(pair_ref.at[t, sl], size(c))
    last = remote(pair_ref.at[t], pair_ref.at[t], fs.at[0], fr.at[0], sibling)
    last.start()
    for c in copies + list(more):
        c.wait()
    turned = nn(wq[...], gm_ref[...]).T
    tg_ref[...] = gh[...] + turned
    for s in range(SPAN):
        from_here = jnp.logical_and(s == me, y == t)
        pl.when(jnp.logical_not(from_here))(
            lambda s=s: remote(fin.at[0], out_ref.at[s], ps.at[0], pr.at[s], sibling).wait_recv()
        )
    for k in range(2):
        for tt in range(2):
            away, stay, same = hand(k, tt)
            pl.when(jnp.logical_not(same))(lambda away=away: away().wait_send())
            pl.when(same)(lambda stay=stay: stay().wait())
    for zt in range(groups):
        swap(zt).wait_send()
        for k in range(2):
            chain2(zt, k).drain()
        for c in range(2):
            second(c, zt).wait_send()
            chain(c, zt).drain()
    last.wait()


def finish(ka, kb, ra, rb, wq, gh, g, tok, groups):
    width = tok.shape[1]
    count = tok.shape[0] // SPAN
    one = width // (SPAN * groups)
    na, nb = ka.shape[2], kb.shape[2]
    half = ka.shape[3]
    buf = lambda *n: pltpu.VMEM(n, bf)
    mix = lambda *n: pltpu.VMEM(n + (one, 3 * HW), bf)
    return pl.pallas_call(
        functools.partial(finish_kernel, groups),
        out_shape=(
            jax.ShapeDtypeStruct((2, na + nb, half), bf),
            jax.ShapeDtypeStruct((count, width), f32),
            jax.ShapeDtypeStruct((SPAN, one, 3 * HW), bf),
        ),
        in_specs=[ANY] * 6 + [VM] * 2,
        out_specs=(VM,) * 3,
        scratch_shapes=[
            buf(groups, 2, na, half), buf(groups, 2, nb, half), buf(groups, 2, na, half), buf(groups, 2, nb, half),
            buf(groups, na, half), buf(groups, nb, half), buf(groups, na, half), buf(groups, nb, half),
            buf(groups, na, half), buf(groups, nb, half),
            dma_sems(4 * groups), dma_sems(2 * groups), dma_sems(2 * groups),
            dma_sems(2 * groups), dma_sems(2 * groups), dma_sems(2 * groups), dma_sems(2 * groups),
            buf(3 * width, count), buf(width, 3 * width), pltpu.VMEM((count, width), f32), dma_sems(2),
            dma_sems(1), dma_sems(1),
            mix(SPAN * groups), mix(groups, 2), mix(groups, 2), mix(groups, 2), mix(2),
            dma_sems(9), dma_sems(9), dma_sems(groups), dma_sems(groups),
            dma_sems(2 * groups), dma_sems(2 * groups), dma_sems(2 * groups), dma_sems(2 * groups),
            dma_sems(4), dma_sems(SPAN), dma_sems(4),
        ],
        compiler_params=comm_params(3),
        name="finish",
    )(ka, kb, ra, rb, wq, gh, g, tok)


def unfold_kernel(pair_ref, part_ref, gate_ref, up_ref, down_ref, out_ref, qkv_ref):
    one = out_ref.shape[0]
    half = pair_ref.shape[2]
    steps = gate_ref.shape[1] // half
    down = down_ref.shape[0]
    for j in range(steps):
        for k, ref in enumerate((gate_ref, up_ref)):
            ref[:, j * half : (j + 1) * half] = pair_ref[k, j * one : (j + 1) * one, :].astype(f32)
    top = (steps - 1) * one
    for k in range(2):
        cols = slice(k * half, (k + 1) * half)
        down_ref[:, cols] = pair_ref[k, top + one : top + one + down, :].astype(f32)
        out_ref[:, cols] = pair_ref[k, top + one + down :, :].astype(f32)
    for k in range(3):
        row = [part_ref[s, :, k * HW : (k + 1) * HW].astype(f32) for s in range(SPAN)]
        qkv_ref[:, k * SPAN * HW : (k + 1) * SPAN * HW] = jnp.concatenate(row, 1)


def unfold(pair, parts, tiles):
    one = parts.shape[1]
    half = pair.shape[2]
    width = 2 * half
    sds = jax.ShapeDtypeStruct
    return pl.pallas_call(
        unfold_kernel,
        out_shape=(
            sds((one, tiles * width), f32), sds((one, tiles * width), f32), sds((tiles * one, width), f32),
            sds((one, width), f32), sds((one, 3 * width), f32),
        ),
        in_specs=[VM] * 2,
        out_specs=(VM,) * 5,
        name="unfold",
    )(pair, parts)


def angle_tables(total):
    half = HEAD_DIM // 2
    freqs = np.float32(1000.0) ** (-np.arange(half, dtype=np.float32) / np.float32(half))
    theta = freqs[:, None].astype(np.float32) * np.arange(total, dtype=np.float32)[None, :]
    return np.cos(theta).astype(np.float32), np.sin(theta).astype(np.float32)


def spread_sum(value):
    part = lax.psum_scatter(value, "dp", scatter_dimension=0, tiled=True)
    return lax.psum(part.astype(bf), "tower").astype(f32)


def local(
    tokens, doc_ids, pad_mask, targets, w_qkv, w_out, ln1_gain, ln1_bias,
    w_gate, w_up, w_down, ln2_gain, ln2_bias,
):
    width = w_out.shape[0]
    rows = tokens[0]
    count = rows.shape[0]
    places = lax.axis_size("dp")
    groups = places // SPAN
    tower = lax.axis_index("tower")
    place = lax.axis_index("dp")
    me = place % SPAN
    member_of = doc_ids[0] % DOCS_GRP
    live = pad_mask[0] == 1
    code = jnp.where(live, member_of, member_of + 4).astype(f32)[None, :]
    docs = groups * DOCS_GRP
    cos, sin = angle_tables(SPAN * count)
    tok_all, codes, qa, ka, va, kt = gather(rows, code, cos, sin, w_qkv)
    heads_out, lse, exact = attn_fwd(codes, qa, ka, va)
    norms = jnp.stack([ln1_gain, ln1_bias, ln2_gain, ln2_bias] + [jnp.zeros_like(ln1_gain)] * 4, 0)
    (
        attended, inner, hidden, grad_mlp, grads, grad_branch, grad_attended, grad_h1, gains, scores_all, loss
    ) = block(heads_out, rows, code, targets, norms, w_out, w_gate, w_up, w_down, groups)
    scores = scores_all.reshape(groups, 8, groups, 8)[:, :DOCS_GRP, :, :DOCS_GRP].reshape(docs, docs)
    by_hand = width % (16 * places) == 0
    if by_hand:
        send_a, keep_a, send_b, keep_b, d_heads, gain_sums = weight_grads(
            groups, grad_attended, gains, inner, grads, hidden, grad_mlp, attended, grad_branch
        )
        exchange = lambda v, bit: lax.ppermute(v, "dp", [(i, i ^ bit) for i in range(places)])
        came_a, came_b = exchange(send_a, 1), exchange(send_b, 2)
    else:
        d_heads = tokens_to_heads(grad_attended, 5, "to_heads")
    mixed = attn_bwd(d_heads, exact, lse, qa, ka, va, kt, cos, sin, codes)
    if by_hand:
        one = width // places
        gains_out = lax.dynamic_slice_in_dim(gain_sums[:4], place * one, one, 1)
        pair, token_grad, qkv_parts = finish(
            keep_a, keep_b, came_a, came_b, w_qkv, grad_h1, mixed, tok_all, groups
        )
        gate_out, up_out, down_out, out_out, qkv_out = unfold(pair, qkv_parts, w_gate.shape[1] // width)
    else:
        grad_mixed = heads_to_tokens(mixed, 6, "to_tokens_back")
        qkv_out = spread_sum(tn(rows, grad_mixed.T))
        side = lambda v: lax.psum_scatter(v, "dp", scatter_dimension=0, tiled=True)
        halves = lambda v: lax.all_gather(side(v).astype(bf), "tower", axis=1, tiled=True).astype(f32)
        both = lambda a, b: tn(a[0], b[0]) + tn(a[1], b[1])
        flat = lambda v: v.transpose(0, 2, 1, 3).reshape(2, count, -1)
        out_out = halves(nn(attended[0], grad_branch[0]) + nn(attended[1], grad_branch[1]))
        two = lax.all_gather(side(both(inner, flat(grads))).astype(bf), "tower").astype(f32)
        gate_out, up_out = two[0], two[1]
        down_out = halves(both(flat(hidden), grad_mlp))
        gains_out = spread_sum(gains[:4].T).T
        token_grad = grad_h1 + lax.dot_general(
            grad_mixed, w_qkv, (((0,), (1,)), ((), ())), preferred_element_type=f32
        )
    return (
        scores, loss[0, 0], token_grad[None], qkv_out, out_out, gains_out[0], gains_out[1],
        gate_out, up_out, down_out, gains_out[2], gains_out[3],
    )


def solution(mesh):
    shard = P("dp", None)
    lone = P("dp")
    return jax.shard_map(
        local,
        mesh=mesh,
        in_specs=(P("tower", "dp", None), P("tower", "dp"), P("tower", "dp")) + (P(),) * 10,
        out_specs=(
            P(), P(), P("tower", "dp", None), shard, shard, lone, lone, shard, shard, shard, lone, lone,
        ),
        check_vma=False,
    )
```

```python
import functools

import jax
import jax.numpy as jnp
import numpy as np
from jax import lax
from jax.experimental import pallas as pl
from jax.experimental.pallas import tpu as pltpu
from jax.sharding import PartitionSpec as P

HEADS = 12
HEAD_DIM = 64
SPAN = 4
DOCS_GRP = 3
NH = HEADS // SPAN
HW = NH * HEAD_DIM
UPWARD = 3
VLIM = 62 * 2**20
MESH = pl.DeviceIdType.MESH
f32 = jnp.float32
bf = jnp.bfloat16
precise = lax.Precision.HIGHEST
norm_eps = 1e-05
ANY = pl.BlockSpec(memory_space=pl.ANY)
VM = pl.BlockSpec(memory_space=pltpu.VMEM)


def nn(a, b):
    return lax.dot_general(a, b, (((1,), (0,)), ((), ())), preferred_element_type=f32)


def nt(a, b):
    return lax.dot_general(a, b, (((1,), (1,)), ((), ())), preferred_element_type=f32)


def tn(a, b):
    return lax.dot_general(a, b, (((0,), (0,)), ((), ())), preferred_element_type=f32)


def split3(v):
    one = v.astype(bf).astype(f32)
    rest = v - one
    two = rest.astype(bf).astype(f32)
    return [one, two, rest - two]


def here():
    t = lax.axis_index("tower")
    p = lax.axis_index("dp")
    x = lax.rem(p, 2)
    y = lax.rem(lax.div(p, 2), 2)
    return t, p, x, y, lax.div(p, SPAN)


def plane_peers():
    t, p, x, y, g = here()
    px = p + 1 - 2 * x
    py = p + 2 - 4 * y
    pd = px + 2 - 4 * y
    return (t, px), (t, py), (t, pd)


def greet(peers):
    barrier = pltpu.get_barrier_semaphore()
    for peer in peers:
        pl.semaphore_signal(barrier, inc=1, device_id=peer, device_id_type=MESH)
    pl.semaphore_wait(barrier, len(peers))


def remote(src, dst, send, recv, peer):
    return pltpu.make_async_remote_copy(
        src_ref=src, dst_ref=dst, send_sem=send, recv_sem=recv, device_id=peer, device_id_type=MESH
    )


def dma_sems(n):
    return pltpu.SemaphoreType.DMA((n,))


def comm_params(cid):
    return pltpu.CompilerParams(collective_id=cid, has_side_effects=True, vmem_limit_bytes=VLIM)


def gather_kernel(
    tok_ref, ids_ref, pads_ref, cos_ref, sin_ref, w_ref, out_ref, codes_ref, qa_ref, ka_ref, va_ref, kt_ref,
    toks, code_ref, codes, wraw, wturn, wt, qa, ka, va, kt, send, recv, csend, crecv, wsem, osem,
):
    t, p, x, y, g = here()
    count, width = tok_ref.shape
    half = count // 2
    me = lax.rem(p, SPAN)
    odd = lax.rem(me, 2)
    wide = wraw.shape[2]
    loads = []
    for k in range(3):
        at = pl.multiple_of(k * width + me * HW - odd * HEAD_DIM, 128)
        loads.append(pltpu.make_async_copy(w_ref.at[:, pl.ds(at, wide)], wraw.at[k], wsem.at[k]))
        loads[-1].start()
    code_ref[...] = lax.rem(ids_ref[...], DOCS_GRP).astype(f32) + 4.0 * (1 - pads_ref[...]).astype(f32)
    ex, ey, ed = plane_peers()
    mx, my, md = (lax.rem(q[1], SPAN) for q in (ex, ey, ed))

    def rows(m, h):
        return pl.ds(pl.multiple_of(m * count + h * half, half), half)

    def whole(m):
        return pl.ds(pl.multiple_of(m * count, count), count)

    greet((ex, ey, ed))
    first = []
    for i, (peer, h) in enumerate(((ex, 0), (ey, 1), (ex, 1), (ey, 0))):
        c = remote(tok_ref.at[pl.ds(h * half, half)], toks.at[rows(me, h)], send.at[i], recv.at[i], peer)
        c.start()
        first.append(c)
    small = []
    for i, peer in enumerate((ex, ey, ed)):
        c = remote(code_ref, codes.at[:, whole(me)], csend.at[i], crecv.at[i], peer)
        c.start()
        small.append(c)
    codes[:, whole(me)] = code_ref[...]
    for k in range(3):
        loads[k].wait()
        wturn[...] = wraw[k].T
        wt[k * HW : (k + 1) * HW, :] = wturn[pl.ds(pl.multiple_of(odd * HEAD_DIM, HEAD_DIM), HW), :]

    def project(rows_ref, m, n):
        sl = whole(m)
        mx = nt(wt[...], rows_ref[...])
        cos, sin = cos_ref[:, sl], sin_ref[:, sl]
        cd = codes[:, sl]
        mem = jnp.where(cd >= 4.0, cd - 4.0, cd)
        pad = [jnp.zeros((13, count), f32)]
        hot = jnp.concatenate([jnp.where(mem == float(d), 1.0, 0.0) for d in range(DOCS_GRP)] + pad, 0)
        neg = jnp.concatenate([jnp.where(cd == float(d), 0.0, -1e30) for d in range(DOCS_GRP)] + pad, 0)
        rest = jnp.zeros((48, count), f32)
        one = jnp.concatenate([jnp.ones((1, count), f32), jnp.zeros((63, count), f32)], 0)

        def rope(u):
            a, b = u[:32], u[32:]
            return jnp.concatenate([a * cos - b * sin, b * cos + a * sin], 0)

        for h in range(NH):
            q = rope(mx[h * HEAD_DIM : (h + 1) * HEAD_DIM]).astype(bf).astype(f32) * 0.125
            k = rope(mx[HW + h * HEAD_DIM : HW + (h + 1) * HEAD_DIM])
            v = mx[2 * HW + h * HEAD_DIM : 2 * HW + (h + 1) * HEAD_DIM]
            qa[h, :, sl] = jnp.concatenate([q, hot, rest], 0).astype(bf)
            ka[h, sl, :] = jnp.concatenate([k, neg, rest], 0).T.astype(bf)
            va[h, :, sl] = jnp.concatenate([v, one], 0).astype(bf)
            kt[h, :, sl] = k.astype(bf)
        puts = (
            (rows_ref, out_ref.at[sl]),
            (qa.at[:, :, sl], qa_ref.at[:, :, sl]),
            (ka.at[:, sl, :], ka_ref.at[:, sl, :]),
            (va.at[:, :, sl], va_ref.at[:, :, sl]),
            (kt.at[:, :, sl], kt_ref.at[:, :, sl]),
        )
        puts = [pltpu.make_async_copy(a, b, osem.at[5 * n + i]) for i, (a, b) in enumerate(puts)]
        for c in puts:
            c.start()
        return puts

    done = project(tok_ref, me, 0)
    first[0].wait_recv()
    f0 = remote(toks.at[rows(mx, 0)], toks.at[rows(mx, 0)], send.at[4], recv.at[4], ey)
    f0.start()
    first[1].wait_recv()
    f1 = remote(toks.at[rows(my, 1)], toks.at[rows(my, 1)], send.at[5], recv.at[5], ex)
    f1.start()
    for c in small:
        c.wait()
    first[2].wait_recv()
    done += project(toks.at[whole(mx)], mx, 1)
    first[3].wait_recv()
    done += project(toks.at[whole(my)], my, 2)
    f0.wait_recv()
    f1.wait_recv()
    done += project(toks.at[whole(md)], md, 3)
    codes_ref[...] = codes[...]
    for c in first + [f0, f1]:
        c.wait_send()
    for c in done:
        c.wait()


def gather(tok, ids, pads, cos, sin, w_qkv):
    count, width = tok.shape
    total = SPAN * count
    shapes = ((NH, 128, total), (NH, total, 128), (NH, 128, total), (NH, HEAD_DIM, total))
    return pl.pallas_call(
        gather_kernel,
        out_shape=(jax.ShapeDtypeStruct((total, width), bf), jax.ShapeDtypeStruct((1, total), f32))
        + tuple(jax.ShapeDtypeStruct(s, bf) for s in shapes),
        in_specs=[VM] * 5 + [ANY],
        out_specs=(ANY, VM) + (ANY,) * 4,
        scratch_shapes=[
            pltpu.VMEM((total, width), bf), pltpu.VMEM((1, count), f32), pltpu.VMEM((1, total), f32), pltpu.VMEM((3, width, 256), bf),
            pltpu.VMEM((256, width), bf), pltpu.VMEM((3 * HW, width), bf),
        ]
        + [pltpu.VMEM(s, bf) for s in shapes]
        + [dma_sems(6), dma_sems(6), dma_sems(3), dma_sems(3), dma_sems(3), dma_sems(20)],
        compiler_params=comm_params(0),
        name="gather",
    )(tok, ids, pads, cos, sin, w_qkv)


def heads_to_tokens_kernel(parts, in_ref, out_ref, send, recv, lsem):
    t, p, x, y, g = here()
    count = out_ref.shape[1]
    me = lax.rem(p, SPAN)
    peers = plane_peers()
    width = parts and out_ref.shape[0] // parts
    greet(peers)
    copies = []
    for i, peer in enumerate((peers[2], peers[0], peers[1])):
        m = lax.rem(peer[1], SPAN)
        for k in range(parts):
            c = remote(
                in_ref.at[pl.ds(k * HW, HW), pl.ds(pl.multiple_of(m * count, count), count)],
                out_ref.at[pl.ds(pl.multiple_of(k * width + me * HW, HW), HW)],
                send.at[i * parts + k],
                recv.at[i * parts + k],
                peer,
            )
            c.start()
            copies.append(c)
    for k in range(parts):
        c = pltpu.make_async_copy(
            in_ref.at[pl.ds(k * HW, HW), pl.ds(pl.multiple_of(me * count, count), count)],
            out_ref.at[pl.ds(pl.multiple_of(k * width + me * HW, HW), HW)],
            lsem.at[k],
        )
        c.start()
        copies.append(c)
    for c in copies:
        c.wait()


def heads_to_tokens(a, cid, name):
    parts = a.shape[0] // HW
    count = a.shape[1] // SPAN
    return pl.pallas_call(
        functools.partial(heads_to_tokens_kernel, parts),
        out_shape=jax.ShapeDtypeStruct((parts * HEADS * HEAD_DIM, count), a.dtype),
        in_specs=[VM],
        out_specs=ANY,
        scratch_shapes=[dma_sems(3 * parts), dma_sems(3 * parts), dma_sems(parts)],
        compiler_params=comm_params(cid),
        name=name,
    )(a)


def tokens_to_heads_kernel(in_ref, out_ref, send, recv, lsem):
    t, p, x, y, g = here()
    count = in_ref.shape[1]
    me = lax.rem(p, SPAN)
    peers = plane_peers()
    greet(peers)
    mine = pl.ds(pl.multiple_of(me * count, count), count)
    copies = []
    for i, peer in enumerate((peers[2], peers[0], peers[1])):
        m = lax.rem(peer[1], SPAN)
        c = remote(
            in_ref.at[pl.ds(pl.multiple_of(m * HW, HW), HW)],
            out_ref.at[:, mine],
            send.at[i],
            recv.at[i],
            peer,
        )
        c.start()
        copies.append(c)
    c = pltpu.make_async_copy(
        in_ref.at[pl.ds(pl.multiple_of(me * HW, HW), HW)], out_ref.at[:, mine], lsem.at[0]
    )
    c.start()
    for c in copies + [c]:
        c.wait()


def tokens_to_heads(a, cid, name):
    return pl.pallas_call(
        tokens_to_heads_kernel,
        out_shape=jax.ShapeDtypeStruct((HW, SPAN * a.shape[1]), a.dtype),
        in_specs=[VM],
        out_specs=ANY,
        scratch_shapes=[dma_sems(3), dma_sems(3), dma_sems(1)],
        compiler_params=comm_params(cid),
        name=name,
    )(a)


def doc_limits(code):
    pad = code >= 4.0
    mem = jnp.where(pad, code - 4.0, code)
    n0 = jnp.sum(jnp.where(mem < 0.5, 1.0, 0.0)).astype(jnp.int32)
    n1 = jnp.sum(jnp.where(mem < 1.5, 1.0, 0.0)).astype(jnp.int32)
    l = [jnp.sum(jnp.where(code == float(d), 1.0, 0.0)).astype(jnp.int32) for d in range(3)]
    return n0, n1, l

def block_range(lims, a, size, total):
    n0, n1, l = lims
    b = a + size - 1
    first = (a >= n0).astype(jnp.int32) + (a >= n1).astype(jnp.int32)
    last = (b >= n0).astype(jnp.int32) + (b >= n1).astype(jnp.int32)
    lo = jnp.where(first == 0, 0, jnp.where(first == 1, n0, n1))
    hi = jnp.where(last == 0, n0, jnp.where(last == 1, n1, total))
    dead = jnp.zeros((), jnp.bool_)
    for d in range(3):
        dead = dead | ((first <= d) & (d <= last) & (l[d] == 0))
    return jnp.where(dead, 0, lo), jnp.where(dead, total, hi)

def fwd_kernel(KB, QB, code_ref, qa_ref, ka_ref, va_ref, out_ref, lse_ref, o32_ref, acc_ref, even_ref, odd_ref):
    T = code_ref.shape[1]
    blocks = T // KB
    lims = doc_limits(code_ref[...])

    def keys(j):
        return pl.ds(pl.multiple_of(j * KB, KB), KB)

    def qblock(i, _):
        a = i * QB
        qs = pl.ds(pl.multiple_of(a, QB), QB)
        lo, hi = block_range(lims, a, QB, T)
        jlo = lo // KB
        pairs = ((hi + KB - 1) // KB - jlo + 1) // 2
        jlo = jnp.minimum(jlo, blocks - 2 * pairs)

        def scores(j, h, ref):
            ref[h] = nn(ka_ref[h, keys(j), :], qa_ref[h, :, qs])

        def absorb(j, h, ref, m):
            s = ref[h]
            mn = jnp.maximum(m, jnp.max(s, 0, keepdims=True))
            p = jnp.exp(s - mn).astype(bf)
            acc_ref[h] = acc_ref[h] * jnp.exp(m - mn) + nn(va_ref[h, :80, keys(j)], p)
            return mn

        for h in range(NH):
            acc_ref[h] = jnp.zeros_like(acc_ref[h])
            scores(jlo, h, even_ref)

        def kv(n, ms):
            j = jlo + 2 * n
            ms = list(ms)
            for h in range(NH):
                scores(j + 1, h, odd_ref)
                ms[h] = absorb(j, h, even_ref, ms[h])
            after = jnp.minimum(j + 2, blocks - 1)
            for h in range(NH):
                scores(after, h, even_ref)
                ms[h] = absorb(j + 1, h, odd_ref, ms[h])
            return tuple(ms)

        ms = lax.fori_loop(0, pairs, kv, tuple(jnp.full((1, QB), -3e38, f32) for _ in range(NH)))
        for h in range(NH):
            tot = acc_ref[h, 64:65, :]
            o = acc_ref[h, :64, :] / tot
            o32_ref[h * HEAD_DIM : (h + 1) * HEAD_DIM, qs] = o
            lse_ref[h : h + 1, qs] = jnp.where(ms[h] < -1e29, 0.0, ms[h] + jnp.log(tot))
            out_ref[h * HEAD_DIM : (h + 1) * HEAD_DIM, qs] = o.astype(bf)
        return 0

    lax.fori_loop(0, T // QB, qblock, 0)


def attn_fwd(code, qa, ka, va, KB=256, QB=512):
    T = code.shape[1]
    sds = jax.ShapeDtypeStruct
    return pl.pallas_call(
        functools.partial(fwd_kernel, KB, QB),
        out_shape=(sds((HW, T), bf), sds((NH, T), f32), sds((HW, T), f32)),
        in_specs=[VM] * 4,
        out_specs=(VM,) * 3,
        scratch_shapes=[pltpu.VMEM((NH, 80, QB), f32)] + [pltpu.VMEM((NH, KB, QB), f32)] * 2,
        compiler_params=pltpu.CompilerParams(vmem_limit_bytes=VLIM),
        name="attn_fwd",
    )(code, qa, ka, va)


def bwd_kernel(KB, QB, do_ref, o32_ref, lse_ref, qa_ref, ka_ref, va_ref, kt_ref, cos_ref, sin_ref, code_ref, g_ref,
               vn_ref, dn_ref, da_ref, qb_ref, acc_ref, dq_ref):
    T = do_ref.shape[1]
    hw = HW
    CH = 512
    lims = doc_limits(code_ref[...])
    def prep(c, _):
        sl = pl.ds(pl.multiple_of(c*CH, CH), CH)
        for h in range(NH):
            do = do_ref[h*HEAD_DIM:(h+1)*HEAD_DIM, sl].astype(f32)
            delta = jnp.sum(do*o32_ref[h*HEAD_DIM:(h+1)*HEAD_DIM, sl], 0, keepdims=True)
            def split(x):
                x1 = x.astype(bf).astype(f32); r = x-x1
                x2 = r.astype(bf).astype(f32); x3 = r-x2
                return [x1, x2, x3]
            z13 = jnp.zeros((13, CH), f32); z48 = jnp.zeros((48, CH), f32)
            da_ref[h, :, sl] = jnp.concatenate([do]+split(-delta)+[z13, z48], 0).astype(bf)
            one = jnp.concatenate([jnp.ones((3, CH), f32), jnp.zeros((61, CH), f32)], 0)
            v = va_ref[h, :64, sl].astype(f32)
            vn_ref[h, sl, :] = jnp.concatenate([v, one], 0).T.astype(bf)
            z64 = jnp.zeros((64, CH), f32)
            q = qa_ref[h, :64, sl].astype(f32)
            dn_ref[h, sl, :] = jnp.concatenate([do, z64], 0).T.astype(bf)
            qb_ref[h, sl, :] = jnp.concatenate([z64, q], 0).T.astype(bf)
            acc_ref[h, sl, :] = jnp.zeros((CH, 128), f32)
        return 0
    lax.fori_loop(0, T//CH, prep, 0)
    def qblock(i, _):
        a = i*QB
        qs = pl.ds(pl.multiple_of(a, QB), QB)
        lo, hi = block_range(lims, a, QB, T)
        jlo = lo//KB; jhi = (hi+KB-1)//KB
        dq_ref[...] = jnp.zeros_like(dq_ref)
        def kv(j, _):
            ks = pl.ds(pl.multiple_of(j*KB, KB), KB)
            for h in range(NH):
                s = nn(ka_ref[h, ks, :], qa_ref[h, :, qs])
                dp = nn(vn_ref[h, ks, :], da_ref[h, :, qs])
                p = jnp.exp(s - lse_ref[h:h+1, qs])
                ds = (p*dp).astype(bf)
                acc_ref[h, ks, :] += nn(p.astype(bf), dn_ref[h, qs, :]) + nn(ds, qb_ref[h, qs, :])
                dq_ref[h] += nn(kt_ref[h, :, ks], ds)
            return 0
        lax.fori_loop(jlo, jhi, kv, 0)
        cos = cos_ref[:, qs]; sin = sin_ref[:, qs]
        for h in range(NH):
            u = dq_ref[h]*0.125
            x1 = u[:32]; x2 = u[32:]
            g_ref[h*HEAD_DIM:(h+1)*HEAD_DIM, qs] = jnp.concatenate([x1*cos+x2*sin, x2*cos-x1*sin], 0).astype(bf)
        return 0
    lax.fori_loop(0, T//QB, qblock, 0)
    def fin(c, _):
        sl = pl.ds(pl.multiple_of(c*CH, CH), CH)
        cos = cos_ref[:, sl]; sin = sin_ref[:, sl]
        for h in range(NH):
            t = acc_ref[h, sl, :].T
            x1 = t[64:96]; x2 = t[96:128]
            g_ref[hw+h*HEAD_DIM:hw+(h+1)*HEAD_DIM, sl] = jnp.concatenate([x1*cos+x2*sin, x2*cos-x1*sin], 0).astype(bf)
            g_ref[2*hw+h*HEAD_DIM:2*hw+(h+1)*HEAD_DIM, sl] = t[:64].astype(bf)
        return 0
    lax.fori_loop(0, T//CH, fin, 0)

def attn_bwd(do, o32, lse, qa, ka, va, kt, cos, sin, code, KB=512, QB=256):
    T = do.shape[1]
    return pl.pallas_call(functools.partial(bwd_kernel, KB, QB),
        out_shape=jax.ShapeDtypeStruct((3*NH*HEAD_DIM, T), bf),
        in_specs=[pl.BlockSpec(memory_space=pltpu.VMEM)]*10, out_specs=pl.BlockSpec(memory_space=pltpu.VMEM),
        scratch_shapes=[pltpu.VMEM((NH,T,128), bf), pltpu.VMEM((NH,T,128), bf), pltpu.VMEM((NH,128,T), bf), pltpu.VMEM((NH,T,128), bf),
                        pltpu.VMEM((NH,T,128), f32), pltpu.VMEM((NH,HEAD_DIM,QB), f32)],
        compiler_params=pltpu.CompilerParams(vmem_limit_bytes=VLIM), name="attn_bwd",
        cost_estimate=pl.CostEstimate(flops=int(10*T*T*128*3), bytes_accessed=12<<20, transcendentals=T*T*3))(do, o32, lse, qa, ka, va, kt, cos, sin, code)


def contrast_part(groups, sums, goals_ref, plane, allp, ge, send, recv, scores_ref, loss_ref):
    t, p, x, y, g = here()
    docs = groups * DOCS_GRP
    size = groups * 8
    peers = plane_peers()
    line = [(t, lax.rem(p + SPAN * k, SPAN * groups)) for k in range(1, groups)]
    plane[3] = sums
    copies = [remote(plane.at[3], plane.at[i], send.at[i], recv.at[i], q) for i, q in enumerate(peers)]
    for c in copies:
        c.start()
    col = lax.broadcasted_iota(jnp.int32, (size, size), 1)
    row = lax.broadcasted_iota(jnp.int32, (size, size), 0)

    def mark(i, hot):
        goal = goals_ref[i]
        at = (row == i // DOCS_GRP * 8 + i % DOCS_GRP) & (col == goal // DOCS_GRP * 8 + goal % DOCS_GRP)
        return hot + jnp.where(at, 1.0, 0.0)

    hot = lax.fori_loop(0, docs, mark, jnp.zeros((size, size), f32))
    for c in copies:
        c.wait()
    own = (plane[3] + plane[0]) + (plane[1] + plane[2])
    allp[t, g] = own
    rows = allp.at[t, g]
    copies = [remote(rows, rows, send.at[3 + i], recv.at[3 + i], q) for i, q in enumerate(line)]
    for c in copies:
        c.start()
    for c in copies:
        c.wait()
    c = remote(allp.at[t], allp.at[t], send.at[2 + groups], recv.at[2 + groups], (1 - t, p))
    c.start()
    c.wait()
    width = allp.shape[3]
    pools = [allp[k].reshape(size, width) for k in range(2)]
    embeds = [v * lax.rsqrt(jnp.sum(v * v, -1, keepdims=True) + 1e-06) for v in pools]
    dot = functools.partial(lax.dot_general, precision=precise, preferred_element_type=f32)
    scores = dot(embeds[0], embeds[1], (((1,), (1,)), ((), ()))) * 50.0
    live = lax.rem(col, 8) < DOCS_GRP
    alive = lax.rem(row, 8) < DOCS_GRP
    masked = jnp.where(live, scores, -1e30)
    top = jnp.max(masked, -1, keepdims=True)
    total = jnp.sum(jnp.exp(masked - top), -1, keepdims=True)
    log_sums = top + jnp.log(total)
    chosen = jnp.sum(hot * scores, -1, keepdims=True)
    each = jnp.where(alive[:, 0:1], log_sums - chosen, 0.0)
    loss_ref[...] = jnp.broadcast_to(jnp.sum(each, 0, keepdims=True) / docs, loss_ref.shape)
    scores_ref[...] = scores
    gs = jnp.where(alive & live, (jnp.exp(masked - log_sums) - hot) / docs, 0.0)
    gq = dot(gs, embeds[1], (((1,), (0,)), ((), ())))
    gd = dot(gs, embeds[0], (((0,), (0,)), ((), ())))
    ge[...] = jnp.where(t == 0, gq, gd) * 50.0
    mine = ge[pl.ds(pl.multiple_of(g * 8, 8), 8), :]
    pooled = allp[t, g]
    inv = lax.rsqrt(jnp.sum(pooled * pooled, -1, keepdims=True) + 1e-06)
    return inv * mine - inv * inv * inv * pooled * jnp.sum(pooled * mine, -1, keepdims=True)


def block_kernel(
    groups, heads_ref, rows_ref, codes_ref, goals_ref, gain1_ref, bias1_ref, gain2_ref, bias2_ref, wo_h, wg_h, wu_h, wd_h,
    att_o, inner_o, hid_o, gm_o, gg_o, gb_o, ga_o, gh1_o, gains_o, scores_o, loss_o,
    att, wo, wg, wu, wd, inner, x1, s1, acc, hid, ab, x2, s2, sec, gm, gm2, gb, gb2, plane, allp, ge,
    wsem, send, recv, lsem, tsend, trecv, osem, csend, crecv,
):
    t, p, x, y, g = here()
    peers = plane_peers()
    sibling = (1 - t, p)
    line = tuple((t, lax.rem(p + SPAN * k, SPAN * groups)) for k in range(1, groups))
    count, width = rows_ref.shape
    half = width // 2
    tiles = wg.shape[0]
    me = lax.rem(p, SPAN)

    def weight(j, k):
        cols = pl.ds(j * width, width)
        src, dst = ((wg_h.at[:, cols], wg.at[j]), (wu_h.at[:, cols], wu.at[j]), (wd_h.at[cols], wd.at[j]))[k]
        return pltpu.make_async_copy(src, dst, wsem.at[1 + 3 * j + k])

    first_load = pltpu.make_async_copy(wo_h, wo, wsem.at[0])
    first_load.start()
    for j in range(tiles):
        for k in range(3):
            weight(j, k).start()
    greet(peers + (sibling,) + line)
    moves = []
    for i, peer in enumerate((peers[2], peers[0], peers[1])):
        m = lax.rem(peer[1], SPAN)
        moves.append(remote(
            heads_ref.at[:, pl.ds(pl.multiple_of(m * count, count), count)],
            att.at[pl.ds(pl.multiple_of(me * HW, HW), HW)], send.at[i], recv.at[i], peer,
        ))
    moves.append(pltpu.make_async_copy(
        heads_ref.at[:, pl.ds(pl.multiple_of(me * count, count), count)],
        att.at[pl.ds(pl.multiple_of(me * HW, HW), HW)], lsem.at[0],
    ))
    for c in moves:
        c.start()
    code = codes_ref[:, pl.ds(pl.multiple_of(me * count, count), count)]
    zero = jnp.zeros((8 - DOCS_GRP, count), f32)
    mem = jnp.concatenate([jnp.where(code == float(d), 1.0, 0.0) for d in range(DOCS_GRP)] + [zero], 0)
    mem = jnp.concatenate([mem, mem, mem, jnp.zeros((8, count), f32)], 0).astype(bf)
    first_load.wait()
    for c in moves:
        c.wait()

    def pair(i, mine, its, out):
        return (
            pltpu.make_async_copy(mine, out.at[0], osem.at[i]),
            remote(its, out.at[1], tsend.at[i], trecv.at[i], sibling),
        )

    def both(i, mine, its, out):
        for c in pair(i, mine, its, out):
            c.start()

    both(0, att, att, att_o)
    acc[...] = tn(att[...], wo[...])
    step = 64
    gain1, bias1, gain2, bias2 = (r[...].reshape(1, width) for r in (gain1_ref, bias1_ref, gain2_ref, bias2_ref))

    def chunk(i):
        return pl.ds(pl.multiple_of(i * step, step), step)

    def norm(h, sl, xs, ss):
        c = h - jnp.mean(h, -1, keepdims=True)
        s = lax.rsqrt(jnp.mean(c * c, -1, keepdims=True) + norm_eps)
        xh = c * s
        xs[sl, :] = xh
        ss[sl, :] = s
        return xh

    def norm_one(i, _):
        sl = chunk(i)
        xh = norm(rows_ref[sl, :].astype(f32) + acc[sl, :], sl, x1, s1)
        v = xh * gain1 + bias1
        inner[sl, :] = v.astype(bf)
        acc[sl, :] = v
        return 0

    lax.fori_loop(0, count // step, norm_one, 0)
    both(1, inner, inner, inner_o)

    def tile_of(j, i, mine, its, out):
        return (
            pltpu.make_async_copy(mine, out.at[0, j], osem.at[i + j]),
            remote(its, out.at[1, j], tsend.at[i + j], trecv.at[i + j], sibling),
        )

    for j in range(tiles):
        for k in range(3):
            weight(j, k).wait()
        gate = nn(inner[...], wg[j])
        upper = nn(inner[...], wu[j])
        sig = jax.nn.sigmoid(gate)
        silu = gate * sig
        hid[j] = (silu * upper).astype(bf)
        ab[0, j] = (upper * (sig * (1.0 + gate * (1.0 - sig)))).astype(bf)
        ab[1, j] = silu.astype(bf)
        for c in tile_of(j, 2, hid.at[j], hid.at[j], hid_o):
            c.start()
        acc[...] += nn(hid[j], wd[j])

    def norm_two(i, _):
        sl = chunk(i)
        v = norm(acc[sl, :], sl, x2, s2) * gain2 + bias2
        for k, part in enumerate(split3(v)):
            sec[k, sl, :] = part.astype(bf)
        return 0

    lax.fori_loop(0, count // step, norm_two, 0)
    sums = (nn(mem[:16], sec[0]) + nn(mem[:16], sec[1]) + nn(mem[:16], sec[2]))[:8]
    top = lax.broadcasted_iota(jnp.int32, sums.shape, 0) < DOCS_GRP
    sums = jnp.where(top, sums, 0.0)
    gp = contrast_part(groups, sums, goals_ref, plane, allp, ge, csend, crecv, scores_o, loss_o)
    gp3 = jnp.concatenate(split3(gp) + [jnp.zeros_like(gp)], 0).astype(bf)
    acc[...] = tn(mem, gp3)

    def fold(v):
        return jnp.sum(v.reshape(step // 8, 8, width), 0)

    def norm_back(gr, xh, s, gain):
        e = gr * gain
        v = e - jnp.mean(e, -1, keepdims=True) - xh * jnp.mean(e * xh, -1, keepdims=True)
        return v * s

    zeros = jnp.zeros((8, width), f32)

    def back_two(i, sums):
        sl = chunk(i)
        gr, xh = acc[sl, :], x2[sl, :]
        v = norm_back(gr, xh, s2[sl, :], gain2)
        acc[sl, :] = v
        low = v.astype(bf)
        gm[sl, :] = low
        gm2[0, sl, :] = low[:, :half]
        gm2[1, sl, :] = low[:, half:]
        return sums[0] + fold(gr * xh), sums[1] + fold(gr)

    g2, b2 = lax.fori_loop(0, count // step, back_two, (zeros, zeros))
    both(2 + 2 * tiles, gm2.at[t], gm2.at[1 - t], gm_o)
    for j in range(tiles):
        gh = nt(gm[...], wd[j])
        gg = (gh * ab[0, j].astype(f32)).astype(bf)
        gu = (gh * ab[1, j].astype(f32)).astype(bf)
        ab[0, j] = gg
        ab[1, j] = gu
        for c in tile_of(j, 2 + tiles, ab.at[t, j], ab.at[1 - t, j], gg_o):
            c.start()
        acc[...] += nt(gg, wg[j]) + nt(gu, wu[j])

    def back_one(i, sums):
        sl = chunk(i)
        gr, xh = acc[sl, :], x1[sl, :]
        v = norm_back(gr, xh, s1[sl, :], gain1)
        gh1_o[sl, :] = v
        low = v.astype(bf)
        gb[sl, :] = low
        gb2[0, sl, :] = low[:, :half]
        gb2[1, sl, :] = low[:, half:]
        return sums[0] + fold(gr * xh), sums[1] + fold(gr)

    g1, b1 = lax.fori_loop(0, count // step, back_one, (zeros, zeros))
    both(3 + 2 * tiles, gb2.at[t], gb2.at[1 - t], gb_o)
    flat = [jnp.sum(v, 0, keepdims=True) for v in (g1, b1, g2, b2)]
    gains_o[...] = jnp.concatenate(flat + [jnp.zeros((4, width), f32)], 0)
    ga_o[...] = nt(wo[...], gb[...]).astype(bf)
    done = [pair(0, att, att, att_o), pair(1, inner, inner, inner_o)]
    for j in range(tiles):
        done.append(tile_of(j, 2, hid.at[j], hid.at[j], hid_o))
        done.append(tile_of(j, 2 + tiles, ab.at[t, j], ab.at[1 - t, j], gg_o))
    done.append(pair(2 + 2 * tiles, gm2.at[t], gm2.at[1 - t], gm_o))
    done.append(pair(3 + 2 * tiles, gb2.at[t], gb2.at[1 - t], gb_o))
    for c in done:
        for d in c:
            d.wait()


def block(heads, rows, codes, goals, norms, w_out, w_gate, w_up, w_down, groups):
    count, width = rows.shape
    tiles = w_gate.shape[1] // width
    half = width // 2
    size = groups * 8
    sds = jax.ShapeDtypeStruct
    vm = lambda *n: pltpu.VMEM(n, bf)
    vf = lambda *n: pltpu.VMEM(n, f32)
    return pl.pallas_call(
        functools.partial(block_kernel, groups),
        out_shape=(
            sds((2, width, count), bf), sds((2, count, width), bf), sds((2, tiles, count, width), bf),
            sds((2, count, half), bf), sds((2, tiles, count, width), bf), sds((2, count, half), bf),
            sds((width, count), bf), sds((count, width), f32), sds((8, width), f32),
            sds((size, size), f32), sds((8, 128), f32),
        ),
        in_specs=[VM, VM, VM, pl.BlockSpec(memory_space=pltpu.SMEM)] + [VM] * 4 + [ANY] * 4,
        out_specs=(ANY,) * 6 + (VM,) * 5,
        scratch_shapes=[
            vm(width, count), vm(width, width), vm(tiles, width, width), vm(tiles, width, width),
            vm(tiles, width, width), vm(count, width), vf(count, width), vf(count, 1), vf(count, width),
            vm(tiles, count, width), vm(2, tiles, count, width), vf(count, width), vf(count, 1),
            vm(3, count, width), vm(count, width), vm(2, count, half), vm(count, width), vm(2, count, half),
            vf(4, 8, width), vf(2, groups, 8, width), vf(size, width),
            dma_sems(1 + 3 * tiles), dma_sems(3), dma_sems(3), dma_sems(1),
            dma_sems(4 + 2 * tiles), dma_sems(4 + 2 * tiles), dma_sems(4 + 2 * tiles),
            dma_sems(3 + groups), dma_sems(3 + groups),
        ],
        compiler_params=comm_params(1),
        name="block",
    )(heads, rows, codes, goals, *norms, w_out, w_gate, w_up, w_down)


def weights_kernel(
    groups, i_ref, g_ref, h_ref, m_ref, a_ref, b_ref, in_ref, gain_ref,
    sa_ref, ka_ref, sb_ref, kb_ref, sc_ref, kc_ref, heads_ref, sum_ref,
    iv, it, gv, hv, mv, av, bv, gs, ds, os, plane, line, isem, osem, send, recv, lsem, nsend, nrecv,
):
    t, p, x, y, g = here()
    level = lax.rem(g, 2)
    peers = plane_peers()
    sibling = (1 - t, p)
    others = tuple((t, lax.rem(p + SPAN * k, SPAN * groups)) for k in range(1, groups))
    greet(peers + (sibling,) + others)
    around = [remote(gain_ref, plane.at[i], nsend.at[i], nrecv.at[i], q) for i, q in enumerate(peers)]
    for c in around:
        c.start()
    tokens = in_ref.shape[1]
    me = lax.rem(p, SPAN)
    mine = pl.ds(pl.multiple_of(me * tokens, tokens), tokens)
    moves = []
    for i, peer in enumerate((peers[2], peers[0], peers[1])):
        m = lax.rem(peer[1], SPAN)
        moves.append(remote(
            in_ref.at[pl.ds(pl.multiple_of(m * HW, HW), HW)], heads_ref.at[:, mine],
            send.at[i], recv.at[i], peer,
        ))
    moves.append(pltpu.make_async_copy(
        in_ref.at[pl.ds(pl.multiple_of(me * HW, HW), HW)], heads_ref.at[:, mine], lsem.at[0]
    ))
    for c in moves:
        c.start()
    count, width = i_ref.shape[1:]
    half = width // 2
    tiles = gv.shape[1]
    shards = SPAN * groups
    one = width // shards
    down = ds.shape[1]

    def load(i, src, dst):
        return pltpu.make_async_copy(src, dst, isem.at[i])

    def tile(ref, j, buf, base):
        return load(base + j, ref.at[:, j], buf.at[:, j])

    few = [load(i, a, b) for i, (a, b) in enumerate(((m_ref, mv), (a_ref, av), (b_ref, bv), (i_ref, iv)))]
    few[0].start()
    for j in range(tiles):
        tile(h_ref, j, hv, 4).start()
    for c in few[1:]:
        c.start()
    for j in range(tiles):
        tile(g_ref, j, gv, 4 + tiles).start()
    few[0].wait()

    def downward(j, _):
        tile(h_ref, j, hv, 4).wait()
        r = tn(hv[0, j], mv[0]) + tn(hv[1, j], mv[1])
        ds[pl.ds(j * (width // down), width // down)] = r.astype(bf).reshape(width // down, down, half)
        return 0

    lax.fori_loop(0, tiles, downward, 0)
    for c in few[1:] + around:
        c.wait()
    line[0] = (gain_ref[...] + plane[0]) + (plane[1] + plane[2])
    ring = [
        remote(line.at[0], line.at[1 + k], nsend.at[3 + k], nrecv.at[3 + k], q) for k, q in enumerate(others)
    ]
    for c in ring:
        c.start()
    r = nn(av[0], bv[0]) + nn(av[1], bv[1])
    os[...] = r.astype(bf).reshape(shards, one, half)
    for i in range(2):
        it[:, i * count : (i + 1) * count] = iv[i].T
    fours = lambda ref, n: ref.reshape(groups, 2, 2, n, half)

    def put(i, src, dst):
        return pltpu.make_async_copy(src, dst, osem.at[i])

    outs = []
    for i, (ref, k) in enumerate(((sb_ref, 1 - y), (kb_ref, y))):
        outs.append(put(4 * i, fours(ds, down).at[:, k], ref.at[:, :, pl.ds(0, down)]))
        outs.append(put(4 * i + 1, fours(os, one).at[:, k], ref.at[:, :, pl.ds(down, one)]))
    for c in outs:
        c.start()

    sideways = sa_ref.shape[2] // one

    def top(j):
        if j < sideways:
            rows = pl.ds(j * one, one)
            piece = fours(gs.at[j], one)
            went, kept = (piece.at[:, :, 1 - x], sa_ref), (piece.at[:, :, x], ka_ref)
        else:
            rows = pl.ds((j - sideways) * one, one)
            piece = gs.at[j].reshape(groups // 2, 2, SPAN, one, half)
            went, kept = (piece.at[:, 1 - level], sc_ref), (piece.at[:, level], kc_ref)
        return (
            put(8 + j, went[0], went[1].at[:, :, rows]),
            put(8 + 2 * tiles + j, kept[0], kept[1].at[:, :, rows]),
        )

    for j in range(tiles):
        tile(g_ref, j, gv, 4 + tiles).wait()
        r = (nn(it[:, :count], gv[0, j]) + nn(it[:, count:], gv[1, j])).astype(bf)
        for h in range(2):
            k = 2 * j + h
            gs[k] = r[:, h * half : (h + 1) * half].reshape(shards, one, half)
            outs.extend(top(k))
            for c in outs[-2:]:
                c.start()
    for c in ring:
        c.wait()
    total = line[0]
    for k in range(1, groups):
        total = total + line[k]
    line[groups] = total
    last = remote(line.at[groups], line.at[groups + 1], nsend.at[2 + groups], nrecv.at[2 + groups], sibling)
    last.start()
    last.wait()
    sum_ref[...] = line[groups] + line[groups + 1]
    for c in outs + moves:
        c.wait()


def weight_grads(groups, grad_heads, gains, inner, grads, hidden, grad_mlp, attended, grad_branch):
    count, width = inner.shape[1:]
    half = width // 2
    shards = SPAN * groups
    one = width // shards
    tiles = grads.shape[1]
    down = tiles * one
    ra = (2 * tiles - UPWARD) * one
    rb = down + one
    part = lambda r: jax.ShapeDtypeStruct((groups, 2, r, half), bf)
    level = jax.ShapeDtypeStruct((groups // 2, SPAN, UPWARD * one, half), bf)
    vm = lambda *n: pltpu.VMEM(n, bf)
    return pl.pallas_call(
        functools.partial(weights_kernel, groups),
        out_shape=(
            part(ra), part(ra), part(rb), part(rb), level, level,
            jax.ShapeDtypeStruct((HW, SPAN * grad_heads.shape[1]), bf), jax.ShapeDtypeStruct(gains.shape, f32),
        ),
        in_specs=[ANY] * 6 + [VM] * 2,
        out_specs=(ANY,) * 7 + (VM,),
        scratch_shapes=[
            vm(2, count, width), vm(width, 2 * count), vm(2, tiles, count, width), vm(2, tiles, count, width),
            vm(2, count, half), vm(2, width, count), vm(2, count, half),
            vm(2 * tiles, shards, one, half), vm(shards, down, half), vm(shards, one, half),
            pltpu.VMEM((3,) + gains.shape, f32), pltpu.VMEM((groups + 2,) + gains.shape, f32),
            dma_sems(4 + 2 * tiles), dma_sems(8 + 4 * tiles), dma_sems(3), dma_sems(3), dma_sems(1),
            dma_sems(3 + groups), dma_sems(3 + groups),
        ],
        compiler_params=comm_params(2),
        name="weight_grads",
        cost_estimate=pl.CostEstimate(
            flops=int(2 * 2 * count * half * width * 8.5), bytes_accessed=30 << 20, transcendentals=0
        ),
    )(inner, grads, hidden, grad_mlp, attended, grad_branch, grad_heads, gains)


def add_rows(dst, a, b, rows):
    step = rows // 3 if rows % 48 == 0 and rows > 48 else rows

    def part(i, _):
        sl = pl.ds(pl.multiple_of(i * step, step), step)
        dst[sl, :] = a[sl, :] + b[sl, :]
        return 0

    lax.fori_loop(0, rows // step, part, 0)


class Line:
    def __init__(self, z, zt, groups, part, up, down, sems, t, p):
        self.z, self.zt, self.groups = z, zt, groups
        self.part, self.up, self.down = part, up, down
        us, ur, ds, dr = sems
        above = (t, lax.rem(p + SPAN, SPAN * groups))
        below = (t, lax.rem(p + SPAN * (groups - 1), SPAN * groups))
        self.up_first = lambda: remote(part, up, us, ur, above)
        self.up_next = lambda: remote(up, up, us, ur, above)
        self.down_first = lambda: remote(part, down, ds, dr, below)
        self.down_next = lambda: remote(down, down, ds, dr, below)

    def start(self):
        if self.zt > 0:
            pl.when(self.z == 0)(lambda: self.up_first().start())
        if self.zt < self.groups - 1:
            pl.when(self.z == self.groups - 1)(lambda: self.down_first().start())

    def relay(self, hop, rows):
        def up():
            self.up_next().wait_recv()
            add_rows(self.up, self.up, self.part, rows)
            self.up_next().start()

        def down():
            self.down_next().wait_recv()
            add_rows(self.down, self.down, self.part, rows)
            self.down_next().start()

        if 0 < hop < self.zt:
            pl.when(self.z == hop)(up)
        if self.zt < self.groups - 1 - hop:
            pl.when(self.z == self.groups - 1 - hop)(down)

    def finish(self, dst, rows):
        def done():
            if self.zt > 0:
                self.up_next().wait_recv()
            if self.zt < self.groups - 1:
                self.down_next().wait_recv()
            if 0 < self.zt < self.groups - 1:
                add_rows(self.up, self.up, self.down, rows)
            add_rows(dst, self.up if self.zt > 0 else self.down, self.part, rows)

        pl.when(self.z == self.zt)(done)

    def drain(self):
        if self.zt > 0:
            pl.when(self.z < self.zt)(lambda: self.up_first().wait_send())
        if self.zt < self.groups - 1:
            pl.when(self.z > self.zt)(lambda: self.down_first().wait_send())


def outward(groups):
    order = []
    lo, hi = 0, groups - 1
    while lo <= hi:
        order.append(hi)
        if lo < hi:
            order.append(lo)
        lo, hi = lo + 1, hi - 1
    return order


def finish_kernel(
    groups, ka_ref, kb_ref, kc_ref, ra_ref, rb_ref, rc_ref, wq_ref, gh_ref, gin_ref, tin_ref,
    pair_ref, tg_ref, out_ref,
    kvc, rvc, r2c, r3c, r4c, csem, cs, cr, kva, kvb, rva, rvb, r2a, r2b, ua, ub, da, db, isem, s2, q2, us, ur, ds, dr,
    gm_ref, wq, gh, g_ref, tok_ref, wsem, fs, fr,
    w2, sib, ub2, db2, fin, send, recv, ts, tr, us2, ur2, ds2, dr2, ps, pr, lsem,
):
    t, p, x, y, z = here()
    ex, ey, ed = plane_peers()
    peers = (ex, ey, ed)
    sibling = (1 - t, p)
    others = [(t, lax.rem(p + SPAN * k, SPAN * groups)) for k in range(1, groups)]
    across = tuple((1 - t, q[1]) for q in peers)
    order = outward(groups)
    colours = (
        (ey, ka_ref, ra_ref, kva, rva, r2a, ua, da, y),
        (ex, kb_ref, rb_ref, kvb, rvb, r2b, ub, db, x),
    )

    def loads(c, zt):
        peer, kr, rr, kv, rv = colours[c][:5]
        i = 2 * (c * groups + zt)
        return (
            pltpu.make_async_copy(kr.at[zt], kv.at[zt], isem.at[i]),
            pltpu.make_async_copy(rr.at[zt], rv.at[zt], isem.at[i + 1]),
        )

    level_loads = [
        [pltpu.make_async_copy(a.at[i], b.at[i], csem.at[2 * i + j]) for j, (a, b) in enumerate(((kc_ref, kvc), (rc_ref, rvc)))]
        for i in range(2)
    ]
    for pair in level_loads:
        for d in pair:
            d.start()
    mixed_loads = (pltpu.make_async_copy(gin_ref, g_ref, wsem.at[2]), pltpu.make_async_copy(tin_ref, tok_ref, wsem.at[3]))
    for i, zt in enumerate(order):
        for c in range(2):
            for d in loads(c, zt):
                d.start()
        if i == 1:
            for c in mixed_loads:
                c.start()
    more = (pltpu.make_async_copy(wq_ref, wq, wsem.at[0]), pltpu.make_async_copy(gh_ref, gh, wsem.at[1]))
    for c in more:
        c.start()
    greet(peers + across + (sibling,) + tuple(others))

    def second(c, zt):
        peer, kr, rr, kv, rv, r2, u, d, mine = colours[c]
        i = c * groups + zt
        return remote(rv.at[zt, 1 - mine], r2.at[zt], s2.at[i], q2.at[i], peer)

    def chain(c, zt):
        peer, kr, rr, kv, rv, r2, u, d, mine = colours[c]
        i = c * groups + zt
        return Line(z, zt, groups, r2.at[zt], u.at[zt], d.at[zt],
                    (us.at[i], ur.at[i], ds.at[i], dr.at[i]), t, p)

    def size(c):
        return colours[c][3].shape[2]

    up = kvc.shape[2]

    def third(i, k):
        at = (k * 2 + 1 - x, (1 - y) * 2 + k)[i]
        n = 2 * i + k
        return remote(rvc.at[i, at], r2c.at[i, k], cs.at[n], cr.at[n], (ex, ey)[i])

    def fourth(i):
        at = (1 - y, 1 - x)[i]
        return remote(r2c.at[i, at], r3c.at[i], cs.at[4 + i], cr.at[4 + i], (ey, ex)[i])

    top = lax.div(z, 2)
    fifth = remote(r3c.at[1 - top], r4c, cs.at[6], cr.at[6], (t, p + 2 * SPAN - 4 * SPAN * top))

    def plus(dst, src, n):
        add_rows(dst, dst, src, n)

    def send_second(zt):
        for c in range(2):
            for d in loads(c, zt):
                d.wait()
            peer, kr, rr, kv, rv, r2, u, d, mine = colours[c]
            plus(rv.at[zt, 1 - mine], kv.at[zt, 1 - mine], size(c))
            second(c, zt).start()

    for i in range(2):
        for d in level_loads[i]:
            d.wait()
        for k in range(2):
            at = (k * 2 + 1 - x, (1 - y) * 2 + k)[i]
            plus(rvc.at[i, at], kvc.at[i, at], up)
            third(i, k).start()
    send_second(order[0])
    send_second(order[1])
    width = gm_ref.shape[0] // 3
    shards = SPAN * groups
    one = width // shards
    half = width // 2
    for c in mixed_loads:
        c.wait()
    for h in range(2):
        r = nn(g_ref[...], tok_ref[:, h * half : (h + 1) * half]).T
        w2[h * (shards // 2) : (h + 1) * (shards // 2)] = r.astype(bf).reshape(shards // 2, one, 3 * HW)

    def swap(zt):
        return remote(w2.at[pl.ds(zt * 4 + (1 - t) * 2, 2)], sib.at[zt], ts.at[zt], tr.at[zt], sibling)

    for zt in order:
        swap(zt).start()

    for i in range(2):
        for k in range(2):
            at = (k * 2 + x, y * 2 + k)[i]
            plus(rvc.at[i, at], kvc.at[i, at], up)
            third(i, k).wait_recv()
            plus(r2c.at[i, k], rvc.at[i, at], up)
        fourth(i).start()
    send_second(order[2])
    send_second(order[3])
    count = gm_ref.shape[1]
    me = lax.rem(p, SPAN)
    copies = []
    for i, peer in enumerate((peers[2], peers[0], peers[1])):
        m = lax.rem(peer[1], SPAN)
        for k in range(3):
            copies.append(remote(
                g_ref.at[pl.ds(k * HW, HW), pl.ds(pl.multiple_of(m * count, count), count)],
                gm_ref.at[pl.ds(pl.multiple_of(k * width + me * HW, HW), HW)],
                send.at[i * 3 + k], recv.at[i * 3 + k], peer,
            ))
    for k in range(3):
        copies.append(pltpu.make_async_copy(
            g_ref.at[pl.ds(k * HW, HW), pl.ds(pl.multiple_of(me * count, count), count)],
            gm_ref.at[pl.ds(pl.multiple_of(k * width + me * HW, HW), HW)],
            lsem.at[k],
        ))
    for c in copies:
        c.start()
    def chain2(zt, k):
        i = zt * 2 + k
        return Line(z, zt, groups, sib.at[zt, k], ub2.at[zt, k], db2.at[zt, k],
                    (us2.at[i], ur2.at[i], ds2.at[i], dr2.at[i]), t, p)

    for zt in order:
        swap(zt).wait_recv()
        for k in range(2):
            dst = sib.at[zt, k]
            add_rows(dst, dst, w2.at[zt * 4 + t * 2 + k], one)
            chain2(zt, k).start()
    for zt in order:
        for c in range(2):
            peer, kr, rr, kv, rv, r2, u, d, mine = colours[c]
            keep = rv.at[zt, mine]
            add_rows(keep, keep, kv.at[zt, mine], size(c))

    def in_plane(zt):
        for c in range(2):
            peer, kr, rr, kv, rv, r2, u, d, mine = colours[c]
            second(c, zt).wait_recv()
            dst = r2.at[zt]
            add_rows(dst, dst, rv.at[zt, mine], size(c))
            chain(c, zt).start()

    def relay(zt, hop):
        for c in range(2):
            chain(c, zt).relay(hop, size(c))


    def relay2(hop):
        for zt in order:
            for k in range(2):
                chain2(zt, k).relay(hop, one)

    in_plane(order[0])
    relay2(1)
    in_plane(order[1])
    for i in range(2):
        fourth(i).wait_recv()
        plus(r3c.at[i], r2c.at[i, (y, x)[i]], up)
    fifth.start()
    relay(order[0], 1)
    relay2(2)
    in_plane(order[2])
    relay(order[1], 1)
    in_plane(order[3])
    relay(order[0], 2)
    relay(order[2], 1)
    relay(order[1], 2)
    relay(order[3], 1)
    for zt in order:
        for k in range(2):
            chain2(zt, k).finish(fin.at[k], one)
    here_id = t * SPAN + me

    def hand(k, tt):
        m = t * 2 + k
        peer = (tt, z * SPAN + m)
        i = k * 2 + tt
        away = lambda: remote(fin.at[k], out_ref.at[me], ps.at[i], pr.at[me], peer)
        stay = lambda: pltpu.make_async_copy(fin.at[k], out_ref.at[me], lsem.at[3])
        return away, stay, (tt * SPAN + m) == here_id

    for k in range(2):
        for tt in range(2):
            away, stay, same = hand(k, tt)
            pl.when(jnp.logical_not(same))(lambda away=away: away().start())
            pl.when(same)(lambda stay=stay: stay().start())
    fifth.wait_recv()
    add_rows(pair_ref.at[t, pl.ds(size(0) + size(1), up)], r3c.at[top], r4c, up)
    for zt in order:
        for c, sl in ((0, pl.ds(0, size(0))), (1, pl.ds(size(0), size(1)))):
            chain(c, zt).finish(pair_ref.at[t, sl], size(c))
    last = remote(pair_ref.at[t], pair_ref.at[t], fs.at[0], fr.at[0], sibling)
    last.start()
    for c in copies + list(more):
        c.wait()
    turned = nn(wq[...], gm_ref[...]).T
    tg_ref[...] = gh[...] + turned
    for s in range(SPAN):
        from_here = jnp.logical_and(s == me, y == t)
        pl.when(jnp.logical_not(from_here))(
            lambda s=s: remote(fin.at[0], out_ref.at[s], ps.at[0], pr.at[s], sibling).wait_recv()
        )
    for k in range(2):
        for tt in range(2):
            away, stay, same = hand(k, tt)
            pl.when(jnp.logical_not(same))(lambda away=away: away().wait_send())
            pl.when(same)(lambda stay=stay: stay().wait())
    for zt in range(groups):
        swap(zt).wait_send()
        for k in range(2):
            chain2(zt, k).drain()
        for c in range(2):
            second(c, zt).wait_send()
            chain(c, zt).drain()
    for i in range(2):
        for k in range(2):
            third(i, k).wait_send()
        fourth(i).wait_send()
    fifth.wait_send()
    last.wait()


def finish(ka, kb, kc, ra, rb, rc, wq, gh, g, tok, groups):
    width = tok.shape[1]
    count = tok.shape[0] // SPAN
    one = width // (SPAN * groups)
    na, nb, nc = ka.shape[2], kb.shape[2], kc.shape[2]
    half = ka.shape[3]
    buf = lambda *n: pltpu.VMEM(n, bf)
    mix = lambda *n: pltpu.VMEM(n + (one, 3 * HW), bf)
    return pl.pallas_call(
        functools.partial(finish_kernel, groups),
        out_shape=(
            jax.ShapeDtypeStruct((2, na + nb + nc, half), bf),
            jax.ShapeDtypeStruct((count, width), f32),
            jax.ShapeDtypeStruct((SPAN, one, 3 * HW), bf),
        ),
        in_specs=[ANY] * 10,
        out_specs=(VM,) * 3,
        scratch_shapes=[
            buf(2, SPAN, nc, half), buf(2, SPAN, nc, half), buf(2, 2, nc, half), buf(2, nc, half), buf(nc, half),
            dma_sems(4), dma_sems(7), dma_sems(7),
            buf(groups, 2, na, half), buf(groups, 2, nb, half), buf(groups, 2, na, half), buf(groups, 2, nb, half),
            buf(groups, na, half), buf(groups, nb, half), buf(groups, na, half), buf(groups, nb, half),
            buf(groups, na, half), buf(groups, nb, half),
            dma_sems(4 * groups), dma_sems(2 * groups), dma_sems(2 * groups),
            dma_sems(2 * groups), dma_sems(2 * groups), dma_sems(2 * groups), dma_sems(2 * groups),
            buf(3 * width, count), buf(width, 3 * width), pltpu.VMEM((count, width), f32),
            buf(*g.shape), buf(*tok.shape), dma_sems(4),
            dma_sems(1), dma_sems(1),
            mix(SPAN * groups), mix(groups, 2), mix(groups, 2), mix(groups, 2), mix(2),
            dma_sems(9), dma_sems(9), dma_sems(groups), dma_sems(groups),
            dma_sems(2 * groups), dma_sems(2 * groups), dma_sems(2 * groups), dma_sems(2 * groups),
            dma_sems(4), dma_sems(SPAN), dma_sems(4),
        ],
        compiler_params=comm_params(3),
        name="finish",
    )(ka, kb, kc, ra, rb, rc, wq, gh, g, tok)


def unfold_kernel(
    groups, pair_ref, part_ref, grad_ref, score_ref, gain_ref, lost_ref,
    gate_ref, up_ref, down_ref, out_ref, qkv_ref, token_ref, scores_ref, loss_ref, *gains_refs,
):
    one = out_ref.shape[0]
    half = pair_ref.shape[2]
    width = 2 * half
    steps = gate_ref.shape[1] // half
    down = down_ref.shape[0]
    token_ref[0] = grad_ref[...]
    top = (steps - UPWARD) * one
    for j in range(steps):
        at = j * one + (0 if j < steps - UPWARD else down + one)
        for k, ref in enumerate((gate_ref, up_ref)):
            ref[:, j * half : (j + 1) * half] = pair_ref[k, at : at + one, :].astype(f32)
    for k in range(2):
        cols = slice(k * half, (k + 1) * half)
        down_ref[:, cols] = pair_ref[k, top : top + down, :].astype(f32)
        out_ref[:, cols] = pair_ref[k, top + down : top + down + one, :].astype(f32)
    for k in range(3):
        row = [part_ref[s, :, k * HW : (k + 1) * HW].astype(f32) for s in range(SPAN)]
        qkv_ref[:, k * width : (k + 1) * width] = jnp.concatenate(row, 1)
    docs, size = scores_ref.shape[0], score_ref.shape[0]
    dot = functools.partial(lax.dot_general, precision=precise, preferred_element_type=f32)
    row = lax.broadcasted_iota(jnp.int32, (docs, size), 0)
    col = lax.broadcasted_iota(jnp.int32, (docs, size), 1)
    pick = jnp.where(row // DOCS_GRP * 8 + lax.rem(row, DOCS_GRP) == col, 1.0, 0.0)
    some = dot(pick, score_ref[...], (((1,), (0,)), ((), ())))
    scores_ref[...] = dot(some, pick, (((1,), (1,)), ((), ())))
    row = lax.broadcasted_iota(jnp.int32, (width, one), 0)
    col = lax.broadcasted_iota(jnp.int32, (width, one), 1)
    mine = jnp.where(row == lax.axis_index("dp") * one + col, 1.0, 0.0)
    gains = dot(gain_ref[...], mine, (((1,), (0,)), ((), ())))
    for k, ref in enumerate(gains_refs):
        ref[...] = gains[k : k + 1, :]
    loss_ref[...] = lost_ref[0:1, 0:1]


def unfold(pair, parts, grad, scores, gains, loss, tiles, groups):
    one = parts.shape[1]
    half = pair.shape[2]
    width = 2 * half
    docs = groups * DOCS_GRP
    sds = jax.ShapeDtypeStruct
    return pl.pallas_call(
        functools.partial(unfold_kernel, groups),
        out_shape=(
            sds((one, tiles * width), f32), sds((one, tiles * width), f32), sds((tiles * one, width), f32),
            sds((one, width), f32), sds((one, 3 * width), f32), sds((1,) + grad.shape, f32),
            sds((docs, docs), f32), sds((1, 1), f32),
        )
        + (sds((1, one), f32),) * 4,
        in_specs=[VM] * 6,
        out_specs=(VM,) * 12,
        name="unfold",
    )(pair, parts, grad, scores, gains, loss)


def angle_tables(total):
    half = HEAD_DIM // 2
    freqs = np.float32(1000.0) ** (-np.arange(half, dtype=np.float32) / np.float32(half))
    theta = freqs[:, None].astype(np.float32) * np.arange(total, dtype=np.float32)[None, :]
    return np.cos(theta).astype(np.float32), np.sin(theta).astype(np.float32)


def spread_sum(value):
    part = lax.psum_scatter(value, "dp", scatter_dimension=0, tiled=True)
    return lax.psum(part.astype(bf), "tower").astype(f32)


def local(
    tokens, doc_ids, pad_mask, targets, w_qkv, w_out, ln1_gain, ln1_bias,
    w_gate, w_up, w_down, ln2_gain, ln2_bias,
):
    width = w_out.shape[0]
    rows = tokens[0]
    count = rows.shape[0]
    places = lax.axis_size("dp")
    groups = places // SPAN
    tower = lax.axis_index("tower")
    place = lax.axis_index("dp")
    me = place % SPAN
    docs = groups * DOCS_GRP
    cos, sin = angle_tables(SPAN * count)
    tok_all, codes, qa, ka, va, kt = gather(rows, doc_ids, pad_mask, cos, sin, w_qkv)
    heads_out, lse, exact = attn_fwd(codes, qa, ka, va)
    norms = (ln1_gain, ln1_bias, ln2_gain, ln2_bias)
    (
        attended, inner, hidden, grad_mlp, grads, grad_branch, grad_attended, grad_h1, gains, scores_all, loss
    ) = block(heads_out, rows, codes, targets, norms, w_out, w_gate, w_up, w_down, groups)
    by_hand = groups == 4 and width % (16 * places) == 0
    if by_hand:
        send_a, keep_a, send_b, keep_b, send_c, keep_c, d_heads, gain_sums = weight_grads(
            groups, grad_attended, gains, inner, grads, hidden, grad_mlp, attended, grad_branch
        )
        exchange = lambda v, bit: lax.ppermute(v, "dp", [(i, i ^ bit) for i in range(places)])
        came_a, came_b, came_c = exchange(send_a, 1), exchange(send_b, 2), exchange(send_c, SPAN)
    else:
        d_heads = tokens_to_heads(grad_attended, 5, "to_heads")
    mixed = attn_bwd(d_heads, exact, lse, qa, ka, va, kt, cos, sin, codes)
    if by_hand:
        pair, grad_tokens, qkv_parts = finish(
            keep_a, keep_b, keep_c, came_a, came_b, came_c, w_qkv, grad_h1, mixed, tok_all, groups
        )
        gate_out, up_out, down_out, out_out, qkv_out, token_grad, scores, loss, *gains_out = unfold(
            pair, qkv_parts, grad_tokens, scores_all, gain_sums, loss, w_gate.shape[1] // width, groups
        )
        gains_out = [v.reshape(-1) for v in gains_out]
    else:
        grad_mixed = heads_to_tokens(mixed, 6, "to_tokens_back")
        qkv_out = spread_sum(tn(rows, grad_mixed.T))
        side = lambda v: lax.psum_scatter(v, "dp", scatter_dimension=0, tiled=True)
        halves = lambda v: lax.all_gather(side(v).astype(bf), "tower", axis=1, tiled=True).astype(f32)
        both = lambda a, b: tn(a[0], b[0]) + tn(a[1], b[1])
        flat = lambda v: v.transpose(0, 2, 1, 3).reshape(2, count, -1)
        out_out = halves(nn(attended[0], grad_branch[0]) + nn(attended[1], grad_branch[1]))
        two = lax.all_gather(side(both(inner, flat(grads))).astype(bf), "tower").astype(f32)
        gate_out, up_out = two[0], two[1]
        down_out = halves(both(flat(hidden), grad_mlp))
        gains_out = spread_sum(gains[:4].T).T
        scores = scores_all.reshape(groups, 8, groups, 8)[:, :DOCS_GRP, :, :DOCS_GRP].reshape(docs, docs)
        token_grad = grad_h1 + lax.dot_general(
            grad_mixed, w_qkv, (((0,), (1,)), ((), ())), preferred_element_type=f32
        )
        token_grad = token_grad[None]
    return (
        scores, loss[0, 0], token_grad, qkv_out, out_out, gains_out[0], gains_out[1],
        gate_out, up_out, down_out, gains_out[2], gains_out[3],
    )


def solution(mesh):
    shard = P("dp", None)
    lone = P("dp")
    return jax.shard_map(
        local,
        mesh=mesh,
        in_specs=(P("tower", "dp", None), P("tower", "dp"), P("tower", "dp")) + (P(),) * 10,
        out_specs=(
            P(), P(), P("tower", "dp", None), shard, shard, lone, lone, shard, shard, shard, lone, lone,
        ),
        check_vma=False,
    )
```

```python
import functools

import jax
import jax.numpy as jnp
import numpy as np
from jax import lax
from jax.experimental import pallas as pl
from jax.experimental.pallas import tpu as pltpu
from jax.sharding import PartitionSpec as P

HEADS = 12
HEAD_DIM = 64
SPAN = 4
DOCS_GRP = 3
NH = HEADS // SPAN
HW = NH * HEAD_DIM
UPWARD = 3
VLIM = 62 * 2**20
MESH = pl.DeviceIdType.MESH
f32 = jnp.float32
bf = jnp.bfloat16
precise = lax.Precision.HIGHEST
norm_eps = 1e-05
ANY = pl.BlockSpec(memory_space=pl.ANY)
VM = pl.BlockSpec(memory_space=pltpu.VMEM)


def nn(a, b):
    return lax.dot_general(a, b, (((1,), (0,)), ((), ())), preferred_element_type=f32)


def nt(a, b):
    return lax.dot_general(a, b, (((1,), (1,)), ((), ())), preferred_element_type=f32)


def tn(a, b):
    return lax.dot_general(a, b, (((0,), (0,)), ((), ())), preferred_element_type=f32)


def split3(v):
    one = v.astype(bf).astype(f32)
    rest = v - one
    two = rest.astype(bf).astype(f32)
    return [one, two, rest - two]


def here():
    t = lax.axis_index("tower")
    p = lax.axis_index("dp")
    x = lax.rem(p, 2)
    y = lax.rem(lax.div(p, 2), 2)
    return t, p, x, y, lax.div(p, SPAN)


def plane_peers():
    t, p, x, y, g = here()
    px = p + 1 - 2 * x
    py = p + 2 - 4 * y
    pd = px + 2 - 4 * y
    return (t, px), (t, py), (t, pd)


def greet(peers):
    barrier = pltpu.get_barrier_semaphore()
    for peer in peers:
        pl.semaphore_signal(barrier, inc=1, device_id=peer, device_id_type=MESH)
    pl.semaphore_wait(barrier, len(peers))


def remote(src, dst, send, recv, peer):
    return pltpu.make_async_remote_copy(
        src_ref=src, dst_ref=dst, send_sem=send, recv_sem=recv, device_id=peer, device_id_type=MESH
    )


def dma_sems(n):
    return pltpu.SemaphoreType.DMA((n,))


def comm_params(cid):
    return pltpu.CompilerParams(collective_id=cid, has_side_effects=True, vmem_limit_bytes=VLIM)


def gather_kernel(
    tok_ref, ids_ref, pads_ref, cos_ref, sin_ref, w_ref, out_ref, codes_ref, qa_ref, ka_ref, va_ref, kt_ref,
    att_ref, lse_ref, exact_ref,
    toks, code_ref, codes, wraw, wturn, wt, qa, ka, va, kt, acc, tops, sooner, later, heads,
    send, recv, csend, crecv, wsem, osem, asend, arecv, asem,
):
    t, p, x, y, g = here()
    count, width = tok_ref.shape
    half = count // 2
    me = lax.rem(p, SPAN)
    odd = lax.rem(me, 2)
    wide = wraw.shape[2]
    loads = []
    for k in range(3):
        at = pl.multiple_of(k * width + me * HW - odd * HEAD_DIM, 128)
        loads.append(pltpu.make_async_copy(w_ref.at[:, pl.ds(at, wide)], wraw.at[k], wsem.at[k]))
        loads[-1].start()
    code_ref[...] = lax.rem(ids_ref[...], DOCS_GRP).astype(f32) + 4.0 * (1 - pads_ref[...]).astype(f32)
    ex, ey, ed = plane_peers()
    mx, my, md = (lax.rem(q[1], SPAN) for q in (ex, ey, ed))

    def rows(m, h):
        return pl.ds(pl.multiple_of(m * count + h * half, half), half)

    def whole(m):
        return pl.ds(pl.multiple_of(m * count, count), count)

    greet((ex, ey, ed))
    first = []
    for i, (peer, h) in enumerate(((ex, 0), (ey, 1), (ex, 1), (ey, 0))):
        c = remote(tok_ref.at[pl.ds(h * half, half)], toks.at[rows(me, h)], send.at[i], recv.at[i], peer)
        c.start()
        first.append(c)
    small = []
    for i, peer in enumerate((ex, ey, ed)):
        c = remote(code_ref, codes.at[:, whole(me)], csend.at[i], crecv.at[i], peer)
        c.start()
        small.append(c)
    codes[:, whole(me)] = code_ref[...]
    for k in range(3):
        loads[k].wait()
        wturn[...] = wraw[k].T
        wt[k * HW : (k + 1) * HW, :] = wturn[pl.ds(pl.multiple_of(odd * HEAD_DIM, HEAD_DIM), HW), :]

    def project(rows_ref, m, n):
        sl = whole(m)
        mx = nt(wt[...], rows_ref[...])
        cos, sin = cos_ref[:, sl], sin_ref[:, sl]
        cd = codes[:, sl]
        mem = jnp.where(cd >= 4.0, cd - 4.0, cd)
        pad = [jnp.zeros((13, count), f32)]
        hot = jnp.concatenate([jnp.where(mem == float(d), 1.0, 0.0) for d in range(DOCS_GRP)] + pad, 0)
        neg = jnp.concatenate([jnp.where(cd == float(d), 0.0, -1e30) for d in range(DOCS_GRP)] + pad, 0)
        rest = jnp.zeros((48, count), f32)
        one = jnp.concatenate([jnp.ones((1, count), f32), jnp.zeros((63, count), f32)], 0)

        def rope(u):
            a, b = u[:32], u[32:]
            return jnp.concatenate([a * cos - b * sin, b * cos + a * sin], 0)

        for h in range(NH):
            q = rope(mx[h * HEAD_DIM : (h + 1) * HEAD_DIM]).astype(bf).astype(f32) * 0.125
            k = rope(mx[HW + h * HEAD_DIM : HW + (h + 1) * HEAD_DIM])
            v = mx[2 * HW + h * HEAD_DIM : 2 * HW + (h + 1) * HEAD_DIM]
            qa[h, :, sl] = jnp.concatenate([q, hot, rest], 0).astype(bf)
            ka[h, sl, :] = jnp.concatenate([k, neg, rest], 0).T.astype(bf)
            va[h, :, sl] = jnp.concatenate([v, one], 0).astype(bf)
            kt[h, :, sl] = k.astype(bf)
        puts = (
            (rows_ref, out_ref.at[sl]),
            (qa.at[:, :, sl], qa_ref.at[:, :, sl]),
            (ka.at[:, sl, :], ka_ref.at[:, sl, :]),
            (va.at[:, :, sl], va_ref.at[:, :, sl]),
            (kt.at[:, :, sl], kt_ref.at[:, :, sl]),
        )
        puts = [pltpu.make_async_copy(a, b, osem.at[5 * n + i]) for i, (a, b) in enumerate(puts)]
        for c in puts:
            c.start()
        return puts

    part = count // 2
    acc[...] = jnp.zeros_like(acc)
    tops[...] = jnp.full_like(tops, -3e38)
    chunks = (me, mx, my, md)
    inside = jnp.where((me == 1) | (me == 2), 1, 0)

    def pick(n, values):
        got = values[-1]
        for i in reversed(range(len(values) - 1)):
            got = jnp.where(n == i, values[i], got)
        return got

    def segment(q, key_of, trips):
        qs = whole(q)

        def keys(n, k):
            return pl.ds(pl.multiple_of(key_of(n) * count + k * part, part), part)

        def scores(n, k, h, ref):
            ref[h] = nn(ka[h, keys(n, k), :], qa[h, :, qs])

        def absorb(n, k, h, ref, m):
            s = ref[h]
            mn = jnp.maximum(m, jnp.max(s, 0, keepdims=True))
            pr = jnp.exp(s - mn).astype(bf)
            acc[q, h] = acc[q, h] * jnp.exp(m - mn) + nn(va[h, :80, keys(n, k)], pr)
            return mn

        for h in range(NH):
            scores(0, 0, h, sooner)

        def step(n, ms):
            ms = list(ms)
            for h in range(NH):
                scores(n, 1, h, later)
                ms[h] = absorb(n, 0, h, sooner, ms[h])
            after = jnp.minimum(n + 1, jnp.maximum(trips - 1, 0))
            for h in range(NH):
                scores(after, 0, h, sooner)
                ms[h] = absorb(n, 1, h, later, ms[h])
            return tuple(ms)

        ms = lax.fori_loop(0, trips, step, tuple(tops[q * NH + h] for h in range(NH)))
        for h in range(NH):
            tops[q * NH + h] = ms[h]

    def finalize(q):
        qs = whole(q)
        edge = jnp.where((q == 0) | (q == SPAN - 1), 1.0, 0.0)
        other = whole(SPAN - 1 - q)
        for h in range(NH):
            m = tops[q * NH + h]
            rest = jnp.sum(va[h, :80, other].astype(f32), 1, keepdims=True)
            full = acc[q, h] + rest * jnp.where(m < -1e29, edge, 0.0)
            tot = full[64:65]
            o = full[:64] / tot
            at = pl.ds(h * HEAD_DIM, HEAD_DIM)
            exact_ref[at, qs] = o
            lse_ref[h : h + 1, qs] = jnp.where(m < -1e29, 0.0, m + jnp.log(tot))
            heads[at, qs] = o.astype(bf)

    done = project(tok_ref, me, 0)
    first[0].wait_recv()
    f0 = remote(toks.at[rows(mx, 0)], toks.at[rows(mx, 0)], send.at[4], recv.at[4], ey)
    f0.start()
    first[1].wait_recv()
    f1 = remote(toks.at[rows(my, 1)], toks.at[rows(my, 1)], send.at[5], recv.at[5], ex)
    f1.start()
    segment(me, lambda n: me, 1)
    for c in small:
        c.wait()
    first[2].wait_recv()
    done += project(toks.at[whole(mx)], mx, 1)
    first[3].wait_recv()
    done += project(toks.at[whole(my)], my, 2)

    def near(s, _):
        q = pick(s, chunks[:3])
        key_of = lambda n: pick(s, (pick(n, (mx, my)), pick(n, (me, mx, my)), pick(n, (me, my, mx))))
        segment(q, key_of, jnp.where(s == 0, 2, 3 - inside))
        return 0

    lax.fori_loop(0, 3, near, 0)
    f0.wait_recv()
    f1.wait_recv()
    done += project(toks.at[whole(md)], md, 3)

    def back(s):
        peer = (ed, ex, ey)[s]
        m = (md, mx, my)[s]
        return remote(
            heads.at[:, whole(m)], att_ref.at[pl.ds(pl.multiple_of(me * HW, HW), HW)], asend.at[s], arecv.at[s], peer
        )

    def far(s, _):
        q = pick(s, (md, mx, my, me))
        key_of = lambda n: jnp.where(s == 0, pick(n, (mx, my, md, me)), md)
        segment(q, key_of, pick(s, (3 + inside, 1, 1, inside)))
        finalize(q)
        for k in range(3):
            pl.when(s == k)(lambda k=k: back(k).start())
        return 0

    lax.fori_loop(0, 4, far, 0)
    own = pltpu.make_async_copy(
        heads.at[:, whole(me)], att_ref.at[pl.ds(pl.multiple_of(me * HW, HW), HW)], asem.at[0]
    )
    own.start()
    codes_ref[...] = codes[...]
    for c in first + [f0, f1]:
        c.wait_send()
    for c in done:
        c.wait()
    own.wait()
    for k in range(3):
        back(k).wait()


def gather(tok, ids, pads, cos, sin, w_qkv):
    count, width = tok.shape
    total = SPAN * count
    shapes = ((NH, 128, total), (NH, total, 128), (NH, 128, total), (NH, HEAD_DIM, total))
    return pl.pallas_call(
        gather_kernel,
        out_shape=(jax.ShapeDtypeStruct((total, width), bf), jax.ShapeDtypeStruct((1, total), f32))
        + tuple(jax.ShapeDtypeStruct(s, bf) for s in shapes)
        + (
            jax.ShapeDtypeStruct((SPAN * HW, count), bf), jax.ShapeDtypeStruct((NH, total), f32),
            jax.ShapeDtypeStruct((HW, total), f32),
        ),
        in_specs=[VM] * 5 + [ANY],
        out_specs=(ANY, VM) + (ANY,) * 5 + (VM,) * 2,
        scratch_shapes=[
            pltpu.VMEM((total, width), bf), pltpu.VMEM((1, count), f32), pltpu.VMEM((1, total), f32), pltpu.VMEM((3, width, 256), bf),
            pltpu.VMEM((256, width), bf), pltpu.VMEM((3 * HW, width), bf),
        ]
        + [pltpu.VMEM(s, bf) for s in shapes]
        + [
            pltpu.VMEM((SPAN, NH, 80, count), f32), pltpu.VMEM((SPAN * NH, 1, count), f32),
            pltpu.VMEM((NH, count // 2, count), f32), pltpu.VMEM((NH, count // 2, count), f32),
            pltpu.VMEM((HW, total), bf),
            dma_sems(6), dma_sems(6), dma_sems(3), dma_sems(3), dma_sems(3), dma_sems(20),
            dma_sems(3), dma_sems(3), dma_sems(1),
        ],
        compiler_params=comm_params(0),
        name="gather",
    )(tok, ids, pads, cos, sin, w_qkv)


def heads_to_tokens_kernel(parts, in_ref, out_ref, send, recv, lsem):
    t, p, x, y, g = here()
    count = out_ref.shape[1]
    me = lax.rem(p, SPAN)
    peers = plane_peers()
    width = parts and out_ref.shape[0] // parts
    greet(peers)
    copies = []
    for i, peer in enumerate((peers[2], peers[0], peers[1])):
        m = lax.rem(peer[1], SPAN)
        for k in range(parts):
            c = remote(
                in_ref.at[pl.ds(k * HW, HW), pl.ds(pl.multiple_of(m * count, count), count)],
                out_ref.at[pl.ds(pl.multiple_of(k * width + me * HW, HW), HW)],
                send.at[i * parts + k],
                recv.at[i * parts + k],
                peer,
            )
            c.start()
            copies.append(c)
    for k in range(parts):
        c = pltpu.make_async_copy(
            in_ref.at[pl.ds(k * HW, HW), pl.ds(pl.multiple_of(me * count, count), count)],
            out_ref.at[pl.ds(pl.multiple_of(k * width + me * HW, HW), HW)],
            lsem.at[k],
        )
        c.start()
        copies.append(c)
    for c in copies:
        c.wait()


def heads_to_tokens(a, cid, name):
    parts = a.shape[0] // HW
    count = a.shape[1] // SPAN
    return pl.pallas_call(
        functools.partial(heads_to_tokens_kernel, parts),
        out_shape=jax.ShapeDtypeStruct((parts * HEADS * HEAD_DIM, count), a.dtype),
        in_specs=[VM],
        out_specs=ANY,
        scratch_shapes=[dma_sems(3 * parts), dma_sems(3 * parts), dma_sems(parts)],
        compiler_params=comm_params(cid),
        name=name,
    )(a)


def tokens_to_heads_kernel(in_ref, out_ref, send, recv, lsem):
    t, p, x, y, g = here()
    count = in_ref.shape[1]
    me = lax.rem(p, SPAN)
    peers = plane_peers()
    greet(peers)
    mine = pl.ds(pl.multiple_of(me * count, count), count)
    copies = []
    for i, peer in enumerate((peers[2], peers[0], peers[1])):
        m = lax.rem(peer[1], SPAN)
        c = remote(
            in_ref.at[pl.ds(pl.multiple_of(m * HW, HW), HW)],
            out_ref.at[:, mine],
            send.at[i],
            recv.at[i],
            peer,
        )
        c.start()
        copies.append(c)
    c = pltpu.make_async_copy(
        in_ref.at[pl.ds(pl.multiple_of(me * HW, HW), HW)], out_ref.at[:, mine], lsem.at[0]
    )
    c.start()
    for c in copies + [c]:
        c.wait()


def tokens_to_heads(a, cid, name):
    return pl.pallas_call(
        tokens_to_heads_kernel,
        out_shape=jax.ShapeDtypeStruct((HW, SPAN * a.shape[1]), a.dtype),
        in_specs=[VM],
        out_specs=ANY,
        scratch_shapes=[dma_sems(3), dma_sems(3), dma_sems(1)],
        compiler_params=comm_params(cid),
        name=name,
    )(a)


def doc_limits(code):
    pad = code >= 4.0
    mem = jnp.where(pad, code - 4.0, code)
    n0 = jnp.sum(jnp.where(mem < 0.5, 1.0, 0.0)).astype(jnp.int32)
    n1 = jnp.sum(jnp.where(mem < 1.5, 1.0, 0.0)).astype(jnp.int32)
    l = [jnp.sum(jnp.where(code == float(d), 1.0, 0.0)).astype(jnp.int32) for d in range(3)]
    return n0, n1, l

def block_range(lims, a, size, total):
    n0, n1, l = lims
    b = a + size - 1
    first = (a >= n0).astype(jnp.int32) + (a >= n1).astype(jnp.int32)
    last = (b >= n0).astype(jnp.int32) + (b >= n1).astype(jnp.int32)
    lo = jnp.where(first == 0, 0, jnp.where(first == 1, n0, n1))
    hi = jnp.where(last == 0, n0, jnp.where(last == 1, n1, total))
    dead = jnp.zeros((), jnp.bool_)
    for d in range(3):
        dead = dead | ((first <= d) & (d <= last) & (l[d] == 0))
    return jnp.where(dead, 0, lo), jnp.where(dead, total, hi)

def bwd_kernel(KB, QB, do_ref, o32_ref, lse_ref, qa_ref, ka_ref, va_ref, kt_ref, cos_ref, sin_ref, code_ref, g_ref,
               vn_ref, dn_ref, da_ref, qb_ref, acc_ref, dq_ref):
    T = do_ref.shape[1]
    hw = HW
    CH = 512
    lims = doc_limits(code_ref[...])
    def prep(c, _):
        sl = pl.ds(pl.multiple_of(c*CH, CH), CH)
        for h in range(NH):
            do = do_ref[h*HEAD_DIM:(h+1)*HEAD_DIM, sl].astype(f32)
            delta = jnp.sum(do*o32_ref[h*HEAD_DIM:(h+1)*HEAD_DIM, sl], 0, keepdims=True)
            def split(x):
                x1 = x.astype(bf).astype(f32); r = x-x1
                x2 = r.astype(bf).astype(f32); x3 = r-x2
                return [x1, x2, x3]
            z13 = jnp.zeros((13, CH), f32); z48 = jnp.zeros((48, CH), f32)
            da_ref[h, :, sl] = jnp.concatenate([do]+split(-delta)+[z13, z48], 0).astype(bf)
            one = jnp.concatenate([jnp.ones((3, CH), f32), jnp.zeros((61, CH), f32)], 0)
            v = va_ref[h, :64, sl].astype(f32)
            vn_ref[h, sl, :] = jnp.concatenate([v, one], 0).T.astype(bf)
            z64 = jnp.zeros((64, CH), f32)
            q = qa_ref[h, :64, sl].astype(f32)
            dn_ref[h, sl, :] = jnp.concatenate([do, z64], 0).T.astype(bf)
            qb_ref[h, sl, :] = jnp.concatenate([z64, q], 0).T.astype(bf)
            acc_ref[h, sl, :] = jnp.zeros((CH, 128), f32)
        return 0
    lax.fori_loop(0, T//CH, prep, 0)
    def qblock(i, _):
        a = i*QB
        qs = pl.ds(pl.multiple_of(a, QB), QB)
        lo, hi = block_range(lims, a, QB, T)
        jlo = lo//KB; jhi = (hi+KB-1)//KB
        dq_ref[...] = jnp.zeros_like(dq_ref)
        def kv(j, _):
            ks = pl.ds(pl.multiple_of(j*KB, KB), KB)
            for h in range(NH):
                s = nn(ka_ref[h, ks, :], qa_ref[h, :, qs])
                dp = nn(vn_ref[h, ks, :], da_ref[h, :, qs])
                p = jnp.exp(s - lse_ref[h:h+1, qs])
                ds = (p*dp).astype(bf)
                acc_ref[h, ks, :] += nn(p.astype(bf), dn_ref[h, qs, :]) + nn(ds, qb_ref[h, qs, :])
                dq_ref[h] += nn(kt_ref[h, :, ks], ds)
            return 0
        lax.fori_loop(jlo, jhi, kv, 0)
        cos = cos_ref[:, qs]; sin = sin_ref[:, qs]
        for h in range(NH):
            u = dq_ref[h]*0.125
            x1 = u[:32]; x2 = u[32:]
            g_ref[h*HEAD_DIM:(h+1)*HEAD_DIM, qs] = jnp.concatenate([x1*cos+x2*sin, x2*cos-x1*sin], 0).astype(bf)
        return 0
    lax.fori_loop(0, T//QB, qblock, 0)
    def fin(c, _):
        sl = pl.ds(pl.multiple_of(c*CH, CH), CH)
        cos = cos_ref[:, sl]; sin = sin_ref[:, sl]
        for h in range(NH):
            t = acc_ref[h, sl, :].T
            x1 = t[64:96]; x2 = t[96:128]
            g_ref[hw+h*HEAD_DIM:hw+(h+1)*HEAD_DIM, sl] = jnp.concatenate([x1*cos+x2*sin, x2*cos-x1*sin], 0).astype(bf)
            g_ref[2*hw+h*HEAD_DIM:2*hw+(h+1)*HEAD_DIM, sl] = t[:64].astype(bf)
        return 0
    lax.fori_loop(0, T//CH, fin, 0)

def attn_bwd(do, o32, lse, qa, ka, va, kt, cos, sin, code, KB=512, QB=256):
    T = do.shape[1]
    return pl.pallas_call(functools.partial(bwd_kernel, KB, QB),
        out_shape=jax.ShapeDtypeStruct((3*NH*HEAD_DIM, T), bf),
        in_specs=[pl.BlockSpec(memory_space=pltpu.VMEM)]*10, out_specs=pl.BlockSpec(memory_space=pltpu.VMEM),
        scratch_shapes=[pltpu.VMEM((NH,T,128), bf), pltpu.VMEM((NH,T,128), bf), pltpu.VMEM((NH,128,T), bf), pltpu.VMEM((NH,T,128), bf),
                        pltpu.VMEM((NH,T,128), f32), pltpu.VMEM((NH,HEAD_DIM,QB), f32)],
        compiler_params=pltpu.CompilerParams(vmem_limit_bytes=VLIM), name="attn_bwd",
        cost_estimate=pl.CostEstimate(flops=int(10*T*T*128*3), bytes_accessed=12<<20, transcendentals=T*T*3))(do, o32, lse, qa, ka, va, kt, cos, sin, code)


def contrast_part(groups, sums, goals_ref, plane, allp, ge, send, recv, scores_ref, loss_ref):
    t, p, x, y, g = here()
    docs = groups * DOCS_GRP
    size = groups * 8
    peers = plane_peers()
    line = [(t, lax.rem(p + SPAN * k, SPAN * groups)) for k in range(1, groups)]
    plane[3] = sums
    copies = [remote(plane.at[3], plane.at[i], send.at[i], recv.at[i], q) for i, q in enumerate(peers)]
    for c in copies:
        c.start()
    col = lax.broadcasted_iota(jnp.int32, (size, size), 1)
    row = lax.broadcasted_iota(jnp.int32, (size, size), 0)

    def mark(i, hot):
        goal = goals_ref[i]
        at = (row == i // DOCS_GRP * 8 + i % DOCS_GRP) & (col == goal // DOCS_GRP * 8 + goal % DOCS_GRP)
        return hot + jnp.where(at, 1.0, 0.0)

    hot = lax.fori_loop(0, docs, mark, jnp.zeros((size, size), f32))
    for c in copies:
        c.wait()
    own = (plane[3] + plane[0]) + (plane[1] + plane[2])
    allp[t, g] = own
    rows = allp.at[t, g]
    copies = [remote(rows, rows, send.at[3 + i], recv.at[3 + i], q) for i, q in enumerate(line)]
    for c in copies:
        c.start()
    for c in copies:
        c.wait()
    c = remote(allp.at[t], allp.at[t], send.at[2 + groups], recv.at[2 + groups], (1 - t, p))
    c.start()
    c.wait()
    width = allp.shape[3]
    pools = [allp[k].reshape(size, width) for k in range(2)]
    embeds = [v * lax.rsqrt(jnp.sum(v * v, -1, keepdims=True) + 1e-06) for v in pools]
    dot = functools.partial(lax.dot_general, precision=precise, preferred_element_type=f32)
    scores = dot(embeds[0], embeds[1], (((1,), (1,)), ((), ()))) * 50.0
    live = lax.rem(col, 8) < DOCS_GRP
    alive = lax.rem(row, 8) < DOCS_GRP
    masked = jnp.where(live, scores, -1e30)
    top = jnp.max(masked, -1, keepdims=True)
    total = jnp.sum(jnp.exp(masked - top), -1, keepdims=True)
    log_sums = top + jnp.log(total)
    chosen = jnp.sum(hot * scores, -1, keepdims=True)
    each = jnp.where(alive[:, 0:1], log_sums - chosen, 0.0)
    loss_ref[...] = jnp.broadcast_to(jnp.sum(each, 0, keepdims=True) / docs, loss_ref.shape)
    scores_ref[...] = scores
    gs = jnp.where(alive & live, (jnp.exp(masked - log_sums) - hot) / docs, 0.0)
    gq = dot(gs, embeds[1], (((1,), (0,)), ((), ())))
    gd = dot(gs, embeds[0], (((0,), (0,)), ((), ())))
    ge[...] = jnp.where(t == 0, gq, gd) * 50.0
    mine = ge[pl.ds(pl.multiple_of(g * 8, 8), 8), :]
    pooled = allp[t, g]
    inv = lax.rsqrt(jnp.sum(pooled * pooled, -1, keepdims=True) + 1e-06)
    return inv * mine - inv * inv * inv * pooled * jnp.sum(pooled * mine, -1, keepdims=True)


def block_kernel(
    groups, heads_ref, rows_ref, codes_ref, goals_ref, gain1_ref, bias1_ref, gain2_ref, bias2_ref, wo_h, wg_h, wu_h, wd_h,
    att_o, inner_o, hid_o, gm_o, gg_o, gb_o, ga_o, gh1_o, gains_o, scores_o, loss_o,
    att, wo, wg, wu, wd, inner, x1, s1, acc, hid, ab, x2, s2, sec, gm, gm2, gb, gb2, plane, allp, ge,
    wsem, lsem, tsend, trecv, osem, csend, crecv,
):
    t, p, x, y, g = here()
    peers = plane_peers()
    sibling = (1 - t, p)
    line = tuple((t, lax.rem(p + SPAN * k, SPAN * groups)) for k in range(1, groups))
    count, width = rows_ref.shape
    half = width // 2
    tiles = wg.shape[0]
    me = lax.rem(p, SPAN)

    def weight(j, k):
        cols = pl.ds(j * width, width)
        src, dst = ((wg_h.at[:, cols], wg.at[j]), (wu_h.at[:, cols], wu.at[j]), (wd_h.at[cols], wd.at[j]))[k]
        return pltpu.make_async_copy(src, dst, wsem.at[1 + 3 * j + k])

    first_load = pltpu.make_async_copy(wo_h, wo, wsem.at[0])
    heads_load = pltpu.make_async_copy(heads_ref, att, lsem.at[0])
    heads_load.start()
    first_load.start()
    for j in range(tiles):
        for k in range(3):
            weight(j, k).start()
    greet(peers + (sibling,) + line)
    code = codes_ref[:, pl.ds(pl.multiple_of(me * count, count), count)]
    zero = jnp.zeros((8 - DOCS_GRP, count), f32)
    mem = jnp.concatenate([jnp.where(code == float(d), 1.0, 0.0) for d in range(DOCS_GRP)] + [zero], 0)
    mem = jnp.concatenate([mem, mem, mem, jnp.zeros((8, count), f32)], 0).astype(bf)
    first_load.wait()
    heads_load.wait()

    def pair(i, mine, its, out):
        return (
            pltpu.make_async_copy(mine, out.at[0], osem.at[i]),
            remote(its, out.at[1], tsend.at[i], trecv.at[i], sibling),
        )

    def both(i, mine, its, out):
        for c in pair(i, mine, its, out):
            c.start()

    both(0, att, att, att_o)
    acc[...] = tn(att[...], wo[...])
    step = 64
    gain1, bias1, gain2, bias2 = (r[...].reshape(1, width) for r in (gain1_ref, bias1_ref, gain2_ref, bias2_ref))

    def chunk(i):
        return pl.ds(pl.multiple_of(i * step, step), step)

    def norm(h, sl, xs, ss):
        c = h - jnp.mean(h, -1, keepdims=True)
        s = lax.rsqrt(jnp.mean(c * c, -1, keepdims=True) + norm_eps)
        xh = c * s
        xs[sl, :] = xh
        ss[sl, :] = s
        return xh

    def norm_one(i, _):
        sl = chunk(i)
        xh = norm(rows_ref[sl, :].astype(f32) + acc[sl, :], sl, x1, s1)
        v = xh * gain1 + bias1
        inner[sl, :] = v.astype(bf)
        acc[sl, :] = v
        return 0

    lax.fori_loop(0, count // step, norm_one, 0)
    both(1, inner, inner, inner_o)

    def tile_of(j, i, mine, its, out):
        return (
            pltpu.make_async_copy(mine, out.at[0, j], osem.at[i + j]),
            remote(its, out.at[1, j], tsend.at[i + j], trecv.at[i + j], sibling),
        )

    for j in range(tiles):
        for k in range(3):
            weight(j, k).wait()
        gate = nn(inner[...], wg[j])
        upper = nn(inner[...], wu[j])
        sig = jax.nn.sigmoid(gate)
        silu = gate * sig
        hid[j] = (silu * upper).astype(bf)
        ab[0, j] = (upper * (sig * (1.0 + gate * (1.0 - sig)))).astype(bf)
        ab[1, j] = silu.astype(bf)
        for c in tile_of(j, 2, hid.at[j], hid.at[j], hid_o):
            c.start()
        acc[...] += nn(hid[j], wd[j])

    def norm_two(i, _):
        sl = chunk(i)
        v = norm(acc[sl, :], sl, x2, s2) * gain2 + bias2
        for k, part in enumerate(split3(v)):
            sec[k, sl, :] = part.astype(bf)
        return 0

    lax.fori_loop(0, count // step, norm_two, 0)
    sums = (nn(mem[:16], sec[0]) + nn(mem[:16], sec[1]) + nn(mem[:16], sec[2]))[:8]
    top = lax.broadcasted_iota(jnp.int32, sums.shape, 0) < DOCS_GRP
    sums = jnp.where(top, sums, 0.0)
    gp = contrast_part(groups, sums, goals_ref, plane, allp, ge, csend, crecv, scores_o, loss_o)
    gp3 = jnp.concatenate(split3(gp) + [jnp.zeros_like(gp)], 0).astype(bf)
    acc[...] = tn(mem, gp3)

    def fold(v):
        return jnp.sum(v.reshape(step // 8, 8, width), 0)

    def norm_back(gr, xh, s, gain):
        e = gr * gain
        v = e - jnp.mean(e, -1, keepdims=True) - xh * jnp.mean(e * xh, -1, keepdims=True)
        return v * s

    zeros = jnp.zeros((8, width), f32)

    def back_two(i, sums):
        sl = chunk(i)
        gr, xh = acc[sl, :], x2[sl, :]
        v = norm_back(gr, xh, s2[sl, :], gain2)
        acc[sl, :] = v
        low = v.astype(bf)
        gm[sl, :] = low
        gm2[0, sl, :] = low[:, :half]
        gm2[1, sl, :] = low[:, half:]
        return sums[0] + fold(gr * xh), sums[1] + fold(gr)

    g2, b2 = lax.fori_loop(0, count // step, back_two, (zeros, zeros))
    both(2 + 2 * tiles, gm2.at[t], gm2.at[1 - t], gm_o)
    for j in range(tiles):
        gh = nt(gm[...], wd[j])
        gg = (gh * ab[0, j].astype(f32)).astype(bf)
        gu = (gh * ab[1, j].astype(f32)).astype(bf)
        ab[0, j] = gg
        ab[1, j] = gu
        for c in tile_of(j, 2 + tiles, ab.at[t, j], ab.at[1 - t, j], gg_o):
            c.start()
        acc[...] += nt(gg, wg[j]) + nt(gu, wu[j])

    def back_one(i, sums):
        sl = chunk(i)
        gr, xh = acc[sl, :], x1[sl, :]
        v = norm_back(gr, xh, s1[sl, :], gain1)
        gh1_o[sl, :] = v
        low = v.astype(bf)
        gb[sl, :] = low
        gb2[0, sl, :] = low[:, :half]
        gb2[1, sl, :] = low[:, half:]
        return sums[0] + fold(gr * xh), sums[1] + fold(gr)

    g1, b1 = lax.fori_loop(0, count // step, back_one, (zeros, zeros))
    both(3 + 2 * tiles, gb2.at[t], gb2.at[1 - t], gb_o)
    flat = [jnp.sum(v, 0, keepdims=True) for v in (g1, b1, g2, b2)]
    gains_o[...] = jnp.concatenate(flat + [jnp.zeros((4, width), f32)], 0)
    ga_o[...] = nt(wo[...], gb[...]).astype(bf)
    done = [pair(0, att, att, att_o), pair(1, inner, inner, inner_o)]
    for j in range(tiles):
        done.append(tile_of(j, 2, hid.at[j], hid.at[j], hid_o))
        done.append(tile_of(j, 2 + tiles, ab.at[t, j], ab.at[1 - t, j], gg_o))
    done.append(pair(2 + 2 * tiles, gm2.at[t], gm2.at[1 - t], gm_o))
    done.append(pair(3 + 2 * tiles, gb2.at[t], gb2.at[1 - t], gb_o))
    for c in done:
        for d in c:
            d.wait()


def block(heads, rows, codes, goals, norms, w_out, w_gate, w_up, w_down, groups):
    count, width = rows.shape
    tiles = w_gate.shape[1] // width
    half = width // 2
    size = groups * 8
    sds = jax.ShapeDtypeStruct
    vm = lambda *n: pltpu.VMEM(n, bf)
    vf = lambda *n: pltpu.VMEM(n, f32)
    return pl.pallas_call(
        functools.partial(block_kernel, groups),
        out_shape=(
            sds((2, width, count), bf), sds((2, count, width), bf), sds((2, tiles, count, width), bf),
            sds((2, count, half), bf), sds((2, tiles, count, width), bf), sds((2, count, half), bf),
            sds((width, count), bf), sds((count, width), f32), sds((8, width), f32),
            sds((size, size), f32), sds((8, 128), f32),
        ),
        in_specs=[ANY, VM, VM, pl.BlockSpec(memory_space=pltpu.SMEM)] + [VM] * 4 + [ANY] * 4,
        out_specs=(ANY,) * 6 + (VM,) * 5,
        scratch_shapes=[
            vm(width, count), vm(width, width), vm(tiles, width, width), vm(tiles, width, width),
            vm(tiles, width, width), vm(count, width), vf(count, width), vf(count, 1), vf(count, width),
            vm(tiles, count, width), vm(2, tiles, count, width), vf(count, width), vf(count, 1),
            vm(3, count, width), vm(count, width), vm(2, count, half), vm(count, width), vm(2, count, half),
            vf(4, 8, width), vf(2, groups, 8, width), vf(size, width),
            dma_sems(1 + 3 * tiles), dma_sems(1),
            dma_sems(4 + 2 * tiles), dma_sems(4 + 2 * tiles), dma_sems(4 + 2 * tiles),
            dma_sems(3 + groups), dma_sems(3 + groups),
        ],
        compiler_params=comm_params(1),
        name="block",
    )(heads, rows, codes, goals, *norms, w_out, w_gate, w_up, w_down)


def weights_kernel(
    groups, i_ref, g_ref, h_ref, m_ref, a_ref, b_ref, in_ref, gain_ref,
    sa_ref, ka_ref, sb_ref, kb_ref, sc_ref, kc_ref, heads_ref, sum_ref,
    iv, it, gv, hv, mv, av, bv, gs, ds, os, plane, line, isem, osem, send, recv, lsem, nsend, nrecv,
):
    t, p, x, y, g = here()
    level = lax.rem(g, 2)
    peers = plane_peers()
    sibling = (1 - t, p)
    others = tuple((t, lax.rem(p + SPAN * k, SPAN * groups)) for k in range(1, groups))
    greet(peers + (sibling,) + others)
    around = [remote(gain_ref, plane.at[i], nsend.at[i], nrecv.at[i], q) for i, q in enumerate(peers)]
    for c in around:
        c.start()
    tokens = in_ref.shape[1]
    me = lax.rem(p, SPAN)
    mine = pl.ds(pl.multiple_of(me * tokens, tokens), tokens)
    moves = []
    for i, peer in enumerate((peers[2], peers[0], peers[1])):
        m = lax.rem(peer[1], SPAN)
        moves.append(remote(
            in_ref.at[pl.ds(pl.multiple_of(m * HW, HW), HW)], heads_ref.at[:, mine],
            send.at[i], recv.at[i], peer,
        ))
    moves.append(pltpu.make_async_copy(
        in_ref.at[pl.ds(pl.multiple_of(me * HW, HW), HW)], heads_ref.at[:, mine], lsem.at[0]
    ))
    for c in moves:
        c.start()
    count, width = i_ref.shape[1:]
    half = width // 2
    tiles = gv.shape[1]
    shards = SPAN * groups
    one = width // shards
    down = ds.shape[1]

    def load(i, src, dst):
        return pltpu.make_async_copy(src, dst, isem.at[i])

    def tile(ref, j, buf, base):
        return load(base + j, ref.at[:, j], buf.at[:, j])

    few = [load(i, a, b) for i, (a, b) in enumerate(((m_ref, mv), (a_ref, av), (b_ref, bv), (i_ref, iv)))]
    few[0].start()
    for j in range(tiles):
        tile(h_ref, j, hv, 4).start()
    for c in few[1:]:
        c.start()
    for j in range(tiles):
        tile(g_ref, j, gv, 4 + tiles).start()
    few[0].wait()

    def downward(j, _):
        tile(h_ref, j, hv, 4).wait()
        r = tn(hv[0, j], mv[0]) + tn(hv[1, j], mv[1])
        ds[pl.ds(j * (width // down), width // down)] = r.astype(bf).reshape(width // down, down, half)
        return 0

    lax.fori_loop(0, tiles, downward, 0)
    for c in few[1:] + around:
        c.wait()
    line[0] = (gain_ref[...] + plane[0]) + (plane[1] + plane[2])
    ring = [
        remote(line.at[0], line.at[1 + k], nsend.at[3 + k], nrecv.at[3 + k], q) for k, q in enumerate(others)
    ]
    for c in ring:
        c.start()
    r = nn(av[0], bv[0]) + nn(av[1], bv[1])
    os[...] = r.astype(bf).reshape(shards, one, half)
    for i in range(2):
        it[:, i * count : (i + 1) * count] = iv[i].T
    fours = lambda ref, n: ref.reshape(groups, 2, 2, n, half)

    def put(i, src, dst):
        return pltpu.make_async_copy(src, dst, osem.at[i])

    outs = []
    for i, (ref, k) in enumerate(((sb_ref, 1 - y), (kb_ref, y))):
        outs.append(put(4 * i, fours(ds, down).at[:, k], ref.at[:, :, pl.ds(0, down)]))
        outs.append(put(4 * i + 1, fours(os, one).at[:, k], ref.at[:, :, pl.ds(down, one)]))
    for c in outs:
        c.start()

    sideways = sa_ref.shape[2] // one

    def top(j):
        if j < sideways:
            rows = pl.ds(j * one, one)
            piece = fours(gs.at[j], one)
            went, kept = (piece.at[:, :, 1 - x], sa_ref), (piece.at[:, :, x], ka_ref)
        else:
            rows = pl.ds((j - sideways) * one, one)
            piece = gs.at[j].reshape(groups // 2, 2, SPAN, one, half)
            went, kept = (piece.at[:, 1 - level], sc_ref), (piece.at[:, level], kc_ref)
        return (
            put(8 + j, went[0], went[1].at[:, :, rows]),
            put(8 + 2 * tiles + j, kept[0], kept[1].at[:, :, rows]),
        )

    for j in range(tiles):
        tile(g_ref, j, gv, 4 + tiles).wait()
        r = (nn(it[:, :count], gv[0, j]) + nn(it[:, count:], gv[1, j])).astype(bf)
        for h in range(2):
            k = 2 * j + h
            gs[k] = r[:, h * half : (h + 1) * half].reshape(shards, one, half)
            outs.extend(top(k))
            for c in outs[-2:]:
                c.start()
    for c in ring:
        c.wait()
    total = line[0]
    for k in range(1, groups):
        total = total + line[k]
    line[groups] = total
    last = remote(line.at[groups], line.at[groups + 1], nsend.at[2 + groups], nrecv.at[2 + groups], sibling)
    last.start()
    last.wait()
    sum_ref[...] = line[groups] + line[groups + 1]
    for c in outs + moves:
        c.wait()


def weight_grads(groups, grad_heads, gains, inner, grads, hidden, grad_mlp, attended, grad_branch):
    count, width = inner.shape[1:]
    half = width // 2
    shards = SPAN * groups
    one = width // shards
    tiles = grads.shape[1]
    down = tiles * one
    ra = (2 * tiles - UPWARD) * one
    rb = down + one
    part = lambda r: jax.ShapeDtypeStruct((groups, 2, r, half), bf)
    level = jax.ShapeDtypeStruct((groups // 2, SPAN, UPWARD * one, half), bf)
    vm = lambda *n: pltpu.VMEM(n, bf)
    return pl.pallas_call(
        functools.partial(weights_kernel, groups),
        out_shape=(
            part(ra), part(ra), part(rb), part(rb), level, level,
            jax.ShapeDtypeStruct((HW, SPAN * grad_heads.shape[1]), bf), jax.ShapeDtypeStruct(gains.shape, f32),
        ),
        in_specs=[ANY] * 6 + [VM] * 2,
        out_specs=(ANY,) * 7 + (VM,),
        scratch_shapes=[
            vm(2, count, width), vm(width, 2 * count), vm(2, tiles, count, width), vm(2, tiles, count, width),
            vm(2, count, half), vm(2, width, count), vm(2, count, half),
            vm(2 * tiles, shards, one, half), vm(shards, down, half), vm(shards, one, half),
            pltpu.VMEM((3,) + gains.shape, f32), pltpu.VMEM((groups + 2,) + gains.shape, f32),
            dma_sems(4 + 2 * tiles), dma_sems(8 + 4 * tiles), dma_sems(3), dma_sems(3), dma_sems(1),
            dma_sems(3 + groups), dma_sems(3 + groups),
        ],
        compiler_params=comm_params(2),
        name="weight_grads",
        cost_estimate=pl.CostEstimate(
            flops=int(2 * 2 * count * half * width * 8.5), bytes_accessed=30 << 20, transcendentals=0
        ),
    )(inner, grads, hidden, grad_mlp, attended, grad_branch, grad_heads, gains)


def add_rows(dst, a, b, rows):
    step = rows // 3 if rows % 48 == 0 and rows > 48 else rows

    def part(i, _):
        sl = pl.ds(pl.multiple_of(i * step, step), step)
        dst[sl, :] = a[sl, :] + b[sl, :]
        return 0

    lax.fori_loop(0, rows // step, part, 0)


class Line:
    def __init__(self, z, zt, groups, part, up, down, sems, t, p):
        self.z, self.zt, self.groups = z, zt, groups
        self.part, self.up, self.down = part, up, down
        us, ur, ds, dr = sems
        above = (t, lax.rem(p + SPAN, SPAN * groups))
        below = (t, lax.rem(p + SPAN * (groups - 1), SPAN * groups))
        self.up_first = lambda: remote(part, up, us, ur, above)
        self.up_next = lambda: remote(up, up, us, ur, above)
        self.down_first = lambda: remote(part, down, ds, dr, below)
        self.down_next = lambda: remote(down, down, ds, dr, below)

    def start(self):
        if self.zt > 0:
            pl.when(self.z == 0)(lambda: self.up_first().start())
        if self.zt < self.groups - 1:
            pl.when(self.z == self.groups - 1)(lambda: self.down_first().start())

    def relay(self, hop, rows):
        def up():
            self.up_next().wait_recv()
            add_rows(self.up, self.up, self.part, rows)
            self.up_next().start()

        def down():
            self.down_next().wait_recv()
            add_rows(self.down, self.down, self.part, rows)
            self.down_next().start()

        if 0 < hop < self.zt:
            pl.when(self.z == hop)(up)
        if self.zt < self.groups - 1 - hop:
            pl.when(self.z == self.groups - 1 - hop)(down)

    def finish(self, dst, rows):
        def done():
            if self.zt > 0:
                self.up_next().wait_recv()
            if self.zt < self.groups - 1:
                self.down_next().wait_recv()
            if 0 < self.zt < self.groups - 1:
                add_rows(self.up, self.up, self.down, rows)
            add_rows(dst, self.up if self.zt > 0 else self.down, self.part, rows)

        pl.when(self.z == self.zt)(done)

    def drain(self):
        if self.zt > 0:
            pl.when(self.z < self.zt)(lambda: self.up_first().wait_send())
        if self.zt < self.groups - 1:
            pl.when(self.z > self.zt)(lambda: self.down_first().wait_send())


def outward(groups):
    order = []
    lo, hi = 0, groups - 1
    while lo <= hi:
        order.append(hi)
        if lo < hi:
            order.append(lo)
        lo, hi = lo + 1, hi - 1
    return order


def finish_kernel(
    groups, ka_ref, kb_ref, kc_ref, ra_ref, rb_ref, rc_ref, wq_ref, gh_ref, gin_ref, tin_ref,
    pair_ref, tg_ref, out_ref,
    kvc, rvc, r2c, r3c, r4c, csem, cs, cr, kva, kvb, rva, rvb, r2a, r2b, ua, ub, da, db, isem, s2, q2, us, ur, ds, dr,
    gm_ref, wq, gh, g_ref, tok_ref, wsem, fs, fr,
    w2, sib, ub2, db2, fin, send, recv, ts, tr, us2, ur2, ds2, dr2, ps, pr, lsem,
):
    t, p, x, y, z = here()
    ex, ey, ed = plane_peers()
    peers = (ex, ey, ed)
    sibling = (1 - t, p)
    others = [(t, lax.rem(p + SPAN * k, SPAN * groups)) for k in range(1, groups)]
    across = tuple((1 - t, q[1]) for q in peers)
    order = outward(groups)
    colours = (
        (ey, ka_ref, ra_ref, kva, rva, r2a, ua, da, y),
        (ex, kb_ref, rb_ref, kvb, rvb, r2b, ub, db, x),
    )

    def loads(c, zt):
        peer, kr, rr, kv, rv = colours[c][:5]
        i = 2 * (c * groups + zt)
        return (
            pltpu.make_async_copy(kr.at[zt], kv.at[zt], isem.at[i]),
            pltpu.make_async_copy(rr.at[zt], rv.at[zt], isem.at[i + 1]),
        )

    level_loads = [
        [pltpu.make_async_copy(a.at[i], b.at[i], csem.at[2 * i + j]) for j, (a, b) in enumerate(((kc_ref, kvc), (rc_ref, rvc)))]
        for i in range(2)
    ]
    for pair in level_loads:
        for d in pair:
            d.start()
    mixed_loads = (pltpu.make_async_copy(gin_ref, g_ref, wsem.at[2]), pltpu.make_async_copy(tin_ref, tok_ref, wsem.at[3]))
    for i, zt in enumerate(order):
        for c in range(2):
            for d in loads(c, zt):
                d.start()
        if i == 1:
            for c in mixed_loads:
                c.start()
    more = (pltpu.make_async_copy(wq_ref, wq, wsem.at[0]), pltpu.make_async_copy(gh_ref, gh, wsem.at[1]))
    for c in more:
        c.start()
    greet(peers + across + (sibling,) + tuple(others))

    def second(c, zt):
        peer, kr, rr, kv, rv, r2, u, d, mine = colours[c]
        i = c * groups + zt
        return remote(rv.at[zt, 1 - mine], r2.at[zt], s2.at[i], q2.at[i], peer)

    def chain(c, zt):
        peer, kr, rr, kv, rv, r2, u, d, mine = colours[c]
        i = c * groups + zt
        return Line(z, zt, groups, r2.at[zt], u.at[zt], d.at[zt],
                    (us.at[i], ur.at[i], ds.at[i], dr.at[i]), t, p)

    def size(c):
        return colours[c][3].shape[2]

    up = kvc.shape[2]

    def third(i, k):
        at = (k * 2 + 1 - x, (1 - y) * 2 + k)[i]
        n = 2 * i + k
        return remote(rvc.at[i, at], r2c.at[i, k], cs.at[n], cr.at[n], (ex, ey)[i])

    def fourth(i):
        at = (1 - y, 1 - x)[i]
        return remote(r2c.at[i, at], r3c.at[i], cs.at[4 + i], cr.at[4 + i], (ey, ex)[i])

    top = lax.div(z, 2)
    fifth = remote(r3c.at[1 - top], r4c, cs.at[6], cr.at[6], (t, p + 2 * SPAN - 4 * SPAN * top))

    def plus(dst, src, n):
        add_rows(dst, dst, src, n)

    def send_second(zt):
        for c in range(2):
            for d in loads(c, zt):
                d.wait()
            peer, kr, rr, kv, rv, r2, u, d, mine = colours[c]
            plus(rv.at[zt, 1 - mine], kv.at[zt, 1 - mine], size(c))
            second(c, zt).start()

    for i in range(2):
        for d in level_loads[i]:
            d.wait()
        for k in range(2):
            at = (k * 2 + 1 - x, (1 - y) * 2 + k)[i]
            plus(rvc.at[i, at], kvc.at[i, at], up)
            third(i, k).start()
    send_second(order[0])
    send_second(order[1])
    width = gm_ref.shape[0] // 3
    shards = SPAN * groups
    one = width // shards
    half = width // 2
    for c in mixed_loads:
        c.wait()
    for h in range(2):
        r = nn(g_ref[...], tok_ref[:, h * half : (h + 1) * half]).T
        w2[h * (shards // 2) : (h + 1) * (shards // 2)] = r.astype(bf).reshape(shards // 2, one, 3 * HW)

    def swap(zt):
        return remote(w2.at[pl.ds(zt * 4 + (1 - t) * 2, 2)], sib.at[zt], ts.at[zt], tr.at[zt], sibling)

    for zt in order:
        swap(zt).start()

    for i in range(2):
        for k in range(2):
            at = (k * 2 + x, y * 2 + k)[i]
            plus(rvc.at[i, at], kvc.at[i, at], up)
            third(i, k).wait_recv()
            plus(r2c.at[i, k], rvc.at[i, at], up)
        fourth(i).start()
    send_second(order[2])
    send_second(order[3])
    count = gm_ref.shape[1]
    me = lax.rem(p, SPAN)
    copies = []
    for i, peer in enumerate((peers[2], peers[0], peers[1])):
        m = lax.rem(peer[1], SPAN)
        for k in range(3):
            copies.append(remote(
                g_ref.at[pl.ds(k * HW, HW), pl.ds(pl.multiple_of(m * count, count), count)],
                gm_ref.at[pl.ds(pl.multiple_of(k * width + me * HW, HW), HW)],
                send.at[i * 3 + k], recv.at[i * 3 + k], peer,
            ))
    for k in range(3):
        copies.append(pltpu.make_async_copy(
            g_ref.at[pl.ds(k * HW, HW), pl.ds(pl.multiple_of(me * count, count), count)],
            gm_ref.at[pl.ds(pl.multiple_of(k * width + me * HW, HW), HW)],
            lsem.at[k],
        ))
    for c in copies:
        c.start()
    def chain2(zt, k):
        i = zt * 2 + k
        return Line(z, zt, groups, sib.at[zt, k], ub2.at[zt, k], db2.at[zt, k],
                    (us2.at[i], ur2.at[i], ds2.at[i], dr2.at[i]), t, p)

    for zt in order:
        swap(zt).wait_recv()
        for k in range(2):
            dst = sib.at[zt, k]
            add_rows(dst, dst, w2.at[zt * 4 + t * 2 + k], one)
            chain2(zt, k).start()
    for zt in order:
        for c in range(2):
            peer, kr, rr, kv, rv, r2, u, d, mine = colours[c]
            keep = rv.at[zt, mine]
            add_rows(keep, keep, kv.at[zt, mine], size(c))

    def in_plane(zt):
        for c in range(2):
            peer, kr, rr, kv, rv, r2, u, d, mine = colours[c]
            second(c, zt).wait_recv()
            dst = r2.at[zt]
            add_rows(dst, dst, rv.at[zt, mine], size(c))
            chain(c, zt).start()

    def relay(zt, hop):
        for c in range(2):
            chain(c, zt).relay(hop, size(c))


    def relay2(hop):
        for zt in order:
            for k in range(2):
                chain2(zt, k).relay(hop, one)

    in_plane(order[0])
    relay2(1)
    in_plane(order[1])
    for i in range(2):
        fourth(i).wait_recv()
        plus(r3c.at[i], r2c.at[i, (y, x)[i]], up)
    fifth.start()
    relay(order[0], 1)
    relay2(2)
    in_plane(order[2])
    relay(order[1], 1)
    in_plane(order[3])
    relay(order[0], 2)
    relay(order[2], 1)
    relay(order[1], 2)
    relay(order[3], 1)
    for zt in order:
        for k in range(2):
            chain2(zt, k).finish(fin.at[k], one)
    here_id = t * SPAN + me

    def hand(k, tt):
        m = t * 2 + k
        peer = (tt, z * SPAN + m)
        i = k * 2 + tt
        away = lambda: remote(fin.at[k], out_ref.at[me], ps.at[i], pr.at[me], peer)
        stay = lambda: pltpu.make_async_copy(fin.at[k], out_ref.at[me], lsem.at[3])
        return away, stay, (tt * SPAN + m) == here_id

    for k in range(2):
        for tt in range(2):
            away, stay, same = hand(k, tt)
            pl.when(jnp.logical_not(same))(lambda away=away: away().start())
            pl.when(same)(lambda stay=stay: stay().start())
    fifth.wait_recv()
    add_rows(pair_ref.at[t, pl.ds(size(0) + size(1), up)], r3c.at[top], r4c, up)
    for zt in order:
        for c, sl in ((0, pl.ds(0, size(0))), (1, pl.ds(size(0), size(1)))):
            chain(c, zt).finish(pair_ref.at[t, sl], size(c))
    last = remote(pair_ref.at[t], pair_ref.at[t], fs.at[0], fr.at[0], sibling)
    last.start()
    for c in copies + list(more):
        c.wait()
    turned = nn(wq[...], gm_ref[...]).T
    tg_ref[...] = gh[...] + turned
    for s in range(SPAN):
        from_here = jnp.logical_and(s == me, y == t)
        pl.when(jnp.logical_not(from_here))(
            lambda s=s: remote(fin.at[0], out_ref.at[s], ps.at[0], pr.at[s], sibling).wait_recv()
        )
    for k in range(2):
        for tt in range(2):
            away, stay, same = hand(k, tt)
            pl.when(jnp.logical_not(same))(lambda away=away: away().wait_send())
            pl.when(same)(lambda stay=stay: stay().wait())
    for zt in range(groups):
        swap(zt).wait_send()
        for k in range(2):
            chain2(zt, k).drain()
        for c in range(2):
            second(c, zt).wait_send()
            chain(c, zt).drain()
    for i in range(2):
        for k in range(2):
            third(i, k).wait_send()
        fourth(i).wait_send()
    fifth.wait_send()
    last.wait()


def finish(ka, kb, kc, ra, rb, rc, wq, gh, g, tok, groups):
    width = tok.shape[1]
    count = tok.shape[0] // SPAN
    one = width // (SPAN * groups)
    na, nb, nc = ka.shape[2], kb.shape[2], kc.shape[2]
    half = ka.shape[3]
    buf = lambda *n: pltpu.VMEM(n, bf)
    mix = lambda *n: pltpu.VMEM(n + (one, 3 * HW), bf)
    return pl.pallas_call(
        functools.partial(finish_kernel, groups),
        out_shape=(
            jax.ShapeDtypeStruct((2, na + nb + nc, half), bf),
            jax.ShapeDtypeStruct((count, width), f32),
            jax.ShapeDtypeStruct((SPAN, one, 3 * HW), bf),
        ),
        in_specs=[ANY] * 10,
        out_specs=(VM,) * 3,
        scratch_shapes=[
            buf(2, SPAN, nc, half), buf(2, SPAN, nc, half), buf(2, 2, nc, half), buf(2, nc, half), buf(nc, half),
            dma_sems(4), dma_sems(7), dma_sems(7),
            buf(groups, 2, na, half), buf(groups, 2, nb, half), buf(groups, 2, na, half), buf(groups, 2, nb, half),
            buf(groups, na, half), buf(groups, nb, half), buf(groups, na, half), buf(groups, nb, half),
            buf(groups, na, half), buf(groups, nb, half),
            dma_sems(4 * groups), dma_sems(2 * groups), dma_sems(2 * groups),
            dma_sems(2 * groups), dma_sems(2 * groups), dma_sems(2 * groups), dma_sems(2 * groups),
            buf(3 * width, count), buf(width, 3 * width), pltpu.VMEM((count, width), f32),
            buf(*g.shape), buf(*tok.shape), dma_sems(4),
            dma_sems(1), dma_sems(1),
            mix(SPAN * groups), mix(groups, 2), mix(groups, 2), mix(groups, 2), mix(2),
            dma_sems(9), dma_sems(9), dma_sems(groups), dma_sems(groups),
            dma_sems(2 * groups), dma_sems(2 * groups), dma_sems(2 * groups), dma_sems(2 * groups),
            dma_sems(4), dma_sems(SPAN), dma_sems(4),
        ],
        compiler_params=comm_params(3),
        name="finish",
    )(ka, kb, kc, ra, rb, rc, wq, gh, g, tok)


def unfold_kernel(
    groups, pair_ref, part_ref, grad_ref, score_ref, gain_ref, lost_ref,
    gate_ref, up_ref, down_ref, out_ref, qkv_ref, token_ref, scores_ref, loss_ref, *gains_refs,
):
    one = out_ref.shape[0]
    half = pair_ref.shape[2]
    width = 2 * half
    steps = gate_ref.shape[1] // half
    down = down_ref.shape[0]
    token_ref[0] = grad_ref[...]
    top = (steps - UPWARD) * one
    for j in range(steps):
        at = j * one + (0 if j < steps - UPWARD else down + one)
        for k, ref in enumerate((gate_ref, up_ref)):
            ref[:, j * half : (j + 1) * half] = pair_ref[k, at : at + one, :].astype(f32)
    for k in range(2):
        cols = slice(k * half, (k + 1) * half)
        down_ref[:, cols] = pair_ref[k, top : top + down, :].astype(f32)
        out_ref[:, cols] = pair_ref[k, top + down : top + down + one, :].astype(f32)
    for k in range(3):
        row = [part_ref[s, :, k * HW : (k + 1) * HW].astype(f32) for s in range(SPAN)]
        qkv_ref[:, k * width : (k + 1) * width] = jnp.concatenate(row, 1)
    docs, size = scores_ref.shape[0], score_ref.shape[0]
    dot = functools.partial(lax.dot_general, precision=precise, preferred_element_type=f32)
    row = lax.broadcasted_iota(jnp.int32, (docs, size), 0)
    col = lax.broadcasted_iota(jnp.int32, (docs, size), 1)
    pick = jnp.where(row // DOCS_GRP * 8 + lax.rem(row, DOCS_GRP) == col, 1.0, 0.0)
    some = dot(pick, score_ref[...], (((1,), (0,)), ((), ())))
    scores_ref[...] = dot(some, pick, (((1,), (1,)), ((), ())))
    row = lax.broadcasted_iota(jnp.int32, (width, one), 0)
    col = lax.broadcasted_iota(jnp.int32, (width, one), 1)
    mine = jnp.where(row == lax.axis_index("dp") * one + col, 1.0, 0.0)
    gains = dot(gain_ref[...], mine, (((1,), (0,)), ((), ())))
    for k, ref in enumerate(gains_refs):
        ref[...] = gains[k : k + 1, :]
    loss_ref[...] = lost_ref[0:1, 0:1]


def unfold(pair, parts, grad, scores, gains, loss, tiles, groups):
    one = parts.shape[1]
    half = pair.shape[2]
    width = 2 * half
    docs = groups * DOCS_GRP
    sds = jax.ShapeDtypeStruct
    return pl.pallas_call(
        functools.partial(unfold_kernel, groups),
        out_shape=(
            sds((one, tiles * width), f32), sds((one, tiles * width), f32), sds((tiles * one, width), f32),
            sds((one, width), f32), sds((one, 3 * width), f32), sds((1,) + grad.shape, f32),
            sds((docs, docs), f32), sds((1, 1), f32),
        )
        + (sds((1, one), f32),) * 4,
        in_specs=[VM] * 6,
        out_specs=(VM,) * 12,
        name="unfold",
    )(pair, parts, grad, scores, gains, loss)


def angle_tables(total):
    half = HEAD_DIM // 2
    freqs = np.float32(1000.0) ** (-np.arange(half, dtype=np.float32) / np.float32(half))
    theta = freqs[:, None].astype(np.float32) * np.arange(total, dtype=np.float32)[None, :]
    return np.cos(theta).astype(np.float32), np.sin(theta).astype(np.float32)


def spread_sum(value):
    part = lax.psum_scatter(value, "dp", scatter_dimension=0, tiled=True)
    return lax.psum(part.astype(bf), "tower").astype(f32)


def local(
    tokens, doc_ids, pad_mask, targets, w_qkv, w_out, ln1_gain, ln1_bias,
    w_gate, w_up, w_down, ln2_gain, ln2_bias,
):
    width = w_out.shape[0]
    rows = tokens[0]
    count = rows.shape[0]
    places = lax.axis_size("dp")
    groups = places // SPAN
    tower = lax.axis_index("tower")
    place = lax.axis_index("dp")
    me = place % SPAN
    docs = groups * DOCS_GRP
    cos, sin = angle_tables(SPAN * count)
    tok_all, codes, qa, ka, va, kt, heads, lse, exact = gather(rows, doc_ids, pad_mask, cos, sin, w_qkv)
    norms = (ln1_gain, ln1_bias, ln2_gain, ln2_bias)
    (
        attended, inner, hidden, grad_mlp, grads, grad_branch, grad_attended, grad_h1, gains, scores_all, loss
    ) = block(heads, rows, codes, targets, norms, w_out, w_gate, w_up, w_down, groups)
    by_hand = groups == 4 and width % (16 * places) == 0
    if by_hand:
        send_a, keep_a, send_b, keep_b, send_c, keep_c, d_heads, gain_sums = weight_grads(
            groups, grad_attended, gains, inner, grads, hidden, grad_mlp, attended, grad_branch
        )
        exchange = lambda v, bit: lax.ppermute(v, "dp", [(i, i ^ bit) for i in range(places)])
        came_a, came_b, came_c = exchange(send_a, 1), exchange(send_b, 2), exchange(send_c, SPAN)
    else:
        d_heads = tokens_to_heads(grad_attended, 5, "to_heads")
    mixed = attn_bwd(d_heads, exact, lse, qa, ka, va, kt, cos, sin, codes)
    if by_hand:
        pair, grad_tokens, qkv_parts = finish(
            keep_a, keep_b, keep_c, came_a, came_b, came_c, w_qkv, grad_h1, mixed, tok_all, groups
        )
        gate_out, up_out, down_out, out_out, qkv_out, token_grad, scores, loss, *gains_out = unfold(
            pair, qkv_parts, grad_tokens, scores_all, gain_sums, loss, w_gate.shape[1] // width, groups
        )
        gains_out = [v.reshape(-1) for v in gains_out]
    else:
        grad_mixed = heads_to_tokens(mixed, 6, "to_tokens_back")
        qkv_out = spread_sum(tn(rows, grad_mixed.T))
        side = lambda v: lax.psum_scatter(v, "dp", scatter_dimension=0, tiled=True)
        halves = lambda v: lax.all_gather(side(v).astype(bf), "tower", axis=1, tiled=True).astype(f32)
        both = lambda a, b: tn(a[0], b[0]) + tn(a[1], b[1])
        flat = lambda v: v.transpose(0, 2, 1, 3).reshape(2, count, -1)
        out_out = halves(nn(attended[0], grad_branch[0]) + nn(attended[1], grad_branch[1]))
        two = lax.all_gather(side(both(inner, flat(grads))).astype(bf), "tower").astype(f32)
        gate_out, up_out = two[0], two[1]
        down_out = halves(both(flat(hidden), grad_mlp))
        gains_out = spread_sum(gains[:4].T).T
        scores = scores_all.reshape(groups, 8, groups, 8)[:, :DOCS_GRP, :, :DOCS_GRP].reshape(docs, docs)
        token_grad = grad_h1 + lax.dot_general(
            grad_mixed, w_qkv, (((0,), (1,)), ((), ())), preferred_element_type=f32
        )
        token_grad = token_grad[None]
    return (
        scores, loss[0, 0], token_grad, qkv_out, out_out, gains_out[0], gains_out[1],
        gate_out, up_out, down_out, gains_out[2], gains_out[3],
    )


def solution(mesh):
    shard = P("dp", None)
    lone = P("dp")
    return jax.shard_map(
        local,
        mesh=mesh,
        in_specs=(P("tower", "dp", None), P("tower", "dp"), P("tower", "dp")) + (P(),) * 10,
        out_specs=(
            P(), P(), P("tower", "dp", None), shard, shard, lone, lone, shard, shard, shard, lone, lone,
        ),
        check_vma=False,
    )
```

```python
import functools

import jax
import jax.numpy as jnp
import numpy as np
from jax import lax
from jax.experimental import pallas as pl
from jax.experimental.pallas import tpu as pltpu
from jax.sharding import PartitionSpec as P

HEADS = 12
HEAD_DIM = 64
SPAN = 4
DOCS_GRP = 3
NH = HEADS // SPAN
HW = NH * HEAD_DIM
UPWARD = 3
VLIM = 62 * 2**20
MESH = pl.DeviceIdType.MESH
f32 = jnp.float32
bf = jnp.bfloat16
precise = lax.Precision.HIGHEST
norm_eps = 1e-05
ANY = pl.BlockSpec(memory_space=pl.ANY)
VM = pl.BlockSpec(memory_space=pltpu.VMEM)


def nn(a, b):
    return lax.dot_general(a, b, (((1,), (0,)), ((), ())), preferred_element_type=f32)


def nt(a, b):
    return lax.dot_general(a, b, (((1,), (1,)), ((), ())), preferred_element_type=f32)


def tn(a, b):
    return lax.dot_general(a, b, (((0,), (0,)), ((), ())), preferred_element_type=f32)


def split3(v):
    one = v.astype(bf).astype(f32)
    rest = v - one
    two = rest.astype(bf).astype(f32)
    return [one, two, rest - two]


def here():
    t = lax.axis_index("tower")
    p = lax.axis_index("dp")
    x = lax.rem(p, 2)
    y = lax.rem(lax.div(p, 2), 2)
    return t, p, x, y, lax.div(p, SPAN)


def plane_peers():
    t, p, x, y, g = here()
    px = p + 1 - 2 * x
    py = p + 2 - 4 * y
    pd = px + 2 - 4 * y
    return (t, px), (t, py), (t, pd)


def hail(peers):
    for peer in peers:
        pl.semaphore_signal(pltpu.get_barrier_semaphore(), inc=1, device_id=peer, device_id_type=MESH)


def greeted(peers):
    pl.semaphore_wait(pltpu.get_barrier_semaphore(), len(peers))


def greet(peers):
    hail(peers)
    greeted(peers)


def remote(src, dst, send, recv, peer):
    return pltpu.make_async_remote_copy(
        src_ref=src, dst_ref=dst, send_sem=send, recv_sem=recv, device_id=peer, device_id_type=MESH
    )


def dma_sems(n):
    return pltpu.SemaphoreType.DMA((n,))


def comm_params(cid):
    return pltpu.CompilerParams(collective_id=cid, has_side_effects=True, vmem_limit_bytes=VLIM)


def fill_angles(base_ref, cos_ref, sin_ref):
    for i in range(cos_ref.shape[1] // 128):
        at = slice(i * 128, (i + 1) * 128)
        ca, sa = base_ref[0, :, i : i + 1], base_ref[1, :, i : i + 1]
        cb, sb = base_ref[2], base_ref[3]
        cos_ref[:, at] = ca * cb - sa * sb
        sin_ref[:, at] = sa * cb + ca * sb


def gather_kernel(
    tok_ref, ids_ref, pads_ref, base_ref, w_ref, out_ref, codes_ref, qa_ref, ka_ref, va_ref, kt_ref,
    att_ref, lse_ref, exact_ref,
    cos_ref, sin_ref, toks, code_ref, codes, wraw, wturn, wt, qa, ka, va, kt, acc, tops, sooner, later, heads,
    send, recv, csend, crecv, wsem, osem, asend, arecv, asem,
):
    t, p, x, y, g = here()
    count, width = tok_ref.shape
    half = count // 2
    me = lax.rem(p, SPAN)
    odd = lax.rem(me, 2)
    wide = wraw.shape[2]
    loads = []
    for k in range(3):
        at = pl.multiple_of(k * width + me * HW - odd * HEAD_DIM, 128)
        loads.append(pltpu.make_async_copy(w_ref.at[:, pl.ds(at, wide)], wraw.at[k], wsem.at[k]))
        loads[-1].start()
    code_ref[...] = lax.rem(ids_ref[...], DOCS_GRP).astype(f32) + 4.0 * (1 - pads_ref[...]).astype(f32)
    ex, ey, ed = plane_peers()
    mx, my, md = (lax.rem(q[1], SPAN) for q in (ex, ey, ed))

    def rows(m, h):
        return pl.ds(pl.multiple_of(m * count + h * half, half), half)

    def whole(m):
        return pl.ds(pl.multiple_of(m * count, count), count)

    greet((ex, ey, ed))
    first = []
    for i, (peer, h) in enumerate(((ex, 0), (ey, 1), (ex, 1), (ey, 0))):
        c = remote(tok_ref.at[pl.ds(h * half, half)], toks.at[rows(me, h)], send.at[i], recv.at[i], peer)
        c.start()
        first.append(c)
    small = []
    for i, peer in enumerate((ex, ey, ed)):
        c = remote(code_ref, codes.at[:, whole(me)], csend.at[i], crecv.at[i], peer)
        c.start()
        small.append(c)
    codes[:, whole(me)] = code_ref[...]
    fill_angles(base_ref, cos_ref, sin_ref)
    for k in range(3):
        loads[k].wait()
        wturn[...] = wraw[k].T
        wt[k * HW : (k + 1) * HW, :] = wturn[pl.ds(pl.multiple_of(odd * HEAD_DIM, HEAD_DIM), HW), :]

    def project(rows_ref, m, n):
        sl = whole(m)
        mx = nt(wt[...], rows_ref[...])
        cos, sin = cos_ref[:, sl], sin_ref[:, sl]
        cd = codes[:, sl]
        mem = jnp.where(cd >= 4.0, cd - 4.0, cd)
        pad = [jnp.zeros((13, count), f32)]
        hot = jnp.concatenate([jnp.where(mem == float(d), 1.0, 0.0) for d in range(DOCS_GRP)] + pad, 0)
        neg = jnp.concatenate([jnp.where(cd == float(d), 0.0, -1e30) for d in range(DOCS_GRP)] + pad, 0)
        rest = jnp.zeros((48, count), f32)
        one = jnp.concatenate([jnp.ones((1, count), f32), jnp.zeros((63, count), f32)], 0)

        def rope(u):
            a, b = u[:32], u[32:]
            return jnp.concatenate([a * cos - b * sin, b * cos + a * sin], 0)

        for h in range(NH):
            q = rope(mx[h * HEAD_DIM : (h + 1) * HEAD_DIM]).astype(bf).astype(f32) * 0.125
            k = rope(mx[HW + h * HEAD_DIM : HW + (h + 1) * HEAD_DIM])
            v = mx[2 * HW + h * HEAD_DIM : 2 * HW + (h + 1) * HEAD_DIM]
            qa[h, :, sl] = jnp.concatenate([q, hot, rest], 0).astype(bf)
            ka[h, sl, :] = jnp.concatenate([k, neg, rest], 0).T.astype(bf)
            va[h, :, sl] = jnp.concatenate([v, one], 0).astype(bf)
            kt[h, :, sl] = k.astype(bf)
        puts = (
            (rows_ref, out_ref.at[sl]),
            (qa.at[:, :, sl], qa_ref.at[:, :, sl]),
            (ka.at[:, sl, :], ka_ref.at[:, sl, :]),
            (va.at[:, :, sl], va_ref.at[:, :, sl]),
            (kt.at[:, :, sl], kt_ref.at[:, :, sl]),
        )
        puts = [pltpu.make_async_copy(a, b, osem.at[5 * n + i]) for i, (a, b) in enumerate(puts)]
        for c in puts:
            c.start()
        return puts

    part = count // 2
    acc[...] = jnp.zeros_like(acc)
    tops[...] = jnp.full_like(tops, -3e38)
    chunks = (me, mx, my, md)
    inside = jnp.where((me == 1) | (me == 2), 1, 0)

    def pick(n, values):
        got = values[-1]
        for i in reversed(range(len(values) - 1)):
            got = jnp.where(n == i, values[i], got)
        return got

    def segment(q, key_of, trips):
        qs = whole(q)

        def keys(n, k):
            return pl.ds(pl.multiple_of(key_of(n) * count + k * part, part), part)

        def scores(n, k, h, ref):
            ref[h] = nn(ka[h, keys(n, k), :], qa[h, :, qs])

        def absorb(n, k, h, ref, m):
            s = ref[h]
            mn = jnp.maximum(m, jnp.max(s, 0, keepdims=True))
            pr = jnp.exp(s - mn).astype(bf)
            acc[q, h] = acc[q, h] * jnp.exp(m - mn) + nn(va[h, :80, keys(n, k)], pr)
            return mn

        for h in range(NH):
            scores(0, 0, h, sooner)

        def step(n, ms):
            ms = list(ms)
            for h in range(NH):
                scores(n, 1, h, later)
                ms[h] = absorb(n, 0, h, sooner, ms[h])
            after = jnp.minimum(n + 1, jnp.maximum(trips - 1, 0))
            for h in range(NH):
                scores(after, 0, h, sooner)
                ms[h] = absorb(n, 1, h, later, ms[h])
            return tuple(ms)

        ms = lax.fori_loop(0, trips, step, tuple(tops[q * NH + h] for h in range(NH)))
        for h in range(NH):
            tops[q * NH + h] = ms[h]

    def finalize(q):
        qs = whole(q)
        edge = jnp.where((q == 0) | (q == SPAN - 1), 1.0, 0.0)
        other = whole(SPAN - 1 - q)
        for h in range(NH):
            m = tops[q * NH + h]
            rest = jnp.sum(va[h, :80, other].astype(f32), 1, keepdims=True)
            full = acc[q, h] + rest * jnp.where(m < -1e29, edge, 0.0)
            tot = full[64:65]
            o = full[:64] / tot
            at = pl.ds(h * HEAD_DIM, HEAD_DIM)
            exact_ref[at, qs] = o
            lse_ref[h : h + 1, qs] = jnp.where(m < -1e29, 0.0, m + jnp.log(tot))
            heads[at, qs] = o.astype(bf)

    done = project(tok_ref, me, 0)
    first[0].wait_recv()
    f0 = remote(toks.at[rows(mx, 0)], toks.at[rows(mx, 0)], send.at[4], recv.at[4], ey)
    f0.start()
    first[1].wait_recv()
    f1 = remote(toks.at[rows(my, 1)], toks.at[rows(my, 1)], send.at[5], recv.at[5], ex)
    f1.start()
    segment(me, lambda n: me, 1)
    for c in small:
        c.wait()
    first[2].wait_recv()
    done += project(toks.at[whole(mx)], mx, 1)
    first[3].wait_recv()
    done += project(toks.at[whole(my)], my, 2)

    def near(s, _):
        q = pick(s, chunks[:3])
        key_of = lambda n: pick(s, (pick(n, (mx, my)), pick(n, (me, mx, my)), pick(n, (me, my, mx))))
        segment(q, key_of, jnp.where(s == 0, 2, 3 - inside))
        return 0

    lax.fori_loop(0, 3, near, 0)
    f0.wait_recv()
    f1.wait_recv()
    done += project(toks.at[whole(md)], md, 3)

    def back(s):
        peer = (ed, ex, ey)[s]
        m = (md, mx, my)[s]
        return remote(
            heads.at[:, whole(m)], att_ref.at[pl.ds(pl.multiple_of(me * HW, HW), HW)], asend.at[s], arecv.at[s], peer
        )

    def far(s, _):
        q = pick(s, (md, mx, my, me))
        key_of = lambda n: jnp.where(s == 0, pick(n, (mx, my, md, me)), md)
        segment(q, key_of, pick(s, (3 + inside, 1, 1, inside)))
        finalize(q)
        for k in range(3):
            pl.when(s == k)(lambda k=k: back(k).start())
        return 0

    lax.fori_loop(0, 4, far, 0)
    own = pltpu.make_async_copy(
        heads.at[:, whole(me)], att_ref.at[pl.ds(pl.multiple_of(me * HW, HW), HW)], asem.at[0]
    )
    own.start()
    codes_ref[...] = codes[...]
    for c in first + [f0, f1]:
        c.wait_send()
    for c in done:
        c.wait()
    own.wait()
    for k in range(3):
        back(k).wait()


def gather(tok, ids, pads, base, w_qkv):
    count, width = tok.shape
    total = SPAN * count
    shapes = ((NH, 128, total), (NH, total, 128), (NH, 128, total), (NH, HEAD_DIM, total))
    return pl.pallas_call(
        gather_kernel,
        out_shape=(jax.ShapeDtypeStruct((total, width), bf), jax.ShapeDtypeStruct((1, total), f32))
        + tuple(jax.ShapeDtypeStruct(s, bf) for s in shapes)
        + (
            jax.ShapeDtypeStruct((SPAN * HW, count), bf), jax.ShapeDtypeStruct((NH, total), f32),
            jax.ShapeDtypeStruct((HW, total), f32),
        ),
        in_specs=[VM] * 4 + [ANY],
        out_specs=(ANY, VM) + (ANY,) * 5 + (VM,) * 2,
        scratch_shapes=[
            pltpu.VMEM((HEAD_DIM // 2, total), f32), pltpu.VMEM((HEAD_DIM // 2, total), f32),
            pltpu.VMEM((total, width), bf), pltpu.VMEM((1, count), f32), pltpu.VMEM((1, total), f32), pltpu.VMEM((3, width, 256), bf),
            pltpu.VMEM((256, width), bf), pltpu.VMEM((3 * HW, width), bf),
        ]
        + [pltpu.VMEM(s, bf) for s in shapes]
        + [
            pltpu.VMEM((SPAN, NH, 80, count), f32), pltpu.VMEM((SPAN * NH, 1, count), f32),
            pltpu.VMEM((NH, count // 2, count), f32), pltpu.VMEM((NH, count // 2, count), f32),
            pltpu.VMEM((HW, total), bf),
            dma_sems(6), dma_sems(6), dma_sems(3), dma_sems(3), dma_sems(3), dma_sems(20),
            dma_sems(3), dma_sems(3), dma_sems(1),
        ],
        compiler_params=comm_params(0),
        name="gather",
    )(tok, ids, pads, base, w_qkv)


def heads_to_tokens_kernel(parts, in_ref, out_ref, send, recv, lsem):
    t, p, x, y, g = here()
    count = out_ref.shape[1]
    me = lax.rem(p, SPAN)
    peers = plane_peers()
    width = parts and out_ref.shape[0] // parts
    greet(peers)
    copies = []
    for i, peer in enumerate((peers[2], peers[0], peers[1])):
        m = lax.rem(peer[1], SPAN)
        for k in range(parts):
            c = remote(
                in_ref.at[pl.ds(k * HW, HW), pl.ds(pl.multiple_of(m * count, count), count)],
                out_ref.at[pl.ds(pl.multiple_of(k * width + me * HW, HW), HW)],
                send.at[i * parts + k],
                recv.at[i * parts + k],
                peer,
            )
            c.start()
            copies.append(c)
    for k in range(parts):
        c = pltpu.make_async_copy(
            in_ref.at[pl.ds(k * HW, HW), pl.ds(pl.multiple_of(me * count, count), count)],
            out_ref.at[pl.ds(pl.multiple_of(k * width + me * HW, HW), HW)],
            lsem.at[k],
        )
        c.start()
        copies.append(c)
    for c in copies:
        c.wait()


def heads_to_tokens(a, cid, name):
    parts = a.shape[0] // HW
    count = a.shape[1] // SPAN
    return pl.pallas_call(
        functools.partial(heads_to_tokens_kernel, parts),
        out_shape=jax.ShapeDtypeStruct((parts * HEADS * HEAD_DIM, count), a.dtype),
        in_specs=[VM],
        out_specs=ANY,
        scratch_shapes=[dma_sems(3 * parts), dma_sems(3 * parts), dma_sems(parts)],
        compiler_params=comm_params(cid),
        name=name,
    )(a)


def tokens_to_heads_kernel(in_ref, out_ref, send, recv, lsem):
    t, p, x, y, g = here()
    count = in_ref.shape[1]
    me = lax.rem(p, SPAN)
    peers = plane_peers()
    greet(peers)
    mine = pl.ds(pl.multiple_of(me * count, count), count)
    copies = []
    for i, peer in enumerate((peers[2], peers[0], peers[1])):
        m = lax.rem(peer[1], SPAN)
        c = remote(
            in_ref.at[pl.ds(pl.multiple_of(m * HW, HW), HW)],
            out_ref.at[:, mine],
            send.at[i],
            recv.at[i],
            peer,
        )
        c.start()
        copies.append(c)
    c = pltpu.make_async_copy(
        in_ref.at[pl.ds(pl.multiple_of(me * HW, HW), HW)], out_ref.at[:, mine], lsem.at[0]
    )
    c.start()
    for c in copies + [c]:
        c.wait()


def tokens_to_heads(a, cid, name):
    return pl.pallas_call(
        tokens_to_heads_kernel,
        out_shape=jax.ShapeDtypeStruct((HW, SPAN * a.shape[1]), a.dtype),
        in_specs=[VM],
        out_specs=ANY,
        scratch_shapes=[dma_sems(3), dma_sems(3), dma_sems(1)],
        compiler_params=comm_params(cid),
        name=name,
    )(a)


def doc_limits(code):
    pad = code >= 4.0
    mem = jnp.where(pad, code - 4.0, code)
    n0 = jnp.sum(jnp.where(mem < 0.5, 1.0, 0.0)).astype(jnp.int32)
    n1 = jnp.sum(jnp.where(mem < 1.5, 1.0, 0.0)).astype(jnp.int32)
    l = [jnp.sum(jnp.where(code == float(d), 1.0, 0.0)).astype(jnp.int32) for d in range(3)]
    return n0, n1, l

def block_range(lims, a, size, total):
    n0, n1, l = lims
    b = a + size - 1
    first = (a >= n0).astype(jnp.int32) + (a >= n1).astype(jnp.int32)
    last = (b >= n0).astype(jnp.int32) + (b >= n1).astype(jnp.int32)
    lo = jnp.where(first == 0, 0, jnp.where(first == 1, n0, n1))
    hi = jnp.where(last == 0, n0, jnp.where(last == 1, n1, total))
    dead = jnp.zeros((), jnp.bool_)
    for d in range(3):
        dead = dead | ((first <= d) & (d <= last) & (l[d] == 0))
    return jnp.where(dead, 0, lo), jnp.where(dead, total, hi)

def bwd_kernel(KB, QB, do_ref, o32_ref, lse_ref, qa_ref, ka_ref, va_ref, kt_ref, base_ref, code_ref, g_ref,
               cos_ref, sin_ref, vn_ref, dn_ref, da_ref, qb_ref, acc_ref, dq_ref):
    T = do_ref.shape[1]
    hw = HW
    CH = 512
    lims = doc_limits(code_ref[...])
    fill_angles(base_ref, cos_ref, sin_ref)
    def prep(c, _):
        sl = pl.ds(pl.multiple_of(c*CH, CH), CH)
        for h in range(NH):
            do = do_ref[h*HEAD_DIM:(h+1)*HEAD_DIM, sl].astype(f32)
            delta = jnp.sum(do*o32_ref[h*HEAD_DIM:(h+1)*HEAD_DIM, sl], 0, keepdims=True)
            def split(x):
                x1 = x.astype(bf).astype(f32); r = x-x1
                x2 = r.astype(bf).astype(f32); x3 = r-x2
                return [x1, x2, x3]
            z13 = jnp.zeros((13, CH), f32); z48 = jnp.zeros((48, CH), f32)
            da_ref[h, :, sl] = jnp.concatenate([do]+split(-delta)+[z13, z48], 0).astype(bf)
            one = jnp.concatenate([jnp.ones((3, CH), f32), jnp.zeros((61, CH), f32)], 0)
            v = va_ref[h, :64, sl].astype(f32)
            vn_ref[h, sl, :] = jnp.concatenate([v, one], 0).T.astype(bf)
            z64 = jnp.zeros((64, CH), f32)
            q = qa_ref[h, :64, sl].astype(f32)
            dn_ref[h, sl, :] = jnp.concatenate([do, z64], 0).T.astype(bf)
            qb_ref[h, sl, :] = jnp.concatenate([z64, q], 0).T.astype(bf)
            acc_ref[h, sl, :] = jnp.zeros((CH, 128), f32)
        return 0
    lax.fori_loop(0, T//CH, prep, 0)
    def qblock(i, _):
        a = i*QB
        qs = pl.ds(pl.multiple_of(a, QB), QB)
        lo, hi = block_range(lims, a, QB, T)
        small = KB // 2
        start = lo // small
        many = (hi + small - 1) // small - start
        dq_ref[...] = jnp.zeros_like(dq_ref)

        def visit(at, size):
            ks = pl.ds(pl.multiple_of(at * small, small), size)
            for h in range(NH):
                s = nn(ka_ref[h, ks, :], qa_ref[h, :, qs])
                dp = nn(vn_ref[h, ks, :], da_ref[h, :, qs])
                p = jnp.exp(s - lse_ref[h:h+1, qs])
                ds = (p*dp).astype(bf)
                acc_ref[h, ks, :] += nn(p.astype(bf), dn_ref[h, qs, :]) + nn(ds, qb_ref[h, qs, :])
                dq_ref[h] += nn(kt_ref[h, :, ks], ds)

        def kv(j, _):
            visit(start + 2 * j, KB)
            return 0
        lax.fori_loop(0, many // 2, kv, 0)
        pl.when(many % 2 == 1)(lambda: visit(start + many - 1, small))
        cos = cos_ref[:, qs]; sin = sin_ref[:, qs]
        for h in range(NH):
            u = dq_ref[h]*0.125
            x1 = u[:32]; x2 = u[32:]
            g_ref[h*HEAD_DIM:(h+1)*HEAD_DIM, qs] = jnp.concatenate([x1*cos+x2*sin, x2*cos-x1*sin], 0).astype(bf)
        return 0
    lax.fori_loop(0, T//QB, qblock, 0)
    def fin(c, _):
        sl = pl.ds(pl.multiple_of(c*CH, CH), CH)
        cos = cos_ref[:, sl]; sin = sin_ref[:, sl]
        for h in range(NH):
            t = acc_ref[h, sl, :].T
            x1 = t[64:96]; x2 = t[96:128]
            g_ref[hw+h*HEAD_DIM:hw+(h+1)*HEAD_DIM, sl] = jnp.concatenate([x1*cos+x2*sin, x2*cos-x1*sin], 0).astype(bf)
            g_ref[2*hw+h*HEAD_DIM:2*hw+(h+1)*HEAD_DIM, sl] = t[:64].astype(bf)
        return 0
    lax.fori_loop(0, T//CH, fin, 0)

def attn_bwd(do, o32, lse, qa, ka, va, kt, base, code, KB=512, QB=256):
    T = do.shape[1]
    return pl.pallas_call(functools.partial(bwd_kernel, KB, QB),
        out_shape=jax.ShapeDtypeStruct((3*NH*HEAD_DIM, T), bf),
        in_specs=[VM] * 9, out_specs=pl.BlockSpec(memory_space=pltpu.VMEM),
        scratch_shapes=[pltpu.VMEM((HEAD_DIM // 2, T), f32), pltpu.VMEM((HEAD_DIM // 2, T), f32), pltpu.VMEM((NH,T,128), bf), pltpu.VMEM((NH,T,128), bf), pltpu.VMEM((NH,128,T), bf), pltpu.VMEM((NH,T,128), bf),
                        pltpu.VMEM((NH,T,128), f32), pltpu.VMEM((NH,HEAD_DIM,QB), f32)],
        compiler_params=pltpu.CompilerParams(vmem_limit_bytes=VLIM), name="attn_bwd",
        cost_estimate=pl.CostEstimate(flops=int(10*T*T*128*3), bytes_accessed=12<<20, transcendentals=T*T*3))(do, o32, lse, qa, ka, va, kt, base, code)


def contrast_part(groups, sums, goals_ref, plane, allp, ge, send, recv, scores_ref, loss_ref):
    t, p, x, y, g = here()
    docs = groups * DOCS_GRP
    size = groups * 8
    peers = plane_peers()
    line = [(t, lax.rem(p + SPAN * k, SPAN * groups)) for k in range(1, groups)]
    plane[3] = sums
    copies = [remote(plane.at[3], plane.at[i], send.at[i], recv.at[i], q) for i, q in enumerate(peers)]
    for c in copies:
        c.start()
    col = lax.broadcasted_iota(jnp.int32, (size, size), 1)
    row = lax.broadcasted_iota(jnp.int32, (size, size), 0)

    def mark(i, hot):
        goal = goals_ref[i]
        at = (row == i // DOCS_GRP * 8 + i % DOCS_GRP) & (col == goal // DOCS_GRP * 8 + goal % DOCS_GRP)
        return hot + jnp.where(at, 1.0, 0.0)

    hot = lax.fori_loop(0, docs, mark, jnp.zeros((size, size), f32))
    for c in copies:
        c.wait()
    own = (plane[3] + plane[0]) + (plane[1] + plane[2])
    allp[t, g] = own
    rows = allp.at[t, g]
    copies = [remote(rows, rows, send.at[3 + i], recv.at[3 + i], q) for i, q in enumerate(line)]
    for c in copies:
        c.start()
    for c in copies:
        c.wait()
    c = remote(allp.at[t], allp.at[t], send.at[2 + groups], recv.at[2 + groups], (1 - t, p))
    c.start()
    c.wait()
    width = allp.shape[3]
    pools = [allp[k].reshape(size, width) for k in range(2)]
    embeds = [v * lax.rsqrt(jnp.sum(v * v, -1, keepdims=True) + 1e-06) for v in pools]
    dot = functools.partial(lax.dot_general, precision=precise, preferred_element_type=f32)
    scores = dot(embeds[0], embeds[1], (((1,), (1,)), ((), ()))) * 50.0
    live = lax.rem(col, 8) < DOCS_GRP
    alive = lax.rem(row, 8) < DOCS_GRP
    masked = jnp.where(live, scores, -1e30)
    top = jnp.max(masked, -1, keepdims=True)
    total = jnp.sum(jnp.exp(masked - top), -1, keepdims=True)
    log_sums = top + jnp.log(total)
    chosen = jnp.sum(hot * scores, -1, keepdims=True)
    each = jnp.where(alive[:, 0:1], log_sums - chosen, 0.0)
    loss_ref[...] = jnp.broadcast_to(jnp.sum(each, 0, keepdims=True) / docs, loss_ref.shape)
    scores_ref[...] = scores
    gs = jnp.where(alive & live, (jnp.exp(masked - log_sums) - hot) / docs, 0.0)
    gq = dot(gs, embeds[1], (((1,), (0,)), ((), ())))
    gd = dot(gs, embeds[0], (((0,), (0,)), ((), ())))
    ge[...] = jnp.where(t == 0, gq, gd) * 50.0
    mine = ge[pl.ds(pl.multiple_of(g * 8, 8), 8), :]
    pooled = allp[t, g]
    inv = lax.rsqrt(jnp.sum(pooled * pooled, -1, keepdims=True) + 1e-06)
    return inv * mine - inv * inv * inv * pooled * jnp.sum(pooled * mine, -1, keepdims=True)


def block_kernel(
    groups, heads_ref, rows_ref, codes_ref, goals_ref, gain1_ref, bias1_ref, gain2_ref, bias2_ref, wo_h, wg_h, wu_h, wd_h,
    att_o, inner_o, hid_o, gm_o, gg_o, gb_o, ga_o, gh1_o, gains_o, scores_o, loss_o,
    att, wo, wg, wu, wd, inner, x1, s1, acc, hid, ab, x2, s2, sec, gm, gm2, gb, gb2, plane, allp, ge,
    wsem, lsem, tsend, trecv, osem, csend, crecv,
):
    t, p, x, y, g = here()
    peers = plane_peers()
    sibling = (1 - t, p)
    line = tuple((t, lax.rem(p + SPAN * k, SPAN * groups)) for k in range(1, groups))
    count, width = rows_ref.shape
    half = width // 2
    tiles = wg.shape[0]
    me = lax.rem(p, SPAN)

    def weight(j, k):
        cols = pl.ds(j * width if isinstance(j, int) else pl.multiple_of(j * width, width), width)
        src, dst = ((wg_h.at[:, cols], wg.at[j]), (wu_h.at[:, cols], wu.at[j]), (wd_h.at[cols], wd.at[j]))[k]
        return pltpu.make_async_copy(src, dst, wsem.at[1 + 3 * j + k])

    first_load = pltpu.make_async_copy(wo_h, wo, wsem.at[0])
    everyone = peers + (sibling,) + line
    hail(everyone)
    heads_load = pltpu.make_async_copy(heads_ref, att, lsem.at[0])
    heads_load.start()
    first_load.start()
    for j in range(tiles):
        for k in range(3):
            weight(j, k).start()
    code = codes_ref[:, pl.ds(pl.multiple_of(me * count, count), count)]
    zero = jnp.zeros((8 - DOCS_GRP, count), f32)
    mem = jnp.concatenate([jnp.where(code == float(d), 1.0, 0.0) for d in range(DOCS_GRP)] + [zero], 0)
    mem = jnp.concatenate([mem, mem, mem, jnp.zeros((8, count), f32)], 0).astype(bf)
    first_load.wait()
    heads_load.wait()

    def pair(i, mine, its, out):
        return (
            pltpu.make_async_copy(mine, out.at[0], osem.at[i]),
            remote(its, out.at[1], tsend.at[i], trecv.at[i], sibling),
        )

    def both(i, mine, its, out):
        for c in pair(i, mine, its, out):
            c.start()

    acc[...] = tn(att[...], wo[...])
    greeted(everyone)
    both(0, att, att, att_o)
    step = 64
    gain1, bias1, gain2, bias2 = (r[...].reshape(1, width) for r in (gain1_ref, bias1_ref, gain2_ref, bias2_ref))

    def chunk(i):
        return pl.ds(pl.multiple_of(i * step, step), step)

    def norm(h, sl, xs, ss):
        c = h - jnp.mean(h, -1, keepdims=True)
        s = lax.rsqrt(jnp.mean(c * c, -1, keepdims=True) + norm_eps)
        xh = c * s
        xs[sl, :] = xh
        ss[sl, :] = s
        return xh

    def norm_one(i, _):
        sl = chunk(i)
        xh = norm(rows_ref[sl, :].astype(f32) + acc[sl, :], sl, x1, s1)
        v = xh * gain1 + bias1
        inner[sl, :] = v.astype(bf)
        acc[sl, :] = v
        return 0

    lax.fori_loop(0, count // step, norm_one, 0)
    both(1, inner, inner, inner_o)

    def tile_of(j, i, mine, its, out):
        return (
            pltpu.make_async_copy(mine, out.at[0, j], osem.at[i + j]),
            remote(its, out.at[1, j], tsend.at[i + j], trecv.at[i + j], sibling),
        )

    def forward(n, _):
        for i in range(2):
            j = 2 * n + i
            for k in range(3):
                weight(j, k).wait()
            gate = nn(inner[...], wg[j])
            upper = nn(inner[...], wu[j])
            sig = jax.nn.sigmoid(gate)
            silu = gate * sig
            hid[j] = (silu * upper).astype(bf)
            ab[0, j] = (upper * (sig * (1.0 + gate * (1.0 - sig)))).astype(bf)
            ab[1, j] = silu.astype(bf)
            for c in tile_of(j, 2, hid.at[j], hid.at[j], hid_o):
                c.start()
            acc[...] += nn(hid[j], wd[j])
        return 0

    lax.fori_loop(0, tiles // 2, forward, 0)

    def norm_two(i, _):
        sl = chunk(i)
        v = norm(acc[sl, :], sl, x2, s2) * gain2 + bias2
        for k, part in enumerate(split3(v)):
            sec[k, sl, :] = part.astype(bf)
        return 0

    lax.fori_loop(0, count // step, norm_two, 0)
    sums = (nn(mem[:16], sec[0]) + nn(mem[:16], sec[1]) + nn(mem[:16], sec[2]))[:8]
    top = lax.broadcasted_iota(jnp.int32, sums.shape, 0) < DOCS_GRP
    sums = jnp.where(top, sums, 0.0)
    gp = contrast_part(groups, sums, goals_ref, plane, allp, ge, csend, crecv, scores_o, loss_o)
    gp3 = jnp.concatenate(split3(gp) + [jnp.zeros_like(gp)], 0).astype(bf)
    acc[...] = tn(mem, gp3)

    def fold(v):
        return jnp.sum(v.reshape(step // 8, 8, width), 0)

    def norm_back(gr, xh, s, gain):
        e = gr * gain
        v = e - jnp.mean(e, -1, keepdims=True) - xh * jnp.mean(e * xh, -1, keepdims=True)
        return v * s

    zeros = jnp.zeros((8, width), f32)

    def back_two(i, sums):
        sl = chunk(i)
        gr, xh = acc[sl, :], x2[sl, :]
        v = norm_back(gr, xh, s2[sl, :], gain2)
        acc[sl, :] = v
        low = v.astype(bf)
        gm[sl, :] = low
        gm2[0, sl, :] = low[:, :half]
        gm2[1, sl, :] = low[:, half:]
        return sums[0] + fold(gr * xh), sums[1] + fold(gr)

    g2, b2 = lax.fori_loop(0, count // step, back_two, (zeros, zeros))
    both(2 + 2 * tiles, gm2.at[t], gm2.at[1 - t], gm_o)
    def backward(n, _):
        for i in range(2):
            j = 2 * n + i
            gh = nt(gm[...], wd[j])
            gg = (gh * ab[0, j].astype(f32)).astype(bf)
            gu = (gh * ab[1, j].astype(f32)).astype(bf)
            ab[0, j] = gg
            ab[1, j] = gu
            for c in tile_of(j, 2 + tiles, ab.at[t, j], ab.at[1 - t, j], gg_o):
                c.start()
            acc[...] += nt(gg, wg[j]) + nt(gu, wu[j])
        return 0

    lax.fori_loop(0, tiles // 2, backward, 0)

    def back_one(i, sums):
        sl = chunk(i)
        gr, xh = acc[sl, :], x1[sl, :]
        v = norm_back(gr, xh, s1[sl, :], gain1)
        gh1_o[sl, :] = v
        low = v.astype(bf)
        gb[sl, :] = low
        gb2[0, sl, :] = low[:, :half]
        gb2[1, sl, :] = low[:, half:]
        return sums[0] + fold(gr * xh), sums[1] + fold(gr)

    g1, b1 = lax.fori_loop(0, count // step, back_one, (zeros, zeros))
    both(3 + 2 * tiles, gb2.at[t], gb2.at[1 - t], gb_o)
    flat = [jnp.sum(v, 0, keepdims=True) for v in (g1, b1, g2, b2)]
    gains_o[...] = jnp.concatenate(flat + [jnp.zeros((4, width), f32)], 0)
    ga_o[...] = nt(wo[...], gb[...]).astype(bf)
    done = [pair(0, att, att, att_o), pair(1, inner, inner, inner_o)]
    for j in range(tiles):
        done.append(tile_of(j, 2, hid.at[j], hid.at[j], hid_o))
        done.append(tile_of(j, 2 + tiles, ab.at[t, j], ab.at[1 - t, j], gg_o))
    done.append(pair(2 + 2 * tiles, gm2.at[t], gm2.at[1 - t], gm_o))
    done.append(pair(3 + 2 * tiles, gb2.at[t], gb2.at[1 - t], gb_o))
    for c in done:
        for d in c:
            d.wait()


def block(heads, rows, codes, goals, norms, w_out, w_gate, w_up, w_down, groups):
    count, width = rows.shape
    tiles = w_gate.shape[1] // width
    half = width // 2
    size = groups * 8
    sds = jax.ShapeDtypeStruct
    vm = lambda *n: pltpu.VMEM(n, bf)
    vf = lambda *n: pltpu.VMEM(n, f32)
    return pl.pallas_call(
        functools.partial(block_kernel, groups),
        out_shape=(
            sds((2, width, count), bf), sds((2, count, width), bf), sds((2, tiles, count, width), bf),
            sds((2, count, half), bf), sds((2, tiles, count, width), bf), sds((2, count, half), bf),
            sds((width, count), bf), sds((count, width), f32), sds((8, width), f32),
            sds((size, size), f32), sds((8, 128), f32),
        ),
        in_specs=[ANY, VM, VM, pl.BlockSpec(memory_space=pltpu.SMEM)] + [VM] * 4 + [ANY] * 4,
        out_specs=(ANY,) * 6 + (VM,) * 5,
        scratch_shapes=[
            vm(width, count), vm(width, width), vm(tiles, width, width), vm(tiles, width, width),
            vm(tiles, width, width), vm(count, width), vf(count, width), vf(count, 1), vf(count, width),
            vm(tiles, count, width), vm(2, tiles, count, width), vf(count, width), vf(count, 1),
            vm(3, count, width), vm(count, width), vm(2, count, half), vm(count, width), vm(2, count, half),
            vf(4, 8, width), vf(2, groups, 8, width), vf(size, width),
            dma_sems(1 + 3 * tiles), dma_sems(1),
            dma_sems(4 + 2 * tiles), dma_sems(4 + 2 * tiles), dma_sems(4 + 2 * tiles),
            dma_sems(3 + groups), dma_sems(3 + groups),
        ],
        compiler_params=comm_params(1),
        name="block",
    )(heads, rows, codes, goals, *norms, w_out, w_gate, w_up, w_down)


def weights_kernel(
    groups, i_ref, g_ref, h_ref, m_ref, a_ref, b_ref, in_ref,
    sa_ref, ka_ref, sb_ref, kb_ref, sc_ref, kc_ref, heads_ref,
    iv, it, gv, hv, mv, av, bv, gs, ds, os, isem, osem, send, recv, lsem,
):
    t, p, x, y, g = here()
    level = lax.rem(g, 2)
    peers = plane_peers()
    count, width = i_ref.shape[1:]
    half = width // 2
    tiles = gv.shape[0]
    shards = SPAN * groups
    one = width // shards
    down = ds.shape[1]

    def load(i, src, dst):
        return pltpu.make_async_copy(src, dst, isem.at[i])

    class Both:
        def __init__(self, *copies):
            self.copies = copies

        def start(self):
            for c in self.copies:
                c.start()

        def wait(self):
            for c in self.copies:
                c.wait()

    def tile(ref, j, buf, base):
        return Both(*(
            load(base + 2 * j + i, ref.at[i, j], buf.at[j, pl.ds(i * count, count)]) for i in range(2)
        ))

    def stack(base, ref, buf):
        return Both(*(load(base + i, ref.at[i], buf.at[pl.ds(i * count, count)]) for i in range(2)))

    def beside(base, ref, buf):
        return Both(*(load(base + i, ref.at[i], buf.at[:, pl.ds(i * count, count)]) for i in range(2)))

    hail(peers)
    few = [stack(0, m_ref, mv), beside(2, a_ref, av), stack(4, b_ref, bv), stack(6, i_ref, iv)]
    few[0].start()
    for j in range(tiles):
        tile(h_ref, j, hv, 8).start()
    for c in few[1:]:
        c.start()
    for j in range(tiles):
        tile(g_ref, j, gv, 8 + 2 * tiles).start()
    greeted(peers)
    tokens = in_ref.shape[1]
    me = lax.rem(p, SPAN)
    mine = pl.ds(pl.multiple_of(me * tokens, tokens), tokens)
    moves = []
    for i, peer in enumerate((peers[2], peers[0], peers[1])):
        m = lax.rem(peer[1], SPAN)
        moves.append(remote(
            in_ref.at[pl.ds(pl.multiple_of(m * HW, HW), HW)], heads_ref.at[:, mine],
            send.at[i], recv.at[i], peer,
        ))
    moves.append(pltpu.make_async_copy(
        in_ref.at[pl.ds(pl.multiple_of(me * HW, HW), HW)], heads_ref.at[:, mine], lsem.at[0]
    ))
    for c in moves:
        c.start()
    few[0].wait()

    def downward(j, _):
        tile(h_ref, j, hv, 8).wait()
        r = tn(hv[j], mv[...])
        ds[pl.ds(j * (width // down), width // down)] = r.astype(bf).reshape(width // down, down, half)
        return 0

    lax.fori_loop(0, tiles, downward, 0)
    for c in few[1:]:
        c.wait()
    r = nn(av[...], bv[...])
    os[...] = r.astype(bf).reshape(shards, one, half)
    it[...] = iv[...].T
    fours = lambda ref, n: ref.reshape(groups, 2, 2, n, half)

    def put(i, src, dst):
        return pltpu.make_async_copy(src, dst, osem.at[i])

    outs = []
    for i, (ref, k) in enumerate(((sb_ref, 1 - y), (kb_ref, y))):
        outs.append(put(4 * i, fours(ds, down).at[:, k], ref.at[:, :, pl.ds(0, down)]))
        outs.append(put(4 * i + 1, fours(os, one).at[:, k], ref.at[:, :, pl.ds(down, one)]))
    for c in outs:
        c.start()

    sideways = sa_ref.shape[2] // one

    def top(j):
        if j < sideways:
            rows = pl.ds(j * one, one)
            piece = fours(gs.at[j], one)
            went, kept = (piece.at[:, :, 1 - x], sa_ref), (piece.at[:, :, x], ka_ref)
        else:
            rows = pl.ds((j - sideways) * one, one)
            piece = gs.at[j].reshape(groups // 2, 2, SPAN, one, half)
            went, kept = (piece.at[:, 1 - level], sc_ref), (piece.at[:, level], kc_ref)
        return (
            put(8 + j, went[0], went[1].at[:, :, rows]),
            put(8 + 2 * tiles + j, kept[0], kept[1].at[:, :, rows]),
        )

    for j in range(tiles):
        tile(g_ref, j, gv, 8 + 2 * tiles).wait()
        r = nn(it[...], gv[j]).astype(bf)
        for h in range(2):
            k = 2 * j + h
            gs[k] = r[:, h * half : (h + 1) * half].reshape(shards, one, half)
            outs.extend(top(k))
            for c in outs[-2:]:
                c.start()
    for c in outs + moves:
        c.wait()


def weight_grads(groups, grad_heads, inner, grads, hidden, grad_mlp, attended, grad_branch):
    count, width = inner.shape[1:]
    half = width // 2
    shards = SPAN * groups
    one = width // shards
    tiles = grads.shape[1]
    down = tiles * one
    ra = (2 * tiles - UPWARD) * one
    rb = down + one
    part = lambda r: jax.ShapeDtypeStruct((groups, 2, r, half), bf)
    level = jax.ShapeDtypeStruct((groups // 2, SPAN, UPWARD * one, half), bf)
    vm = lambda *n: pltpu.VMEM(n, bf)
    return pl.pallas_call(
        functools.partial(weights_kernel, groups),
        out_shape=(
            part(ra), part(ra), part(rb), part(rb), level, level,
            jax.ShapeDtypeStruct((HW, SPAN * grad_heads.shape[1]), bf),
        ),
        in_specs=[ANY] * 6 + [VM],
        out_specs=(ANY,) * 7,
        scratch_shapes=[
            vm(2 * count, width), vm(width, 2 * count), vm(tiles, 2 * count, width), vm(tiles, 2 * count, width),
            vm(2 * count, half), vm(width, 2 * count), vm(2 * count, half),
            vm(2 * tiles, shards, one, half), vm(shards, down, half), vm(shards, one, half),
            dma_sems(8 + 4 * tiles), dma_sems(8 + 4 * tiles), dma_sems(3), dma_sems(3), dma_sems(1),
        ],
        compiler_params=comm_params(2),
        name="weight_grads",
        cost_estimate=pl.CostEstimate(
            flops=int(2 * 2 * count * half * width * 8.5), bytes_accessed=30 << 20, transcendentals=0
        ),
    )(inner, grads, hidden, grad_mlp, attended, grad_branch, grad_heads)


def add_rows(dst, a, b, rows):
    step = rows // 3 if rows % 48 == 0 and rows > 48 else rows

    def part(i, _):
        sl = pl.ds(pl.multiple_of(i * step, step), step)
        dst[sl, :] = a[sl, :] + b[sl, :]
        return 0

    lax.fori_loop(0, rows // step, part, 0)


class Line:
    def __init__(self, z, zt, groups, part, up, down, sems, t, p):
        self.z, self.zt, self.groups = z, zt, groups
        self.part, self.up, self.down = part, up, down
        us, ur, ds, dr = sems
        above = (t, lax.rem(p + SPAN, SPAN * groups))
        below = (t, lax.rem(p + SPAN * (groups - 1), SPAN * groups))
        self.up_first = lambda: remote(part, up, us, ur, above)
        self.up_next = lambda: remote(up, up, us, ur, above)
        self.down_first = lambda: remote(part, down, ds, dr, below)
        self.down_next = lambda: remote(down, down, ds, dr, below)

    def start(self):
        if self.zt > 0:
            pl.when(self.z == 0)(lambda: self.up_first().start())
        if self.zt < self.groups - 1:
            pl.when(self.z == self.groups - 1)(lambda: self.down_first().start())

    def relay(self, hop, rows):
        def up():
            self.up_next().wait_recv()
            add_rows(self.up, self.up, self.part, rows)
            self.up_next().start()

        def down():
            self.down_next().wait_recv()
            add_rows(self.down, self.down, self.part, rows)
            self.down_next().start()

        if 0 < hop < self.zt:
            pl.when(self.z == hop)(up)
        if self.zt < self.groups - 1 - hop:
            pl.when(self.z == self.groups - 1 - hop)(down)

    def finish(self, dst, rows):
        def done():
            if self.zt > 0:
                self.up_next().wait_recv()
            if self.zt < self.groups - 1:
                self.down_next().wait_recv()
            if 0 < self.zt < self.groups - 1:
                add_rows(self.up, self.up, self.down, rows)
            add_rows(dst, self.up if self.zt > 0 else self.down, self.part, rows)

        pl.when(self.z == self.zt)(done)

    def drain(self):
        if self.zt > 0:
            pl.when(self.z < self.zt)(lambda: self.up_first().wait_send())
        if self.zt < self.groups - 1:
            pl.when(self.z > self.zt)(lambda: self.down_first().wait_send())


def outward(groups):
    order = []
    lo, hi = 0, groups - 1
    while lo <= hi:
        order.append(hi)
        if lo < hi:
            order.append(lo)
        lo, hi = lo + 1, hi - 1
    return order


def finish_kernel(
    groups, ka_ref, kb_ref, kc_ref, ra_ref, rb_ref, rc_ref, wq_ref, gh_ref, gin_ref, tin_ref, gain_ref,
    pair_ref, tg_ref, out_ref, sum_ref,
    plane, line, nsend, nrecv,
    kvc, rvc, r2c, r3c, r4c, csem, cs, cr, kva, kvb, rva, rvb, r2a, r2b, ua, ub, da, db, isem, s2, q2, us, ur, ds, dr,
    gm_ref, wq, gh, g_ref, tok_ref, wsem, fs, fr,
    w2, sib, ub2, db2, fin, send, recv, ts, tr, us2, ur2, ds2, dr2, ps, pr, lsem,
):
    t, p, x, y, z = here()
    ex, ey, ed = plane_peers()
    peers = (ex, ey, ed)
    sibling = (1 - t, p)
    others = [(t, lax.rem(p + SPAN * k, SPAN * groups)) for k in range(1, groups)]
    across = tuple((1 - t, q[1]) for q in peers)
    order = outward(groups)
    colours = (
        (ey, ka_ref, ra_ref, kva, rva, r2a, ua, da, y),
        (ex, kb_ref, rb_ref, kvb, rvb, r2b, ub, db, x),
    )

    def loads(c, zt):
        peer, kr, rr, kv, rv = colours[c][:5]
        i = 2 * (c * groups + zt)
        return (
            pltpu.make_async_copy(kr.at[zt], kv.at[zt], isem.at[i]),
            pltpu.make_async_copy(rr.at[zt], rv.at[zt], isem.at[i + 1]),
        )

    level_loads = [
        [pltpu.make_async_copy(a.at[i], b.at[i], csem.at[2 * i + j]) for j, (a, b) in enumerate(((kc_ref, kvc), (rc_ref, rvc)))]
        for i in range(2)
    ]
    for pair in level_loads:
        for d in pair:
            d.start()
    mixed_loads = (pltpu.make_async_copy(gin_ref, g_ref, wsem.at[2]), pltpu.make_async_copy(tin_ref, tok_ref, wsem.at[3]))
    for i, zt in enumerate(order):
        for c in range(2):
            for d in loads(c, zt):
                d.start()
        if i == 1:
            for c in mixed_loads:
                c.start()
    more = (pltpu.make_async_copy(wq_ref, wq, wsem.at[0]), pltpu.make_async_copy(gh_ref, gh, wsem.at[1]))
    for c in more:
        c.start()
    greet(peers + across + (sibling,) + tuple(others))
    around = [remote(gain_ref, plane.at[i], nsend.at[i], nrecv.at[i], q) for i, q in enumerate(peers)]
    for c in around:
        c.start()

    def second(c, zt):
        peer, kr, rr, kv, rv, r2, u, d, mine = colours[c]
        i = c * groups + zt
        return remote(rv.at[zt, 1 - mine], r2.at[zt], s2.at[i], q2.at[i], peer)

    def chain(c, zt):
        peer, kr, rr, kv, rv, r2, u, d, mine = colours[c]
        i = c * groups + zt
        return Line(z, zt, groups, r2.at[zt], u.at[zt], d.at[zt],
                    (us.at[i], ur.at[i], ds.at[i], dr.at[i]), t, p)

    def size(c):
        return colours[c][3].shape[2]

    up = kvc.shape[2]

    def third(i, k):
        at = (k * 2 + 1 - x, (1 - y) * 2 + k)[i]
        n = 2 * i + k
        return remote(rvc.at[i, at], r2c.at[i, k], cs.at[n], cr.at[n], (ex, ey)[i])

    def fourth(i):
        at = (1 - y, 1 - x)[i]
        return remote(r2c.at[i, at], r3c.at[i], cs.at[4 + i], cr.at[4 + i], (ey, ex)[i])

    top = lax.div(z, 2)
    fifth = remote(r3c.at[1 - top], r4c, cs.at[6], cr.at[6], (t, p + 2 * SPAN - 4 * SPAN * top))

    def plus(dst, src, n):
        add_rows(dst, dst, src, n)

    def send_second(zt):
        for c in range(2):
            for d in loads(c, zt):
                d.wait()
            peer, kr, rr, kv, rv, r2, u, d, mine = colours[c]
            plus(rv.at[zt, 1 - mine], kv.at[zt, 1 - mine], size(c))
            second(c, zt).start()

    for i in range(2):
        for d in level_loads[i]:
            d.wait()
        for k in range(2):
            at = (k * 2 + 1 - x, (1 - y) * 2 + k)[i]
            plus(rvc.at[i, at], kvc.at[i, at], up)
            third(i, k).start()
    send_second(order[0])
    send_second(order[1])
    width = gm_ref.shape[0] // 3
    shards = SPAN * groups
    one = width // shards
    half = width // 2
    for c in mixed_loads:
        c.wait()
    for h in range(2):
        r = nn(g_ref[...], tok_ref[:, h * half : (h + 1) * half]).T
        w2[h * (shards // 2) : (h + 1) * (shards // 2)] = r.astype(bf).reshape(shards // 2, one, 3 * HW)

    def swap(zt):
        return remote(w2.at[pl.ds(zt * 4 + (1 - t) * 2, 2)], sib.at[zt], ts.at[zt], tr.at[zt], sibling)

    for zt in order:
        swap(zt).start()

    for i in range(2):
        for k in range(2):
            at = (k * 2 + x, y * 2 + k)[i]
            plus(rvc.at[i, at], kvc.at[i, at], up)
            third(i, k).wait_recv()
            plus(r2c.at[i, k], rvc.at[i, at], up)
        fourth(i).start()
    send_second(order[2])
    send_second(order[3])
    count = gm_ref.shape[1]
    me = lax.rem(p, SPAN)
    copies = []
    for i, peer in enumerate((peers[2], peers[0], peers[1])):
        m = lax.rem(peer[1], SPAN)
        for k in range(3):
            copies.append(remote(
                g_ref.at[pl.ds(k * HW, HW), pl.ds(pl.multiple_of(m * count, count), count)],
                gm_ref.at[pl.ds(pl.multiple_of(k * width + me * HW, HW), HW)],
                send.at[i * 3 + k], recv.at[i * 3 + k], peer,
            ))
    for k in range(3):
        copies.append(pltpu.make_async_copy(
            g_ref.at[pl.ds(k * HW, HW), pl.ds(pl.multiple_of(me * count, count), count)],
            gm_ref.at[pl.ds(pl.multiple_of(k * width + me * HW, HW), HW)],
            lsem.at[k],
        ))
    for c in copies:
        c.start()
    def chain2(zt, k):
        i = zt * 2 + k
        return Line(z, zt, groups, sib.at[zt, k], ub2.at[zt, k], db2.at[zt, k],
                    (us2.at[i], ur2.at[i], ds2.at[i], dr2.at[i]), t, p)

    for zt in order:
        swap(zt).wait_recv()
        for k in range(2):
            dst = sib.at[zt, k]
            add_rows(dst, dst, w2.at[zt * 4 + t * 2 + k], one)
            chain2(zt, k).start()
    for zt in order:
        for c in range(2):
            peer, kr, rr, kv, rv, r2, u, d, mine = colours[c]
            keep = rv.at[zt, mine]
            add_rows(keep, keep, kv.at[zt, mine], size(c))

    def in_plane(zt):
        for c in range(2):
            peer, kr, rr, kv, rv, r2, u, d, mine = colours[c]
            second(c, zt).wait_recv()
            dst = r2.at[zt]
            add_rows(dst, dst, rv.at[zt, mine], size(c))
            chain(c, zt).start()

    def relay(zt, hop):
        for c in range(2):
            chain(c, zt).relay(hop, size(c))


    def relay2(hop):
        for zt in order:
            for k in range(2):
                chain2(zt, k).relay(hop, one)

    in_plane(order[0])
    relay2(1)
    in_plane(order[1])
    for i in range(2):
        fourth(i).wait_recv()
        plus(r3c.at[i], r2c.at[i, (y, x)[i]], up)
    fifth.start()
    relay(order[0], 1)
    relay2(2)
    for c in around:
        c.wait()
    line[0] = (gain_ref[...] + plane[0]) + (plane[1] + plane[2])
    ring = [
        remote(line.at[0], line.at[1 + k], nsend.at[3 + k], nrecv.at[3 + k], q) for k, q in enumerate(others)
    ]
    for c in ring:
        c.start()
    in_plane(order[2])
    relay(order[1], 1)
    in_plane(order[3])
    relay(order[0], 2)
    relay(order[2], 1)
    relay(order[1], 2)
    relay(order[3], 1)
    for zt in order:
        for k in range(2):
            chain2(zt, k).finish(fin.at[k], one)
    here_id = t * SPAN + me

    def hand(k, tt):
        m = t * 2 + k
        peer = (tt, z * SPAN + m)
        i = k * 2 + tt
        away = lambda: remote(fin.at[k], out_ref.at[me], ps.at[i], pr.at[me], peer)
        stay = lambda: pltpu.make_async_copy(fin.at[k], out_ref.at[me], lsem.at[3])
        return away, stay, (tt * SPAN + m) == here_id

    for k in range(2):
        for tt in range(2):
            away, stay, same = hand(k, tt)
            pl.when(jnp.logical_not(same))(lambda away=away: away().start())
            pl.when(same)(lambda stay=stay: stay().start())
    for c in ring:
        c.wait()
    total = line[0]
    for k in range(1, groups):
        total = total + line[k]
    line[groups] = total
    gained = remote(line.at[groups], line.at[groups + 1], nsend.at[2 + groups], nrecv.at[2 + groups], sibling)
    gained.start()
    for c in copies + list(more):
        c.wait()
    turned = nn(wq[...], gm_ref[...]).T
    tg_ref[...] = gh[...] + turned
    fifth.wait_recv()
    add_rows(pair_ref.at[t, pl.ds(size(0) + size(1), up)], r3c.at[top], r4c, up)
    for zt in order:
        for c, sl in ((0, pl.ds(0, size(0))), (1, pl.ds(size(0), size(1)))):
            chain(c, zt).finish(pair_ref.at[t, sl], size(c))
    last = remote(pair_ref.at[t], pair_ref.at[t], fs.at[0], fr.at[0], sibling)
    last.start()
    for s in range(SPAN):
        from_here = jnp.logical_and(s == me, y == t)
        pl.when(jnp.logical_not(from_here))(
            lambda s=s: remote(fin.at[0], out_ref.at[s], ps.at[0], pr.at[s], sibling).wait_recv()
        )
    for k in range(2):
        for tt in range(2):
            away, stay, same = hand(k, tt)
            pl.when(jnp.logical_not(same))(lambda away=away: away().wait_send())
            pl.when(same)(lambda stay=stay: stay().wait())
    for zt in range(groups):
        swap(zt).wait_send()
        for k in range(2):
            chain2(zt, k).drain()
        for c in range(2):
            second(c, zt).wait_send()
            chain(c, zt).drain()
    for i in range(2):
        for k in range(2):
            third(i, k).wait_send()
        fourth(i).wait_send()
    fifth.wait_send()
    gained.wait()
    sum_ref[...] = line[groups] + line[groups + 1]
    last.wait()


def finish(ka, kb, kc, ra, rb, rc, wq, gh, g, tok, gains, groups):
    width = tok.shape[1]
    count = tok.shape[0] // SPAN
    one = width // (SPAN * groups)
    na, nb, nc = ka.shape[2], kb.shape[2], kc.shape[2]
    half = ka.shape[3]
    buf = lambda *n: pltpu.VMEM(n, bf)
    mix = lambda *n: pltpu.VMEM(n + (one, 3 * HW), bf)
    return pl.pallas_call(
        functools.partial(finish_kernel, groups),
        out_shape=(
            jax.ShapeDtypeStruct((2, na + nb + nc, half), bf),
            jax.ShapeDtypeStruct((count, width), f32),
            jax.ShapeDtypeStruct((SPAN, one, 3 * HW), bf),
            jax.ShapeDtypeStruct(gains.shape, f32),
        ),
        in_specs=[ANY] * 10 + [VM],
        out_specs=(VM,) * 4,
        scratch_shapes=[
            pltpu.VMEM((3,) + gains.shape, f32), pltpu.VMEM((groups + 2,) + gains.shape, f32),
            dma_sems(3 + groups), dma_sems(3 + groups),
            buf(2, SPAN, nc, half), buf(2, SPAN, nc, half), buf(2, 2, nc, half), buf(2, nc, half), buf(nc, half),
            dma_sems(4), dma_sems(7), dma_sems(7),
            buf(groups, 2, na, half), buf(groups, 2, nb, half), buf(groups, 2, na, half), buf(groups, 2, nb, half),
            buf(groups, na, half), buf(groups, nb, half), buf(groups, na, half), buf(groups, nb, half),
            buf(groups, na, half), buf(groups, nb, half),
            dma_sems(4 * groups), dma_sems(2 * groups), dma_sems(2 * groups),
            dma_sems(2 * groups), dma_sems(2 * groups), dma_sems(2 * groups), dma_sems(2 * groups),
            buf(3 * width, count), buf(width, 3 * width), pltpu.VMEM((count, width), f32),
            buf(*g.shape), buf(*tok.shape), dma_sems(4),
            dma_sems(1), dma_sems(1),
            mix(SPAN * groups), mix(groups, 2), mix(groups, 2), mix(groups, 2), mix(2),
            dma_sems(9), dma_sems(9), dma_sems(groups), dma_sems(groups),
            dma_sems(2 * groups), dma_sems(2 * groups), dma_sems(2 * groups), dma_sems(2 * groups),
            dma_sems(4), dma_sems(SPAN), dma_sems(4),
        ],
        compiler_params=comm_params(3),
        name="finish",
    )(ka, kb, kc, ra, rb, rc, wq, gh, g, tok, gains)


def unfold_kernel(
    groups, pair_ref, part_ref, grad_ref, score_ref, gain_ref, lost_ref,
    gate_ref, up_ref, down_ref, out_ref, qkv_ref, token_ref, scores_ref, loss_ref, *gains_refs,
):
    one = out_ref.shape[0]
    half = pair_ref.shape[2]
    width = 2 * half
    steps = gate_ref.shape[1] // half
    down = down_ref.shape[0]
    token_ref[0] = grad_ref[...]
    top = (steps - UPWARD) * one
    for j in range(steps):
        at = j * one + (0 if j < steps - UPWARD else down + one)
        for k, ref in enumerate((gate_ref, up_ref)):
            ref[:, j * half : (j + 1) * half] = pair_ref[k, at : at + one, :].astype(f32)
    for k in range(2):
        cols = slice(k * half, (k + 1) * half)
        down_ref[:, cols] = pair_ref[k, top : top + down, :].astype(f32)
        out_ref[:, cols] = pair_ref[k, top + down : top + down + one, :].astype(f32)
    for k in range(3):
        row = [part_ref[s, :, k * HW : (k + 1) * HW].astype(f32) for s in range(SPAN)]
        qkv_ref[:, k * width : (k + 1) * width] = jnp.concatenate(row, 1)
    docs, size = scores_ref.shape[0], score_ref.shape[0]
    dot = functools.partial(lax.dot_general, precision=precise, preferred_element_type=f32)
    row = lax.broadcasted_iota(jnp.int32, (docs, size), 0)
    col = lax.broadcasted_iota(jnp.int32, (docs, size), 1)
    pick = jnp.where(row // DOCS_GRP * 8 + lax.rem(row, DOCS_GRP) == col, 1.0, 0.0)
    some = dot(pick, score_ref[...], (((1,), (0,)), ((), ())))
    scores_ref[...] = dot(some, pick, (((1,), (1,)), ((), ())))
    row = lax.broadcasted_iota(jnp.int32, (width, one), 0)
    col = lax.broadcasted_iota(jnp.int32, (width, one), 1)
    mine = jnp.where(row == lax.axis_index("dp") * one + col, 1.0, 0.0)
    gains = dot(gain_ref[...], mine, (((1,), (0,)), ((), ())))
    for k, ref in enumerate(gains_refs):
        ref[...] = gains[k : k + 1, :]
    loss_ref[...] = lost_ref[0:1, 0:1]


def unfold(pair, parts, grad, scores, gains, loss, tiles, groups):
    one = parts.shape[1]
    half = pair.shape[2]
    width = 2 * half
    docs = groups * DOCS_GRP
    sds = jax.ShapeDtypeStruct
    return pl.pallas_call(
        functools.partial(unfold_kernel, groups),
        out_shape=(
            sds((one, tiles * width), f32), sds((one, tiles * width), f32), sds((tiles * one, width), f32),
            sds((one, width), f32), sds((one, 3 * width), f32), sds((1,) + grad.shape, f32),
            sds((docs, docs), f32), sds((1, 1), f32),
        )
        + (sds((1, one), f32),) * 4,
        in_specs=[VM] * 6,
        out_specs=(VM,) * 12,
        name="unfold",
    )(pair, parts, grad, scores, gains, loss)


def angle_bases():
    half = HEAD_DIM // 2
    freqs = np.float32(1000.0) ** (-np.arange(half, dtype=np.float32) / np.float32(half))
    steps = np.arange(128, dtype=np.float64)
    far = freqs[:, None].astype(np.float64) * (128.0 * steps)[None, :]
    near = freqs[:, None].astype(np.float64) * steps[None, :]
    return np.stack([np.cos(far), np.sin(far), np.cos(near), np.sin(near)]).astype(np.float32)


def spread_sum(value):
    part = lax.psum_scatter(value, "dp", scatter_dimension=0, tiled=True)
    return lax.psum(part.astype(bf), "tower").astype(f32)


def local(
    tokens, doc_ids, pad_mask, targets, w_qkv, w_out, ln1_gain, ln1_bias,
    w_gate, w_up, w_down, ln2_gain, ln2_bias,
):
    width = w_out.shape[0]
    rows = tokens[0]
    count = rows.shape[0]
    places = lax.axis_size("dp")
    groups = places // SPAN
    tower = lax.axis_index("tower")
    place = lax.axis_index("dp")
    me = place % SPAN
    docs = groups * DOCS_GRP
    base = angle_bases()
    tok_all, codes, qa, ka, va, kt, heads, lse, exact = gather(rows, doc_ids, pad_mask, base, w_qkv)
    norms = (ln1_gain, ln1_bias, ln2_gain, ln2_bias)
    (
        attended, inner, hidden, grad_mlp, grads, grad_branch, grad_attended, grad_h1, gains, scores_all, loss
    ) = block(heads, rows, codes, targets, norms, w_out, w_gate, w_up, w_down, groups)
    by_hand = groups == 4 and width % (16 * places) == 0
    if by_hand:
        send_a, keep_a, send_b, keep_b, send_c, keep_c, d_heads = weight_grads(
            groups, grad_attended, inner, grads, hidden, grad_mlp, attended, grad_branch
        )
        exchange = lambda v, bit: lax.ppermute(v, "dp", [(i, i ^ bit) for i in range(places)])
        came_a, came_b, came_c = exchange(send_a, 1), exchange(send_b, 2), exchange(send_c, SPAN)
    else:
        d_heads = tokens_to_heads(grad_attended, 5, "to_heads")
    mixed = attn_bwd(d_heads, exact, lse, qa, ka, va, kt, base, codes)
    if by_hand:
        pair, grad_tokens, qkv_parts, gain_sums = finish(
            keep_a, keep_b, keep_c, came_a, came_b, came_c, w_qkv, grad_h1, mixed, tok_all, gains, groups
        )
        gate_out, up_out, down_out, out_out, qkv_out, token_grad, scores, loss, *gains_out = unfold(
            pair, qkv_parts, grad_tokens, scores_all, gain_sums, loss, w_gate.shape[1] // width, groups
        )
        gains_out = [v.reshape(-1) for v in gains_out]
    else:
        grad_mixed = heads_to_tokens(mixed, 6, "to_tokens_back")
        qkv_out = spread_sum(tn(rows, grad_mixed.T))
        side = lambda v: lax.psum_scatter(v, "dp", scatter_dimension=0, tiled=True)
        halves = lambda v: lax.all_gather(side(v).astype(bf), "tower", axis=1, tiled=True).astype(f32)
        both = lambda a, b: tn(a[0], b[0]) + tn(a[1], b[1])
        flat = lambda v: v.transpose(0, 2, 1, 3).reshape(2, count, -1)
        out_out = halves(nn(attended[0], grad_branch[0]) + nn(attended[1], grad_branch[1]))
        two = lax.all_gather(side(both(inner, flat(grads))).astype(bf), "tower").astype(f32)
        gate_out, up_out = two[0], two[1]
        down_out = halves(both(flat(hidden), grad_mlp))
        gains_out = spread_sum(gains[:4].T).T
        scores = scores_all.reshape(groups, 8, groups, 8)[:, :DOCS_GRP, :, :DOCS_GRP].reshape(docs, docs)
        token_grad = grad_h1 + lax.dot_general(
            grad_mixed, w_qkv, (((0,), (1,)), ((), ())), preferred_element_type=f32
        )
        token_grad = token_grad[None]
    return (
        scores, loss[0, 0], token_grad, qkv_out, out_out, gains_out[0], gains_out[1],
        gate_out, up_out, down_out, gains_out[2], gains_out[3],
    )


def solution(mesh):
    shard = P("dp", None)
    lone = P("dp")
    return jax.shard_map(
        local,
        mesh=mesh,
        in_specs=(P("tower", "dp", None), P("tower", "dp"), P("tower", "dp")) + (P(),) * 10,
        out_specs=(
            P(), P(), P("tower", "dp", None), shard, shard, lone, lone, shard, shard, shard, lone, lone,
        ),
        check_vma=False,
    )
```

```python
import functools

import jax
import jax.numpy as jnp
import numpy as np
from jax import lax
from jax.experimental import pallas as pl
from jax.experimental.pallas import tpu as pltpu
from jax.sharding import PartitionSpec as P

HEADS = 12
HEAD_DIM = 64
SPAN = 4
DOCS_GRP = 3
NH = HEADS // SPAN
HW = NH * HEAD_DIM
UPWARD = 4
VLIM = 62 * 2**20
MESH = pl.DeviceIdType.MESH
f32 = jnp.float32
bf = jnp.bfloat16
precise = lax.Precision.HIGHEST
norm_eps = 1e-05
ANY = pl.BlockSpec(memory_space=pl.ANY)
VM = pl.BlockSpec(memory_space=pltpu.VMEM)


def nn(a, b):
    return lax.dot_general(a, b, (((1,), (0,)), ((), ())), preferred_element_type=f32)


def nt(a, b):
    return lax.dot_general(a, b, (((1,), (1,)), ((), ())), preferred_element_type=f32)


def tn(a, b):
    return lax.dot_general(a, b, (((0,), (0,)), ((), ())), preferred_element_type=f32)


def split3(v):
    one = v.astype(bf).astype(f32)
    rest = v - one
    two = rest.astype(bf).astype(f32)
    return [one, two, rest - two]


def here():
    t = lax.axis_index("tower")
    p = lax.axis_index("dp")
    x = lax.rem(p, 2)
    y = lax.rem(lax.div(p, 2), 2)
    return t, p, x, y, lax.div(p, SPAN)


def plane_peers():
    t, p, x, y, g = here()
    px = p + 1 - 2 * x
    py = p + 2 - 4 * y
    pd = px + 2 - 4 * y
    return (t, px), (t, py), (t, pd)


def hail(peers):
    for peer in peers:
        pl.semaphore_signal(pltpu.get_barrier_semaphore(), inc=1, device_id=peer, device_id_type=MESH)


def greeted(peers):
    pl.semaphore_wait(pltpu.get_barrier_semaphore(), len(peers))


def greet(peers):
    hail(peers)
    greeted(peers)


def remote(src, dst, send, recv, peer):
    return pltpu.make_async_remote_copy(
        src_ref=src, dst_ref=dst, send_sem=send, recv_sem=recv, device_id=peer, device_id_type=MESH
    )


def dma_sems(n):
    return pltpu.SemaphoreType.DMA((n,))


def comm_params(cid):
    return pltpu.CompilerParams(collective_id=cid, has_side_effects=True, vmem_limit_bytes=VLIM)


def fill_angles(base_ref, cos_ref, sin_ref):
    for i in range(cos_ref.shape[1] // 128):
        at = slice(i * 128, (i + 1) * 128)
        ca, sa = base_ref[0, :, i : i + 1], base_ref[1, :, i : i + 1]
        cb, sb = base_ref[2], base_ref[3]
        cos_ref[:, at] = ca * cb - sa * sb
        sin_ref[:, at] = sa * cb + ca * sb


def gather_kernel(
    tok_ref, ids_ref, pads_ref, base_ref, w_ref, out_ref, codes_ref, qa_ref, ka_ref, va_ref, kt_ref,
    att_ref, lse_ref, exact_ref,
    cos_ref, sin_ref, toks, code_ref, codes, wraw, wturn, wt, qa, ka, va, kt, acc, tops, sooner, later, heads,
    send, recv, csend, crecv, wsem, osem, asend, arecv, asem,
):
    t, p, x, y, g = here()
    count, width = tok_ref.shape
    half = count // 2
    me = lax.rem(p, SPAN)
    odd = lax.rem(me, 2)
    wide = wraw.shape[2]
    loads = []
    for k in range(3):
        at = pl.multiple_of(k * width + me * HW - odd * HEAD_DIM, 128)
        loads.append(pltpu.make_async_copy(w_ref.at[:, pl.ds(at, wide)], wraw.at[k], wsem.at[k]))
        loads[-1].start()
    code_ref[...] = lax.rem(ids_ref[...], DOCS_GRP).astype(f32) + 4.0 * (1 - pads_ref[...]).astype(f32)
    ex, ey, ed = plane_peers()
    mx, my, md = (lax.rem(q[1], SPAN) for q in (ex, ey, ed))

    def rows(m, h):
        return pl.ds(pl.multiple_of(m * count + h * half, half), half)

    def whole(m):
        return pl.ds(pl.multiple_of(m * count, count), count)

    greet((ex, ey, ed))
    first = []
    for i, (peer, h) in enumerate(((ex, 0), (ey, 1), (ex, 1), (ey, 0))):
        c = remote(tok_ref.at[pl.ds(h * half, half)], toks.at[rows(me, h)], send.at[i], recv.at[i], peer)
        c.start()
        first.append(c)
    small = []
    for i, peer in enumerate((ex, ey, ed)):
        c = remote(code_ref, codes.at[:, whole(me)], csend.at[i], crecv.at[i], peer)
        c.start()
        small.append(c)
    codes[:, whole(me)] = code_ref[...]
    fill_angles(base_ref, cos_ref, sin_ref)
    for k in range(3):
        loads[k].wait()
        wturn[...] = wraw[k].T
        wt[k * HW : (k + 1) * HW, :] = wturn[pl.ds(pl.multiple_of(odd * HEAD_DIM, HEAD_DIM), HW), :]

    def project(rows_ref, m, n):
        sl = whole(m)
        mx = nt(wt[...], rows_ref[...])
        cos, sin = cos_ref[:, sl], sin_ref[:, sl]
        cd = codes[:, sl]
        mem = jnp.where(cd >= 4.0, cd - 4.0, cd)
        pad = [jnp.zeros((13, count), f32)]
        hot = jnp.concatenate([jnp.where(mem == float(d), 1.0, 0.0) for d in range(DOCS_GRP)] + pad, 0)
        neg = jnp.concatenate([jnp.where(cd == float(d), 0.0, -1e30) for d in range(DOCS_GRP)] + pad, 0)
        rest = jnp.zeros((48, count), f32)
        one = jnp.concatenate([jnp.ones((1, count), f32), jnp.zeros((63, count), f32)], 0)

        def rope(u):
            a, b = u[:32], u[32:]
            return jnp.concatenate([a * cos - b * sin, b * cos + a * sin], 0)

        for h in range(NH):
            q = rope(mx[h * HEAD_DIM : (h + 1) * HEAD_DIM]).astype(bf).astype(f32) * 0.125
            k = rope(mx[HW + h * HEAD_DIM : HW + (h + 1) * HEAD_DIM])
            v = mx[2 * HW + h * HEAD_DIM : 2 * HW + (h + 1) * HEAD_DIM]
            qa[h, :, sl] = jnp.concatenate([q, hot, rest], 0).astype(bf)
            ka[h, sl, :] = jnp.concatenate([k, neg, rest], 0).T.astype(bf)
            va[h, :, sl] = jnp.concatenate([v, one], 0).astype(bf)
            kt[h, :, sl] = k.astype(bf)
        puts = (
            (rows_ref, out_ref.at[sl]),
            (qa.at[:, :, sl], qa_ref.at[:, :, sl]),
            (ka.at[:, sl, :], ka_ref.at[:, sl, :]),
            (va.at[:, :, sl], va_ref.at[:, :, sl]),
            (kt.at[:, :, sl], kt_ref.at[:, :, sl]),
        )
        puts = [pltpu.make_async_copy(a, b, osem.at[5 * n + i]) for i, (a, b) in enumerate(puts)]
        for c in puts:
            c.start()
        return puts

    part = count // 2
    acc[...] = jnp.zeros_like(acc)
    tops[...] = jnp.full_like(tops, -3e38)
    chunks = (me, mx, my, md)
    inside = jnp.where((me == 1) | (me == 2), 1, 0)

    def pick(n, values):
        got = values[-1]
        for i in reversed(range(len(values) - 1)):
            got = jnp.where(n == i, values[i], got)
        return got

    def segment(q, key_of, trips):
        qs = whole(q)

        def keys(n, k):
            return pl.ds(pl.multiple_of(key_of(n) * count + k * part, part), part)

        def scores(n, k, h, ref):
            ref[h] = nn(ka[h, keys(n, k), :], qa[h, :, qs])

        def absorb(n, k, h, ref, m):
            s = ref[h]
            mn = jnp.maximum(m, jnp.max(s, 0, keepdims=True))
            pr = jnp.exp(s - mn).astype(bf)
            acc[q, h] = acc[q, h] * jnp.exp(m - mn) + nn(va[h, :80, keys(n, k)], pr)
            return mn

        for h in range(NH):
            scores(0, 0, h, sooner)

        def step(n, ms):
            ms = list(ms)
            for h in range(NH):
                scores(n, 1, h, later)
                ms[h] = absorb(n, 0, h, sooner, ms[h])
            after = jnp.minimum(n + 1, jnp.maximum(trips - 1, 0))
            for h in range(NH):
                scores(after, 0, h, sooner)
                ms[h] = absorb(n, 1, h, later, ms[h])
            return tuple(ms)

        ms = lax.fori_loop(0, trips, step, tuple(tops[q * NH + h] for h in range(NH)))
        for h in range(NH):
            tops[q * NH + h] = ms[h]

    def finalize(q):
        qs = whole(q)
        edge = jnp.where((q == 0) | (q == SPAN - 1), 1.0, 0.0)
        other = whole(SPAN - 1 - q)
        for h in range(NH):
            m = tops[q * NH + h]
            rest = jnp.sum(va[h, :80, other].astype(f32), 1, keepdims=True)
            full = acc[q, h] + rest * jnp.where(m < -1e29, edge, 0.0)
            tot = full[64:65]
            o = full[:64] / tot
            at = pl.ds(h * HEAD_DIM, HEAD_DIM)
            exact_ref[at, qs] = o
            lse_ref[h : h + 1, qs] = jnp.where(m < -1e29, 0.0, m + jnp.log(tot))
            heads[at, qs] = o.astype(bf)

    done = project(tok_ref, me, 0)
    first[0].wait_recv()
    f0 = remote(toks.at[rows(mx, 0)], toks.at[rows(mx, 0)], send.at[4], recv.at[4], ey)
    f0.start()
    first[1].wait_recv()
    f1 = remote(toks.at[rows(my, 1)], toks.at[rows(my, 1)], send.at[5], recv.at[5], ex)
    f1.start()
    segment(me, lambda n: me, 1)
    for c in small:
        c.wait()
    first[2].wait_recv()
    done += project(toks.at[whole(mx)], mx, 1)
    first[3].wait_recv()
    done += project(toks.at[whole(my)], my, 2)

    def near(s, _):
        q = pick(s, chunks[:3])
        key_of = lambda n: pick(s, (pick(n, (mx, my)), pick(n, (me, mx, my)), pick(n, (me, my, mx))))
        segment(q, key_of, jnp.where(s == 0, 2, 3 - inside))
        return 0

    lax.fori_loop(0, 3, near, 0)
    f0.wait_recv()
    f1.wait_recv()
    done += project(toks.at[whole(md)], md, 3)

    def back(s):
        peer = (ed, ex, ey)[s]
        m = (md, mx, my)[s]
        return remote(
            heads.at[:, whole(m)], att_ref.at[pl.ds(pl.multiple_of(me * HW, HW), HW)], asend.at[s], arecv.at[s], peer
        )

    def far(s, _):
        q = pick(s, (md, mx, my, me))
        key_of = lambda n: jnp.where(s == 0, pick(n, (mx, my, md, me)), md)
        segment(q, key_of, pick(s, (3 + inside, 1, 1, inside)))
        finalize(q)
        for k in range(3):
            pl.when(s == k)(lambda k=k: back(k).start())
        return 0

    lax.fori_loop(0, 4, far, 0)
    own = pltpu.make_async_copy(
        heads.at[:, whole(me)], att_ref.at[pl.ds(pl.multiple_of(me * HW, HW), HW)], asem.at[0]
    )
    own.start()
    codes_ref[...] = codes[...]
    for c in first + [f0, f1]:
        c.wait_send()
    for c in done:
        c.wait()
    own.wait()
    for k in range(3):
        back(k).wait()


def gather(tok, ids, pads, base, w_qkv):
    count, width = tok.shape
    total = SPAN * count
    shapes = ((NH, 128, total), (NH, total, 128), (NH, 128, total), (NH, HEAD_DIM, total))
    return pl.pallas_call(
        gather_kernel,
        out_shape=(jax.ShapeDtypeStruct((total, width), bf), jax.ShapeDtypeStruct((1, total), f32))
        + tuple(jax.ShapeDtypeStruct(s, bf) for s in shapes)
        + (
            jax.ShapeDtypeStruct((SPAN * HW, count), bf), jax.ShapeDtypeStruct((NH, total), f32),
            jax.ShapeDtypeStruct((HW, total), f32),
        ),
        in_specs=[VM] * 4 + [ANY],
        out_specs=(ANY, VM) + (ANY,) * 5 + (VM,) * 2,
        scratch_shapes=[
            pltpu.VMEM((HEAD_DIM // 2, total), f32), pltpu.VMEM((HEAD_DIM // 2, total), f32),
            pltpu.VMEM((total, width), bf), pltpu.VMEM((1, count), f32), pltpu.VMEM((1, total), f32), pltpu.VMEM((3, width, 256), bf),
            pltpu.VMEM((256, width), bf), pltpu.VMEM((3 * HW, width), bf),
        ]
        + [pltpu.VMEM(s, bf) for s in shapes]
        + [
            pltpu.VMEM((SPAN, NH, 80, count), f32), pltpu.VMEM((SPAN * NH, 1, count), f32),
            pltpu.VMEM((NH, count // 2, count), f32), pltpu.VMEM((NH, count // 2, count), f32),
            pltpu.VMEM((HW, total), bf),
            dma_sems(6), dma_sems(6), dma_sems(3), dma_sems(3), dma_sems(3), dma_sems(20),
            dma_sems(3), dma_sems(3), dma_sems(1),
        ],
        compiler_params=comm_params(0),
        name="gather",
    )(tok, ids, pads, base, w_qkv)


def heads_to_tokens_kernel(parts, in_ref, out_ref, send, recv, lsem):
    t, p, x, y, g = here()
    count = out_ref.shape[1]
    me = lax.rem(p, SPAN)
    peers = plane_peers()
    width = parts and out_ref.shape[0] // parts
    greet(peers)
    copies = []
    for i, peer in enumerate((peers[2], peers[0], peers[1])):
        m = lax.rem(peer[1], SPAN)
        for k in range(parts):
            c = remote(
                in_ref.at[pl.ds(k * HW, HW), pl.ds(pl.multiple_of(m * count, count), count)],
                out_ref.at[pl.ds(pl.multiple_of(k * width + me * HW, HW), HW)],
                send.at[i * parts + k],
                recv.at[i * parts + k],
                peer,
            )
            c.start()
            copies.append(c)
    for k in range(parts):
        c = pltpu.make_async_copy(
            in_ref.at[pl.ds(k * HW, HW), pl.ds(pl.multiple_of(me * count, count), count)],
            out_ref.at[pl.ds(pl.multiple_of(k * width + me * HW, HW), HW)],
            lsem.at[k],
        )
        c.start()
        copies.append(c)
    for c in copies:
        c.wait()


def heads_to_tokens(a, cid, name):
    parts = a.shape[0] // HW
    count = a.shape[1] // SPAN
    return pl.pallas_call(
        functools.partial(heads_to_tokens_kernel, parts),
        out_shape=jax.ShapeDtypeStruct((parts * HEADS * HEAD_DIM, count), a.dtype),
        in_specs=[VM],
        out_specs=ANY,
        scratch_shapes=[dma_sems(3 * parts), dma_sems(3 * parts), dma_sems(parts)],
        compiler_params=comm_params(cid),
        name=name,
    )(a)


def tokens_to_heads_kernel(in_ref, out_ref, send, recv, lsem):
    t, p, x, y, g = here()
    count = in_ref.shape[1]
    me = lax.rem(p, SPAN)
    peers = plane_peers()
    greet(peers)
    mine = pl.ds(pl.multiple_of(me * count, count), count)
    copies = []
    for i, peer in enumerate((peers[2], peers[0], peers[1])):
        m = lax.rem(peer[1], SPAN)
        c = remote(
            in_ref.at[pl.ds(pl.multiple_of(m * HW, HW), HW)],
            out_ref.at[:, mine],
            send.at[i],
            recv.at[i],
            peer,
        )
        c.start()
        copies.append(c)
    c = pltpu.make_async_copy(
        in_ref.at[pl.ds(pl.multiple_of(me * HW, HW), HW)], out_ref.at[:, mine], lsem.at[0]
    )
    c.start()
    for c in copies + [c]:
        c.wait()


def tokens_to_heads(a, cid, name):
    return pl.pallas_call(
        tokens_to_heads_kernel,
        out_shape=jax.ShapeDtypeStruct((HW, SPAN * a.shape[1]), a.dtype),
        in_specs=[VM],
        out_specs=ANY,
        scratch_shapes=[dma_sems(3), dma_sems(3), dma_sems(1)],
        compiler_params=comm_params(cid),
        name=name,
    )(a)


def doc_limits(code):
    pad = code >= 4.0
    mem = jnp.where(pad, code - 4.0, code)
    n0 = jnp.sum(jnp.where(mem < 0.5, 1.0, 0.0)).astype(jnp.int32)
    n1 = jnp.sum(jnp.where(mem < 1.5, 1.0, 0.0)).astype(jnp.int32)
    l = [jnp.sum(jnp.where(code == float(d), 1.0, 0.0)).astype(jnp.int32) for d in range(3)]
    return n0, n1, l

def block_range(lims, a, size, total):
    n0, n1, l = lims
    b = a + size - 1
    first = (a >= n0).astype(jnp.int32) + (a >= n1).astype(jnp.int32)
    last = (b >= n0).astype(jnp.int32) + (b >= n1).astype(jnp.int32)
    lo = jnp.where(first == 0, 0, jnp.where(first == 1, n0, n1))
    hi = jnp.where(last == 0, n0, jnp.where(last == 1, n1, total))
    dead = jnp.zeros((), jnp.bool_)
    for d in range(3):
        dead = dead | ((first <= d) & (d <= last) & (l[d] == 0))
    return jnp.where(dead, 0, lo), jnp.where(dead, total, hi)

def bwd_kernel(KB, QB, do_ref, o32_ref, lse_ref, qa_ref, ka_ref, va_ref, kt_ref, base_ref, code_ref, g_ref,
               cos_ref, sin_ref, vn_ref, dn_ref, da_ref, qb_ref, acc_ref, dq_ref):
    T = do_ref.shape[1]
    hw = HW
    CH = 512
    lims = doc_limits(code_ref[...])
    fill_angles(base_ref, cos_ref, sin_ref)
    def prep(c, _):
        sl = pl.ds(pl.multiple_of(c*CH, CH), CH)
        for h in range(NH):
            do = do_ref[h*HEAD_DIM:(h+1)*HEAD_DIM, sl].astype(f32)
            delta = jnp.sum(do*o32_ref[h*HEAD_DIM:(h+1)*HEAD_DIM, sl], 0, keepdims=True)
            def split(x):
                x1 = x.astype(bf).astype(f32); r = x-x1
                x2 = r.astype(bf).astype(f32); x3 = r-x2
                return [x1, x2, x3]
            z13 = jnp.zeros((13, CH), f32); z48 = jnp.zeros((48, CH), f32)
            da_ref[h, :, sl] = jnp.concatenate([do]+split(-delta)+[z13, z48], 0).astype(bf)
            one = jnp.concatenate([jnp.ones((3, CH), f32), jnp.zeros((61, CH), f32)], 0)
            v = va_ref[h, :64, sl].astype(f32)
            vn_ref[h, sl, :] = jnp.concatenate([v, one], 0).T.astype(bf)
            z64 = jnp.zeros((64, CH), f32)
            q = qa_ref[h, :64, sl].astype(f32)
            dn_ref[h, sl, :] = jnp.concatenate([do, z64], 0).T.astype(bf)
            qb_ref[h, sl, :] = jnp.concatenate([z64, q], 0).T.astype(bf)
            acc_ref[h, sl, :] = jnp.zeros((CH, 128), f32)
        return 0
    lax.fori_loop(0, T//CH, prep, 0)
    def qblock(i, _):
        a = i*QB
        qs = pl.ds(pl.multiple_of(a, QB), QB)
        lo, hi = block_range(lims, a, QB, T)
        small = KB // 2
        start = lo // small
        many = (hi + small - 1) // small - start
        dq_ref[...] = jnp.zeros_like(dq_ref)

        def visit(at, size):
            ks = pl.ds(pl.multiple_of(at * small, small), size)
            for h in range(NH):
                s = nn(ka_ref[h, ks, :], qa_ref[h, :, qs])
                dp = nn(vn_ref[h, ks, :], da_ref[h, :, qs])
                p = jnp.exp(s - lse_ref[h:h+1, qs])
                ds = (p*dp).astype(bf)
                acc_ref[h, ks, :] += nn(p.astype(bf), dn_ref[h, qs, :]) + nn(ds, qb_ref[h, qs, :])
                dq_ref[h] += nn(kt_ref[h, :, ks], ds)

        def kv(j, _):
            visit(start + 2 * j, KB)
            return 0
        lax.fori_loop(0, many // 2, kv, 0)
        pl.when(many % 2 == 1)(lambda: visit(start + many - 1, small))
        cos = cos_ref[:, qs]; sin = sin_ref[:, qs]
        for h in range(NH):
            u = dq_ref[h]*0.125
            x1 = u[:32]; x2 = u[32:]
            g_ref[h*HEAD_DIM:(h+1)*HEAD_DIM, qs] = jnp.concatenate([x1*cos+x2*sin, x2*cos-x1*sin], 0).astype(bf)
        return 0
    lax.fori_loop(0, T//QB, qblock, 0)
    def fin(c, _):
        sl = pl.ds(pl.multiple_of(c*CH, CH), CH)
        cos = cos_ref[:, sl]; sin = sin_ref[:, sl]
        for h in range(NH):
            t = acc_ref[h, sl, :].T
            x1 = t[64:96]; x2 = t[96:128]
            g_ref[hw+h*HEAD_DIM:hw+(h+1)*HEAD_DIM, sl] = jnp.concatenate([x1*cos+x2*sin, x2*cos-x1*sin], 0).astype(bf)
            g_ref[2*hw+h*HEAD_DIM:2*hw+(h+1)*HEAD_DIM, sl] = t[:64].astype(bf)
        return 0
    lax.fori_loop(0, T//CH, fin, 0)

def attn_bwd(do, o32, lse, qa, ka, va, kt, base, code, KB=512, QB=256):
    T = do.shape[1]
    return pl.pallas_call(functools.partial(bwd_kernel, KB, QB),
        out_shape=jax.ShapeDtypeStruct((3*NH*HEAD_DIM, T), bf),
        in_specs=[VM] * 9, out_specs=pl.BlockSpec(memory_space=pltpu.VMEM),
        scratch_shapes=[pltpu.VMEM((HEAD_DIM // 2, T), f32), pltpu.VMEM((HEAD_DIM // 2, T), f32), pltpu.VMEM((NH,T,128), bf), pltpu.VMEM((NH,T,128), bf), pltpu.VMEM((NH,128,T), bf), pltpu.VMEM((NH,T,128), bf),
                        pltpu.VMEM((NH,T,128), f32), pltpu.VMEM((NH,HEAD_DIM,QB), f32)],
        compiler_params=pltpu.CompilerParams(vmem_limit_bytes=VLIM), name="attn_bwd",
        cost_estimate=pl.CostEstimate(flops=int(10*T*T*128*3), bytes_accessed=12<<20, transcendentals=T*T*3))(do, o32, lse, qa, ka, va, kt, base, code)


def contrast_part(groups, sums, goals_ref, plane, allp, ge, send, recv, scores_ref, loss_ref):
    t, p, x, y, g = here()
    docs = groups * DOCS_GRP
    size = groups * 8
    peers = plane_peers()
    line = [(t, lax.rem(p + SPAN * k, SPAN * groups)) for k in range(1, groups)]
    plane[3] = sums
    copies = [remote(plane.at[3], plane.at[i], send.at[i], recv.at[i], q) for i, q in enumerate(peers)]
    for c in copies:
        c.start()
    col = lax.broadcasted_iota(jnp.int32, (size, size), 1)
    row = lax.broadcasted_iota(jnp.int32, (size, size), 0)

    def mark(i, hot):
        goal = goals_ref[i]
        at = (row == i // DOCS_GRP * 8 + i % DOCS_GRP) & (col == goal // DOCS_GRP * 8 + goal % DOCS_GRP)
        return hot + jnp.where(at, 1.0, 0.0)

    hot = lax.fori_loop(0, docs, mark, jnp.zeros((size, size), f32))
    for c in copies:
        c.wait()
    own = (plane[3] + plane[0]) + (plane[1] + plane[2])
    allp[t, g] = own
    rows = allp.at[t, g]
    copies = [remote(rows, rows, send.at[3 + i], recv.at[3 + i], q) for i, q in enumerate(line)]
    for c in copies:
        c.start()
    for c in copies:
        c.wait()
    c = remote(allp.at[t], allp.at[t], send.at[2 + groups], recv.at[2 + groups], (1 - t, p))
    c.start()
    c.wait()
    width = allp.shape[3]
    pools = [allp[k].reshape(size, width) for k in range(2)]
    embeds = [v * lax.rsqrt(jnp.sum(v * v, -1, keepdims=True) + 1e-06) for v in pools]
    dot = functools.partial(lax.dot_general, precision=precise, preferred_element_type=f32)
    scores = dot(embeds[0], embeds[1], (((1,), (1,)), ((), ()))) * 50.0
    live = lax.rem(col, 8) < DOCS_GRP
    alive = lax.rem(row, 8) < DOCS_GRP
    masked = jnp.where(live, scores, -1e30)
    top = jnp.max(masked, -1, keepdims=True)
    total = jnp.sum(jnp.exp(masked - top), -1, keepdims=True)
    log_sums = top + jnp.log(total)
    chosen = jnp.sum(hot * scores, -1, keepdims=True)
    each = jnp.where(alive[:, 0:1], log_sums - chosen, 0.0)
    loss_ref[...] = jnp.broadcast_to(jnp.sum(each, 0, keepdims=True) / docs, loss_ref.shape)
    scores_ref[...] = scores
    gs = jnp.where(alive & live, (jnp.exp(masked - log_sums) - hot) / docs, 0.0)
    gq = dot(gs, embeds[1], (((1,), (0,)), ((), ())))
    gd = dot(gs, embeds[0], (((0,), (0,)), ((), ())))
    ge[...] = jnp.where(t == 0, gq, gd) * 50.0
    mine = ge[pl.ds(pl.multiple_of(g * 8, 8), 8), :]
    pooled = allp[t, g]
    inv = lax.rsqrt(jnp.sum(pooled * pooled, -1, keepdims=True) + 1e-06)
    return inv * mine - inv * inv * inv * pooled * jnp.sum(pooled * mine, -1, keepdims=True)


def block_kernel(
    groups, heads_ref, rows_ref, codes_ref, goals_ref, gain1_ref, bias1_ref, gain2_ref, bias2_ref, wo_h, wg_h, wu_h, wd_h,
    att_o, inner_o, hid_o, gm_o, gg_o, gb_o, ga_o, gh1_o, gains_o, scores_o, loss_o,
    att, wo, wg, wu, wd, inner, x1, s1, acc, hid, ab, x2, s2, sec, gm, gm2, gb, gb2, plane, allp, ge,
    wsem, lsem, tsend, trecv, osem, csend, crecv,
):
    t, p, x, y, g = here()
    peers = plane_peers()
    sibling = (1 - t, p)
    line = tuple((t, lax.rem(p + SPAN * k, SPAN * groups)) for k in range(1, groups))
    count, width = rows_ref.shape
    half = width // 2
    tiles = wg.shape[0]
    me = lax.rem(p, SPAN)

    def weight(j, k):
        cols = pl.ds(j * width if isinstance(j, int) else pl.multiple_of(j * width, width), width)
        src, dst = ((wg_h.at[:, cols], wg.at[j]), (wu_h.at[:, cols], wu.at[j]), (wd_h.at[cols], wd.at[j]))[k]
        return pltpu.make_async_copy(src, dst, wsem.at[1 + 3 * j + k])

    first_load = pltpu.make_async_copy(wo_h, wo, wsem.at[0])
    everyone = peers + (sibling,) + line
    hail(everyone)
    heads_load = pltpu.make_async_copy(heads_ref, att, lsem.at[0])
    heads_load.start()
    first_load.start()
    for j in range(tiles):
        for k in range(3):
            weight(j, k).start()
    code = codes_ref[:, pl.ds(pl.multiple_of(me * count, count), count)]
    zero = jnp.zeros((8 - DOCS_GRP, count), f32)
    mem = jnp.concatenate([jnp.where(code == float(d), 1.0, 0.0) for d in range(DOCS_GRP)] + [zero], 0)
    mem = jnp.concatenate([mem, mem, mem, jnp.zeros((8, count), f32)], 0).astype(bf)
    first_load.wait()
    heads_load.wait()

    def pair(i, mine, its, out):
        return (
            pltpu.make_async_copy(mine, out.at[0], osem.at[i]),
            remote(its, out.at[1], tsend.at[i], trecv.at[i], sibling),
        )

    def both(i, mine, its, out):
        for c in pair(i, mine, its, out):
            c.start()

    acc[...] = tn(att[...], wo[...])
    greeted(everyone)
    both(0, att, att, att_o)
    step = 64
    gain1, bias1, gain2, bias2 = (r[...].reshape(1, width) for r in (gain1_ref, bias1_ref, gain2_ref, bias2_ref))

    def chunk(i):
        return pl.ds(pl.multiple_of(i * step, step), step)

    def norm(h, sl, xs, ss):
        c = h - jnp.mean(h, -1, keepdims=True)
        s = lax.rsqrt(jnp.mean(c * c, -1, keepdims=True) + norm_eps)
        xh = c * s
        xs[sl, :] = xh
        ss[sl, :] = s
        return xh

    def norm_one(i, _):
        sl = chunk(i)
        xh = norm(rows_ref[sl, :].astype(f32) + acc[sl, :], sl, x1, s1)
        v = xh * gain1 + bias1
        inner[sl, :] = v.astype(bf)
        acc[sl, :] = v
        return 0

    lax.fori_loop(0, count // step, norm_one, 0)
    both(1, inner, inner, inner_o)

    def tile_of(j, i, mine, its, out):
        return (
            pltpu.make_async_copy(mine, out.at[0, j], osem.at[i + j]),
            remote(its, out.at[1, j], tsend.at[i + j], trecv.at[i + j], sibling),
        )

    def forward(n, _):
        for i in range(2):
            j = 2 * n + i
            for k in range(3):
                weight(j, k).wait()
            gate = nn(inner[...], wg[j])
            upper = nn(inner[...], wu[j])
            sig = jax.nn.sigmoid(gate)
            silu = gate * sig
            hid[j] = (silu * upper).astype(bf)
            ab[0, j] = (upper * (sig * (1.0 + gate * (1.0 - sig)))).astype(bf)
            ab[1, j] = silu.astype(bf)
            for c in tile_of(j, 2, hid.at[j], hid.at[j], hid_o):
                c.start()
            acc[...] += nn(hid[j], wd[j])
        return 0

    lax.fori_loop(0, tiles // 2, forward, 0)

    def norm_two(i, _):
        sl = chunk(i)
        v = norm(acc[sl, :], sl, x2, s2) * gain2 + bias2
        for k, part in enumerate(split3(v)):
            sec[k, sl, :] = part.astype(bf)
        return 0

    lax.fori_loop(0, count // step, norm_two, 0)
    sums = (nn(mem[:16], sec[0]) + nn(mem[:16], sec[1]) + nn(mem[:16], sec[2]))[:8]
    top = lax.broadcasted_iota(jnp.int32, sums.shape, 0) < DOCS_GRP
    sums = jnp.where(top, sums, 0.0)
    gp = contrast_part(groups, sums, goals_ref, plane, allp, ge, csend, crecv, scores_o, loss_o)
    gp3 = jnp.concatenate(split3(gp) + [jnp.zeros_like(gp)], 0).astype(bf)
    acc[...] = tn(mem, gp3)

    def fold(v):
        return jnp.sum(v.reshape(step // 8, 8, width), 0)

    def norm_back(gr, xh, s, gain):
        e = gr * gain
        v = e - jnp.mean(e, -1, keepdims=True) - xh * jnp.mean(e * xh, -1, keepdims=True)
        return v * s

    zeros = jnp.zeros((8, width), f32)

    def back_two(i, sums):
        sl = chunk(i)
        gr, xh = acc[sl, :], x2[sl, :]
        v = norm_back(gr, xh, s2[sl, :], gain2)
        acc[sl, :] = v
        low = v.astype(bf)
        gm[sl, :] = low
        gm2[0, sl, :] = low[:, :half]
        gm2[1, sl, :] = low[:, half:]
        return sums[0] + fold(gr * xh), sums[1] + fold(gr)

    g2, b2 = lax.fori_loop(0, count // step, back_two, (zeros, zeros))
    both(2 + 2 * tiles, gm2.at[t], gm2.at[1 - t], gm_o)
    def backward(n, _):
        for j in range(tiles):
            gh = nt(gm[...], wd[j])
            gg = (gh * ab[0, j].astype(f32)).astype(bf)
            gu = (gh * ab[1, j].astype(f32)).astype(bf)
            ab[0, j] = gg
            ab[1, j] = gu
            for c in tile_of(j, 2 + tiles, ab.at[t, j], ab.at[1 - t, j], gg_o):
                c.start()
            acc[...] += nt(gg, wg[j]) + nt(gu, wu[j])
        return 0

    backward(0, 0)

    def back_one(i, sums):
        sl = chunk(i)
        gr, xh = acc[sl, :], x1[sl, :]
        v = norm_back(gr, xh, s1[sl, :], gain1)
        gh1_o[sl, :] = v
        low = v.astype(bf)
        gb[sl, :] = low
        gb2[0, sl, :] = low[:, :half]
        gb2[1, sl, :] = low[:, half:]
        return sums[0] + fold(gr * xh), sums[1] + fold(gr)

    g1, b1 = lax.fori_loop(0, count // step, back_one, (zeros, zeros))
    both(3 + 2 * tiles, gb2.at[t], gb2.at[1 - t], gb_o)
    flat = [jnp.sum(v, 0, keepdims=True) for v in (g1, b1, g2, b2)]
    gains_o[...] = jnp.concatenate(flat + [jnp.zeros((4, width), f32)], 0)
    ga_o[...] = nt(wo[...], gb[...]).astype(bf)
    done = [pair(0, att, att, att_o), pair(1, inner, inner, inner_o)]
    for j in range(tiles):
        done.append(tile_of(j, 2, hid.at[j], hid.at[j], hid_o))
        done.append(tile_of(j, 2 + tiles, ab.at[t, j], ab.at[1 - t, j], gg_o))
    done.append(pair(2 + 2 * tiles, gm2.at[t], gm2.at[1 - t], gm_o))
    done.append(pair(3 + 2 * tiles, gb2.at[t], gb2.at[1 - t], gb_o))
    for c in done:
        for d in c:
            d.wait()


def block(heads, rows, codes, goals, norms, w_out, w_gate, w_up, w_down, groups):
    count, width = rows.shape
    tiles = w_gate.shape[1] // width
    half = width // 2
    size = groups * 8
    sds = jax.ShapeDtypeStruct
    vm = lambda *n: pltpu.VMEM(n, bf)
    vf = lambda *n: pltpu.VMEM(n, f32)
    return pl.pallas_call(
        functools.partial(block_kernel, groups),
        out_shape=(
            sds((2, width, count), bf), sds((2, count, width), bf), sds((2, tiles, count, width), bf),
            sds((2, count, half), bf), sds((2, tiles, count, width), bf), sds((2, count, half), bf),
            sds((width, count), bf), sds((count, width), f32), sds((8, width), f32),
            sds((size, size), f32), sds((8, 128), f32),
        ),
        in_specs=[ANY, VM, VM, pl.BlockSpec(memory_space=pltpu.SMEM)] + [VM] * 4 + [ANY] * 4,
        out_specs=(ANY,) * 6 + (VM,) * 5,
        scratch_shapes=[
            vm(width, count), vm(width, width), vm(tiles, width, width), vm(tiles, width, width),
            vm(tiles, width, width), vm(count, width), vf(count, width), vf(count, 1), vf(count, width),
            vm(tiles, count, width), vm(2, tiles, count, width), vf(count, width), vf(count, 1),
            vm(3, count, width), vm(count, width), vm(2, count, half), vm(count, width), vm(2, count, half),
            vf(4, 8, width), vf(2, groups, 8, width), vf(size, width),
            dma_sems(1 + 3 * tiles), dma_sems(1),
            dma_sems(4 + 2 * tiles), dma_sems(4 + 2 * tiles), dma_sems(4 + 2 * tiles),
            dma_sems(3 + groups), dma_sems(3 + groups),
        ],
        compiler_params=comm_params(1),
        name="block",
    )(heads, rows, codes, goals, *norms, w_out, w_gate, w_up, w_down)


def weights_kernel(
    groups, i_ref, g_ref, h_ref, m_ref, a_ref, b_ref, in_ref,
    sa_ref, ka_ref, sb_ref, kb_ref, sc_ref, kc_ref, heads_ref,
    iv, it, gv, hv, mv, av, bv, gs, ds, os, isem, osem, send, recv, lsem,
):
    t, p, x, y, g = here()
    level = lax.rem(g, 2)
    peers = plane_peers()
    count, width = i_ref.shape[1:]
    half = width // 2
    tiles = gv.shape[0]
    shards = SPAN * groups
    one = width // shards
    down = ds.shape[1]

    def load(i, src, dst):
        return pltpu.make_async_copy(src, dst, isem.at[i])

    class Both:
        def __init__(self, *copies):
            self.copies = copies

        def start(self):
            for c in self.copies:
                c.start()

        def wait(self):
            for c in self.copies:
                c.wait()

    def tile(ref, j, buf, base):
        return Both(*(
            load(base + 2 * j + i, ref.at[i, j], buf.at[j, pl.ds(i * count, count)]) for i in range(2)
        ))

    def stack(base, ref, buf):
        return Both(*(load(base + i, ref.at[i], buf.at[pl.ds(i * count, count)]) for i in range(2)))

    def beside(base, ref, buf):
        return Both(*(load(base + i, ref.at[i], buf.at[:, pl.ds(i * count, count)]) for i in range(2)))

    hail(peers)
    few = [stack(0, m_ref, mv), beside(2, a_ref, av), stack(4, b_ref, bv), stack(6, i_ref, iv)]
    few[0].start()
    for j in range(tiles):
        tile(h_ref, j, hv, 8).start()
    for c in few[1:]:
        c.start()
    for j in range(tiles):
        tile(g_ref, j, gv, 8 + 2 * tiles).start()
    greeted(peers)
    tokens = in_ref.shape[1]
    me = lax.rem(p, SPAN)
    mine = pl.ds(pl.multiple_of(me * tokens, tokens), tokens)
    moves = []
    for i, peer in enumerate((peers[2], peers[0], peers[1])):
        m = lax.rem(peer[1], SPAN)
        moves.append(remote(
            in_ref.at[pl.ds(pl.multiple_of(m * HW, HW), HW)], heads_ref.at[:, mine],
            send.at[i], recv.at[i], peer,
        ))
    moves.append(pltpu.make_async_copy(
        in_ref.at[pl.ds(pl.multiple_of(me * HW, HW), HW)], heads_ref.at[:, mine], lsem.at[0]
    ))
    for c in moves:
        c.start()
    few[0].wait()

    def downward(j, _):
        tile(h_ref, j, hv, 8).wait()
        r = tn(hv[j], mv[...])
        ds[pl.ds(j * (width // down), width // down)] = r.astype(bf).reshape(width // down, down, half)
        return 0

    lax.fori_loop(0, tiles, downward, 0)
    for c in few[1:]:
        c.wait()
    r = nn(av[...], bv[...])
    os[...] = r.astype(bf).reshape(shards, one, half)
    it[...] = iv[...].T
    third = one // 3
    fours = lambda ref, n: ref.reshape(groups, 2, 2, n, half)

    def put(i, src, dst):
        return pltpu.make_async_copy(src, dst, osem.at[i])

    outs = []
    for i, (ref, k) in enumerate(((sb_ref, 1 - y), (kb_ref, y))):
        outs.append(put(4 * i, fours(ds, down).at[:, k], ref.at[:, :, pl.ds(0, down)]))
        outs.append(put(4 * i + 1, fours(os, one).at[:, k, :, pl.ds(third, third)], ref.at[:, :, pl.ds(down, third)]))
    for i, (ref, k) in enumerate(((sa_ref, 1 - x), (ka_ref, x))):
        to = ref.at[:, :, pl.ds(ref.shape[2] - third, third)]
        outs.append(put(2 + i, fours(os, one).at[:, :, k, pl.ds(0, third)], to))
    levels = os.reshape(groups // 2, 2, SPAN, one, half)
    for i, (ref, k) in enumerate(((sc_ref, 1 - level), (kc_ref, level))):
        to = ref.at[:, :, pl.ds(ref.shape[2] - third, third)]
        outs.append(put(6 + i, levels.at[:, k, :, pl.ds(2 * third, third)], to))
    for c in outs:
        c.start()

    sideways = sa_ref.shape[2] // one

    def top(j):
        if j < sideways:
            rows = pl.ds(j * one, one)
            piece = fours(gs.at[j], one)
            went, kept = (piece.at[:, :, 1 - x], sa_ref), (piece.at[:, :, x], ka_ref)
        else:
            rows = pl.ds((j - sideways) * one, one)
            piece = gs.at[j].reshape(groups // 2, 2, SPAN, one, half)
            went, kept = (piece.at[:, 1 - level], sc_ref), (piece.at[:, level], kc_ref)
        return (
            put(8 + j, went[0], went[1].at[:, :, rows]),
            put(8 + 2 * tiles + j, kept[0], kept[1].at[:, :, rows]),
        )

    for j in range(tiles):
        tile(g_ref, j, gv, 8 + 2 * tiles).wait()
        r = nn(it[...], gv[j]).astype(bf)
        for h in range(2):
            k = 2 * j + h
            gs[k] = r[:, h * half : (h + 1) * half].reshape(shards, one, half)
            outs.extend(top(k))
            for c in outs[-2:]:
                c.start()
    for c in outs + moves:
        c.wait()


def weight_grads(groups, grad_heads, inner, grads, hidden, grad_mlp, attended, grad_branch):
    count, width = inner.shape[1:]
    half = width // 2
    shards = SPAN * groups
    one = width // shards
    tiles = grads.shape[1]
    down = tiles * one
    third = one // 3
    ra = (2 * tiles - UPWARD) * one + third
    rb = down + third
    part = lambda r: jax.ShapeDtypeStruct((groups, 2, r, half), bf)
    level = jax.ShapeDtypeStruct((groups // 2, SPAN, UPWARD * one + third, half), bf)
    vm = lambda *n: pltpu.VMEM(n, bf)
    return pl.pallas_call(
        functools.partial(weights_kernel, groups),
        out_shape=(
            part(ra), part(ra), part(rb), part(rb), level, level,
            jax.ShapeDtypeStruct((HW, SPAN * grad_heads.shape[1]), bf),
        ),
        in_specs=[ANY] * 6 + [VM],
        out_specs=(ANY,) * 7,
        scratch_shapes=[
            vm(2 * count, width), vm(width, 2 * count), vm(tiles, 2 * count, width), vm(tiles, 2 * count, width),
            vm(2 * count, half), vm(width, 2 * count), vm(2 * count, half),
            vm(2 * tiles, shards, one, half), vm(shards, down, half), vm(shards, one, half),
            dma_sems(8 + 4 * tiles), dma_sems(8 + 4 * tiles), dma_sems(3), dma_sems(3), dma_sems(1),
        ],
        compiler_params=comm_params(2),
        name="weight_grads",
        cost_estimate=pl.CostEstimate(
            flops=int(2 * 2 * count * half * width * 8.5), bytes_accessed=30 << 20, transcendentals=0
        ),
    )(inner, grads, hidden, grad_mlp, attended, grad_branch, grad_heads)


def add_rows(dst, a, b, rows):
    step = rows // 3 if rows % 48 == 0 and rows > 48 else rows

    def part(i, _):
        sl = pl.ds(pl.multiple_of(i * step, step), step)
        dst[sl, :] = a[sl, :] + b[sl, :]
        return 0

    lax.fori_loop(0, rows // step, part, 0)


class Line:
    def __init__(self, z, zt, groups, part, up, down, sems, t, p):
        self.z, self.zt, self.groups = z, zt, groups
        self.part, self.up, self.down = part, up, down
        us, ur, ds, dr = sems
        above = (t, lax.rem(p + SPAN, SPAN * groups))
        below = (t, lax.rem(p + SPAN * (groups - 1), SPAN * groups))
        self.up_first = lambda: remote(part, up, us, ur, above)
        self.up_next = lambda: remote(up, up, us, ur, above)
        self.down_first = lambda: remote(part, down, ds, dr, below)
        self.down_next = lambda: remote(down, down, ds, dr, below)

    def start(self):
        if self.zt > 0:
            pl.when(self.z == 0)(lambda: self.up_first().start())
        if self.zt < self.groups - 1:
            pl.when(self.z == self.groups - 1)(lambda: self.down_first().start())

    def relay(self, hop, rows):
        def up():
            self.up_next().wait_recv()
            add_rows(self.up, self.up, self.part, rows)
            self.up_next().start()

        def down():
            self.down_next().wait_recv()
            add_rows(self.down, self.down, self.part, rows)
            self.down_next().start()

        if 0 < hop < self.zt:
            pl.when(self.z == hop)(up)
        if self.zt < self.groups - 1 - hop:
            pl.when(self.z == self.groups - 1 - hop)(down)

    def finish(self, dst, rows):
        def done():
            if self.zt > 0:
                self.up_next().wait_recv()
            if self.zt < self.groups - 1:
                self.down_next().wait_recv()
            if 0 < self.zt < self.groups - 1:
                add_rows(self.up, self.up, self.down, rows)
            add_rows(dst, self.up if self.zt > 0 else self.down, self.part, rows)

        pl.when(self.z == self.zt)(done)

    def drain(self):
        if self.zt > 0:
            pl.when(self.z < self.zt)(lambda: self.up_first().wait_send())
        if self.zt < self.groups - 1:
            pl.when(self.z > self.zt)(lambda: self.down_first().wait_send())


def outward(groups):
    order = []
    lo, hi = 0, groups - 1
    while lo <= hi:
        order.append(hi)
        if lo < hi:
            order.append(lo)
        lo, hi = lo + 1, hi - 1
    return order


def finish_kernel(
    groups, ka_ref, kb_ref, kc_ref, ra_ref, rb_ref, rc_ref, wq_ref, gh_ref, gin_ref, tin_ref, gain_ref,
    pair_ref, tg_ref, out_ref, sum_ref,
    plane, line, nsend, nrecv,
    kvc, rvc, r2c, r3c, r4c, csem, cs, cr, kva, kvb, rva, rvb, r2a, r2b, ua, ub, da, db, isem, s2, q2, us, ur, ds, dr,
    gm_ref, wq, gh, g_ref, tok_ref, wsem, fs, fr,
    w2, sib, ub2, db2, fin, send, recv, ts, tr, us2, ur2, ds2, dr2, ps, pr, lsem,
):
    t, p, x, y, z = here()
    ex, ey, ed = plane_peers()
    peers = (ex, ey, ed)
    sibling = (1 - t, p)
    others = [(t, lax.rem(p + SPAN * k, SPAN * groups)) for k in range(1, groups)]
    across = tuple((1 - t, q[1]) for q in peers)
    order = outward(groups)
    colours = (
        (ey, ka_ref, ra_ref, kva, rva, r2a, ua, da, y),
        (ex, kb_ref, rb_ref, kvb, rvb, r2b, ub, db, x),
    )

    def loads(c, zt):
        peer, kr, rr, kv, rv = colours[c][:5]
        i = 2 * (c * groups + zt)
        return (
            pltpu.make_async_copy(kr.at[zt], kv.at[zt], isem.at[i]),
            pltpu.make_async_copy(rr.at[zt], rv.at[zt], isem.at[i + 1]),
        )

    level_loads = [
        [pltpu.make_async_copy(a.at[i], b.at[i], csem.at[2 * i + j]) for j, (a, b) in enumerate(((kc_ref, kvc), (rc_ref, rvc)))]
        for i in range(2)
    ]
    for pair in level_loads:
        for d in pair:
            d.start()
    mixed_loads = (pltpu.make_async_copy(gin_ref, g_ref, wsem.at[2]), pltpu.make_async_copy(tin_ref, tok_ref, wsem.at[3]))
    for i, zt in enumerate(order):
        for c in range(2):
            for d in loads(c, zt):
                d.start()
        if i == 1:
            for c in mixed_loads:
                c.start()
    more = (pltpu.make_async_copy(wq_ref, wq, wsem.at[0]), pltpu.make_async_copy(gh_ref, gh, wsem.at[1]))
    for c in more:
        c.start()
    greet(peers + across + (sibling,) + tuple(others))
    around = [remote(gain_ref, plane.at[i], nsend.at[i], nrecv.at[i], q) for i, q in enumerate(peers)]
    for c in around:
        c.start()

    def second(c, zt):
        peer, kr, rr, kv, rv, r2, u, d, mine = colours[c]
        i = c * groups + zt
        return remote(rv.at[zt, 1 - mine], r2.at[zt], s2.at[i], q2.at[i], peer)

    def chain(c, zt):
        peer, kr, rr, kv, rv, r2, u, d, mine = colours[c]
        i = c * groups + zt
        return Line(z, zt, groups, r2.at[zt], u.at[zt], d.at[zt],
                    (us.at[i], ur.at[i], ds.at[i], dr.at[i]), t, p)

    def size(c):
        return colours[c][3].shape[2]

    up = kvc.shape[2]

    def third(i, k):
        at = (k * 2 + 1 - x, (1 - y) * 2 + k)[i]
        n = 2 * i + k
        return remote(rvc.at[i, at], r2c.at[i, k], cs.at[n], cr.at[n], (ex, ey)[i])

    def fourth(i):
        at = (1 - y, 1 - x)[i]
        return remote(r2c.at[i, at], r3c.at[i], cs.at[4 + i], cr.at[4 + i], (ey, ex)[i])

    top = lax.div(z, 2)
    fifth = remote(r3c.at[1 - top], r4c, cs.at[6], cr.at[6], (t, p + 2 * SPAN - 4 * SPAN * top))

    def plus(dst, src, n):
        add_rows(dst, dst, src, n)

    def send_second(zt):
        for c in range(2):
            for d in loads(c, zt):
                d.wait()
            peer, kr, rr, kv, rv, r2, u, d, mine = colours[c]
            plus(rv.at[zt, 1 - mine], kv.at[zt, 1 - mine], size(c))
            second(c, zt).start()

    for i in range(2):
        for d in level_loads[i]:
            d.wait()
        for k in range(2):
            at = (k * 2 + 1 - x, (1 - y) * 2 + k)[i]
            plus(rvc.at[i, at], kvc.at[i, at], up)
            third(i, k).start()
    send_second(order[0])
    send_second(order[1])
    width = gm_ref.shape[0] // 3
    shards = SPAN * groups
    one = width // shards
    half = width // 2
    for c in mixed_loads:
        c.wait()
    for h in range(2):
        r = nn(g_ref[...], tok_ref[:, h * half : (h + 1) * half]).T
        w2[h * (shards // 2) : (h + 1) * (shards // 2)] = r.astype(bf).reshape(shards // 2, one, 3 * HW)

    def swap(zt):
        return remote(w2.at[pl.ds(zt * 4 + (1 - t) * 2, 2)], sib.at[zt], ts.at[zt], tr.at[zt], sibling)

    for zt in order:
        swap(zt).start()

    for i in range(2):
        for k in range(2):
            at = (k * 2 + x, y * 2 + k)[i]
            plus(rvc.at[i, at], kvc.at[i, at], up)
            third(i, k).wait_recv()
            plus(r2c.at[i, k], rvc.at[i, at], up)
        fourth(i).start()
    send_second(order[2])
    send_second(order[3])
    count = gm_ref.shape[1]
    me = lax.rem(p, SPAN)
    copies = []
    for i, peer in enumerate((peers[2], peers[0], peers[1])):
        m = lax.rem(peer[1], SPAN)
        for k in range(3):
            copies.append(remote(
                g_ref.at[pl.ds(k * HW, HW), pl.ds(pl.multiple_of(m * count, count), count)],
                gm_ref.at[pl.ds(pl.multiple_of(k * width + me * HW, HW), HW)],
                send.at[i * 3 + k], recv.at[i * 3 + k], peer,
            ))
    for k in range(3):
        copies.append(pltpu.make_async_copy(
            g_ref.at[pl.ds(k * HW, HW), pl.ds(pl.multiple_of(me * count, count), count)],
            gm_ref.at[pl.ds(pl.multiple_of(k * width + me * HW, HW), HW)],
            lsem.at[k],
        ))
    for c in copies:
        c.start()
    def chain2(zt, k):
        i = zt * 2 + k
        return Line(z, zt, groups, sib.at[zt, k], ub2.at[zt, k], db2.at[zt, k],
                    (us2.at[i], ur2.at[i], ds2.at[i], dr2.at[i]), t, p)

    for zt in order:
        swap(zt).wait_recv()
        for k in range(2):
            dst = sib.at[zt, k]
            add_rows(dst, dst, w2.at[zt * 4 + t * 2 + k], one)
            chain2(zt, k).start()
    for zt in order:
        for c in range(2):
            peer, kr, rr, kv, rv, r2, u, d, mine = colours[c]
            keep = rv.at[zt, mine]
            add_rows(keep, keep, kv.at[zt, mine], size(c))

    def in_plane(zt):
        for c in range(2):
            peer, kr, rr, kv, rv, r2, u, d, mine = colours[c]
            second(c, zt).wait_recv()
            dst = r2.at[zt]
            add_rows(dst, dst, rv.at[zt, mine], size(c))
            chain(c, zt).start()

    def relay(zt, hop):
        for c in range(2):
            chain(c, zt).relay(hop, size(c))


    def relay2(hop):
        for zt in order:
            for k in range(2):
                chain2(zt, k).relay(hop, one)

    in_plane(order[0])
    relay2(1)
    in_plane(order[1])
    for i in range(2):
        fourth(i).wait_recv()
        plus(r3c.at[i], r2c.at[i, (y, x)[i]], up)
    fifth.start()
    relay(order[0], 1)
    relay2(2)
    for c in around:
        c.wait()
    line[0] = (gain_ref[...] + plane[0]) + (plane[1] + plane[2])
    ring = [
        remote(line.at[0], line.at[1 + k], nsend.at[3 + k], nrecv.at[3 + k], q) for k, q in enumerate(others)
    ]
    for c in ring:
        c.start()
    in_plane(order[2])
    relay(order[1], 1)
    in_plane(order[3])
    relay(order[0], 2)
    relay(order[2], 1)
    relay(order[1], 2)
    relay(order[3], 1)
    for zt in order:
        for k in range(2):
            chain2(zt, k).finish(fin.at[k], one)
    here_id = t * SPAN + me

    def hand(k, tt):
        m = t * 2 + k
        peer = (tt, z * SPAN + m)
        i = k * 2 + tt
        away = lambda: remote(fin.at[k], out_ref.at[me], ps.at[i], pr.at[me], peer)
        stay = lambda: pltpu.make_async_copy(fin.at[k], out_ref.at[me], lsem.at[3])
        return away, stay, (tt * SPAN + m) == here_id

    for k in range(2):
        for tt in range(2):
            away, stay, same = hand(k, tt)
            pl.when(jnp.logical_not(same))(lambda away=away: away().start())
            pl.when(same)(lambda stay=stay: stay().start())
    for c in ring:
        c.wait()
    total = line[0]
    for k in range(1, groups):
        total = total + line[k]
    line[groups] = total
    gained = remote(line.at[groups], line.at[groups + 1], nsend.at[2 + groups], nrecv.at[2 + groups], sibling)
    gained.start()
    for c in copies + list(more):
        c.wait()
    turned = nn(wq[...], gm_ref[...]).T
    tg_ref[...] = gh[...] + turned
    fifth.wait_recv()
    add_rows(pair_ref.at[t, pl.ds(size(0) + size(1), up)], r3c.at[top], r4c, up)
    for zt in order:
        for c, sl in ((0, pl.ds(0, size(0))), (1, pl.ds(size(0), size(1)))):
            chain(c, zt).finish(pair_ref.at[t, sl], size(c))
    last = remote(pair_ref.at[t], pair_ref.at[t], fs.at[0], fr.at[0], sibling)
    last.start()
    for s in range(SPAN):
        from_here = jnp.logical_and(s == me, y == t)
        pl.when(jnp.logical_not(from_here))(
            lambda s=s: remote(fin.at[0], out_ref.at[s], ps.at[0], pr.at[s], sibling).wait_recv()
        )
    for k in range(2):
        for tt in range(2):
            away, stay, same = hand(k, tt)
            pl.when(jnp.logical_not(same))(lambda away=away: away().wait_send())
            pl.when(same)(lambda stay=stay: stay().wait())
    for zt in range(groups):
        swap(zt).wait_send()
        for k in range(2):
            chain2(zt, k).drain()
        for c in range(2):
            second(c, zt).wait_send()
            chain(c, zt).drain()
    for i in range(2):
        for k in range(2):
            third(i, k).wait_send()
        fourth(i).wait_send()
    fifth.wait_send()
    gained.wait()
    sum_ref[...] = line[groups] + line[groups + 1]
    last.wait()


def finish(ka, kb, kc, ra, rb, rc, wq, gh, g, tok, gains, groups):
    width = tok.shape[1]
    count = tok.shape[0] // SPAN
    one = width // (SPAN * groups)
    na, nb, nc = ka.shape[2], kb.shape[2], kc.shape[2]
    half = ka.shape[3]
    buf = lambda *n: pltpu.VMEM(n, bf)
    mix = lambda *n: pltpu.VMEM(n + (one, 3 * HW), bf)
    return pl.pallas_call(
        functools.partial(finish_kernel, groups),
        out_shape=(
            jax.ShapeDtypeStruct((2, na + nb + nc, half), bf),
            jax.ShapeDtypeStruct((count, width), f32),
            jax.ShapeDtypeStruct((SPAN, one, 3 * HW), bf),
            jax.ShapeDtypeStruct(gains.shape, f32),
        ),
        in_specs=[ANY] * 10 + [VM],
        out_specs=(VM,) * 4,
        scratch_shapes=[
            pltpu.VMEM((3,) + gains.shape, f32), pltpu.VMEM((groups + 2,) + gains.shape, f32),
            dma_sems(3 + groups), dma_sems(3 + groups),
            buf(2, SPAN, nc, half), buf(2, SPAN, nc, half), buf(2, 2, nc, half), buf(2, nc, half), buf(nc, half),
            dma_sems(4), dma_sems(7), dma_sems(7),
            buf(groups, 2, na, half), buf(groups, 2, nb, half), buf(groups, 2, na, half), buf(groups, 2, nb, half),
            buf(groups, na, half), buf(groups, nb, half), buf(groups, na, half), buf(groups, nb, half),
            buf(groups, na, half), buf(groups, nb, half),
            dma_sems(4 * groups), dma_sems(2 * groups), dma_sems(2 * groups),
            dma_sems(2 * groups), dma_sems(2 * groups), dma_sems(2 * groups), dma_sems(2 * groups),
            buf(3 * width, count), buf(width, 3 * width), pltpu.VMEM((count, width), f32),
            buf(*g.shape), buf(*tok.shape), dma_sems(4),
            dma_sems(1), dma_sems(1),
            mix(SPAN * groups), mix(groups, 2), mix(groups, 2), mix(groups, 2), mix(2),
            dma_sems(9), dma_sems(9), dma_sems(groups), dma_sems(groups),
            dma_sems(2 * groups), dma_sems(2 * groups), dma_sems(2 * groups), dma_sems(2 * groups),
            dma_sems(4), dma_sems(SPAN), dma_sems(4),
        ],
        compiler_params=comm_params(3),
        name="finish",
    )(ka, kb, kc, ra, rb, rc, wq, gh, g, tok, gains)


def unfold_kernel(
    groups, pair_ref, part_ref, grad_ref, score_ref, gain_ref, lost_ref,
    gate_ref, up_ref, down_ref, out_ref, qkv_ref, token_ref, scores_ref, loss_ref, *gains_refs,
):
    one = out_ref.shape[0]
    half = pair_ref.shape[2]
    width = 2 * half
    steps = gate_ref.shape[1] // half
    down = down_ref.shape[0]
    token_ref[0] = grad_ref[...]
    third = one // 3
    ends = ((steps - UPWARD) * one, (steps - UPWARD) * one + third + down, pair_ref.shape[1] - third)
    for j in range(steps):
        at = j * one + (0 if j < steps - UPWARD else down + 2 * third)
        for k, ref in enumerate((gate_ref, up_ref)):
            ref[:, j * half : (j + 1) * half] = pair_ref[k, at : at + one, :].astype(f32)
    for k in range(2):
        cols = slice(k * half, (k + 1) * half)
        down_ref[:, cols] = pair_ref[k, ends[1] - down : ends[1], :].astype(f32)
        for i, at in enumerate(ends):
            out_ref[i * third : (i + 1) * third, cols] = pair_ref[k, at : at + third, :].astype(f32)
    for k in range(3):
        row = [part_ref[s, :, k * HW : (k + 1) * HW].astype(f32) for s in range(SPAN)]
        qkv_ref[:, k * width : (k + 1) * width] = jnp.concatenate(row, 1)
    docs, size = scores_ref.shape[0], score_ref.shape[0]
    dot = functools.partial(lax.dot_general, precision=precise, preferred_element_type=f32)
    row = lax.broadcasted_iota(jnp.int32, (docs, size), 0)
    col = lax.broadcasted_iota(jnp.int32, (docs, size), 1)
    pick = jnp.where(row // DOCS_GRP * 8 + lax.rem(row, DOCS_GRP) == col, 1.0, 0.0)
    some = dot(pick, score_ref[...], (((1,), (0,)), ((), ())))
    scores_ref[...] = dot(some, pick, (((1,), (1,)), ((), ())))
    row = lax.broadcasted_iota(jnp.int32, (width, one), 0)
    col = lax.broadcasted_iota(jnp.int32, (width, one), 1)
    mine = jnp.where(row == lax.axis_index("dp") * one + col, 1.0, 0.0)
    gains = dot(gain_ref[...], mine, (((1,), (0,)), ((), ())))
    for k, ref in enumerate(gains_refs):
        ref[...] = gains[k : k + 1, :]
    loss_ref[...] = lost_ref[0:1, 0:1]


def unfold(pair, parts, grad, scores, gains, loss, tiles, groups):
    one = parts.shape[1]
    half = pair.shape[2]
    width = 2 * half
    docs = groups * DOCS_GRP
    sds = jax.ShapeDtypeStruct
    return pl.pallas_call(
        functools.partial(unfold_kernel, groups),
        out_shape=(
            sds((one, tiles * width), f32), sds((one, tiles * width), f32), sds((tiles * one, width), f32),
            sds((one, width), f32), sds((one, 3 * width), f32), sds((1,) + grad.shape, f32),
            sds((docs, docs), f32), sds((1, 1), f32),
        )
        + (sds((1, one), f32),) * 4,
        in_specs=[VM] * 6,
        out_specs=(VM,) * 12,
        name="unfold",
    )(pair, parts, grad, scores, gains, loss)


def angle_bases():
    half = HEAD_DIM // 2
    freqs = np.float32(1000.0) ** (-np.arange(half, dtype=np.float32) / np.float32(half))
    steps = np.arange(128, dtype=np.float64)
    far = freqs[:, None].astype(np.float64) * (128.0 * steps)[None, :]
    near = freqs[:, None].astype(np.float64) * steps[None, :]
    return np.stack([np.cos(far), np.sin(far), np.cos(near), np.sin(near)]).astype(np.float32)


def spread_sum(value):
    part = lax.psum_scatter(value, "dp", scatter_dimension=0, tiled=True)
    return lax.psum(part.astype(bf), "tower").astype(f32)


def local(
    tokens, doc_ids, pad_mask, targets, w_qkv, w_out, ln1_gain, ln1_bias,
    w_gate, w_up, w_down, ln2_gain, ln2_bias,
):
    width = w_out.shape[0]
    rows = tokens[0]
    count = rows.shape[0]
    places = lax.axis_size("dp")
    groups = places // SPAN
    tower = lax.axis_index("tower")
    place = lax.axis_index("dp")
    me = place % SPAN
    docs = groups * DOCS_GRP
    base = angle_bases()
    tok_all, codes, qa, ka, va, kt, heads, lse, exact = gather(rows, doc_ids, pad_mask, base, w_qkv)
    norms = (ln1_gain, ln1_bias, ln2_gain, ln2_bias)
    (
        attended, inner, hidden, grad_mlp, grads, grad_branch, grad_attended, grad_h1, gains, scores_all, loss
    ) = block(heads, rows, codes, targets, norms, w_out, w_gate, w_up, w_down, groups)
    by_hand = groups == 4 and width % (48 * places) == 0
    if by_hand:
        send_a, keep_a, send_b, keep_b, send_c, keep_c, d_heads = weight_grads(
            groups, grad_attended, inner, grads, hidden, grad_mlp, attended, grad_branch
        )
        exchange = lambda v, bit: lax.ppermute(v, "dp", [(i, i ^ bit) for i in range(places)])
        came_a, came_b, came_c = exchange(send_a, 1), exchange(send_b, 2), exchange(send_c, SPAN)
    else:
        d_heads = tokens_to_heads(grad_attended, 5, "to_heads")
    mixed = attn_bwd(d_heads, exact, lse, qa, ka, va, kt, base, codes)
    if by_hand:
        pair, grad_tokens, qkv_parts, gain_sums = finish(
            keep_a, keep_b, keep_c, came_a, came_b, came_c, w_qkv, grad_h1, mixed, tok_all, gains, groups
        )
        gate_out, up_out, down_out, out_out, qkv_out, token_grad, scores, loss, *gains_out = unfold(
            pair, qkv_parts, grad_tokens, scores_all, gain_sums, loss, w_gate.shape[1] // width, groups
        )
        gains_out = [v.reshape(-1) for v in gains_out]
    else:
        grad_mixed = heads_to_tokens(mixed, 6, "to_tokens_back")
        qkv_out = spread_sum(tn(rows, grad_mixed.T))
        side = lambda v: lax.psum_scatter(v, "dp", scatter_dimension=0, tiled=True)
        halves = lambda v: lax.all_gather(side(v).astype(bf), "tower", axis=1, tiled=True).astype(f32)
        both = lambda a, b: tn(a[0], b[0]) + tn(a[1], b[1])
        flat = lambda v: v.transpose(0, 2, 1, 3).reshape(2, count, -1)
        out_out = halves(nn(attended[0], grad_branch[0]) + nn(attended[1], grad_branch[1]))
        two = lax.all_gather(side(both(inner, flat(grads))).astype(bf), "tower").astype(f32)
        gate_out, up_out = two[0], two[1]
        down_out = halves(both(flat(hidden), grad_mlp))
        gains_out = spread_sum(gains[:4].T).T
        scores = scores_all.reshape(groups, 8, groups, 8)[:, :DOCS_GRP, :, :DOCS_GRP].reshape(docs, docs)
        token_grad = grad_h1 + lax.dot_general(
            grad_mixed, w_qkv, (((0,), (1,)), ((), ())), preferred_element_type=f32
        )
        token_grad = token_grad[None]
    return (
        scores, loss[0, 0], token_grad, qkv_out, out_out, gains_out[0], gains_out[1],
        gate_out, up_out, down_out, gains_out[2], gains_out[3],
    )


def solution(mesh):
    shard = P("dp", None)
    lone = P("dp")
    return jax.shard_map(
        local,
        mesh=mesh,
        in_specs=(P("tower", "dp", None), P("tower", "dp"), P("tower", "dp")) + (P(),) * 10,
        out_specs=(
            P(), P(), P("tower", "dp", None), shard, shard, lone, lone, shard, shard, shard, lone, lone,
        ),
        check_vma=False,
    )
```

```python
import functools

import jax
import jax.numpy as jnp
import numpy as np
from jax import lax
from jax.experimental import pallas as pl
from jax.experimental.pallas import tpu as pltpu
from jax.sharding import PartitionSpec as P

HEADS = 12
HEAD_DIM = 64
SPAN = 4
DOCS_GRP = 3
NH = HEADS // SPAN
HW = NH * HEAD_DIM
UPWARD = 4
VLIM = 62 * 2**20
MESH = pl.DeviceIdType.MESH
f32 = jnp.float32
bf = jnp.bfloat16
precise = lax.Precision.HIGHEST
norm_eps = 1e-05
ANY = pl.BlockSpec(memory_space=pl.ANY)
VM = pl.BlockSpec(memory_space=pltpu.VMEM)


def nn(a, b):
    return lax.dot_general(a, b, (((1,), (0,)), ((), ())), preferred_element_type=f32)


def nt(a, b):
    return lax.dot_general(a, b, (((1,), (1,)), ((), ())), preferred_element_type=f32)


def tn(a, b):
    return lax.dot_general(a, b, (((0,), (0,)), ((), ())), preferred_element_type=f32)


def split3(v):
    one = v.astype(bf).astype(f32)
    rest = v - one
    two = rest.astype(bf).astype(f32)
    return [one, two, rest - two]


def here():
    t = lax.axis_index("tower")
    p = lax.axis_index("dp")
    x = lax.rem(p, 2)
    y = lax.rem(lax.div(p, 2), 2)
    return t, p, x, y, lax.div(p, SPAN)


def plane_peers():
    t, p, x, y, g = here()
    px = p + 1 - 2 * x
    py = p + 2 - 4 * y
    pd = px + 2 - 4 * y
    return (t, px), (t, py), (t, pd)


def hail(peers):
    for peer in peers:
        pl.semaphore_signal(pltpu.get_barrier_semaphore(), inc=1, device_id=peer, device_id_type=MESH)


def greeted(peers):
    pl.semaphore_wait(pltpu.get_barrier_semaphore(), len(peers))


def greet(peers):
    hail(peers)
    greeted(peers)


def remote(src, dst, send, recv, peer):
    return pltpu.make_async_remote_copy(
        src_ref=src, dst_ref=dst, send_sem=send, recv_sem=recv, device_id=peer, device_id_type=MESH
    )


def dma_sems(n):
    return pltpu.SemaphoreType.DMA((n,))


def comm_params(cid):
    return pltpu.CompilerParams(collective_id=cid, has_side_effects=True, vmem_limit_bytes=VLIM)


def fill_angles(base_ref, cos_ref, sin_ref):
    for i in range(cos_ref.shape[1] // 128):
        at = slice(i * 128, (i + 1) * 128)
        ca, sa = base_ref[0, :, i : i + 1], base_ref[1, :, i : i + 1]
        cb, sb = base_ref[2], base_ref[3]
        cos_ref[:, at] = ca * cb - sa * sb
        sin_ref[:, at] = sa * cb + ca * sb


def gather_kernel(
    tok_ref, ids_ref, pads_ref, base_ref, w_ref, out_ref, codes_ref, qa_ref, ka_ref, va_ref, kt_ref,
    att_ref, lse_ref, exact_ref,
    cos_ref, sin_ref, toks, code_ref, codes, wraw, wturn, wt, qa, ka, va, kt, acc, tops, sooner, later, heads,
    send, recv, csend, crecv, wsem, osem, asend, arecv, asem,
):
    t, p, x, y, g = here()
    count, width = tok_ref.shape
    half = count // 2
    me = lax.rem(p, SPAN)
    odd = lax.rem(me, 2)
    wide = wraw.shape[2]
    loads = []
    for k in range(3):
        at = pl.multiple_of(k * width + me * HW - odd * HEAD_DIM, 128)
        loads.append(pltpu.make_async_copy(w_ref.at[:, pl.ds(at, wide)], wraw.at[k], wsem.at[k]))
        loads[-1].start()
    code_ref[...] = lax.rem(ids_ref[...], DOCS_GRP).astype(f32) + 4.0 * (1 - pads_ref[...]).astype(f32)
    ex, ey, ed = plane_peers()
    mx, my, md = (lax.rem(q[1], SPAN) for q in (ex, ey, ed))

    def rows(m, h):
        return pl.ds(pl.multiple_of(m * count + h * half, half), half)

    def whole(m):
        return pl.ds(pl.multiple_of(m * count, count), count)

    greet((ex, ey, ed))
    first = []
    for i, (peer, h) in enumerate(((ex, 0), (ey, 1), (ex, 1), (ey, 0))):
        c = remote(tok_ref.at[pl.ds(h * half, half)], toks.at[rows(me, h)], send.at[i], recv.at[i], peer)
        c.start()
        first.append(c)
    small = []
    for i, peer in enumerate((ex, ey, ed)):
        c = remote(code_ref, codes.at[:, whole(me)], csend.at[i], crecv.at[i], peer)
        c.start()
        small.append(c)
    codes[:, whole(me)] = code_ref[...]
    fill_angles(base_ref, cos_ref, sin_ref)
    for k in range(3):
        loads[k].wait()
        wturn[...] = wraw[k].T
        wt[k * HW : (k + 1) * HW, :] = wturn[pl.ds(pl.multiple_of(odd * HEAD_DIM, HEAD_DIM), HW), :]

    def project(rows_ref, m, n):
        sl = whole(m)
        mx = nt(wt[...], rows_ref[...])
        cos, sin = cos_ref[:, sl], sin_ref[:, sl]
        cd = codes[:, sl]
        mem = jnp.where(cd >= 4.0, cd - 4.0, cd)
        pad = [jnp.zeros((13, count), f32)]
        hot = jnp.concatenate([jnp.where(mem == float(d), 1.0, 0.0) for d in range(DOCS_GRP)] + pad, 0)
        neg = jnp.concatenate([jnp.where(cd == float(d), 0.0, -1e30) for d in range(DOCS_GRP)] + pad, 0)
        rest = jnp.zeros((48, count), f32)
        one = jnp.concatenate([jnp.ones((1, count), f32), jnp.zeros((63, count), f32)], 0)

        def rope(u):
            a, b = u[:32], u[32:]
            return jnp.concatenate([a * cos - b * sin, b * cos + a * sin], 0)

        for h in range(NH):
            q = rope(mx[h * HEAD_DIM : (h + 1) * HEAD_DIM]).astype(bf).astype(f32) * 0.125
            k = rope(mx[HW + h * HEAD_DIM : HW + (h + 1) * HEAD_DIM])
            v = mx[2 * HW + h * HEAD_DIM : 2 * HW + (h + 1) * HEAD_DIM]
            qa[h, :, sl] = jnp.concatenate([q, hot, rest], 0).astype(bf)
            ka[h, sl, :] = jnp.concatenate([k, neg, rest], 0).T.astype(bf)
            va[h, :, sl] = jnp.concatenate([v, one], 0).astype(bf)
            kt[h, :, sl] = k.astype(bf)
        puts = (
            (rows_ref, out_ref.at[sl]),
            (qa.at[:, :, sl], qa_ref.at[:, :, sl]),
            (ka.at[:, sl, :], ka_ref.at[:, sl, :]),
            (va.at[:, :, sl], va_ref.at[:, :, sl]),
            (kt.at[:, :, sl], kt_ref.at[:, :, sl]),
        )
        puts = [pltpu.make_async_copy(a, b, osem.at[5 * n + i]) for i, (a, b) in enumerate(puts)]
        for c in puts:
            c.start()
        return puts

    part = count // 2
    acc[...] = jnp.zeros_like(acc)
    tops[...] = jnp.full_like(tops, -3e38)
    chunks = (me, mx, my, md)
    inside = jnp.where((me == 1) | (me == 2), 1, 0)

    def pick(n, values):
        got = values[-1]
        for i in reversed(range(len(values) - 1)):
            got = jnp.where(n == i, values[i], got)
        return got

    def segment(q, key_of, trips):
        qs = whole(q)

        def keys(n, k):
            return pl.ds(pl.multiple_of(key_of(n) * count + k * part, part), part)

        def scores(n, k, h, ref):
            ref[h] = nn(ka[h, keys(n, k), :], qa[h, :, qs])

        def absorb(n, k, h, ref, m):
            s = ref[h]
            mn = jnp.maximum(m, jnp.max(s, 0, keepdims=True))
            pr = jnp.exp(s - mn).astype(bf)
            acc[q, h] = acc[q, h] * jnp.exp(m - mn) + nn(va[h, :80, keys(n, k)], pr)
            return mn

        for h in range(NH):
            scores(0, 0, h, sooner)

        def step(n, ms):
            ms = list(ms)
            for h in range(NH):
                scores(n, 1, h, later)
                ms[h] = absorb(n, 0, h, sooner, ms[h])
            after = jnp.minimum(n + 1, jnp.maximum(trips - 1, 0))
            for h in range(NH):
                scores(after, 0, h, sooner)
                ms[h] = absorb(n, 1, h, later, ms[h])
            return tuple(ms)

        ms = lax.fori_loop(0, trips, step, tuple(tops[q * NH + h] for h in range(NH)))
        for h in range(NH):
            tops[q * NH + h] = ms[h]

    def finalize(q):
        qs = whole(q)
        edge = jnp.where((q == 0) | (q == SPAN - 1), 1.0, 0.0)
        other = whole(SPAN - 1 - q)
        for h in range(NH):
            m = tops[q * NH + h]
            rest = jnp.sum(va[h, :80, other].astype(f32), 1, keepdims=True)
            full = acc[q, h] + rest * jnp.where(m < -1e29, edge, 0.0)
            tot = full[64:65]
            o = full[:64] / tot
            at = pl.ds(h * HEAD_DIM, HEAD_DIM)
            exact_ref[at, qs] = o
            lse_ref[h : h + 1, qs] = jnp.where(m < -1e29, 0.0, m + jnp.log(tot))
            heads[at, qs] = o.astype(bf)

    done = project(tok_ref, me, 0)
    first[0].wait_recv()
    f0 = remote(toks.at[rows(mx, 0)], toks.at[rows(mx, 0)], send.at[4], recv.at[4], ey)
    f0.start()
    first[1].wait_recv()
    f1 = remote(toks.at[rows(my, 1)], toks.at[rows(my, 1)], send.at[5], recv.at[5], ex)
    f1.start()
    segment(me, lambda n: me, 1)
    for c in small:
        c.wait()
    first[2].wait_recv()
    done += project(toks.at[whole(mx)], mx, 1)
    first[3].wait_recv()
    done += project(toks.at[whole(my)], my, 2)

    def near(s, _):
        q = pick(s, chunks[:3])
        key_of = lambda n: pick(s, (pick(n, (mx, my)), pick(n, (me, mx, my)), pick(n, (me, my, mx))))
        segment(q, key_of, jnp.where(s == 0, 2, 3 - inside))
        return 0

    lax.fori_loop(0, 3, near, 0)
    f0.wait_recv()
    f1.wait_recv()
    done += project(toks.at[whole(md)], md, 3)

    def back(s):
        peer = (ed, ex, ey)[s]
        m = (md, mx, my)[s]
        return remote(
            heads.at[:, whole(m)], att_ref.at[pl.ds(pl.multiple_of(me * HW, HW), HW)], asend.at[s], arecv.at[s], peer
        )

    def far(s, _):
        q = pick(s, (md, mx, my, me))
        key_of = lambda n: jnp.where(s == 0, pick(n, (mx, my, md, me)), md)
        segment(q, key_of, pick(s, (3 + inside, 1, 1, inside)))
        finalize(q)
        for k in range(3):
            pl.when(s == k)(lambda k=k: back(k).start())
        return 0

    lax.fori_loop(0, 4, far, 0)
    own = pltpu.make_async_copy(
        heads.at[:, whole(me)], att_ref.at[pl.ds(pl.multiple_of(me * HW, HW), HW)], asem.at[0]
    )
    own.start()
    codes_ref[...] = codes[...]
    for c in first + [f0, f1]:
        c.wait_send()
    for c in done:
        c.wait()
    own.wait()
    for k in range(3):
        back(k).wait()


def gather(tok, ids, pads, base, w_qkv):
    count, width = tok.shape
    total = SPAN * count
    shapes = ((NH, 128, total), (NH, total, 128), (NH, 128, total), (NH, HEAD_DIM, total))
    return pl.pallas_call(
        gather_kernel,
        out_shape=(jax.ShapeDtypeStruct((total, width), bf), jax.ShapeDtypeStruct((1, total), f32))
        + tuple(jax.ShapeDtypeStruct(s, bf) for s in shapes)
        + (
            jax.ShapeDtypeStruct((SPAN * HW, count), bf), jax.ShapeDtypeStruct((NH, total), f32),
            jax.ShapeDtypeStruct((HW, total), f32),
        ),
        in_specs=[VM] * 4 + [ANY],
        out_specs=(ANY, VM) + (ANY,) * 5 + (VM,) * 2,
        scratch_shapes=[
            pltpu.VMEM((HEAD_DIM // 2, total), f32), pltpu.VMEM((HEAD_DIM // 2, total), f32),
            pltpu.VMEM((total, width), bf), pltpu.VMEM((1, count), f32), pltpu.VMEM((1, total), f32), pltpu.VMEM((3, width, 256), bf),
            pltpu.VMEM((256, width), bf), pltpu.VMEM((3 * HW, width), bf),
        ]
        + [pltpu.VMEM(s, bf) for s in shapes]
        + [
            pltpu.VMEM((SPAN, NH, 80, count), f32), pltpu.VMEM((SPAN * NH, 1, count), f32),
            pltpu.VMEM((NH, count // 2, count), f32), pltpu.VMEM((NH, count // 2, count), f32),
            pltpu.VMEM((HW, total), bf),
            dma_sems(6), dma_sems(6), dma_sems(3), dma_sems(3), dma_sems(3), dma_sems(20),
            dma_sems(3), dma_sems(3), dma_sems(1),
        ],
        compiler_params=comm_params(0),
        name="gather",
    )(tok, ids, pads, base, w_qkv)


def heads_to_tokens_kernel(parts, in_ref, out_ref, send, recv, lsem):
    t, p, x, y, g = here()
    count = out_ref.shape[1]
    me = lax.rem(p, SPAN)
    peers = plane_peers()
    width = parts and out_ref.shape[0] // parts
    greet(peers)
    copies = []
    for i, peer in enumerate((peers[2], peers[0], peers[1])):
        m = lax.rem(peer[1], SPAN)
        for k in range(parts):
            c = remote(
                in_ref.at[pl.ds(k * HW, HW), pl.ds(pl.multiple_of(m * count, count), count)],
                out_ref.at[pl.ds(pl.multiple_of(k * width + me * HW, HW), HW)],
                send.at[i * parts + k],
                recv.at[i * parts + k],
                peer,
            )
            c.start()
            copies.append(c)
    for k in range(parts):
        c = pltpu.make_async_copy(
            in_ref.at[pl.ds(k * HW, HW), pl.ds(pl.multiple_of(me * count, count), count)],
            out_ref.at[pl.ds(pl.multiple_of(k * width + me * HW, HW), HW)],
            lsem.at[k],
        )
        c.start()
        copies.append(c)
    for c in copies:
        c.wait()


def heads_to_tokens(a, cid, name):
    parts = a.shape[0] // HW
    count = a.shape[1] // SPAN
    return pl.pallas_call(
        functools.partial(heads_to_tokens_kernel, parts),
        out_shape=jax.ShapeDtypeStruct((parts * HEADS * HEAD_DIM, count), a.dtype),
        in_specs=[VM],
        out_specs=ANY,
        scratch_shapes=[dma_sems(3 * parts), dma_sems(3 * parts), dma_sems(parts)],
        compiler_params=comm_params(cid),
        name=name,
    )(a)


def tokens_to_heads_kernel(in_ref, out_ref, send, recv, lsem):
    t, p, x, y, g = here()
    count = in_ref.shape[1]
    me = lax.rem(p, SPAN)
    peers = plane_peers()
    greet(peers)
    mine = pl.ds(pl.multiple_of(me * count, count), count)
    copies = []
    for i, peer in enumerate((peers[2], peers[0], peers[1])):
        m = lax.rem(peer[1], SPAN)
        c = remote(
            in_ref.at[pl.ds(pl.multiple_of(m * HW, HW), HW)],
            out_ref.at[:, mine],
            send.at[i],
            recv.at[i],
            peer,
        )
        c.start()
        copies.append(c)
    c = pltpu.make_async_copy(
        in_ref.at[pl.ds(pl.multiple_of(me * HW, HW), HW)], out_ref.at[:, mine], lsem.at[0]
    )
    c.start()
    for c in copies + [c]:
        c.wait()


def tokens_to_heads(a, cid, name):
    return pl.pallas_call(
        tokens_to_heads_kernel,
        out_shape=jax.ShapeDtypeStruct((HW, SPAN * a.shape[1]), a.dtype),
        in_specs=[VM],
        out_specs=ANY,
        scratch_shapes=[dma_sems(3), dma_sems(3), dma_sems(1)],
        compiler_params=comm_params(cid),
        name=name,
    )(a)


def doc_limits(code):
    pad = code >= 4.0
    mem = jnp.where(pad, code - 4.0, code)
    n0 = jnp.sum(jnp.where(mem < 0.5, 1.0, 0.0)).astype(jnp.int32)
    n1 = jnp.sum(jnp.where(mem < 1.5, 1.0, 0.0)).astype(jnp.int32)
    l = [jnp.sum(jnp.where(code == float(d), 1.0, 0.0)).astype(jnp.int32) for d in range(3)]
    return n0, n1, l

def block_range(lims, a, size, total):
    n0, n1, l = lims
    b = a + size - 1
    first = (a >= n0).astype(jnp.int32) + (a >= n1).astype(jnp.int32)
    last = (b >= n0).astype(jnp.int32) + (b >= n1).astype(jnp.int32)
    lo = jnp.where(first == 0, 0, jnp.where(first == 1, n0, n1))
    hi = jnp.where(last == 0, n0, jnp.where(last == 1, n1, total))
    dead = jnp.zeros((), jnp.bool_)
    for d in range(3):
        dead = dead | ((first <= d) & (d <= last) & (l[d] == 0))
    return jnp.where(dead, 0, lo), jnp.where(dead, total, hi)

def bwd_kernel(KB, QB, do_ref, o32_ref, lse_ref, qa_ref, ka_ref, va_ref, kt_ref, base_ref, code_ref, g_ref,
               cos_ref, sin_ref, vn_ref, dn_ref, da_ref, qb_ref, acc_ref, dq_ref):
    T = do_ref.shape[1]
    hw = HW
    CH = 512
    lims = doc_limits(code_ref[...])
    fill_angles(base_ref, cos_ref, sin_ref)
    def prep(c, _):
        sl = pl.ds(pl.multiple_of(c*CH, CH), CH)
        for h in range(NH):
            do = do_ref[h*HEAD_DIM:(h+1)*HEAD_DIM, sl].astype(f32)
            delta = jnp.sum(do*o32_ref[h*HEAD_DIM:(h+1)*HEAD_DIM, sl], 0, keepdims=True)
            def split(x):
                x1 = x.astype(bf).astype(f32); r = x-x1
                x2 = r.astype(bf).astype(f32); x3 = r-x2
                return [x1, x2, x3]
            z13 = jnp.zeros((13, CH), f32); z48 = jnp.zeros((48, CH), f32)
            da_ref[h, :, sl] = jnp.concatenate([do]+split(-delta)+[z13, z48], 0).astype(bf)
            one = jnp.concatenate([jnp.ones((3, CH), f32), jnp.zeros((61, CH), f32)], 0)
            v = va_ref[h, :64, sl].astype(f32)
            vn_ref[h, sl, :] = jnp.concatenate([v, one], 0).T.astype(bf)
            z64 = jnp.zeros((64, CH), f32)
            q = qa_ref[h, :64, sl].astype(f32)
            dn_ref[h, sl, :] = jnp.concatenate([do, z64], 0).T.astype(bf)
            qb_ref[h, sl, :] = jnp.concatenate([z64, q], 0).T.astype(bf)
            acc_ref[h, sl, :] = jnp.zeros((CH, 128), f32)
        return 0
    lax.fori_loop(0, T//CH, prep, 0)
    def qblock(i, _):
        a = i*QB
        qs = pl.ds(pl.multiple_of(a, QB), QB)
        lo, hi = block_range(lims, a, QB, T)
        small = KB // 2
        start = lo // small
        many = (hi + small - 1) // small - start
        dq_ref[...] = jnp.zeros_like(dq_ref)

        def visit(at, size):
            ks = pl.ds(pl.multiple_of(at * small, small), size)
            for h in range(NH):
                s = nn(ka_ref[h, ks, :], qa_ref[h, :, qs])
                dp = nn(vn_ref[h, ks, :], da_ref[h, :, qs])
                p = jnp.exp(s - lse_ref[h:h+1, qs])
                ds = (p*dp).astype(bf)
                acc_ref[h, ks, :] += nn(p.astype(bf), dn_ref[h, qs, :]) + nn(ds, qb_ref[h, qs, :])
                dq_ref[h] += nn(kt_ref[h, :, ks], ds)

        def kv(j, _):
            visit(start + 2 * j, KB)
            return 0
        lax.fori_loop(0, many // 2, kv, 0)
        pl.when(many % 2 == 1)(lambda: visit(start + many - 1, small))
        cos = cos_ref[:, qs]; sin = sin_ref[:, qs]
        for h in range(NH):
            u = dq_ref[h]*0.125
            x1 = u[:32]; x2 = u[32:]
            g_ref[h*HEAD_DIM:(h+1)*HEAD_DIM, qs] = jnp.concatenate([x1*cos+x2*sin, x2*cos-x1*sin], 0).astype(bf)
        return 0
    lax.fori_loop(0, T//QB, qblock, 0)
    def fin(c, _):
        sl = pl.ds(pl.multiple_of(c*CH, CH), CH)
        cos = cos_ref[:, sl]; sin = sin_ref[:, sl]
        for h in range(NH):
            t = acc_ref[h, sl, :].T
            x1 = t[64:96]; x2 = t[96:128]
            g_ref[hw+h*HEAD_DIM:hw+(h+1)*HEAD_DIM, sl] = jnp.concatenate([x1*cos+x2*sin, x2*cos-x1*sin], 0).astype(bf)
            g_ref[2*hw+h*HEAD_DIM:2*hw+(h+1)*HEAD_DIM, sl] = t[:64].astype(bf)
        return 0
    lax.fori_loop(0, T//CH, fin, 0)

def attn_bwd(do, o32, lse, qa, ka, va, kt, base, code, KB=512, QB=256):
    T = do.shape[1]
    return pl.pallas_call(functools.partial(bwd_kernel, KB, QB),
        out_shape=jax.ShapeDtypeStruct((3*NH*HEAD_DIM, T), bf),
        in_specs=[VM] * 9, out_specs=pl.BlockSpec(memory_space=pltpu.VMEM),
        scratch_shapes=[pltpu.VMEM((HEAD_DIM // 2, T), f32), pltpu.VMEM((HEAD_DIM // 2, T), f32), pltpu.VMEM((NH,T,128), bf), pltpu.VMEM((NH,T,128), bf), pltpu.VMEM((NH,128,T), bf), pltpu.VMEM((NH,T,128), bf),
                        pltpu.VMEM((NH,T,128), f32), pltpu.VMEM((NH,HEAD_DIM,QB), f32)],
        compiler_params=pltpu.CompilerParams(vmem_limit_bytes=67043328), name="attn_bwd",
        cost_estimate=pl.CostEstimate(flops=int(10*T*T*128*3), bytes_accessed=12<<20, transcendentals=T*T*3))(do, o32, lse, qa, ka, va, kt, base, code)


def contrast_part(groups, sums, goals_ref, plane, allp, ge, send, recv, scores_ref, loss_ref):
    t, p, x, y, g = here()
    docs = groups * DOCS_GRP
    size = groups * 8
    peers = plane_peers()
    line = [(t, lax.rem(p + SPAN * k, SPAN * groups)) for k in range(1, groups)]
    plane[3] = sums
    copies = [remote(plane.at[3], plane.at[i], send.at[i], recv.at[i], q) for i, q in enumerate(peers)]
    for c in copies:
        c.start()
    col = lax.broadcasted_iota(jnp.int32, (size, size), 1)
    row = lax.broadcasted_iota(jnp.int32, (size, size), 0)

    def mark(i, hot):
        goal = goals_ref[i]
        at = (row == i // DOCS_GRP * 8 + i % DOCS_GRP) & (col == goal // DOCS_GRP * 8 + goal % DOCS_GRP)
        return hot + jnp.where(at, 1.0, 0.0)

    hot = lax.fori_loop(0, docs, mark, jnp.zeros((size, size), f32))
    for c in copies:
        c.wait()
    own = (plane[3] + plane[0]) + (plane[1] + plane[2])
    allp[t, g] = own
    rows = allp.at[t, g]
    copies = [remote(rows, rows, send.at[3 + i], recv.at[3 + i], q) for i, q in enumerate(line)]
    for c in copies:
        c.start()
    for c in copies:
        c.wait()
    c = remote(allp.at[t], allp.at[t], send.at[2 + groups], recv.at[2 + groups], (1 - t, p))
    c.start()
    c.wait()
    width = allp.shape[3]
    pools = [allp[k].reshape(size, width) for k in range(2)]
    embeds = [v * lax.rsqrt(jnp.sum(v * v, -1, keepdims=True) + 1e-06) for v in pools]
    dot = functools.partial(lax.dot_general, precision=precise, preferred_element_type=f32)
    scores = dot(embeds[0], embeds[1], (((1,), (1,)), ((), ()))) * 50.0
    live = lax.rem(col, 8) < DOCS_GRP
    alive = lax.rem(row, 8) < DOCS_GRP
    masked = jnp.where(live, scores, -1e30)
    top = jnp.max(masked, -1, keepdims=True)
    total = jnp.sum(jnp.exp(masked - top), -1, keepdims=True)
    log_sums = top + jnp.log(total)
    chosen = jnp.sum(hot * scores, -1, keepdims=True)
    each = jnp.where(alive[:, 0:1], log_sums - chosen, 0.0)
    loss_ref[...] = jnp.broadcast_to(jnp.sum(each, 0, keepdims=True) / docs, loss_ref.shape)
    scores_ref[...] = scores
    gs = jnp.where(alive & live, (jnp.exp(masked - log_sums) - hot) / docs, 0.0)
    gq = dot(gs, embeds[1], (((1,), (0,)), ((), ())))
    gd = dot(gs, embeds[0], (((0,), (0,)), ((), ())))
    ge[...] = jnp.where(t == 0, gq, gd) * 50.0
    mine = ge[pl.ds(pl.multiple_of(g * 8, 8), 8), :]
    pooled = allp[t, g]
    inv = lax.rsqrt(jnp.sum(pooled * pooled, -1, keepdims=True) + 1e-06)
    return inv * mine - inv * inv * inv * pooled * jnp.sum(pooled * mine, -1, keepdims=True)


def block_kernel(
    groups, heads_ref, rows_ref, codes_ref, goals_ref, gain1_ref, bias1_ref, gain2_ref, bias2_ref, wo_h, wg_h, wu_h, wd_h,
    att_o, inner_o, hid_o, gm_o, gg_o, gb_o, ga_o, gh1_o, gains_o, scores_o, loss_o,
    att, wo, wg, wu, wd, inner, x1, s1, acc, hid, ab, x2, s2, sec, gm, gm2, gb, gb2, plane, allp, ge,
    wsem, lsem, tsend, trecv, osem, csend, crecv,
):
    t, p, x, y, g = here()
    peers = plane_peers()
    sibling = (1 - t, p)
    line = tuple((t, lax.rem(p + SPAN * k, SPAN * groups)) for k in range(1, groups))
    count, width = rows_ref.shape
    half = width // 2
    tiles = wg.shape[0]
    me = lax.rem(p, SPAN)

    def weight(j, k):
        cols = pl.ds(j * width if isinstance(j, int) else pl.multiple_of(j * width, width), width)
        src, dst = ((wg_h.at[:, cols], wg.at[j]), (wu_h.at[:, cols], wu.at[j]), (wd_h.at[cols], wd.at[j]))[k]
        return pltpu.make_async_copy(src, dst, wsem.at[1 + 3 * j + k])

    first_load = pltpu.make_async_copy(wo_h, wo, wsem.at[0])
    everyone = peers + (sibling,) + line
    hail(everyone)
    heads_load = pltpu.make_async_copy(heads_ref, att, lsem.at[0])
    heads_load.start()
    first_load.start()
    for j in range(tiles):
        for k in range(3):
            weight(j, k).start()
    code = codes_ref[:, pl.ds(pl.multiple_of(me * count, count), count)]
    zero = jnp.zeros((8 - DOCS_GRP, count), f32)
    mem = jnp.concatenate([jnp.where(code == float(d), 1.0, 0.0) for d in range(DOCS_GRP)] + [zero], 0)
    mem = jnp.concatenate([mem, mem, mem, jnp.zeros((8, count), f32)], 0).astype(bf)
    first_load.wait()
    heads_load.wait()

    def pair(i, mine, its, out):
        return (
            pltpu.make_async_copy(mine, out.at[0], osem.at[i]),
            remote(its, out.at[1], tsend.at[i], trecv.at[i], sibling),
        )

    def both(i, mine, its, out):
        for c in pair(i, mine, its, out):
            c.start()

    acc[...] = tn(att[...], wo[...])
    greeted(everyone)
    both(0, att, att, att_o)
    step = 64
    gain1, bias1, gain2, bias2 = (r[...].reshape(1, width) for r in (gain1_ref, bias1_ref, gain2_ref, bias2_ref))

    def chunk(i):
        return pl.ds(pl.multiple_of(i * step, step), step)

    def norm(h, sl, xs, ss):
        c = h - jnp.mean(h, -1, keepdims=True)
        s = lax.rsqrt(jnp.mean(c * c, -1, keepdims=True) + norm_eps)
        xh = c * s
        xs[sl, :] = xh
        ss[sl, :] = s
        return xh

    def norm_one(i, _):
        sl = chunk(i)
        xh = norm(rows_ref[sl, :].astype(f32) + acc[sl, :], sl, x1, s1)
        v = xh * gain1 + bias1
        inner[sl, :] = v.astype(bf)
        acc[sl, :] = v
        return 0

    lax.fori_loop(0, count // step, norm_one, 0)
    both(1, inner, inner, inner_o)

    def tile_of(j, i, mine, its, out):
        return (
            pltpu.make_async_copy(mine, out.at[0, j], osem.at[i + j]),
            remote(its, out.at[1, j], tsend.at[i + j], trecv.at[i + j], sibling),
        )

    def forward(n, _):
        for i in range(2):
            j = 2 * n + i
            for k in range(3):
                weight(j, k).wait()
            gate = nn(inner[...], wg[j])
            upper = nn(inner[...], wu[j])
            sig = jax.nn.sigmoid(gate)
            silu = gate * sig
            hid[j] = (silu * upper).astype(bf)
            ab[0, j] = (upper * (sig * (1.0 + gate * (1.0 - sig)))).astype(bf)
            ab[1, j] = silu.astype(bf)
            for c in tile_of(j, 2, hid.at[j], hid.at[j], hid_o):
                c.start()
            acc[...] += nn(hid[j], wd[j])
        return 0

    lax.fori_loop(0, tiles // 2, forward, 0)

    def norm_two(i, _):
        sl = chunk(i)
        v = norm(acc[sl, :], sl, x2, s2) * gain2 + bias2
        for k, part in enumerate(split3(v)):
            sec[k, sl, :] = part.astype(bf)
        return 0

    lax.fori_loop(0, count // step, norm_two, 0)
    sums = (nn(mem[:16], sec[0]) + nn(mem[:16], sec[1]) + nn(mem[:16], sec[2]))[:8]
    top = lax.broadcasted_iota(jnp.int32, sums.shape, 0) < DOCS_GRP
    sums = jnp.where(top, sums, 0.0)
    gp = contrast_part(groups, sums, goals_ref, plane, allp, ge, csend, crecv, scores_o, loss_o)
    gp3 = jnp.concatenate(split3(gp) + [jnp.zeros_like(gp)], 0).astype(bf)
    acc[...] = tn(mem, gp3)

    def fold(v):
        return jnp.sum(v.reshape(step // 8, 8, width), 0)

    def norm_back(gr, xh, s, gain):
        e = gr * gain
        v = e - jnp.mean(e, -1, keepdims=True) - xh * jnp.mean(e * xh, -1, keepdims=True)
        return v * s

    zeros = jnp.zeros((8, width), f32)

    def back_two(i, sums):
        sl = chunk(i)
        gr, xh = acc[sl, :], x2[sl, :]
        v = norm_back(gr, xh, s2[sl, :], gain2)
        acc[sl, :] = v
        low = v.astype(bf)
        gm[sl, :] = low
        gm2[0, sl, :] = low[:, :half]
        gm2[1, sl, :] = low[:, half:]
        return sums[0] + fold(gr * xh), sums[1] + fold(gr)

    g2, b2 = lax.fori_loop(0, count // step, back_two, (zeros, zeros))
    both(2 + 2 * tiles, gm2.at[t], gm2.at[1 - t], gm_o)
    def backward(n, _):
        for j in range(tiles):
            gh = nt(gm[...], wd[j])
            gg = (gh * ab[0, j].astype(f32)).astype(bf)
            gu = (gh * ab[1, j].astype(f32)).astype(bf)
            ab[0, j] = gg
            ab[1, j] = gu
            for c in tile_of(j, 2 + tiles, ab.at[t, j], ab.at[1 - t, j], gg_o):
                c.start()
            acc[...] += nt(gg, wg[j]) + nt(gu, wu[j])
        return 0

    backward(0, 0)

    def back_one(i, sums):
        sl = chunk(i)
        gr, xh = acc[sl, :], x1[sl, :]
        v = norm_back(gr, xh, s1[sl, :], gain1)
        gh1_o[sl, :] = v
        low = v.astype(bf)
        gb[sl, :] = low
        gb2[0, sl, :] = low[:, :half]
        gb2[1, sl, :] = low[:, half:]
        return sums[0] + fold(gr * xh), sums[1] + fold(gr)

    g1, b1 = lax.fori_loop(0, count // step, back_one, (zeros, zeros))
    both(3 + 2 * tiles, gb2.at[t], gb2.at[1 - t], gb_o)
    flat = [jnp.sum(v, 0, keepdims=True) for v in (g1, b1, g2, b2)]
    gains_o[...] = jnp.concatenate(flat + [jnp.zeros((4, width), f32)], 0)
    ga_o[...] = nt(wo[...], gb[...]).astype(bf)
    done = [pair(0, att, att, att_o), pair(1, inner, inner, inner_o)]
    for j in range(tiles):
        done.append(tile_of(j, 2, hid.at[j], hid.at[j], hid_o))
        done.append(tile_of(j, 2 + tiles, ab.at[t, j], ab.at[1 - t, j], gg_o))
    done.append(pair(2 + 2 * tiles, gm2.at[t], gm2.at[1 - t], gm_o))
    done.append(pair(3 + 2 * tiles, gb2.at[t], gb2.at[1 - t], gb_o))
    for c in done:
        for d in c:
            d.wait()


def block(heads, rows, codes, goals, norms, w_out, w_gate, w_up, w_down, groups):
    count, width = rows.shape
    tiles = w_gate.shape[1] // width
    half = width // 2
    size = groups * 8
    sds = jax.ShapeDtypeStruct
    vm = lambda *n: pltpu.VMEM(n, bf)
    vf = lambda *n: pltpu.VMEM(n, f32)
    return pl.pallas_call(
        functools.partial(block_kernel, groups),
        out_shape=(
            sds((2, width, count), bf), sds((2, count, width), bf), sds((2, tiles, count, width), bf),
            sds((2, count, half), bf), sds((2, tiles, count, width), bf), sds((2, count, half), bf),
            sds((width, count), bf), sds((count, width), f32), sds((8, width), f32),
            sds((size, size), f32), sds((8, 128), f32),
        ),
        in_specs=[ANY, VM, VM, pl.BlockSpec(memory_space=pltpu.SMEM)] + [VM] * 4 + [ANY] * 4,
        out_specs=(ANY,) * 6 + (VM,) * 5,
        scratch_shapes=[
            vm(width, count), vm(width, width), vm(tiles, width, width), vm(tiles, width, width),
            vm(tiles, width, width), vm(count, width), vf(count, width), vf(count, 1), vf(count, width),
            vm(tiles, count, width), vm(2, tiles, count, width), vf(count, width), vf(count, 1),
            vm(3, count, width), vm(count, width), vm(2, count, half), vm(count, width), vm(2, count, half),
            vf(4, 8, width), vf(2, groups, 8, width), vf(size, width),
            dma_sems(1 + 3 * tiles), dma_sems(1),
            dma_sems(4 + 2 * tiles), dma_sems(4 + 2 * tiles), dma_sems(4 + 2 * tiles),
            dma_sems(3 + groups), dma_sems(3 + groups),
        ],
        compiler_params=comm_params(1),
        name="block",
    )(heads, rows, codes, goals, *norms, w_out, w_gate, w_up, w_down)


def weights_kernel(
    groups, i_ref, g_ref, h_ref, m_ref, a_ref, b_ref, in_ref,
    sa_ref, ka_ref, sb_ref, kb_ref, sc_ref, kc_ref, heads_ref,
    iv, it, gv, hv, mv, av, bv, gs, ds, os, isem, osem, send, recv, lsem,
):
    t, p, x, y, g = here()
    level = lax.rem(g, 2)
    peers = plane_peers()
    count, width = i_ref.shape[1:]
    half = width // 2
    tiles = gv.shape[0]
    shards = SPAN * groups
    one = width // shards
    down = ds.shape[1]

    def load(i, src, dst):
        return pltpu.make_async_copy(src, dst, isem.at[i])

    class Both:
        def __init__(self, *copies):
            self.copies = copies

        def start(self):
            for c in self.copies:
                c.start()

        def wait(self):
            for c in self.copies:
                c.wait()

    def tile(ref, j, buf, base):
        return Both(*(
            load(base + 2 * j + i, ref.at[i, j], buf.at[j, pl.ds(i * count, count)]) for i in range(2)
        ))

    def stack(base, ref, buf):
        return Both(*(load(base + i, ref.at[i], buf.at[pl.ds(i * count, count)]) for i in range(2)))

    def beside(base, ref, buf):
        return Both(*(load(base + i, ref.at[i], buf.at[:, pl.ds(i * count, count)]) for i in range(2)))

    hail(peers)
    few = [stack(0, m_ref, mv), beside(2, a_ref, av), stack(4, b_ref, bv), stack(6, i_ref, iv)]
    few[0].start()
    for j in range(tiles):
        tile(h_ref, j, hv, 8).start()
    for c in few[1:]:
        c.start()
    for j in range(tiles):
        tile(g_ref, j, gv, 8 + 2 * tiles).start()
    greeted(peers)
    tokens = in_ref.shape[1]
    me = lax.rem(p, SPAN)
    mine = pl.ds(pl.multiple_of(me * tokens, tokens), tokens)
    moves = []
    for i, peer in enumerate((peers[2], peers[0], peers[1])):
        m = lax.rem(peer[1], SPAN)
        moves.append(remote(
            in_ref.at[pl.ds(pl.multiple_of(m * HW, HW), HW)], heads_ref.at[:, mine],
            send.at[i], recv.at[i], peer,
        ))
    moves.append(pltpu.make_async_copy(
        in_ref.at[pl.ds(pl.multiple_of(me * HW, HW), HW)], heads_ref.at[:, mine], lsem.at[0]
    ))
    for c in moves:
        c.start()
    few[0].wait()

    def downward(j, _):
        tile(h_ref, j, hv, 8).wait()
        r = tn(hv[j], mv[...])
        ds[pl.ds(j * (width // down), width // down)] = r.astype(bf).reshape(width // down, down, half)
        return 0

    lax.fori_loop(0, tiles, downward, 0)
    for c in few[1:]:
        c.wait()
    r = nn(av[...], bv[...])
    os[...] = r.astype(bf).reshape(shards, one, half)
    it[...] = iv[...].T
    third = one // 3
    fours = lambda ref, n: ref.reshape(groups, 2, 2, n, half)

    def put(i, src, dst):
        return pltpu.make_async_copy(src, dst, osem.at[i])

    outs = []
    for i, (ref, k) in enumerate(((sb_ref, 1 - y), (kb_ref, y))):
        outs.append(put(4 * i, fours(ds, down).at[:, k], ref.at[:, :, pl.ds(0, down)]))
        outs.append(put(4 * i + 1, fours(os, one).at[:, k, :, pl.ds(third, third)], ref.at[:, :, pl.ds(down, third)]))
    for i, (ref, k) in enumerate(((sa_ref, 1 - x), (ka_ref, x))):
        to = ref.at[:, :, pl.ds(ref.shape[2] - third, third)]
        outs.append(put(2 + i, fours(os, one).at[:, :, k, pl.ds(0, third)], to))
    levels = os.reshape(groups // 2, 2, SPAN, one, half)
    for i, (ref, k) in enumerate(((sc_ref, 1 - level), (kc_ref, level))):
        to = ref.at[:, :, pl.ds(ref.shape[2] - third, third)]
        outs.append(put(6 + i, levels.at[:, k, :, pl.ds(2 * third, third)], to))
    for c in outs:
        c.start()

    sideways = sa_ref.shape[2] // one

    def top(j):
        if j < sideways:
            rows = pl.ds(j * one, one)
            piece = fours(gs.at[j], one)
            went, kept = (piece.at[:, :, 1 - x], sa_ref), (piece.at[:, :, x], ka_ref)
        else:
            rows = pl.ds((j - sideways) * one, one)
            piece = gs.at[j].reshape(groups // 2, 2, SPAN, one, half)
            went, kept = (piece.at[:, 1 - level], sc_ref), (piece.at[:, level], kc_ref)
        return (
            put(8 + j, went[0], went[1].at[:, :, rows]),
            put(8 + 2 * tiles + j, kept[0], kept[1].at[:, :, rows]),
        )

    for j in range(tiles):
        tile(g_ref, j, gv, 8 + 2 * tiles).wait()
        r = nn(it[...], gv[j]).astype(bf)
        for h in range(2):
            k = 2 * j + h
            gs[k] = r[:, h * half : (h + 1) * half].reshape(shards, one, half)
            outs.extend(top(k))
            for c in outs[-2:]:
                c.start()
    for c in outs + moves:
        c.wait()


def weight_grads(groups, grad_heads, inner, grads, hidden, grad_mlp, attended, grad_branch):
    count, width = inner.shape[1:]
    half = width // 2
    shards = SPAN * groups
    one = width // shards
    tiles = grads.shape[1]
    down = tiles * one
    third = one // 3
    ra = (2 * tiles - UPWARD) * one + third
    rb = down + third
    part = lambda r: jax.ShapeDtypeStruct((groups, 2, r, half), bf)
    level = jax.ShapeDtypeStruct((groups // 2, SPAN, UPWARD * one + third, half), bf)
    vm = lambda *n: pltpu.VMEM(n, bf)
    return pl.pallas_call(
        functools.partial(weights_kernel, groups),
        out_shape=(
            part(ra), part(ra), part(rb), part(rb), level, level,
            jax.ShapeDtypeStruct((HW, SPAN * grad_heads.shape[1]), bf),
        ),
        in_specs=[ANY] * 6 + [VM],
        out_specs=(ANY,) * 7,
        scratch_shapes=[
            vm(2 * count, width), vm(width, 2 * count), vm(tiles, 2 * count, width), vm(tiles, 2 * count, width),
            vm(2 * count, half), vm(width, 2 * count), vm(2 * count, half),
            vm(2 * tiles, shards, one, half), vm(shards, down, half), vm(shards, one, half),
            dma_sems(8 + 4 * tiles), dma_sems(8 + 4 * tiles), dma_sems(3), dma_sems(3), dma_sems(1),
        ],
        compiler_params=comm_params(2),
        name="weight_grads",
        cost_estimate=pl.CostEstimate(
            flops=int(2 * 2 * count * half * width * 8.5), bytes_accessed=30 << 20, transcendentals=0
        ),
    )(inner, grads, hidden, grad_mlp, attended, grad_branch, grad_heads)


def add_rows(dst, a, b, rows):
    step = rows // 3 if rows % 48 == 0 and rows > 48 else rows

    def part(i, _):
        sl = pl.ds(pl.multiple_of(i * step, step), step)
        dst[sl, :] = a[sl, :] + b[sl, :]
        return 0

    lax.fori_loop(0, rows // step, part, 0)


class Line:
    def __init__(self, z, zt, groups, part, up, down, sems, t, p):
        self.z, self.zt, self.groups = z, zt, groups
        self.part, self.up, self.down = part, up, down
        us, ur, ds, dr = sems
        above = (t, lax.rem(p + SPAN, SPAN * groups))
        below = (t, lax.rem(p + SPAN * (groups - 1), SPAN * groups))
        self.up_first = lambda: remote(part, up, us, ur, above)
        self.up_next = lambda: remote(up, up, us, ur, above)
        self.down_first = lambda: remote(part, down, ds, dr, below)
        self.down_next = lambda: remote(down, down, ds, dr, below)

    def start(self):
        if self.zt > 0:
            pl.when(self.z == 0)(lambda: self.up_first().start())
        if self.zt < self.groups - 1:
            pl.when(self.z == self.groups - 1)(lambda: self.down_first().start())

    def relay(self, hop, rows):
        def up():
            self.up_next().wait_recv()
            add_rows(self.up, self.up, self.part, rows)
            self.up_next().start()

        def down():
            self.down_next().wait_recv()
            add_rows(self.down, self.down, self.part, rows)
            self.down_next().start()

        if 0 < hop < self.zt:
            pl.when(self.z == hop)(up)
        if self.zt < self.groups - 1 - hop:
            pl.when(self.z == self.groups - 1 - hop)(down)

    def finish(self, dst, rows):
        def done():
            if self.zt > 0:
                self.up_next().wait_recv()
            if self.zt < self.groups - 1:
                self.down_next().wait_recv()
            if 0 < self.zt < self.groups - 1:
                add_rows(self.up, self.up, self.down, rows)
            add_rows(dst, self.up if self.zt > 0 else self.down, self.part, rows)

        pl.when(self.z == self.zt)(done)

    def drain(self):
        if self.zt > 0:
            pl.when(self.z < self.zt)(lambda: self.up_first().wait_send())
        if self.zt < self.groups - 1:
            pl.when(self.z > self.zt)(lambda: self.down_first().wait_send())


def outward(groups):
    order = []
    lo, hi = 0, groups - 1
    while lo <= hi:
        order.append(hi)
        if lo < hi:
            order.append(lo)
        lo, hi = lo + 1, hi - 1
    return order


def finish_kernel(
    groups, ka_ref, kb_ref, kc_ref, ra_ref, rb_ref, rc_ref, wq_ref, gh_ref, gin_ref, tin_ref, gain_ref,
    pair_ref, tg_ref, out_ref, sum_ref,
    plane, line, nsend, nrecv,
    kvc, rvc, r2c, r3c, r4c, csem, cs, cr, kva, kvb, rva, rvb, r2a, r2b, ua, ub, da, db, isem, s2, q2, us, ur, ds, dr,
    gm_ref, wq, gh, g_ref, tok_ref, wsem, fs, fr,
    w2, sib, ub2, db2, fin, send, recv, ts, tr, us2, ur2, ds2, dr2, ps, pr, lsem,
):
    t, p, x, y, z = here()
    ex, ey, ed = plane_peers()
    peers = (ex, ey, ed)
    sibling = (1 - t, p)
    others = [(t, lax.rem(p + SPAN * k, SPAN * groups)) for k in range(1, groups)]
    across = tuple((1 - t, q[1]) for q in peers)
    order = outward(groups)
    colours = (
        (ey, ka_ref, ra_ref, kva, rva, r2a, ua, da, y),
        (ex, kb_ref, rb_ref, kvb, rvb, r2b, ub, db, x),
    )

    def loads(c, zt):
        peer, kr, rr, kv, rv = colours[c][:5]
        i = 2 * (c * groups + zt)
        return (
            pltpu.make_async_copy(kr.at[zt], kv.at[zt], isem.at[i]),
            pltpu.make_async_copy(rr.at[zt], rv.at[zt], isem.at[i + 1]),
        )

    level_loads = [
        [pltpu.make_async_copy(a.at[i], b.at[i], csem.at[2 * i + j]) for j, (a, b) in enumerate(((kc_ref, kvc), (rc_ref, rvc)))]
        for i in range(2)
    ]
    for pair in level_loads:
        for d in pair:
            d.start()
    mixed_loads = (pltpu.make_async_copy(gin_ref, g_ref, wsem.at[2]), pltpu.make_async_copy(tin_ref, tok_ref, wsem.at[3]))
    for i, zt in enumerate(order):
        for c in range(2):
            for d in loads(c, zt):
                d.start()
        if i == 1:
            for c in mixed_loads:
                c.start()
    more = (pltpu.make_async_copy(wq_ref, wq, wsem.at[0]), pltpu.make_async_copy(gh_ref, gh, wsem.at[1]))
    for c in more:
        c.start()
    greet(peers + across + (sibling,) + tuple(others))
    around = [remote(gain_ref, plane.at[i], nsend.at[i], nrecv.at[i], q) for i, q in enumerate(peers)]
    for c in around:
        c.start()

    def second(c, zt):
        peer, kr, rr, kv, rv, r2, u, d, mine = colours[c]
        i = c * groups + zt
        return remote(rv.at[zt, 1 - mine], r2.at[zt], s2.at[i], q2.at[i], peer)

    def chain(c, zt):
        peer, kr, rr, kv, rv, r2, u, d, mine = colours[c]
        i = c * groups + zt
        return Line(z, zt, groups, r2.at[zt], u.at[zt], d.at[zt],
                    (us.at[i], ur.at[i], ds.at[i], dr.at[i]), t, p)

    def size(c):
        return colours[c][3].shape[2]

    up = kvc.shape[2]

    def third(i, k):
        at = (k * 2 + 1 - x, (1 - y) * 2 + k)[i]
        n = 2 * i + k
        return remote(rvc.at[i, at], r2c.at[i, k], cs.at[n], cr.at[n], (ex, ey)[i])

    def fourth(i):
        at = (1 - y, 1 - x)[i]
        return remote(r2c.at[i, at], r3c.at[i], cs.at[4 + i], cr.at[4 + i], (ey, ex)[i])

    top = lax.div(z, 2)
    fifth = remote(r3c.at[1 - top], r4c, cs.at[6], cr.at[6], (t, p + 2 * SPAN - 4 * SPAN * top))

    def plus(dst, src, n):
        add_rows(dst, dst, src, n)

    def send_second(zt):
        for c in range(2):
            for d in loads(c, zt):
                d.wait()
            peer, kr, rr, kv, rv, r2, u, d, mine = colours[c]
            plus(rv.at[zt, 1 - mine], kv.at[zt, 1 - mine], size(c))
            second(c, zt).start()

    for i in range(2):
        for d in level_loads[i]:
            d.wait()
        for k in range(2):
            at = (k * 2 + 1 - x, (1 - y) * 2 + k)[i]
            plus(rvc.at[i, at], kvc.at[i, at], up)
            third(i, k).start()
    send_second(order[0])
    send_second(order[1])
    width = gm_ref.shape[0] // 3
    shards = SPAN * groups
    one = width // shards
    half = width // 2
    for c in mixed_loads:
        c.wait()
    for h in range(2):
        r = nn(g_ref[...], tok_ref[:, h * half : (h + 1) * half]).T
        w2[h * (shards // 2) : (h + 1) * (shards // 2)] = r.astype(bf).reshape(shards // 2, one, 3 * HW)

    def swap(zt):
        return remote(w2.at[pl.ds(zt * 4 + (1 - t) * 2, 2)], sib.at[zt], ts.at[zt], tr.at[zt], sibling)

    for zt in order:
        swap(zt).start()

    for i in range(2):
        for k in range(2):
            at = (k * 2 + x, y * 2 + k)[i]
            plus(rvc.at[i, at], kvc.at[i, at], up)
            third(i, k).wait_recv()
            plus(r2c.at[i, k], rvc.at[i, at], up)
        fourth(i).start()
    send_second(order[2])
    send_second(order[3])
    count = gm_ref.shape[1]
    me = lax.rem(p, SPAN)
    copies = []
    for i, peer in enumerate((peers[2], peers[0], peers[1])):
        m = lax.rem(peer[1], SPAN)
        for k in range(3):
            copies.append(remote(
                g_ref.at[pl.ds(k * HW, HW), pl.ds(pl.multiple_of(m * count, count), count)],
                gm_ref.at[pl.ds(pl.multiple_of(k * width + me * HW, HW), HW)],
                send.at[i * 3 + k], recv.at[i * 3 + k], peer,
            ))
    for k in range(3):
        copies.append(pltpu.make_async_copy(
            g_ref.at[pl.ds(k * HW, HW), pl.ds(pl.multiple_of(me * count, count), count)],
            gm_ref.at[pl.ds(pl.multiple_of(k * width + me * HW, HW), HW)],
            lsem.at[k],
        ))
    for c in copies:
        c.start()
    def chain2(zt, k):
        i = zt * 2 + k
        return Line(z, zt, groups, sib.at[zt, k], ub2.at[zt, k], db2.at[zt, k],
                    (us2.at[i], ur2.at[i], ds2.at[i], dr2.at[i]), t, p)

    for zt in order:
        swap(zt).wait_recv()
        for k in range(2):
            dst = sib.at[zt, k]
            add_rows(dst, dst, w2.at[zt * 4 + t * 2 + k], one)
            chain2(zt, k).start()
    for zt in order:
        for c in range(2):
            peer, kr, rr, kv, rv, r2, u, d, mine = colours[c]
            keep = rv.at[zt, mine]
            add_rows(keep, keep, kv.at[zt, mine], size(c))

    def in_plane(zt):
        for c in range(2):
            peer, kr, rr, kv, rv, r2, u, d, mine = colours[c]
            second(c, zt).wait_recv()
            dst = r2.at[zt]
            add_rows(dst, dst, rv.at[zt, mine], size(c))
            chain(c, zt).start()

    def relay(zt, hop):
        for c in range(2):
            chain(c, zt).relay(hop, size(c))


    def relay2(hop):
        for zt in order:
            for k in range(2):
                chain2(zt, k).relay(hop, one)

    in_plane(order[0])
    relay2(1)
    in_plane(order[1])
    for i in range(2):
        fourth(i).wait_recv()
        plus(r3c.at[i], r2c.at[i, (y, x)[i]], up)
    fifth.start()
    relay(order[0], 1)
    relay2(2)
    for c in around:
        c.wait()
    line[0] = (gain_ref[...] + plane[0]) + (plane[1] + plane[2])
    ring = [
        remote(line.at[0], line.at[1 + k], nsend.at[3 + k], nrecv.at[3 + k], q) for k, q in enumerate(others)
    ]
    for c in ring:
        c.start()
    in_plane(order[2])
    relay(order[1], 1)
    in_plane(order[3])
    relay(order[0], 2)
    relay(order[2], 1)
    relay(order[1], 2)
    relay(order[3], 1)
    for zt in order:
        for k in range(2):
            chain2(zt, k).finish(fin.at[k], one)
    here_id = t * SPAN + me

    def hand(k, tt):
        m = t * 2 + k
        peer = (tt, z * SPAN + m)
        i = k * 2 + tt
        away = lambda: remote(fin.at[k], out_ref.at[me], ps.at[i], pr.at[me], peer)
        stay = lambda: pltpu.make_async_copy(fin.at[k], out_ref.at[me], lsem.at[3])
        return away, stay, (tt * SPAN + m) == here_id

    for k in range(2):
        for tt in range(2):
            away, stay, same = hand(k, tt)
            pl.when(jnp.logical_not(same))(lambda away=away: away().start())
            pl.when(same)(lambda stay=stay: stay().start())
    for c in ring:
        c.wait()
    total = line[0]
    for k in range(1, groups):
        total = total + line[k]
    line[groups] = total
    gained = remote(line.at[groups], line.at[groups + 1], nsend.at[2 + groups], nrecv.at[2 + groups], sibling)
    gained.start()
    for c in copies + list(more):
        c.wait()
    turned = nn(wq[...], gm_ref[...]).T
    gh[...] = gh[...] + turned
    result = pltpu.make_async_copy(gh, tg_ref, wsem.at[4])
    result.start()
    fifth.wait_recv()
    add_rows(pair_ref.at[t, pl.ds(size(0) + size(1), up)], r3c.at[top], r4c, up)
    for zt in order:
        for c, sl in ((0, pl.ds(0, size(0))), (1, pl.ds(size(0), size(1)))):
            chain(c, zt).finish(pair_ref.at[t, sl], size(c))
    last = remote(pair_ref.at[t], pair_ref.at[t], fs.at[0], fr.at[0], sibling)
    last.start()
    for s in range(SPAN):
        from_here = jnp.logical_and(s == me, y == t)
        pl.when(jnp.logical_not(from_here))(
            lambda s=s: remote(fin.at[0], out_ref.at[s], ps.at[0], pr.at[s], sibling).wait_recv()
        )
    for k in range(2):
        for tt in range(2):
            away, stay, same = hand(k, tt)
            pl.when(jnp.logical_not(same))(lambda away=away: away().wait_send())
            pl.when(same)(lambda stay=stay: stay().wait())
    for zt in range(groups):
        swap(zt).wait_send()
        for k in range(2):
            chain2(zt, k).drain()
        for c in range(2):
            second(c, zt).wait_send()
            chain(c, zt).drain()
    for i in range(2):
        for k in range(2):
            third(i, k).wait_send()
        fourth(i).wait_send()
    fifth.wait_send()
    gained.wait()
    sum_ref[...] = line[groups] + line[groups + 1]
    result.wait()
    last.wait()


def finish(ka, kb, kc, ra, rb, rc, wq, gh, g, tok, gains, groups):
    width = tok.shape[1]
    count = tok.shape[0] // SPAN
    one = width // (SPAN * groups)
    na, nb, nc = ka.shape[2], kb.shape[2], kc.shape[2]
    half = ka.shape[3]
    buf = lambda *n: pltpu.VMEM(n, bf)
    mix = lambda *n: pltpu.VMEM(n + (one, 3 * HW), bf)
    return pl.pallas_call(
        functools.partial(finish_kernel, groups),
        out_shape=(
            jax.ShapeDtypeStruct((2, na + nb + nc, half), bf),
            jax.ShapeDtypeStruct((count, width), f32),
            jax.ShapeDtypeStruct((SPAN, one, 3 * HW), bf),
            jax.ShapeDtypeStruct(gains.shape, f32),
        ),
        in_specs=[ANY] * 10 + [VM],
        out_specs=(VM, ANY, VM, VM),
        scratch_shapes=[
            pltpu.VMEM((3,) + gains.shape, f32), pltpu.VMEM((groups + 2,) + gains.shape, f32),
            dma_sems(3 + groups), dma_sems(3 + groups),
            buf(2, SPAN, nc, half), buf(2, SPAN, nc, half), buf(2, 2, nc, half), buf(2, nc, half), buf(nc, half),
            dma_sems(4), dma_sems(7), dma_sems(7),
            buf(groups, 2, na, half), buf(groups, 2, nb, half), buf(groups, 2, na, half), buf(groups, 2, nb, half),
            buf(groups, na, half), buf(groups, nb, half), buf(groups, na, half), buf(groups, nb, half),
            buf(groups, na, half), buf(groups, nb, half),
            dma_sems(4 * groups), dma_sems(2 * groups), dma_sems(2 * groups),
            dma_sems(2 * groups), dma_sems(2 * groups), dma_sems(2 * groups), dma_sems(2 * groups),
            buf(3 * width, count), buf(width, 3 * width), pltpu.VMEM((count, width), f32),
            buf(*g.shape), buf(*tok.shape), dma_sems(5),
            dma_sems(1), dma_sems(1),
            mix(SPAN * groups), mix(groups, 2), mix(groups, 2), mix(groups, 2), mix(2),
            dma_sems(9), dma_sems(9), dma_sems(groups), dma_sems(groups),
            dma_sems(2 * groups), dma_sems(2 * groups), dma_sems(2 * groups), dma_sems(2 * groups),
            dma_sems(4), dma_sems(SPAN), dma_sems(4),
        ],
        compiler_params=comm_params(3),
        name="finish",
    )(ka, kb, kc, ra, rb, rc, wq, gh, g, tok, gains)


def unfold_kernel(
    groups, pair_ref, part_ref, grad_ref, score_ref, gain_ref, lost_ref,
    gate_ref, up_ref, down_ref, out_ref, qkv_ref, token_ref, scores_ref, loss_ref, *gains_refs,
):
    one = out_ref.shape[0]
    half = pair_ref.shape[2]
    width = 2 * half
    steps = gate_ref.shape[1] // half
    down = down_ref.shape[0]
    token_ref[0] = grad_ref[...]
    third = one // 3
    ends = ((steps - UPWARD) * one, (steps - UPWARD) * one + third + down, pair_ref.shape[1] - third)
    for j in range(steps):
        at = j * one + (0 if j < steps - UPWARD else down + 2 * third)
        for k, ref in enumerate((gate_ref, up_ref)):
            ref[:, j * half : (j + 1) * half] = pair_ref[k, at : at + one, :].astype(f32)
    for k in range(2):
        cols = slice(k * half, (k + 1) * half)
        down_ref[:, cols] = pair_ref[k, ends[1] - down : ends[1], :].astype(f32)
        for i, at in enumerate(ends):
            out_ref[i * third : (i + 1) * third, cols] = pair_ref[k, at : at + third, :].astype(f32)
    for k in range(3):
        row = [part_ref[s, :, k * HW : (k + 1) * HW].astype(f32) for s in range(SPAN)]
        qkv_ref[:, k * width : (k + 1) * width] = jnp.concatenate(row, 1)
    docs, size = scores_ref.shape[0], score_ref.shape[0]
    dot = functools.partial(lax.dot_general, precision=precise, preferred_element_type=f32)
    row = lax.broadcasted_iota(jnp.int32, (docs, size), 0)
    col = lax.broadcasted_iota(jnp.int32, (docs, size), 1)
    pick = jnp.where(row // DOCS_GRP * 8 + lax.rem(row, DOCS_GRP) == col, 1.0, 0.0)
    some = dot(pick, score_ref[...], (((1,), (0,)), ((), ())))
    scores_ref[...] = dot(some, pick, (((1,), (1,)), ((), ())))
    row = lax.broadcasted_iota(jnp.int32, (width, one), 0)
    col = lax.broadcasted_iota(jnp.int32, (width, one), 1)
    mine = jnp.where(row == lax.axis_index("dp") * one + col, 1.0, 0.0)
    gains = dot(gain_ref[...], mine, (((1,), (0,)), ((), ())))
    for k, ref in enumerate(gains_refs):
        ref[...] = gains[k : k + 1, :]
    loss_ref[...] = lost_ref[0:1, 0:1]


def unfold(pair, parts, grad, scores, gains, loss, tiles, groups):
    one = parts.shape[1]
    half = pair.shape[2]
    width = 2 * half
    docs = groups * DOCS_GRP
    sds = jax.ShapeDtypeStruct
    return pl.pallas_call(
        functools.partial(unfold_kernel, groups),
        out_shape=(
            sds((one, tiles * width), f32), sds((one, tiles * width), f32), sds((tiles * one, width), f32),
            sds((one, width), f32), sds((one, 3 * width), f32), sds((1,) + grad.shape, f32),
            sds((docs, docs), f32), sds((1, 1), f32),
        )
        + (sds((1, one), f32),) * 4,
        in_specs=[VM] * 6,
        out_specs=(VM,) * 12,
        name="unfold",
    )(pair, parts, grad, scores, gains, loss)


def angle_bases():
    half = HEAD_DIM // 2
    freqs = np.float32(1000.0) ** (-np.arange(half, dtype=np.float32) / np.float32(half))
    steps = np.arange(128, dtype=np.float64)
    far = freqs[:, None].astype(np.float64) * (128.0 * steps)[None, :]
    near = freqs[:, None].astype(np.float64) * steps[None, :]
    return np.stack([np.cos(far), np.sin(far), np.cos(near), np.sin(near)]).astype(np.float32)


def spread_sum(value):
    part = lax.psum_scatter(value, "dp", scatter_dimension=0, tiled=True)
    return lax.psum(part.astype(bf), "tower").astype(f32)


def local(
    tokens, doc_ids, pad_mask, targets, w_qkv, w_out, ln1_gain, ln1_bias,
    w_gate, w_up, w_down, ln2_gain, ln2_bias,
):
    width = w_out.shape[0]
    rows = tokens[0]
    count = rows.shape[0]
    places = lax.axis_size("dp")
    groups = places // SPAN
    tower = lax.axis_index("tower")
    place = lax.axis_index("dp")
    me = place % SPAN
    docs = groups * DOCS_GRP
    base = angle_bases()
    tok_all, codes, qa, ka, va, kt, heads, lse, exact = gather(rows, doc_ids, pad_mask, base, w_qkv)
    norms = (ln1_gain, ln1_bias, ln2_gain, ln2_bias)
    (
        attended, inner, hidden, grad_mlp, grads, grad_branch, grad_attended, grad_h1, gains, scores_all, loss
    ) = block(heads, rows, codes, targets, norms, w_out, w_gate, w_up, w_down, groups)
    by_hand = groups == 4 and width % (48 * places) == 0
    if by_hand:
        send_a, keep_a, send_b, keep_b, send_c, keep_c, d_heads = weight_grads(
            groups, grad_attended, inner, grads, hidden, grad_mlp, attended, grad_branch
        )
        exchange = lambda v, bit: lax.ppermute(v, "dp", [(i, i ^ bit) for i in range(places)])
        came_a, came_b, came_c = exchange(send_a, 1), exchange(send_b, 2), exchange(send_c, SPAN)
    else:
        d_heads = tokens_to_heads(grad_attended, 5, "to_heads")
    mixed = attn_bwd(d_heads, exact, lse, qa, ka, va, kt, base, codes)
    if by_hand:
        pair, grad_tokens, qkv_parts, gain_sums = finish(
            keep_a, keep_b, keep_c, came_a, came_b, came_c, w_qkv, grad_h1, mixed, tok_all, gains, groups
        )
        gate_out, up_out, down_out, out_out, qkv_out, token_grad, scores, loss, *gains_out = unfold(
            pair, qkv_parts, grad_tokens, scores_all, gain_sums, loss, w_gate.shape[1] // width, groups
        )
        gains_out = [v.reshape(-1) for v in gains_out]
    else:
        grad_mixed = heads_to_tokens(mixed, 6, "to_tokens_back")
        qkv_out = spread_sum(tn(rows, grad_mixed.T))
        side = lambda v: lax.psum_scatter(v, "dp", scatter_dimension=0, tiled=True)
        halves = lambda v: lax.all_gather(side(v).astype(bf), "tower", axis=1, tiled=True).astype(f32)
        both = lambda a, b: tn(a[0], b[0]) + tn(a[1], b[1])
        flat = lambda v: v.transpose(0, 2, 1, 3).reshape(2, count, -1)
        out_out = halves(nn(attended[0], grad_branch[0]) + nn(attended[1], grad_branch[1]))
        two = lax.all_gather(side(both(inner, flat(grads))).astype(bf), "tower").astype(f32)
        gate_out, up_out = two[0], two[1]
        down_out = halves(both(flat(hidden), grad_mlp))
        gains_out = spread_sum(gains[:4].T).T
        scores = scores_all.reshape(groups, 8, groups, 8)[:, :DOCS_GRP, :, :DOCS_GRP].reshape(docs, docs)
        token_grad = grad_h1 + lax.dot_general(
            grad_mixed, w_qkv, (((0,), (1,)), ((), ())), preferred_element_type=f32
        )
        token_grad = token_grad[None]
    return (
        scores, loss[0, 0], token_grad, qkv_out, out_out, gains_out[0], gains_out[1],
        gate_out, up_out, down_out, gains_out[2], gains_out[3],
    )


def solution(mesh):
    shard = P("dp", None)
    lone = P("dp")
    return jax.shard_map(
        local,
        mesh=mesh,
        in_specs=(P("tower", "dp", None), P("tower", "dp"), P("tower", "dp")) + (P(),) * 10,
        out_specs=(
            P(), P(), P("tower", "dp", None), shard, shard, lone, lone, shard, shard, shard, lone, lone,
        ),
        check_vma=False,
    )
```
